32 devices in a mesh: seq: 16 (over z, y, core), head: 2 (over x).
Axes of the slice: x: 2, y: 2, z: 4, core: 2. Of those that a mesh axis runs over, the one named last changes fastest.
Arguments:
- tokens: bfloat16 [16384, 768], P(('seq', 'head')), may hold values from -6 to 6
- w_query: bfloat16 [768, 768], replicated, may hold values from -0.3125 to 0.3125
- w_key: bfloat16 [768, 768], replicated, may hold values from -0.21875 to 0.21875
- w_value: bfloat16 [768, 768], replicated, may hold values from -0.21875 to 0.21875
- w_out: bfloat16 [768, 768], replicated, may hold values from -3.5 to 3.5
- gain_attn: float32 [768], replicated, may hold values from 0.5 to 1.5
- shift_attn: float32 [768], replicated, may hold values from -3 to 3
- w_up: bfloat16 [768, 3072], replicated, may hold values from -0.21875 to 0.21875
- w_down: bfloat16 [3072, 768], replicated, may hold values from -0.109375 to 0.109375
- gain_mlp: float32 [768], replicated, may hold values from 0.5 to 1.5
- shift_mlp: float32 [768], replicated, may hold values from -3 to 3
- cotangent: bfloat16 [16384, 768], P(('seq', 'head')), may hold values from -6 to 6
- lengths: int32 [8], replicated, may hold values from 1 to 64, 256 in all
- seq_order: int32 [8], replicated, may hold values from 0 to 7, each once
- rand_blocks: int32 [256, 3], P('seq'), may hold values from 0 to 65535
Outputs:
- output: bfloat16 [16384, 768], P(('seq', 'head'))
- grad_tokens: float32 [16384, 768], P(('seq', 'head'))
- grad_w_query: float32 [768, 768], P('seq')
- grad_w_key: float32 [768, 768], P('seq')
- grad_w_value: float32 [768, 768], P('seq')
- grad_w_out: float32 [768, 768], P('seq')
- grad_gain_attn: float32 [768], P('seq')
- grad_shift_attn: float32 [768], P('seq')
- grad_w_up: float32 [768, 3072], P('seq')
- grad_w_down: float32 [3072, 768], P('seq')
- grad_gain_mlp: float32 [768], P('seq')
- grad_shift_mlp: float32 [768], P('seq')
The draws below stay inside these ranges and needn't reach their ends.
Inputs may be any that keep to these rules, and one draw needn't show every extreme that they name: lengths of the 8 sequences in blocks of 64 tokens; they sum to 256 and the longest is exactly 64. `seq_order`: each of 0 to 7 once.
All inputs are finite; a program needn't handle non-finite values.
Results may differ from the reference program's by a relative error of at most 0.017.
Values may be sent and summed in bfloat16 or wider, within the bound.
A program may use at most 320 MiB of HBM per device.

```python
import math
import jax
import jax.numpy as jnp
import numpy as np
from jax import lax

D = 768
H = 12
DH = 64
FF = 3072
BLK = 64
NRAND = 3
MAXB = 64
TOKENS = 16384
NB = 256
SEQS = 8


def touch_ends(entries, key, least, top_value):
    spot = [jax.random.randint(jax.random.fold_in(key, axis), (), 0, length) for axis, length in enumerate(entries.shape)]
    main_axis = entries.shape.index(max(entries.shape))
    neighbour = spot[:main_axis] + [(spot[main_axis] + 1) % entries.shape[main_axis]] + spot[main_axis + 1:]
    return entries.at[tuple(spot)].set(least).at[tuple(neighbour)].set(top_value)


def steps_of(key, dims, shards, smallest, top_value):
    loudness, own = 1.0, jax.random.fold_in(key, 6)
    for axis_at, blocks in shards:
        draws = jnp.exp(jax.random.uniform(jax.random.fold_in(own, axis_at), (blocks,), jnp.float32, smallest / len(shards), top_value / len(shards)))
        loudness = loudness * jnp.repeat(draws, dims[axis_at] // blocks).reshape([-1 if axis == axis_at else 1 for axis in range(len(dims))])
    return loudness


def profile(amount, total, bound, slope):
    weights = [(1 << 20) // math.isqrt(grade ** slope) + 1 for grade in range(2, amount + 1)]
    rest, counts = total - bound - (amount - 1), [1] * (amount - 1)
    while rest > 0:
        candidates = [i for i in range(amount - 1) if counts[i] < bound]
        pool, left = sum([weights[i] for i in candidates]), rest
        for i in candidates:
            addition = min(bound - counts[i], max(1, left * weights[i] // pool), rest)
            counts[i] = counts[i] + addition
            rest = rest - addition
    return np.array([bound] + counts)


def ragged_sizes(stream_key, number_of, total, limit, skew):
    if number_of == 2:
        one = jax.random.randint(stream_key, (), max(1, total - limit), min(limit, total - 1) + 1)
        return jnp.stack([one, total - one])
    sizes = jnp.asarray(profile(number_of, total, limit, skew), jnp.int32)
    pairs = (number_of - 1) // 2
    donor, sink = sizes[1:1 + 2 * pairs:2], sizes[2:2 + 2 * pairs:2]
    room = jnp.minimum(donor - 1, limit - sink)
    passed = jax.random.randint(jax.random.fold_in(stream_key, 1), (pairs,), 0, 1 << 20) % (room + 1)
    sizes = sizes.at[1:1 + 2 * pairs:2].set(donor - passed).at[2:2 + 2 * pairs:2].set(sink + passed)
    return sizes[jax.random.permutation(jax.random.fold_in(stream_key, 2), number_of)]


def centred(stream_key, extent, scale, most, shards=(), held_as=jnp.bfloat16):
    loudness = steps_of(stream_key, extent, shards, -0.22, 0.18) if shards else 1.0
    entries = jax.random.normal(stream_key, extent, jnp.float32) * scale * loudness
    return jnp.minimum(jnp.maximum(entries, -most), most).astype(held_as)


def setup_inputs(seed: int = 0) -> dict:
    arg_keys = jax.random.split(jax.random.key(seed), 16)
    tokens = centred(arg_keys[0], (TOKENS, D), 1.0, 6.0, ((0, 32),))
    w_query = centred(arg_keys[1], (D, D), (D // 2) ** -0.5, 0.3125)
    w_key = centred(arg_keys[2], (D, D), D ** -0.5, 0.21875)
    w_value = centred(arg_keys[3], (D, D), D ** -0.5, 0.21875)
    w_out = centred(arg_keys[4], (D, D), (max(1, D // 256)) ** -0.5, 3.5)
    gain_attn = jnp.clip(1.0 + 0.1 * jax.random.normal(arg_keys[5], (D,), jnp.float32), 0.5, 1.5)
    shift_attn = centred(arg_keys[6], (D,), 0.5, 3.0, (), jnp.float32)
    w_up = centred(arg_keys[7], (D, FF), D ** -0.5, 0.21875)
    w_down = centred(arg_keys[8], (FF, D), FF ** -0.5, 0.109375)
    gain_mlp = jnp.clip(1.0 + 0.1 * jax.random.normal(arg_keys[9], (D,), jnp.float32), 0.5, 1.5)
    shift_mlp = centred(arg_keys[10], (D,), 0.5, 3.0, (), jnp.float32)
    cotangent = centred(arg_keys[11], (TOKENS, D), 1.0, 6.0, ((0, 32),))
    lengths = ragged_sizes(arg_keys[12], SEQS, NB, MAXB, 2).astype(jnp.int32)
    seq_order = jax.random.permutation(arg_keys[13], SEQS).astype(jnp.int32)
    rand_blocks = touch_ends(jax.random.randint(arg_keys[14], (NB, NRAND), 0, 65536), jax.random.fold_in(arg_keys[14], 1), 0, 65535).astype(jnp.int32)
    return dict(tokens=tokens, w_query=w_query, w_key=w_key, w_value=w_value, w_out=w_out, gain_attn=gain_attn, shift_attn=shift_attn, w_up=w_up, w_down=w_down, gain_mlp=gain_mlp, shift_mlp=shift_mlp, cotangent=cotangent, lengths=lengths, seq_order=seq_order, rand_blocks=rand_blocks)


eps_norm = 1e-06
highest = lax.Precision.HIGHEST

@jax.custom_vjp
def low(v):
    return lax.optimization_barrier(v.astype(jnp.bfloat16)).astype(jnp.float32)

@jax.custom_vjp
def low_back(v):
    return v

def low_keep(v):
    return (low(v), None)

def low_pass(kept, grad):
    return (grad,)

def back_keep(v):
    return (v, None)

def back_low(kept, grad):
    return (low(grad),)
low.defvjp(low_keep, low_pass)
low_back.defvjp(back_keep, back_low)

def both_ways(values):
    return low(low_back(values))

def block_slots(blocks, rand_rows, lengths, seq_order):
    seq_count = lengths.shape[0]
    seq_ids = jnp.arange(seq_count, dtype=jnp.int32)
    packed = lax.optimization_barrier(jnp.sum(jnp.where(seq_order[:, None] == seq_ids[None, :], lengths[None, :], 0), axis=1)).astype(jnp.int32)
    seq_ends = jnp.cumsum(packed).astype(jnp.int32)
    starts = (seq_ends - packed).astype(jnp.int32)
    holder = lax.optimization_barrier(jnp.sum((seq_ends[None, :] <= blocks[:, None]).astype(jnp.int32), axis=1)).astype(jnp.int32)
    chosen = holder[:, None] == seq_ids[None, :]
    seq_first = lax.optimization_barrier(jnp.sum(jnp.where(chosen, starts[None, :], 0), axis=1)).astype(jnp.int32)
    seq_span = lax.optimization_barrier(jnp.sum(jnp.where(chosen, packed[None, :], 0), axis=1)).astype(jnp.int32)
    offset = (blocks - seq_first).astype(jnp.int32)
    rand_pos = (seq_first[:, None] + jnp.mod(rand_rows, seq_span[:, None])).astype(jnp.int32)
    fixed_cand = jnp.stack([blocks - 1, blocks, blocks + 1, seq_first, seq_first + seq_span - 1], axis=1).astype(jnp.int32)
    candidate = jnp.concatenate([fixed_cand, rand_pos], axis=1).astype(jnp.int32)
    fixed_live = jnp.stack([offset > 0, offset >= 0, offset < seq_span - 1, offset >= 0, offset >= 0], axis=1)
    usable = jnp.concatenate([fixed_live, rand_pos >= 0], axis=1)
    kept_list = []
    for column in range(candidate.shape[1]):
        unique = usable[:, column]
        for earlier in range(column):
            unique = unique & jnp.logical_not(kept_list[earlier] & (candidate[:, earlier] == candidate[:, column]))
        kept_list.append(unique)
    is_live = jnp.stack(kept_list, axis=1)
    key_blocks = jnp.where(is_live, candidate, blocks[:, None]).astype(jnp.int32)
    return (key_blocks, is_live)

def layer_norm(values, gain_vec, shift_vec):
    center = values - lax.optimization_barrier(jnp.mean(values, axis=-1, keepdims=True))
    spread = lax.optimization_barrier(jnp.mean(center * center, axis=-1, keepdims=True))
    return center * lax.rsqrt(spread + eps_norm) * gain_vec + shift_vec

def attend_group(q_group, index_group, live_group, key_all, value_all):
    key_rows = key_all[index_group]
    value_rows = value_all[index_group]
    scores = jnp.einsum('cqhd,cskhd->chqsk', q_group, key_rows, precision=highest) * DH ** (-0.5)
    scores = low_back(scores)
    scores = jnp.where(live_group[:, None, None, :, None], scores, -1e+30)
    flat_scores = scores.reshape(scores.shape[0], scores.shape[1], scores.shape[2], -1)
    attn_probs = low(jax.nn.softmax(flat_scores, axis=-1)).reshape(scores.shape)
    return jnp.einsum('chqsk,cskhd->cqhd', attn_probs, value_rows, precision=highest)

def reference(tokens, w_query, w_key, w_value, w_out, gain_attn, shift_attn, w_up, w_down, gain_mlp, shift_mlp, cotangent, lengths, seq_order, rand_blocks):
    blocks = jnp.arange(NB, dtype=jnp.int32)
    key_blocks, is_live = block_slots(blocks, rand_blocks, lengths, seq_order)
    groups = NB // 64
    slot_count = key_blocks.shape[1]
    index_groups = key_blocks.reshape(groups, 64, slot_count)
    live_groups = is_live.reshape(groups, 64, slot_count)

    def forward(tok_in, wq_in, wk_in, wv_in, wo_in, g_one, e_one, wu_in, wd_in, g_two, e_two):
        queries = both_ways(jnp.dot(tok_in, wq_in, precision=highest))
        keys_proj = both_ways(jnp.dot(tok_in, wk_in, precision=highest))
        values_proj = both_ways(jnp.dot(tok_in, wv_in, precision=highest))
        q_groups = queries.reshape(groups, 64, BLK, H, DH)
        key_all = keys_proj.reshape(NB, BLK, H, DH)
        value_all = values_proj.reshape(NB, BLK, H, DH)

        def one_group(pieces):
            return attend_group(pieces[0], pieces[1], pieces[2], key_all, value_all)
        context = lax.map(jax.checkpoint(one_group), (q_groups, index_groups, live_groups))
        context = both_ways(context.reshape(TOKENS, D))
        attn_out = low_back(jnp.dot(context, wo_in, precision=highest))
        normed = layer_norm(tok_in + attn_out, g_one, e_one)
        hidden_pre = low_back(jnp.dot(low(normed), wu_in, precision=highest))
        hidden = low(jax.nn.gelu(hidden_pre, approximate=True))
        mlp_out = low_back(jnp.dot(hidden, wd_in, precision=highest))
        return layer_norm(normed + mlp_out, g_two, e_two)
    inputs = (tokens.astype(jnp.float32), w_query.astype(jnp.float32), w_key.astype(jnp.float32), w_value.astype(jnp.float32), w_out.astype(jnp.float32), gain_attn.astype(jnp.float32), shift_attn.astype(jnp.float32), w_up.astype(jnp.float32), w_down.astype(jnp.float32), gain_mlp.astype(jnp.float32), shift_mlp.astype(jnp.float32))
    result, pullback = jax.vjp(forward, *inputs)
    gradients = pullback(cotangent.astype(jnp.float32))
    return (result.astype(jnp.bfloat16), gradients[0], gradients[1], gradients[2], gradients[3], gradients[4], gradients[5], gradients[6], gradients[7], gradients[8], gradients[9], gradients[10])
```

```python
import functools

import jax
import jax.numpy as jnp
from jax import lax
from jax.experimental import pallas as pl
from jax.experimental.pallas import tpu as pltpu
from jax.sharding import PartitionSpec as P

DH = 64
BLK = 64
MAXB = 64
SLOTS = 8
HG = 3
WQ = HG * DH
WIN = 256
AXES = ("seq", "head")
NEG = -1e30

eps_norm = 1e-06


def xor_swap(value, bits):
    count = lax.axis_size("seq") * lax.axis_size("head")
    return lax.ppermute(value, AXES, [(d, d ^ bits) for d in range(count)])


def plane_shift(value, steps):
    count = lax.axis_size("seq") * lax.axis_size("head")
    gap = 8 * steps
    return lax.ppermute(
        value, AXES, [(d, d + gap) for d in range(count) if 0 <= d + gap < count]
    )


def block_slots(blocks, rand_rows, lengths, seq_order):
    seq_count = lengths.shape[0]
    seq_ids = jnp.arange(seq_count, dtype=jnp.int32)
    packed = jnp.sum(jnp.where(seq_order[:, None] == seq_ids[None, :], lengths[None, :], 0), axis=1)
    seq_ends = jnp.cumsum(packed)
    starts = seq_ends - packed
    holder = jnp.sum((seq_ends[None, :] <= blocks[:, None]).astype(jnp.int32), axis=1)
    chosen = holder[:, None] == seq_ids[None, :]
    seq_first = jnp.sum(jnp.where(chosen, starts[None, :], 0), axis=1)
    seq_span = jnp.sum(jnp.where(chosen, packed[None, :], 0), axis=1)
    offset = blocks - seq_first
    rand_pos = seq_first[:, None] + jnp.mod(rand_rows, seq_span[:, None])
    fixed_cand = jnp.stack(
        [blocks - 1, blocks, blocks + 1, seq_first, seq_first + seq_span - 1], axis=1
    )
    candidate = jnp.concatenate([fixed_cand, rand_pos], axis=1)
    fixed_live = jnp.stack(
        [offset > 0, offset >= 0, offset < seq_span - 1, offset >= 0, offset >= 0], axis=1
    )
    usable = jnp.concatenate([fixed_live, rand_pos >= 0], axis=1)
    kept_list = []
    for column in range(candidate.shape[1]):
        unique = usable[:, column]
        for earlier in range(column):
            unique = unique & jnp.logical_not(
                kept_list[earlier] & (candidate[:, earlier] == candidate[:, column])
            )
        kept_list.append(unique)
    is_live = jnp.stack(kept_list, axis=1)
    key_blocks = jnp.where(is_live, candidate, blocks[:, None])
    return (key_blocks, is_live)


def norm_forward(values, gain_vec, shift_vec):
    center = values - jnp.mean(values, axis=-1, keepdims=True)
    spread = jnp.mean(center * center, axis=-1, keepdims=True)
    inv_dev = lax.rsqrt(spread + eps_norm)
    x_hat = center * inv_dev
    return (x_hat * gain_vec + shift_vec, x_hat, inv_dev)


def norm_backward(grad_in, x_hat, inv_dev, gain_vec):
    grad_gain = jnp.sum(grad_in * x_hat, axis=0)
    grad_shift = jnp.sum(grad_in, axis=0)
    grad_hat = grad_in * gain_vec
    grad_mean = jnp.mean(grad_hat, axis=-1, keepdims=True)
    grad_proj = jnp.mean(grad_hat * x_hat, axis=-1, keepdims=True)
    return (inv_dev * (grad_hat - grad_mean - x_hat * grad_proj), grad_gain, grad_shift)


def gelu_tanh(values):
    return jax.nn.gelu(values, approximate=True)


def lane_groups(rows, offset):
    lane = lax.broadcasted_iota(jnp.int32, (rows, WIN), 1) - offset
    return [jnp.logical_and(lane >= h * DH, lane < (h + 1) * DH) for h in range(HG)]


def spread_heads(block, offset):
    zero = jnp.zeros_like(block)
    return jnp.concatenate([jnp.where(m, block, zero) for m in lane_groups(BLK, offset)], axis=0)


def fold_heads(stacked, offset):
    masks = lane_groups(BLK, offset)
    total = jnp.where(masks[0], stacked[:BLK], 0.0)
    for h in range(1, HG):
        total = total + jnp.where(masks[h], stacked[h * BLK : (h + 1) * BLK], 0.0)
    return total


def fetch(pieces, kv, sems):
    rows = pieces[0].shape[0]
    for n, piece in enumerate(pieces):
        pltpu.make_async_copy(piece, kv.at[pl.ds(n * rows, rows)], sems.at[n]).start()
    for n, piece in enumerate(pieces):
        pltpu.make_async_copy(piece, kv.at[pl.ds(n * rows, rows)], sems.at[n]).wait()


def nt(a, b):
    return lax.dot_general(a, b, (((1,), (1,)), ((), ())), preferred_element_type=jnp.float32)


def tn(a, b):
    return lax.dot_general(a, b, (((0,), (0,)), ((), ())), preferred_element_type=jnp.float32)


def forward_kernel(idx_ref, bias_ref, q_ref, *refs):
    pieces, ctx_ref, kv, sems = refs[:6], refs[6], refs[7], refs[8]
    fetch(pieces, kv, sems)

    def step(i, carry):
        q_rows = pl.multiple_of(i * BLK, BLK)
        qexp = spread_heads(q_ref[pl.ds(q_rows, BLK), :], 0)
        rows = [
            pl.multiple_of(idx_ref[i * SLOTS + s] * BLK, BLK) for s in range(SLOTS)
        ]
        keys = jnp.concatenate([kv[pl.ds(r, BLK), 0:WIN] for r in rows], axis=0)
        values = jnp.concatenate([kv[pl.ds(r, BLK), 128 : 128 + WIN] for r in rows], axis=0)
        scores = nt(qexp, keys) + bias_ref[pl.ds(i, 1), :]
        top = jnp.max(scores, axis=1, keepdims=True)
        e = jnp.exp(scores - top)
        total = jnp.sum(e, axis=1, keepdims=True)
        out = jnp.dot(e.astype(jnp.bfloat16), values, preferred_element_type=jnp.float32)
        ctx_ref[pl.ds(q_rows, BLK), :] = fold_heads(out / total, 64).astype(jnp.bfloat16)
        return carry

    lax.fori_loop(0, q_ref.shape[0] // BLK, step, 0)


def backward_kernel(idx_ref, live_ref, q_ref, do_ref, *refs):
    pieces, dq_ref, outs = refs[:6], refs[6], refs[7:13]
    kv, acc, sems = refs[13:]
    rows_piece = pieces[0].shape[0]

    def clear(n, carry):
        acc[pl.ds(pl.multiple_of(n * 256, 256), 256), :] = jnp.zeros((256, 2 * WQ), jnp.float32)
        return carry

    for n, piece in enumerate(pieces):
        pltpu.make_async_copy(piece, kv.at[pl.ds(n * rows_piece, rows_piece)], sems.at[n]).start()
    lax.fori_loop(0, acc.shape[0] // 256, clear, 0)
    for n, piece in enumerate(pieces):
        pltpu.make_async_copy(piece, kv.at[pl.ds(n * rows_piece, rows_piece)], sems.at[n]).wait()

    def step(i, carry):
        q_rows = pl.multiple_of(i * BLK, BLK)
        qexp = spread_heads(q_ref[pl.ds(q_rows, BLK), :], 0)
        doexp = spread_heads(do_ref[pl.ds(q_rows, BLK), :], 64)
        rows = [
            pl.multiple_of(idx_ref[i * SLOTS + s] * BLK, BLK) for s in range(SLOTS)
        ]
        keys = jnp.concatenate([kv[pl.ds(r, BLK), 0:WIN] for r in rows], axis=0)
        values = jnp.concatenate([kv[pl.ds(r, BLK), 128 : 128 + WIN] for r in rows], axis=0)
        raw = nt(keys, qexp)
        scores = jnp.concatenate(
            [
                jnp.where(live_ref[i * SLOTS + s] > 0, raw[s * BLK : (s + 1) * BLK], NEG)
                for s in range(SLOTS)
            ],
            axis=0,
        )
        top = jnp.max(scores, axis=0, keepdims=True)
        e = jnp.exp(scores - top)
        probs = e * (1.0 / jnp.sum(e, axis=0, keepdims=True))
        grad_probs = nt(values, doexp)
        inner = jnp.sum(probs * grad_probs, axis=0, keepdims=True)
        grad_scores = (probs * (grad_probs - inner)).astype(jnp.bfloat16)
        dk = jnp.dot(grad_scores, qexp, preferred_element_type=jnp.float32)
        dv = jnp.dot(probs.astype(jnp.bfloat16), doexp, preferred_element_type=jnp.float32)
        dq = tn(grad_scores, keys)
        dq_ref[pl.ds(q_rows, BLK), :] = (fold_heads(dq, 0) * DH ** (-0.5)).astype(jnp.bfloat16)
        for s in range(SLOTS):
            k_s, v_s = dk[s * BLK : (s + 1) * BLK], dv[s * BLK : (s + 1) * BLK]
            at = pl.ds(rows[s], BLK)
            acc[at, 0:128] += k_s[:, :128]
            acc[at, 128:256] += k_s[:, 128:] + v_s[:, :128]
            acc[at, 256:384] += v_s[:, 128:]
        return carry

    lax.fori_loop(0, q_ref.shape[0] // BLK, step, 0)

    def emit(n, carry):
        at = pl.multiple_of(n * 256, 256)
        for j in range(6):
            part = acc[pl.ds(j * rows_piece + at, 256), :]
            outs[j][pl.ds(at, 256), :] = part.astype(jnp.bfloat16)
        return carry

    lax.fori_loop(0, rows_piece // 256, emit, 0)


VMEM = pl.BlockSpec(memory_space=pltpu.VMEM)
SMEM = pl.BlockSpec(memory_space=pltpu.SMEM)
ANY = pl.BlockSpec(memory_space=pl.ANY)


def attend(idx, bias, queries, pieces):
    rows, width = pieces[0].shape
    count = queries.shape[0]
    return pl.pallas_call(
        forward_kernel,
        out_shape=jax.ShapeDtypeStruct((count, WIN), jnp.bfloat16),
        in_specs=[SMEM, VMEM, VMEM] + [ANY] * 6,
        out_specs=VMEM,
        scratch_shapes=[
            pltpu.VMEM((6 * rows, width), jnp.bfloat16),
            pltpu.SemaphoreType.DMA((6,)),
        ],
        compiler_params=pltpu.CompilerParams(vmem_limit_bytes=24 << 20),
        cost_estimate=pl.CostEstimate(
            flops=2 * 4 * count * 3 * 256 * 512, bytes_accessed=12 * rows * width, transcendentals=count * 3 * 512
        ),
        name="attend",
    )(idx, bias, queries, *pieces)


def attend_back(idx, live, queries, grads, pieces):
    rows, width = pieces[0].shape
    count = queries.shape[0]
    kv_shape = jax.ShapeDtypeStruct((rows, width), jnp.bfloat16)
    return pl.pallas_call(
        backward_kernel,
        out_shape=[jax.ShapeDtypeStruct((count, WIN), jnp.bfloat16)] + [kv_shape] * 6,
        in_specs=[SMEM, SMEM, VMEM, VMEM] + [ANY] * 6,
        out_specs=[VMEM] * 7,
        scratch_shapes=[
            pltpu.VMEM((6 * rows, width), jnp.bfloat16),
            pltpu.VMEM((6 * rows, width), jnp.float32),
            pltpu.SemaphoreType.DMA((6,)),
        ],
        compiler_params=pltpu.CompilerParams(vmem_limit_bytes=56 << 20),
        cost_estimate=pl.CostEstimate(
            flops=2 * 10 * count * 3 * 256 * 512, bytes_accessed=24 * rows * width, transcendentals=count * 3 * 512
        ),
        name="attend_back",
    )(idx, live, queries, grads, *pieces)


def add_low(*terms):
    total = terms[0].astype(jnp.float32)
    for term in terms[1:]:
        total = total + term.astype(jnp.float32)
    return total


def pick(array, at, axis):
    return lax.dynamic_index_in_dim(array, at, axis, keepdims=False)


def plane_sum(slabs, plane, count):
    terms = [pick(slabs, plane, 0)]
    for gap in range(1, count):
        up = pick(slabs, jnp.minimum(plane + gap, count - 1), 0)
        down = pick(slabs, jnp.maximum(plane - gap, 0), 0)
        terms.append(plane_shift(up, gap))
        terms.append(plane_shift(down, -gap))
    return add_low(*terms)


def core_half(slabs, core, axis):
    got = xor_swap(pick(slabs, 1 - core, axis), 2)
    return add_low(pick(slabs, core, axis), got).astype(jnp.bfloat16)


def body(
    tokens,
    w_query,
    w_key,
    w_value,
    w_out,
    gain_attn,
    shift_attn,
    w_up,
    w_down,
    gain_mlp,
    shift_mlp,
    cotangent,
    lengths,
    seq_order,
    rand_blocks,
):
    piece, width = tokens.shape
    seqs, heads = lax.axis_size("seq"), lax.axis_size("head")
    planes = seqs // 4
    piece_blocks = piece // BLK
    assert heads == 2 and 8 * piece == MAXB * BLK and width == 4 * WQ
    seq_at, x_at = lax.axis_index("seq"), lax.axis_index("head")
    plane, y_at, core = seq_at // 4, (seq_at // 2) % 2, seq_at % 2
    group = y_at * 2 + x_at

    from_x = xor_swap(tokens, 1)
    from_y = xor_swap(tokens, 4)
    from_xy = xor_swap(tokens, 5)
    rand_y = lax.ppermute(rand_blocks, "seq", [(s, s ^ 2) for s in range(seqs)])

    def columns(weights):
        return lax.dynamic_slice_in_dim(weights, group * WQ, WQ, 1)

    wq_own = jnp.pad(columns(w_query) * jnp.bfloat16(DH ** (-0.5)), ((0, 0), (0, WIN - WQ)))
    wkv_own = jnp.concatenate([columns(w_key), columns(w_value)], axis=1)
    order = [group ^ j for j in range(4)]
    wout_own = jnp.concatenate(
        [
            jnp.pad(lax.dynamic_slice_in_dim(w_out, g * WQ, WQ, 0), ((WIN - WQ, 0), (0, 0)))
            for g in order
        ],
        axis=0,
    )

    local = jnp.arange(4 * piece_blocks, dtype=jnp.int32)
    far, near = local // piece_blocks, local % piece_blocks
    half = 4 * piece_blocks
    blocks = (
        plane * MAXB
        + (y_at ^ (far >> 1)) * half
        + core * (2 * piece_blocks)
        + (x_at ^ (far & 1)) * piece_blocks
        + near
    )
    here = rand_blocks.reshape(2, piece_blocks, -1)
    there = rand_y.reshape(2, piece_blocks, -1)
    rand_rows = jnp.concatenate(
        [pick(here, x_at, 0), pick(here, 1 - x_at, 0), pick(there, x_at, 0), pick(there, 1 - x_at, 0)],
        axis=0,
    )
    key_blocks, is_live = block_slots(blocks, rand_rows, lengths, seq_order)
    rel = key_blocks // MAXB - plane + 1
    in_plane = key_blocks % MAXB
    y_of, rest = in_plane // half, in_plane % half
    core_of, rest = rest // (2 * piece_blocks), rest % (2 * piece_blocks)
    x_of, near_of = rest // piece_blocks, rest % piece_blocks
    idx = (
        ((rel * 2 + (core_of ^ core)) * 4 + ((y_of ^ y_at) * 2 + (x_of ^ x_at))) * piece_blocks
        + near_of
    ).reshape(-1)
    live = is_live.astype(jnp.int32).reshape(-1)
    bias = jnp.repeat(jnp.where(is_live, 0.0, NEG).astype(jnp.float32), BLK, axis=1)

    def low_dot(a, b):
        return jnp.dot(a, b, preferred_element_type=jnp.float32).astype(jnp.bfloat16)

    stretch = jnp.concatenate([tokens, from_x, from_y, from_xy], axis=0)
    kv_own = low_dot(stretch, wkv_own)
    queries = low_dot(stretch, wq_own)
    kv_below = plane_shift(kv_own, 1)
    kv_above = plane_shift(kv_own, -1)
    pieces = [
        kv_below,
        xor_swap(kv_below, 2),
        kv_own,
        xor_swap(kv_own, 2),
        kv_above,
        xor_swap(kv_above, 2),
    ]
    context = attend(idx, bias, queries, pieces)

    def to_owners(array):
        parts = array.reshape(4, piece, -1)
        return [parts[0], xor_swap(parts[1], 1), xor_swap(parts[2], 4), xor_swap(parts[3], 5)]

    context_tok = jnp.concatenate(to_owners(context), axis=1)
    attn_out = jnp.dot(context_tok, wout_own, preferred_element_type=jnp.float32)
    normed, hat_one, dev_one = norm_forward(
        tokens.astype(jnp.float32) + attn_out, gain_attn, shift_attn
    )
    normed_low = normed.astype(jnp.bfloat16)
    hidden_pre = jnp.dot(normed_low, w_up, preferred_element_type=jnp.float32)
    hidden = gelu_tanh(hidden_pre).astype(jnp.bfloat16)
    mlp_out = jnp.dot(hidden, w_down, preferred_element_type=jnp.float32)
    output, hat_two, dev_two = norm_forward(normed + mlp_out, gain_mlp, shift_mlp)
    grad_two, grad_gain_mlp, grad_shift_mlp = norm_backward(
        cotangent.astype(jnp.float32), hat_two, dev_two, gain_mlp
    )
    grad_mlp = grad_two.astype(jnp.bfloat16)
    grad_hidden = jnp.dot(grad_mlp, w_down.T, preferred_element_type=jnp.float32)
    gelu_out, gelu_pull = jax.vjp(gelu_tanh, hidden_pre)
    grad_pre = gelu_pull(grad_hidden)[0].astype(jnp.bfloat16)
    grad_normed = grad_two + jnp.dot(grad_pre, w_up.T, preferred_element_type=jnp.float32)
    grad_one, grad_gain_attn, grad_shift_attn = norm_backward(
        grad_normed, hat_one, dev_one, gain_attn
    )
    grad_attn = grad_one.astype(jnp.bfloat16)
    grad_context = low_dot(grad_attn, wout_own.T)
    cols = [grad_context[:, j * WIN : (j + 1) * WIN] for j in range(4)]
    grad_ctx = jnp.concatenate(
        [cols[0], xor_swap(cols[1], 1), xor_swap(cols[2], 4), xor_swap(cols[3], 5)], axis=0
    )

    grad_w_down = low_dot(hidden.T, grad_mlp)
    grad_w_up = low_dot(normed_low.T, grad_pre)
    grad_w_out = low_dot(context_tok.T, grad_attn).reshape(4, WIN, width)[:, WIN - WQ :]
    grad_w_out = jnp.concatenate([pick(grad_w_out, g, 0) for g in order], axis=0)

    norm_rows = jnp.stack([grad_gain_attn, grad_shift_attn, grad_gain_mlp, grad_shift_mlp])
    share = width // seqs
    norm_rows = norm_rows.reshape(4, seqs, share).transpose(1, 0, 2).reshape(seqs, 1, 4 * share)
    norm_rows = jnp.pad(norm_rows, ((0, 0), (0, 15), (0, width - 4 * share))).astype(jnp.bfloat16)
    out_slabs = jnp.concatenate([grad_w_out.reshape(seqs, share, width), norm_rows], axis=1)
    up_slabs = grad_w_up.reshape(seqs, share, -1)
    down_slabs = grad_w_down.reshape(seqs, -1, width)

    def y_then_x(slabs):
        slabs = slabs.reshape((planes, 2, 2) + slabs.shape[1:])
        slabs = core_half(slabs, core, 2)
        got = xor_swap(pick(slabs, 1 - y_at, 1), 4)
        slabs = add_low(pick(slabs, y_at, 1), got).astype(jnp.bfloat16)
        mine = plane_sum(slabs, plane, planes).astype(jnp.bfloat16)
        return add_low(mine, xor_swap(mine, 1))

    def x_then_y(slabs):
        slabs = slabs.reshape((planes, 2, 2) + slabs.shape[1:])
        slabs = core_half(slabs, core, 2)
        slabs = slabs.reshape(planes, 2, 2, slabs.shape[2] // 2, -1)
        got = xor_swap(pick(slabs, 1 - x_at, 2), 1)
        slabs = add_low(pick(slabs, x_at, 2), got).astype(jnp.bfloat16)
        got = xor_swap(pick(slabs, 1 - y_at, 1), 4)
        slabs = add_low(pick(slabs, y_at, 1), got).astype(jnp.bfloat16)
        mine = plane_sum(slabs, plane, planes).astype(jnp.bfloat16)
        other = xor_swap(mine, 1)
        low_x = x_at == 0
        return jnp.concatenate(
            [jnp.where(low_x, mine, other), jnp.where(low_x, other, mine)], axis=0
        ).astype(jnp.float32)

    down_total = x_then_y(down_slabs)
    up_total = y_then_x(up_slabs)
    out_total = y_then_x(out_slabs)

    back = attend_back(idx, live, queries, grad_ctx, pieces)
    grad_q, kv_parts = back[0], back[1:]
    sums = [add_low(kv_parts[2 * r], xor_swap(kv_parts[2 * r + 1], 2)) for r in range(3)]
    grad_kv = (
        sums[1]
        + plane_shift(sums[0].astype(jnp.bfloat16), -1).astype(jnp.float32)
        + plane_shift(sums[2].astype(jnp.bfloat16), 1).astype(jnp.float32)
    ).astype(jnp.bfloat16)
    wq_plain = jnp.pad(columns(w_query), ((0, 0), (0, WIN - WQ)))
    grad_stretch = jnp.dot(grad_q, wq_plain.T, preferred_element_type=jnp.float32) + jnp.dot(
        grad_kv, wkv_own.T, preferred_element_type=jnp.float32
    )
    sent = grad_stretch.astype(jnp.bfloat16).reshape(4, piece, width)
    grad_tokens = grad_one + grad_stretch[:piece] + add_low(
        xor_swap(sent[1], 1), xor_swap(sent[2], 4), xor_swap(sent[3], 5)
    )

    grad_wq = low_dot(stretch.T, grad_q)[:, :WQ]
    grad_wkv = low_dot(stretch.T, grad_kv)
    proj = jnp.concatenate([grad_wq, grad_wkv], axis=1).reshape(planes, 2, 2, share, 3 * WQ)
    proj = core_half(proj, core, 2)
    proj = plane_sum(proj, plane, planes).astype(jnp.bfloat16)
    kept, given = pick(proj, y_at, 0), pick(proj, 1 - y_at, 0)
    quarters = jnp.stack([kept, xor_swap(kept, 1), xor_swap(given, 4), xor_swap(given, 5)])
    quarters = [pick(quarters, g, 0) for g in order]

    def whole(n):
        return jnp.concatenate([q[:, n * WQ : (n + 1) * WQ] for q in quarters], axis=1).astype(
            jnp.float32
        )

    norm_row = out_total[share]

    def norm_grad(n):
        return norm_row[n * share : (n + 1) * share]

    return (
        output.astype(jnp.bfloat16),
        grad_tokens,
        whole(0),
        whole(1),
        whole(2),
        out_total[:share],
        norm_grad(0),
        norm_grad(1),
        up_total,
        down_total,
        norm_grad(2),
        norm_grad(3),
    )


def solution(mesh):
    rows = P(("seq", "head"), None)
    seq_rows, seq_only = P("seq", None), P("seq")
    return jax.shard_map(
        body,
        mesh=mesh,
        in_specs=(rows,) + (P(),) * 10 + (rows, P(), P(), seq_rows),
        out_specs=(
            rows,
            rows,
            seq_rows,
            seq_rows,
            seq_rows,
            seq_rows,
            seq_only,
            seq_only,
            seq_rows,
            seq_rows,
            seq_only,
            seq_only,
        ),
        check_vma=False,
    )
```

```python
import functools

import jax
import jax.numpy as jnp
from jax import lax
from jax.experimental import pallas as pl
from jax.experimental.pallas import tpu as pltpu
from jax.sharding import PartitionSpec as P

DH = 64
BLK = 64
MAXB = 64
SLOTS = 8
HG = 3
WQ = HG * DH
WIN = 256
AXES = ("seq", "head")
NEG = -1e30

eps_norm = 1e-06


def xor_swap(value, bits):
    count = lax.axis_size("seq") * lax.axis_size("head")
    return lax.ppermute(value, AXES, [(d, d ^ bits) for d in range(count)])


def plane_shift(value, steps):
    count = lax.axis_size("seq") * lax.axis_size("head")
    gap = 8 * steps
    return lax.ppermute(
        value, AXES, [(d, d + gap) for d in range(count) if 0 <= d + gap < count]
    )


def block_slots(blocks, rand_rows, lengths, seq_order):
    seq_count = lengths.shape[0]
    seq_ids = jnp.arange(seq_count, dtype=jnp.int32)
    packed = jnp.sum(jnp.where(seq_order[:, None] == seq_ids[None, :], lengths[None, :], 0), axis=1)
    seq_ends = jnp.cumsum(packed)
    starts = seq_ends - packed
    holder = jnp.sum((seq_ends[None, :] <= blocks[:, None]).astype(jnp.int32), axis=1)
    chosen = holder[:, None] == seq_ids[None, :]
    seq_first = jnp.sum(jnp.where(chosen, starts[None, :], 0), axis=1)
    seq_span = jnp.sum(jnp.where(chosen, packed[None, :], 0), axis=1)
    offset = blocks - seq_first
    rand_pos = seq_first[:, None] + jnp.mod(rand_rows, seq_span[:, None])
    fixed_cand = jnp.stack(
        [blocks - 1, blocks, blocks + 1, seq_first, seq_first + seq_span - 1], axis=1
    )
    candidate = jnp.concatenate([fixed_cand, rand_pos], axis=1)
    fixed_live = jnp.stack(
        [offset > 0, offset >= 0, offset < seq_span - 1, offset >= 0, offset >= 0], axis=1
    )
    usable = jnp.concatenate([fixed_live, rand_pos >= 0], axis=1)
    kept_list = []
    for column in range(candidate.shape[1]):
        unique = usable[:, column]
        for earlier in range(column):
            unique = unique & jnp.logical_not(
                kept_list[earlier] & (candidate[:, earlier] == candidate[:, column])
            )
        kept_list.append(unique)
    is_live = jnp.stack(kept_list, axis=1)
    key_blocks = jnp.where(is_live, candidate, blocks[:, None])
    return (key_blocks, is_live)


def norm_forward(values, gain_vec, shift_vec):
    center = values - jnp.mean(values, axis=-1, keepdims=True)
    spread = jnp.mean(center * center, axis=-1, keepdims=True)
    inv_dev = lax.rsqrt(spread + eps_norm)
    x_hat = center * inv_dev
    return (x_hat * gain_vec + shift_vec, x_hat, inv_dev)


def norm_backward(grad_in, x_hat, inv_dev, gain_vec):
    grad_gain = jnp.sum(grad_in * x_hat, axis=0)
    grad_shift = jnp.sum(grad_in, axis=0)
    grad_hat = grad_in * gain_vec
    grad_mean = jnp.mean(grad_hat, axis=-1, keepdims=True)
    grad_proj = jnp.mean(grad_hat * x_hat, axis=-1, keepdims=True)
    return (inv_dev * (grad_hat - grad_mean - x_hat * grad_proj), grad_gain, grad_shift)


def gelu_tanh(values):
    return jax.nn.gelu(values, approximate=True)


def lane_groups(rows, offset):
    lane = lax.broadcasted_iota(jnp.int32, (rows, WIN), 1) - offset
    return [jnp.logical_and(lane >= h * DH, lane < (h + 1) * DH) for h in range(HG)]


def spread_heads(block, offset):
    zero = jnp.zeros_like(block)
    return jnp.concatenate([jnp.where(m, block, zero) for m in lane_groups(BLK, offset)], axis=0)


def fold_heads(stacked, offset):
    masks = lane_groups(BLK, offset)
    total = jnp.where(masks[0], stacked[:BLK], 0.0)
    for h in range(1, HG):
        total = total + jnp.where(masks[h], stacked[h * BLK : (h + 1) * BLK], 0.0)
    return total


def fetch(source, kv, sems):
    copy = pltpu.make_async_copy(source, kv, sems.at[0])
    copy.start()
    copy.wait()


def nt(a, b):
    return lax.dot_general(a, b, (((1,), (1,)), ((), ())), preferred_element_type=jnp.float32)


def tn(a, b):
    return lax.dot_general(a, b, (((0,), (0,)), ((), ())), preferred_element_type=jnp.float32)


def forward_kernel(idx_ref, bias_ref, q_ref, *refs):
    kv_ref, ctx_ref, kv, sems = refs
    fetch(kv_ref, kv, sems)

    def step(i, carry):
        q_rows = pl.multiple_of(i * BLK, BLK)
        qexp = spread_heads(q_ref[pl.ds(q_rows, BLK), :], 0)
        rows = [
            pl.multiple_of(idx_ref[i * SLOTS + s] * BLK, BLK) for s in range(SLOTS)
        ]
        keys = jnp.concatenate([kv[pl.ds(r, BLK), 0:WIN] for r in rows], axis=0)
        values = jnp.concatenate([kv[pl.ds(r, BLK), 128 : 128 + WIN] for r in rows], axis=0)
        scores = nt(qexp, keys) + bias_ref[pl.ds(i, 1), :]
        top = jnp.max(scores, axis=1, keepdims=True)
        e = jnp.exp(scores - top)
        total = jnp.sum(e, axis=1, keepdims=True)
        out = jnp.dot(e.astype(jnp.bfloat16), values, preferred_element_type=jnp.float32)
        ctx_ref[pl.ds(q_rows, BLK), :] = fold_heads(out / total, 64).astype(jnp.bfloat16)
        return carry

    lax.fori_loop(0, q_ref.shape[0] // BLK, step, 0)


def backward_kernel(idx_ref, live_ref, q_ref, do_ref, *refs):
    kv_ref, dq_ref, dkv_ref, kv, acc, sems = refs

    def clear(n, carry):
        acc[pl.ds(pl.multiple_of(n * 256, 256), 256), :] = jnp.zeros((256, 2 * WQ), jnp.float32)
        return carry

    copy = pltpu.make_async_copy(kv_ref, kv, sems.at[0])
    copy.start()
    lax.fori_loop(0, acc.shape[0] // 256, clear, 0)
    copy.wait()

    def step(i, carry):
        q_rows = pl.multiple_of(i * BLK, BLK)
        qexp = spread_heads(q_ref[pl.ds(q_rows, BLK), :], 0)
        doexp = spread_heads(do_ref[pl.ds(q_rows, BLK), :], 64)
        rows = [
            pl.multiple_of(idx_ref[i * SLOTS + s] * BLK, BLK) for s in range(SLOTS)
        ]
        keys = jnp.concatenate([kv[pl.ds(r, BLK), 0:WIN] for r in rows], axis=0)
        values = jnp.concatenate([kv[pl.ds(r, BLK), 128 : 128 + WIN] for r in rows], axis=0)
        raw = nt(keys, qexp)
        scores = jnp.concatenate(
            [
                jnp.where(live_ref[i * SLOTS + s] > 0, raw[s * BLK : (s + 1) * BLK], NEG)
                for s in range(SLOTS)
            ],
            axis=0,
        )
        top = jnp.max(scores, axis=0, keepdims=True)
        e = jnp.exp(scores - top)
        probs = e * (1.0 / jnp.sum(e, axis=0, keepdims=True))
        grad_probs = nt(values, doexp)
        inner = jnp.sum(probs * grad_probs, axis=0, keepdims=True)
        grad_scores = (probs * (grad_probs - inner)).astype(jnp.bfloat16)
        dk = jnp.dot(grad_scores, qexp, preferred_element_type=jnp.float32)
        dv = jnp.dot(probs.astype(jnp.bfloat16), doexp, preferred_element_type=jnp.float32)
        dq = tn(grad_scores, keys)
        dq_ref[pl.ds(q_rows, BLK), :] = (fold_heads(dq, 0) * DH ** (-0.5)).astype(jnp.bfloat16)
        for s in range(SLOTS):
            k_s, v_s = dk[s * BLK : (s + 1) * BLK], dv[s * BLK : (s + 1) * BLK]
            at = pl.ds(rows[s], BLK)
            acc[at, 0:128] += k_s[:, :128]
            acc[at, 128:256] += k_s[:, 128:] + v_s[:, :128]
            acc[at, 256:384] += v_s[:, 128:]
        return carry

    lax.fori_loop(0, q_ref.shape[0] // BLK, step, 0)

    def emit(n, carry):
        at = pl.ds(pl.multiple_of(n * 256, 256), 256)
        dkv_ref[at, :] = acc[at, :].astype(jnp.bfloat16)
        return carry

    lax.fori_loop(0, acc.shape[0] // 256, emit, 0)


VMEM = pl.BlockSpec(memory_space=pltpu.VMEM)
SMEM = pl.BlockSpec(memory_space=pltpu.SMEM)
ANY = pl.BlockSpec(memory_space=pl.ANY)


def device_at(plane, y_at, core, x_at):
    return (plane * 4 + y_at * 2 + core, x_at)


def place():
    seq_at, x_at = lax.axis_index("seq"), lax.axis_index("head")
    return seq_at // 4, (seq_at // 2) % 2, seq_at % 2, x_at


def remote(src, dst, sems, recvs, at, device):
    return pltpu.make_async_remote_copy(
        src_ref=src,
        dst_ref=dst,
        send_sem=sems.at[at],
        recv_sem=recvs.at[at],
        device_id=device,
        device_id_type=pl.DeviceIdType.MESH,
    )


def greet(partners):
    barrier = pltpu.get_barrier_semaphore()
    for device in partners:
        pl.semaphore_signal(
            barrier, inc=1, device_id=device, device_id_type=pl.DeviceIdType.MESH
        )
    pl.semaphore_wait(barrier, len(partners))


CHUNK_ORDER = (0, 1, 2, 4, 3, 5, 6, 7)


def gather_kernel(planes, tok_ref, wq_ref, wkv_ref, kv_out, q_ref, x_out, xs, kvs, *sems):
    x_send, x_recv, k_send, k_recv, up_send, up_recv, dn_send, dn_recv = sems[:8]
    f_send, f_recv, g_send, g_recv, l_sem, s_sem = sems[8:]
    plane, y_at, core, x_at = place()
    piece = tok_ref.shape[0]
    rows = piece // 2
    part = 4 * piece
    by_x = device_at(plane, y_at, core, 1 - x_at)
    by_y = device_at(plane, 1 - y_at, core, x_at)
    by_core = device_at(plane, y_at, 1 - core, x_at)
    above = device_at(plane + 1, y_at, core, x_at)
    below = device_at(plane - 1, y_at, core, x_at)
    has_above, has_below = plane < planes - 1, plane > 0
    ring = [device_at(lax.rem(plane + g, planes), y_at, core, x_at) for g in (1, planes - 1)]
    greet([by_x, by_y, by_core] + ring)

    def x_rows(c):
        return xs.at[pl.ds((c - 2) * rows, rows)]

    def tok_rows(c):
        return tok_ref.at[pl.ds(c * rows, rows)]

    hops = {
        2: remote(tok_rows(0), x_rows(2), x_send, x_recv, 0, by_x),
        4: remote(tok_rows(0), x_rows(4), x_send, x_recv, 2, by_y),
        3: remote(tok_rows(1), x_rows(3), x_send, x_recv, 1, by_x),
        5: remote(tok_rows(1), x_rows(5), x_send, x_recv, 3, by_y),
        6: remote(x_rows(2), x_rows(6), x_send, x_recv, 4, by_y),
        7: remote(x_rows(5), x_rows(7), x_send, x_recv, 5, by_x),
    }
    for c in (2, 4, 3, 5):
        hops[c].start()

    def kv_rows(part_at, c):
        return kv_out.at[pl.ds(part_at * part + c * rows, rows)]

    to_core, to_above, to_below, pass_up, pass_down = {}, {}, {}, {}, {}
    stores = {}
    for c in range(8):
        mine = kvs.at[pl.ds(c * rows, rows)]
        to_core[c] = remote(mine, kv_rows(3, c), k_send, k_recv, c, by_core)
        to_above[c] = remote(mine, kv_rows(0, c), up_send, up_recv, c, above)
        to_below[c] = remote(mine, kv_rows(4, c), dn_send, dn_recv, c, below)
        pass_up[c] = remote(kv_rows(0, c), kv_rows(1, c), f_send, f_recv, c, by_core)
        pass_down[c] = remote(kv_rows(4, c), kv_rows(5, c), g_send, g_recv, c, by_core)
        stores[c] = pltpu.make_async_copy(mine, kv_rows(2, c), l_sem.at[c])
    keeps = {
        c: pltpu.make_async_copy(
            tok_rows(c) if c < 2 else x_rows(c), x_out.at[pl.ds(c * rows, rows)], s_sem.at[c]
        )
        for c in range(8)
    }

    def relay(c):
        @pl.when(has_below)
        def _():
            to_above[c].wait_recv()
            pass_up[c].start()

        @pl.when(has_above)
        def _():
            to_below[c].wait_recv()
            pass_down[c].start()

    for n, c in enumerate(CHUNK_ORDER):
        if c >= 2:
            hops[c].wait_recv()
        if c == 2:
            hops[6].start()
        if c == 5:
            hops[7].start()
        keeps[c].start()
        block = tok_ref[pl.ds(c * rows, rows), :] if c < 2 else xs[pl.ds((c - 2) * rows, rows), :]
        kvs[pl.ds(c * rows, rows), :] = jnp.dot(
            block, wkv_ref[...], preferred_element_type=jnp.float32
        ).astype(jnp.bfloat16)

        @pl.when(has_above)
        def _(c=c):
            to_above[c].start()

        @pl.when(has_below)
        def _(c=c):
            to_below[c].start()

        to_core[c].start()
        stores[c].start()
        q_ref[pl.ds(c * rows, rows), :] = jnp.dot(
            block, wq_ref[...], preferred_element_type=jnp.float32
        ).astype(jnp.bfloat16)
        if n >= 3:
            relay(CHUNK_ORDER[n - 3])
    for c in CHUNK_ORDER[5:]:
        relay(c)
    for c in (2, 4, 3, 5, 6, 7):
        hops[c].wait_send()
    for c in range(8):
        to_core[c].wait()
        stores[c].wait()
        keeps[c].wait()

        @pl.when(has_above)
        def _(c=c):
            to_above[c].wait_send()
            pass_down[c].wait()

        @pl.when(has_below)
        def _(c=c):
            to_below[c].wait_send()
            pass_up[c].wait()


def gather_project(tokens, wq_own, wkv_own, planes):
    piece, width = tokens.shape
    dma = pltpu.SemaphoreType.DMA
    return pl.pallas_call(
        functools.partial(gather_kernel, planes),
        out_shape=[
            jax.ShapeDtypeStruct((24 * piece, 2 * WQ), jnp.bfloat16),
            jax.ShapeDtypeStruct((4 * piece, WIN), jnp.bfloat16),
            jax.ShapeDtypeStruct((4 * piece, width), jnp.bfloat16),
        ],
        in_specs=[VMEM] * 3,
        out_specs=[ANY, VMEM, ANY],
        scratch_shapes=[
            pltpu.VMEM((3 * piece, width), jnp.bfloat16),
            pltpu.VMEM((4 * piece, 2 * WQ), jnp.bfloat16),
            dma((6,)),
            dma((6,)),
        ]
        + [dma((8,))] * 12,
        compiler_params=pltpu.CompilerParams(
            collective_id=0, has_side_effects=True, vmem_limit_bytes=20 << 20
        ),
        cost_estimate=pl.CostEstimate(
            flops=2 * 4 * piece * width * 640, bytes_accessed=40 << 20, transcendentals=0
        ),
        name="gather_project",
    )(tokens, wq_own, wkv_own)


def attend(idx, bias, queries, keys_values):
    rows, width = keys_values.shape[0] // 6, keys_values.shape[1]
    count = queries.shape[0]
    return pl.pallas_call(
        forward_kernel,
        out_shape=jax.ShapeDtypeStruct((count, WIN), jnp.bfloat16),
        in_specs=[SMEM, VMEM, VMEM] + [ANY],
        out_specs=VMEM,
        scratch_shapes=[
            pltpu.VMEM((6 * rows, width), jnp.bfloat16),
            pltpu.SemaphoreType.DMA((1,)),
        ],
        compiler_params=pltpu.CompilerParams(vmem_limit_bytes=24 << 20),
        cost_estimate=pl.CostEstimate(
            flops=2 * 4 * count * 3 * 256 * 512, bytes_accessed=12 * rows * width, transcendentals=count * 3 * 512
        ),
        name="attend",
    )(idx, bias, queries, keys_values)


def attend_back(idx, live, queries, grads, keys_values):
    rows, width = keys_values.shape[0] // 6, keys_values.shape[1]
    count = queries.shape[0]
    kv_shape = jax.ShapeDtypeStruct((6 * rows, width), jnp.bfloat16)
    return pl.pallas_call(
        backward_kernel,
        out_shape=[jax.ShapeDtypeStruct((count, WIN), jnp.bfloat16)] + [kv_shape],
        in_specs=[SMEM, SMEM, VMEM, VMEM] + [ANY],
        out_specs=[VMEM] * 2,
        scratch_shapes=[
            pltpu.VMEM((6 * rows, width), jnp.bfloat16),
            pltpu.VMEM((6 * rows, width), jnp.float32),
            pltpu.SemaphoreType.DMA((1,)),
        ],
        compiler_params=pltpu.CompilerParams(vmem_limit_bytes=56 << 20),
        cost_estimate=pl.CostEstimate(
            flops=2 * 10 * count * 3 * 256 * 512, bytes_accessed=24 * rows * width, transcendentals=count * 3 * 512
        ),
        name="attend_back",
    )(idx, live, queries, grads, keys_values)


JORDER = (3, 1, 2, 0)


def reduce_kernel(planes, n_own, *refs):
    (dkv_in, dq_ref, x_ref, wq_ref, wkv_ref, up_a, up_b, out_a, out_b, down_a, down_b) = refs[:11]
    attn_out, proj_out, up_out, down_out, side_out = refs[11:16]
    (own, core_in, z_out, z_in, g_all, dx_out, dx_in, acc) = refs[16:24]
    (p_slab, p_core, p_z, p_zin, p_fin) = refs[24:29]
    w_sum, w_got, w_two, w_zin = refs[29:32], refs[32:35], refs[35:38], refs[38:41]
    (l_sem, c_s, c_r, u_s, u_r, d_s, d_r, x_s, x_r) = refs[41:50]
    (pk_s, pk_r, pz_s, pz_r, pf_s, pf_r) = refs[50:56]
    (w2_s, w2_r, w3_s, w3_r, w4_s, w4_r) = refs[56:62]
    plane, y_at, core, x_at = place()
    piece = attn_out.shape[0]
    part = 4 * piece
    rest = planes - 1

    def there(j):
        return device_at(plane, y_at ^ (j >> 1), core, x_at ^ (j & 1))

    by_x, by_y, by_xy = there(1), there(2), there(3)
    by_core = device_at(plane, y_at, 1 - core, x_at)
    others = [device_at(lax.rem(plane + g, planes), y_at, core, x_at) for g in range(1, planes)]

    greet([by_x, by_y, by_xy, by_core] + others)

    has_above, has_below = plane < planes - 1, plane > 0
    above = device_at(plane + 1, y_at, core, x_at)
    below = device_at(plane - 1, y_at, core, x_at)

    def rows(r, j):
        return pl.ds(r * part + j * piece, piece)

    def in_rows(r, kk, j):
        return pl.ds((2 * r + kk) * part + j * piece, piece)

    turns = [(r, j) for j in JORDER for r in (0, 2)] + [(1, j) for j in JORDER]
    loads, to_core = {}, {}
    for n, (r, j) in enumerate(turns):
        loads[r, j] = pltpu.make_async_copy(
            dkv_in.at[in_rows(r, 0, j)], own.at[rows(r, j)], l_sem.at[n]
        )
        to_core[r, j] = remote(
            dkv_in.at[in_rows(r, 1, j)], core_in.at[rows(r, j)], c_s, c_r, n, by_core
        )
    for key in turns:
        to_core[key].start()
        loads[key].start()

    halves = [up_a.shape[2] // 2, out_a.shape[2] // 2]
    pairs = [(up_a, up_b), (out_a, out_b)]
    w2 = []
    for n in range(2):
        a, b = pairs[n]
        for p in range(planes):
            w_sum[n][p] = (a[p].astype(jnp.float32) + b[p].astype(jnp.float32)).astype(jnp.bfloat16)
        give = pl.ds(pl.multiple_of((1 - x_at) * halves[n], 128), halves[n])
        w2.append(remote(w_sum[n].at[:, :, give], w_got[n], w2_s, w2_r, n, by_x))
        w2[n].start()
    for p in range(planes):
        for y in range(2):
            w_sum[2][p, y] = (
                down_a[p, y].astype(jnp.float32) + down_b[p, y].astype(jnp.float32)
            ).astype(jnp.bfloat16)
    w2.append(remote(w_sum[2].at[:, 1 - y_at], w_got[2], w2_s, w2_r, 2, by_y))
    w2[2].start()

    to_below, to_above = {}, {}
    for n, j in enumerate(JORDER):
        to_below[j] = remote(
            z_out.at[rows(0, j)], z_in.at[rows(0, j)], d_s, d_r, n, below
        )
        to_above[j] = remote(
            z_out.at[rows(1, j)], z_in.at[rows(1, j)], u_s, u_r, n, above
        )

    def both(r, j):
        to_core[r, j].wait_recv()
        loads[r, j].wait()
        at = rows(r, j)
        return own[at, :].astype(jnp.float32) + core_in[at, :].astype(jnp.float32)

    for j in JORDER:
        z_out[rows(0, j), :] = both(0, j).astype(jnp.bfloat16)

        @pl.when(has_below)
        def _(j=j):
            to_below[j].start()

        z_out[rows(1, j), :] = both(2, j).astype(jnp.bfloat16)

        @pl.when(has_above)
        def _(j=j):
            to_above[j].start()

    w3 = []
    for n in range(3):
        w2[n].wait_recv()
        for p in range(planes):
            if n < 2:
                keep = w_sum[n][p, :, pl.ds(pl.multiple_of(x_at * halves[n], 128), halves[n])]
            else:
                keep = w_sum[n][p, y_at]
            w_two[n][p] = (
                keep.astype(jnp.float32) + w_got[n][p].astype(jnp.float32)
            ).astype(jnp.bfloat16)
        for g in range(1, planes):
            w3.append(
                remote(
                    w_two[n].at[lax.rem(plane + g, planes)],
                    w_zin[n].at[g - 1],
                    w3_s,
                    w3_r,
                    n * rest + g - 1,
                    others[g - 1],
                )
            )
            w3[-1].start()

    to_owner = {
        j: remote(
            dx_out.at[pl.ds((j - 1) * piece, piece)],
            dx_in.at[pl.ds((j - 1) * piece, piece)],
            x_s,
            x_r,
            j - 1,
            there(j),
        )
        for j in (1, 2, 3)
    }
    first = True
    for j in JORDER:
        g_all[:, 2 * WQ :] = dq_ref[pl.ds(j * piece, piece), :]
        g_all[:, : 2 * WQ] = both(1, j).astype(jnp.bfloat16)

        @pl.when(has_above)
        def _(j=j):
            to_below[j].wait_recv()
            g_all[:, : 2 * WQ] = (
                g_all[:, : 2 * WQ].astype(jnp.float32) + z_in[rows(0, j), :].astype(jnp.float32)
            ).astype(jnp.bfloat16)

        @pl.when(has_below)
        def _(j=j):
            to_above[j].wait_recv()
            g_all[:, : 2 * WQ] = (
                g_all[:, : 2 * WQ].astype(jnp.float32) + z_in[rows(1, j), :].astype(jnp.float32)
            ).astype(jnp.bfloat16)

        grads = g_all[...]
        dx = nt(grads[:, 2 * WQ :], wq_ref[...]) + nt(grads[:, : 2 * WQ], wkv_ref[...])
        if j:
            dx_out[pl.ds((j - 1) * piece, piece), :] = dx.astype(jnp.bfloat16)
            to_owner[j].start()
        else:
            attn_out[...] = dx
        step = tn(x_ref[pl.ds(j * piece, piece), :], grads)
        acc[...] = step if first else acc[...] + step
        first = False

    share = p_slab.shape[3]
    for p in range(planes):
        for y in range(2):
            for k in range(2):
                at = ((p * 2 + y) * 2 + k) * share
                p_slab[k, p, y] = acc[at : at + share, :].astype(jnp.bfloat16)
    pk = remote(p_slab.at[1 - core], p_core, pk_s, pk_r, 0, by_core)
    pk.start()

    outs = [up_out, side_out, down_out]
    w4 = []
    for n in range(3):
        total = w_two[n][plane].astype(jnp.float32)
        for g in range(1, planes):
            w3[n * rest + g - 1].wait_recv()
            total = total + w_zin[n][g - 1].astype(jnp.float32)
        outs[n][x_at] = total.astype(jnp.bfloat16)
        w4.append(remote(outs[n].at[x_at], outs[n].at[x_at], w4_s, w4_r, n, by_x))
        w4[n].start()

    pk.wait_recv()
    for p in range(planes):
        p_z[p] = (
            p_slab[core, p].astype(jnp.float32) + p_core[p].astype(jnp.float32)
        ).astype(jnp.bfloat16)
    pz = []
    for g in range(1, planes):
        pz.append(
            remote(
                p_z.at[lax.rem(plane + g, planes)], p_zin.at[g - 1], pz_s, pz_r, g - 1, others[g - 1]
            )
        )
        pz[-1].start()

    total = attn_out[...]
    for j in (3, 1, 2):
        to_owner[j].wait_recv()
        total = total + dx_in[pl.ds((j - 1) * piece, piece), :].astype(jnp.float32)
    attn_out[...] = total

    total = p_z[plane].astype(jnp.float32)
    for g in range(1, planes):
        pz[g - 1].wait_recv()
        total = total + p_zin[g - 1].astype(jnp.float32)
    p_fin[...] = total.astype(jnp.bfloat16)
    pf = []
    for j in (1, 2, 3):
        pf.append(
            remote(p_fin.at[y_at ^ (j >> 1)], proj_out.at[j], pf_s, pf_r, j - 1, there(j))
        )
        pf[-1].start()
    proj_out[0] = p_fin[y_at]
    for copy in pf:
        copy.wait()
    for copy in w4:
        copy.wait()
    for copy in w2 + w3 + pz + [pk]:
        copy.wait_send()
    for key in turns:
        to_core[key].wait_send()
    for j in (1, 2, 3):
        to_owner[j].wait_send()
    for j in JORDER:

        @pl.when(has_below)
        def _(j=j):
            to_below[j].wait_send()

        @pl.when(has_above)
        def _(j=j):
            to_above[j].wait_send()


def reduce_all(dkv, dq, stretch, wq, wkv, up, out, down, planes):
    low = jnp.bfloat16
    piece = dq.shape[0] // 4
    width = stretch.shape[1]
    share = up[0].shape[1]
    rest = planes - 1
    dma = pltpu.SemaphoreType.DMA
    vm = pltpu.VMEM
    side = out[0].shape[1]
    kinds = [(share, up[0].shape[2] // 2), (side, width // 2), (down[0].shape[2], down[0].shape[3])]
    cols = 2 * WQ + WIN
    sds = jax.ShapeDtypeStruct
    return pl.pallas_call(
        functools.partial(reduce_kernel, planes, 0),
        out_shape=[
            sds((piece, width), jnp.float32),
            sds((4, share, cols), low),
            sds((2,) + kinds[0], low),
            sds((2,) + kinds[2], low),
            sds((2,) + kinds[1], low),
        ],
        in_specs=[ANY] + [VMEM] * 10,
        out_specs=[VMEM] * 5,
        scratch_shapes=[
            vm((12 * piece, 2 * WQ), low),
            vm((12 * piece, 2 * WQ), low),
            vm((8 * piece, 2 * WQ), low),
            vm((8 * piece, 2 * WQ), low),
            vm((piece, cols), low),
            vm((3 * piece, width), low),
            vm((3 * piece, width), low),
            vm((width, cols), jnp.float32),
            vm((2, planes, 2, share, cols), low),
            vm((planes, 2, share, cols), low),
            vm((planes, 2, share, cols), low),
            vm((rest, 2, share, cols), low),
            vm((2, share, cols), low),
            vm(up[0].shape, low),
            vm(out[0].shape, low),
            vm(down[0].shape, low),
        ]
        + [vm((planes,) + k, low) for k in kinds] * 2
        + [vm((rest,) + k, low) for k in kinds]
        + [dma((12,))] * 3
        + [dma((4,))] * 4
        + [dma((3,))] * 2
        + [dma((1,))] * 2
        + [dma((rest,))] * 2
        + [dma((3,))] * 2
        + [dma((3,))] * 2
        + [dma((3 * rest,))] * 2
        + [dma((3,))] * 2,
        compiler_params=pltpu.CompilerParams(
            collective_id=1, has_side_effects=True, vmem_limit_bytes=58 << 20
        ),
        cost_estimate=pl.CostEstimate(
            flops=4 * 4 * piece * width * cols, bytes_accessed=40 << 20, transcendentals=0
        ),
        name="reduce_all",
    )(dkv, dq, stretch, wq, wkv, up[0], up[1], out[0], out[1], down[0], down[1])


def add_low(*terms):
    total = terms[0].astype(jnp.float32)
    for term in terms[1:]:
        total = total + term.astype(jnp.float32)
    return total


def pick(array, at, axis):
    return lax.dynamic_index_in_dim(array, at, axis, keepdims=False)


def plane_sum(slabs, plane, count):
    terms = [pick(slabs, plane, 0)]
    for gap in range(1, count):
        up = pick(slabs, jnp.minimum(plane + gap, count - 1), 0)
        down = pick(slabs, jnp.maximum(plane - gap, 0), 0)
        terms.append(plane_shift(up, gap))
        terms.append(plane_shift(down, -gap))
    return add_low(*terms)


def core_half(slabs, core, axis):
    got = xor_swap(pick(slabs, 1 - core, axis), 2)
    return add_low(pick(slabs, core, axis), got).astype(jnp.bfloat16)


def body(
    tokens,
    w_query,
    w_key,
    w_value,
    w_out,
    gain_attn,
    shift_attn,
    w_up,
    w_down,
    gain_mlp,
    shift_mlp,
    cotangent,
    lengths,
    seq_order,
    rand_blocks,
):
    piece, width = tokens.shape
    seqs, heads = lax.axis_size("seq"), lax.axis_size("head")
    planes = seqs // 4
    piece_blocks = piece // BLK
    assert heads == 2 and 8 * piece == MAXB * BLK and width == 4 * WQ
    seq_at, x_at = lax.axis_index("seq"), lax.axis_index("head")
    plane, y_at, core = seq_at // 4, (seq_at // 2) % 2, seq_at % 2
    group = y_at * 2 + x_at

    rand_y = lax.ppermute(rand_blocks, "seq", [(s, s ^ 2) for s in range(seqs)])

    def columns(weights):
        return lax.dynamic_slice_in_dim(weights, group * WQ, WQ, 1)

    wq_own = jnp.pad(columns(w_query) * jnp.bfloat16(DH ** (-0.5)), ((0, 0), (0, WIN - WQ)))
    wkv_own = jnp.concatenate([columns(w_key), columns(w_value)], axis=1)
    order = [group ^ j for j in range(4)]
    wout_own = jnp.concatenate(
        [
            jnp.pad(lax.dynamic_slice_in_dim(w_out, g * WQ, WQ, 0), ((WIN - WQ, 0), (0, 0)))
            for g in order
        ],
        axis=0,
    )

    local = jnp.arange(4 * piece_blocks, dtype=jnp.int32)
    far, near = local // piece_blocks, local % piece_blocks
    half = 4 * piece_blocks
    blocks = (
        plane * MAXB
        + (y_at ^ (far >> 1)) * half
        + core * (2 * piece_blocks)
        + (x_at ^ (far & 1)) * piece_blocks
        + near
    )
    here = rand_blocks.reshape(2, piece_blocks, -1)
    there = rand_y.reshape(2, piece_blocks, -1)
    rand_rows = jnp.concatenate(
        [pick(here, x_at, 0), pick(here, 1 - x_at, 0), pick(there, x_at, 0), pick(there, 1 - x_at, 0)],
        axis=0,
    )
    key_blocks, is_live = block_slots(blocks, rand_rows, lengths, seq_order)
    rel = key_blocks // MAXB - plane + 1
    in_plane = key_blocks % MAXB
    y_of, rest = in_plane // half, in_plane % half
    core_of, rest = rest // (2 * piece_blocks), rest % (2 * piece_blocks)
    x_of, near_of = rest // piece_blocks, rest % piece_blocks
    idx = (
        ((rel * 2 + (core_of ^ core)) * 4 + ((y_of ^ y_at) * 2 + (x_of ^ x_at))) * piece_blocks
        + near_of
    ).reshape(-1)
    live = is_live.astype(jnp.int32).reshape(-1)
    bias = jnp.repeat(jnp.where(is_live, 0.0, NEG).astype(jnp.float32), BLK, axis=1)

    def low_dot(a, b):
        return jnp.dot(a, b, preferred_element_type=jnp.float32).astype(jnp.bfloat16)

    keys_values, queries, stretch = gather_project(tokens, wq_own, wkv_own, planes)
    context = attend(idx, bias, queries, keys_values)

    def to_owners(array):
        parts = array.reshape(4, piece, -1)
        return [parts[0], xor_swap(parts[1], 1), xor_swap(parts[2], 4), xor_swap(parts[3], 5)]

    context_tok = jnp.concatenate(to_owners(context), axis=1)
    attn_out = jnp.dot(context_tok, wout_own, preferred_element_type=jnp.float32)
    normed, hat_one, dev_one = norm_forward(
        tokens.astype(jnp.float32) + attn_out, gain_attn, shift_attn
    )
    normed_low = normed.astype(jnp.bfloat16)
    hidden_pre = jnp.dot(normed_low, w_up, preferred_element_type=jnp.float32)
    hidden = gelu_tanh(hidden_pre).astype(jnp.bfloat16)
    mlp_out = jnp.dot(hidden, w_down, preferred_element_type=jnp.float32)
    output, hat_two, dev_two = norm_forward(normed + mlp_out, gain_mlp, shift_mlp)
    grad_two, grad_gain_mlp, grad_shift_mlp = norm_backward(
        cotangent.astype(jnp.float32), hat_two, dev_two, gain_mlp
    )
    grad_mlp = grad_two.astype(jnp.bfloat16)
    grad_hidden = jnp.dot(grad_mlp, w_down.T, preferred_element_type=jnp.float32)
    gelu_out, gelu_pull = jax.vjp(gelu_tanh, hidden_pre)
    grad_pre = gelu_pull(grad_hidden)[0].astype(jnp.bfloat16)
    grad_normed = grad_two + jnp.dot(grad_pre, w_up.T, preferred_element_type=jnp.float32)
    grad_one, grad_gain_attn, grad_shift_attn = norm_backward(
        grad_normed, hat_one, dev_one, gain_attn
    )
    grad_attn = grad_one.astype(jnp.bfloat16)
    grad_context = low_dot(grad_attn, wout_own.T)
    cols = [grad_context[:, j * WIN : (j + 1) * WIN] for j in range(4)]
    grad_ctx = jnp.concatenate(
        [cols[0], xor_swap(cols[1], 1), xor_swap(cols[2], 4), xor_swap(cols[3], 5)], axis=0
    )

    grad_w_down = low_dot(hidden.T, grad_mlp)
    grad_w_up = low_dot(normed_low.T, grad_pre)
    grad_w_out = low_dot(context_tok.T, grad_attn).reshape(4, WIN, width)[:, WIN - WQ :]
    grad_w_out = jnp.concatenate([pick(grad_w_out, g, 0) for g in order], axis=0)

    norm_rows = jnp.stack([grad_gain_attn, grad_shift_attn, grad_gain_mlp, grad_shift_mlp])
    share = width // seqs
    norm_rows = norm_rows.reshape(4, seqs, share).transpose(1, 0, 2).reshape(seqs, 1, 4 * share)
    norm_rows = jnp.pad(norm_rows, ((0, 0), (0, 15), (0, width - 4 * share))).astype(jnp.bfloat16)
    out_slabs = jnp.concatenate([grad_w_out.reshape(seqs, share, width), norm_rows], axis=1)
    up_slabs = grad_w_up.reshape(seqs, share, -1)
    down_slabs = grad_w_down.reshape(seqs, -1, width)

    def y_first(slabs):
        slabs = slabs.reshape((planes, 2, 2) + slabs.shape[1:])
        slabs = core_half(slabs, core, 2)
        return pick(slabs, y_at, 1), xor_swap(pick(slabs, 1 - y_at, 1), 4)

    def x_first(slabs):
        slabs = slabs.reshape((planes, 2, 2) + slabs.shape[1:])
        slabs = core_half(slabs, core, 2)
        size = slabs.shape[3] // 2

        def side(at):
            return lax.dynamic_slice_in_dim(slabs, at * size, size, 3)

        return side(x_at), xor_swap(side(1 - x_at), 1)

    down_pair = x_first(down_slabs)
    up_pair = y_first(up_slabs)
    out_pair = y_first(out_slabs)

    grad_q, grad_kv = attend_back(idx, live, queries, grad_ctx, keys_values)
    wq_plain = jnp.pad(columns(w_query), ((0, 0), (0, WIN - WQ)))
    grad_attend, quarters, up_two, down_two, out_two = reduce_all(
        grad_kv, grad_q, stretch, wq_plain, wkv_own, up_pair, out_pair, down_pair, planes
    )
    grad_tokens = grad_one + grad_attend

    def joined(two):
        return jnp.concatenate([two[0], two[1]], axis=1).astype(jnp.float32)

    up_total, down_total, out_total = joined(up_two), joined(down_two), joined(out_two)
    quarters = [pick(quarters, g, 0) for g in order]

    def whole(at):
        return jnp.concatenate([q[:, at : at + WQ] for q in quarters], axis=1).astype(jnp.float32)

    norm_row = out_total[share]

    def norm_grad(n):
        return norm_row[n * share : (n + 1) * share]

    return (
        output.astype(jnp.bfloat16),
        grad_tokens,
        whole(2 * WQ),
        whole(0),
        whole(WQ),
        out_total[:share],
        norm_grad(0),
        norm_grad(1),
        up_total,
        down_total,
        norm_grad(2),
        norm_grad(3),
    )


def solution(mesh):
    rows = P(("seq", "head"), None)
    seq_rows, seq_only = P("seq", None), P("seq")
    return jax.shard_map(
        body,
        mesh=mesh,
        in_specs=(rows,) + (P(),) * 10 + (rows, P(), P(), seq_rows),
        out_specs=(
            rows,
            rows,
            seq_rows,
            seq_rows,
            seq_rows,
            seq_rows,
            seq_only,
            seq_only,
            seq_rows,
            seq_rows,
            seq_only,
            seq_only,
        ),
        check_vma=False,
    )
```

```python
import functools

import jax
import jax.numpy as jnp
from jax import lax
from jax.experimental import pallas as pl
from jax.experimental.pallas import tpu as pltpu
from jax.sharding import PartitionSpec as P

DH = 64
BLK = 64
MAXB = 64
SLOTS = 8
HG = 3
WQ = HG * DH
WIN = 256
AXES = ("seq", "head")
NEG = -1e30

eps_norm = 1e-06


def xor_swap(value, bits):
    count = lax.axis_size("seq") * lax.axis_size("head")
    return lax.ppermute(value, AXES, [(d, d ^ bits) for d in range(count)])


def plane_shift(value, steps):
    count = lax.axis_size("seq") * lax.axis_size("head")
    gap = 8 * steps
    return lax.ppermute(
        value, AXES, [(d, d + gap) for d in range(count) if 0 <= d + gap < count]
    )


def block_slots(blocks, rand_rows, lengths, seq_order):
    seq_count = lengths.shape[0]
    seq_ids = jnp.arange(seq_count, dtype=jnp.int32)
    packed = jnp.sum(jnp.where(seq_order[:, None] == seq_ids[None, :], lengths[None, :], 0), axis=1)
    seq_ends = jnp.cumsum(packed)
    starts = seq_ends - packed
    holder = jnp.sum((seq_ends[None, :] <= blocks[:, None]).astype(jnp.int32), axis=1)
    chosen = holder[:, None] == seq_ids[None, :]
    seq_first = jnp.sum(jnp.where(chosen, starts[None, :], 0), axis=1)
    seq_span = jnp.sum(jnp.where(chosen, packed[None, :], 0), axis=1)
    offset = blocks - seq_first
    rand_pos = seq_first[:, None] + jnp.mod(rand_rows, seq_span[:, None])
    fixed_cand = jnp.stack(
        [blocks - 1, blocks, blocks + 1, seq_first, seq_first + seq_span - 1], axis=1
    )
    candidate = jnp.concatenate([fixed_cand, rand_pos], axis=1)
    fixed_live = jnp.stack(
        [offset > 0, offset >= 0, offset < seq_span - 1, offset >= 0, offset >= 0], axis=1
    )
    usable = jnp.concatenate([fixed_live, rand_pos >= 0], axis=1)
    kept_list = []
    for column in range(candidate.shape[1]):
        unique = usable[:, column]
        for earlier in range(column):
            unique = unique & jnp.logical_not(
                kept_list[earlier] & (candidate[:, earlier] == candidate[:, column])
            )
        kept_list.append(unique)
    is_live = jnp.stack(kept_list, axis=1)
    key_blocks = jnp.where(is_live, candidate, blocks[:, None])
    return (key_blocks, is_live)


def norm_forward(values, gain_vec, shift_vec):
    center = values - jnp.mean(values, axis=-1, keepdims=True)
    spread = jnp.mean(center * center, axis=-1, keepdims=True)
    inv_dev = lax.rsqrt(spread + eps_norm)
    x_hat = center * inv_dev
    return (x_hat * gain_vec + shift_vec, x_hat, inv_dev)


def norm_backward(grad_in, x_hat, inv_dev, gain_vec):
    grad_gain = jnp.sum(grad_in * x_hat, axis=0)
    grad_shift = jnp.sum(grad_in, axis=0)
    grad_hat = grad_in * gain_vec
    grad_mean = jnp.mean(grad_hat, axis=-1, keepdims=True)
    grad_proj = jnp.mean(grad_hat * x_hat, axis=-1, keepdims=True)
    return (inv_dev * (grad_hat - grad_mean - x_hat * grad_proj), grad_gain, grad_shift)


def gelu_tanh(values):
    return jax.nn.gelu(values, approximate=True)


def lane_groups(rows, offset):
    lane = lax.broadcasted_iota(jnp.int32, (rows, WIN), 1) - offset
    return [jnp.logical_and(lane >= h * DH, lane < (h + 1) * DH) for h in range(HG)]


def spread_heads(block, offset):
    zero = jnp.zeros_like(block)
    return jnp.concatenate([jnp.where(m, block, zero) for m in lane_groups(BLK, offset)], axis=0)


def fold_heads(stacked, offset):
    masks = lane_groups(BLK, offset)
    total = jnp.where(masks[0], stacked[:BLK], 0.0)
    for h in range(1, HG):
        total = total + jnp.where(masks[h], stacked[h * BLK : (h + 1) * BLK], 0.0)
    return total


def fetch(source, kv, sems):
    copy = pltpu.make_async_copy(source, kv, sems.at[0])
    copy.start()
    copy.wait()


def nt(a, b):
    return lax.dot_general(a, b, (((1,), (1,)), ((), ())), preferred_element_type=jnp.float32)


def tn(a, b):
    return lax.dot_general(a, b, (((0,), (0,)), ((), ())), preferred_element_type=jnp.float32)


def forward_kernel(idx_ref, bias_ref, q_ref, *refs):
    kv_ref, ctx_ref, kv, sems = refs
    fetch(kv_ref, kv, sems)

    def step(i, carry):
        q_rows = pl.multiple_of(i * BLK, BLK)
        qexp = spread_heads(q_ref[pl.ds(q_rows, BLK), :], 0)
        rows = [
            pl.multiple_of(idx_ref[i * SLOTS + s] * BLK, BLK) for s in range(SLOTS)
        ]
        keys = jnp.concatenate([kv[pl.ds(r, BLK), 0:WIN] for r in rows], axis=0)
        values = jnp.concatenate([kv[pl.ds(r, BLK), 128 : 128 + WIN] for r in rows], axis=0)
        scores = nt(qexp, keys) + bias_ref[pl.ds(i, 1), :]
        top = jnp.max(scores, axis=1, keepdims=True)
        e = jnp.exp(scores - top)
        total = jnp.sum(e, axis=1, keepdims=True)
        out = jnp.dot(e.astype(jnp.bfloat16), values, preferred_element_type=jnp.float32)
        ctx_ref[pl.ds(q_rows, BLK), :] = fold_heads(out / total, 64).astype(jnp.bfloat16)
        return carry

    lax.fori_loop(0, q_ref.shape[0] // BLK, step, 0)


def backward_kernel(idx_ref, live_ref, q_ref, do_ref, *refs):
    kv_ref, dq_ref, dkv_ref, kv, acc, sems = refs

    def clear(n, carry):
        acc[pl.ds(pl.multiple_of(n * 256, 256), 256), :] = jnp.zeros((256, 2 * WQ), jnp.float32)
        return carry

    copy = pltpu.make_async_copy(kv_ref, kv, sems.at[0])
    copy.start()
    lax.fori_loop(0, acc.shape[0] // 256, clear, 0)
    copy.wait()

    def step(i, carry):
        q_rows = pl.multiple_of(i * BLK, BLK)
        qexp = spread_heads(q_ref[pl.ds(q_rows, BLK), :], 0)
        doexp = spread_heads(do_ref[pl.ds(q_rows, BLK), :], 64)
        rows = [
            pl.multiple_of(idx_ref[i * SLOTS + s] * BLK, BLK) for s in range(SLOTS)
        ]
        keys = jnp.concatenate([kv[pl.ds(r, BLK), 0:WIN] for r in rows], axis=0)
        values = jnp.concatenate([kv[pl.ds(r, BLK), 128 : 128 + WIN] for r in rows], axis=0)
        raw = nt(keys, qexp)
        scores = jnp.concatenate(
            [
                jnp.where(live_ref[i * SLOTS + s] > 0, raw[s * BLK : (s + 1) * BLK], NEG)
                for s in range(SLOTS)
            ],
            axis=0,
        )
        top = jnp.max(scores, axis=0, keepdims=True)
        e = jnp.exp(scores - top)
        probs = e * (1.0 / jnp.sum(e, axis=0, keepdims=True))
        grad_probs = nt(values, doexp)
        inner = jnp.sum(probs * grad_probs, axis=0, keepdims=True)
        grad_scores = (probs * (grad_probs - inner)).astype(jnp.bfloat16)
        dk = jnp.dot(grad_scores, qexp, preferred_element_type=jnp.float32)
        dv = jnp.dot(probs.astype(jnp.bfloat16), doexp, preferred_element_type=jnp.float32)
        dq = tn(grad_scores, keys)
        dq_ref[pl.ds(q_rows, BLK), :] = (fold_heads(dq, 0) * DH ** (-0.5)).astype(jnp.bfloat16)
        for s in range(SLOTS):
            k_s, v_s = dk[s * BLK : (s + 1) * BLK], dv[s * BLK : (s + 1) * BLK]
            at = pl.ds(rows[s], BLK)
            acc[at, 0:128] += k_s[:, :128]
            acc[at, 128:256] += k_s[:, 128:] + v_s[:, :128]
            acc[at, 256:384] += v_s[:, 128:]
        return carry

    lax.fori_loop(0, q_ref.shape[0] // BLK, step, 0)

    def emit(n, carry):
        at = pl.ds(pl.multiple_of(n * 256, 256), 256)
        dkv_ref[at, :] = acc[at, :].astype(jnp.bfloat16)
        return carry

    lax.fori_loop(0, acc.shape[0] // 256, emit, 0)


VMEM = pl.BlockSpec(memory_space=pltpu.VMEM)
SMEM = pl.BlockSpec(memory_space=pltpu.SMEM)
ANY = pl.BlockSpec(memory_space=pl.ANY)


def device_at(plane, y_at, core, x_at):
    return (plane * 4 + y_at * 2 + core, x_at)


def place():
    seq_at, x_at = lax.axis_index("seq"), lax.axis_index("head")
    return seq_at // 4, (seq_at // 2) % 2, seq_at % 2, x_at


def remote(src, dst, sems, recvs, at, device):
    return pltpu.make_async_remote_copy(
        src_ref=src,
        dst_ref=dst,
        send_sem=sems.at[at],
        recv_sem=recvs.at[at],
        device_id=device,
        device_id_type=pl.DeviceIdType.MESH,
    )


def greet(partners):
    barrier = pltpu.get_barrier_semaphore()
    for device in partners:
        pl.semaphore_signal(
            barrier, inc=1, device_id=device, device_id_type=pl.DeviceIdType.MESH
        )
    pl.semaphore_wait(barrier, len(partners))


CHUNK_ORDER = (0, 1, 2, 4, 3, 5, 6, 7)


def gather_kernel(planes, tok_ref, wq_ref, wkv_ref, kv_out, q_ref, x_out, xs, kvs, *sems):
    x_send, x_recv, k_send, k_recv, up_send, up_recv, dn_send, dn_recv = sems[:8]
    f_send, f_recv, g_send, g_recv, l_sem, s_sem = sems[8:]
    plane, y_at, core, x_at = place()
    piece = tok_ref.shape[0]
    rows = piece // 2
    part = 4 * piece
    by_x = device_at(plane, y_at, core, 1 - x_at)
    by_y = device_at(plane, 1 - y_at, core, x_at)
    by_core = device_at(plane, y_at, 1 - core, x_at)
    above = device_at(plane + 1, y_at, core, x_at)
    below = device_at(plane - 1, y_at, core, x_at)
    has_above, has_below = plane < planes - 1, plane > 0
    ring = [device_at(lax.rem(plane + g, planes), y_at, core, x_at) for g in (1, planes - 1)]
    greet([by_x, by_y, by_core] + ring)

    def x_rows(c):
        return xs.at[pl.ds((c - 2) * rows, rows)]

    def tok_rows(c):
        return tok_ref.at[pl.ds(c * rows, rows)]

    hops = {
        2: remote(tok_rows(0), x_rows(2), x_send, x_recv, 0, by_x),
        4: remote(tok_rows(0), x_rows(4), x_send, x_recv, 2, by_y),
        3: remote(tok_rows(1), x_rows(3), x_send, x_recv, 1, by_x),
        5: remote(tok_rows(1), x_rows(5), x_send, x_recv, 3, by_y),
        6: remote(x_rows(2), x_rows(6), x_send, x_recv, 4, by_y),
        7: remote(x_rows(5), x_rows(7), x_send, x_recv, 5, by_x),
    }
    for c in (2, 4, 3, 5):
        hops[c].start()

    def kv_rows(part_at, c):
        return kv_out.at[pl.ds(part_at * part + c * rows, rows)]

    to_core, to_above, to_below, pass_up, pass_down = {}, {}, {}, {}, {}
    stores = {}
    for c in range(8):
        mine = kvs.at[pl.ds(c * rows, rows)]
        to_core[c] = remote(mine, kv_rows(3, c), k_send, k_recv, c, by_core)
        to_above[c] = remote(mine, kv_rows(0, c), up_send, up_recv, c, above)
        to_below[c] = remote(mine, kv_rows(4, c), dn_send, dn_recv, c, below)
        pass_up[c] = remote(kv_rows(0, c), kv_rows(1, c), f_send, f_recv, c, by_core)
        pass_down[c] = remote(kv_rows(4, c), kv_rows(5, c), g_send, g_recv, c, by_core)
        stores[c] = pltpu.make_async_copy(mine, kv_rows(2, c), l_sem.at[c])
    keeps = {
        c: pltpu.make_async_copy(
            tok_rows(c) if c < 2 else x_rows(c), x_out.at[pl.ds(c * rows, rows)], s_sem.at[c]
        )
        for c in range(8)
    }

    def relay(c):
        @pl.when(has_below)
        def _():
            to_above[c].wait_recv()
            pass_up[c].start()

        @pl.when(has_above)
        def _():
            to_below[c].wait_recv()
            pass_down[c].start()

    for n, c in enumerate(CHUNK_ORDER):
        if c >= 2:
            hops[c].wait_recv()
        if c == 2:
            hops[6].start()
        if c == 5:
            hops[7].start()
        keeps[c].start()
        block = tok_ref[pl.ds(c * rows, rows), :] if c < 2 else xs[pl.ds((c - 2) * rows, rows), :]
        kvs[pl.ds(c * rows, rows), :] = jnp.dot(
            block, wkv_ref[...], preferred_element_type=jnp.float32
        ).astype(jnp.bfloat16)

        @pl.when(has_above)
        def _(c=c):
            to_above[c].start()

        @pl.when(has_below)
        def _(c=c):
            to_below[c].start()

        to_core[c].start()
        stores[c].start()
        q_ref[pl.ds(c * rows, rows), :] = jnp.dot(
            block, wq_ref[...], preferred_element_type=jnp.float32
        ).astype(jnp.bfloat16)
        if n >= 3:
            relay(CHUNK_ORDER[n - 3])
    for c in CHUNK_ORDER[5:]:
        relay(c)
    for c in (2, 4, 3, 5, 6, 7):
        hops[c].wait_send()
    for c in range(8):
        to_core[c].wait()
        stores[c].wait()
        keeps[c].wait()

        @pl.when(has_above)
        def _(c=c):
            to_above[c].wait_send()
            pass_down[c].wait()

        @pl.when(has_below)
        def _(c=c):
            to_below[c].wait_send()
            pass_up[c].wait()


def gather_project(tokens, wq_own, wkv_own, planes):
    piece, width = tokens.shape
    dma = pltpu.SemaphoreType.DMA
    return pl.pallas_call(
        functools.partial(gather_kernel, planes),
        out_shape=[
            jax.ShapeDtypeStruct((24 * piece, 2 * WQ), jnp.bfloat16),
            jax.ShapeDtypeStruct((4 * piece, WIN), jnp.bfloat16),
            jax.ShapeDtypeStruct((4 * piece, width), jnp.bfloat16),
        ],
        in_specs=[VMEM] * 3,
        out_specs=[ANY, VMEM, ANY],
        scratch_shapes=[
            pltpu.VMEM((3 * piece, width), jnp.bfloat16),
            pltpu.VMEM((4 * piece, 2 * WQ), jnp.bfloat16),
            dma((6,)),
            dma((6,)),
        ]
        + [dma((8,))] * 12,
        compiler_params=pltpu.CompilerParams(
            collective_id=0, has_side_effects=True, vmem_limit_bytes=20 << 20
        ),
        cost_estimate=pl.CostEstimate(
            flops=2 * 4 * piece * width * 640, bytes_accessed=40 << 20, transcendentals=0
        ),
        name="gather_project",
    )(tokens, wq_own, wkv_own)


def attend(idx, bias, queries, keys_values):
    rows, width = keys_values.shape[0] // 6, keys_values.shape[1]
    count = queries.shape[0]
    return pl.pallas_call(
        forward_kernel,
        out_shape=jax.ShapeDtypeStruct((count, WIN), jnp.bfloat16),
        in_specs=[SMEM, VMEM, VMEM] + [ANY],
        out_specs=VMEM,
        scratch_shapes=[
            pltpu.VMEM((6 * rows, width), jnp.bfloat16),
            pltpu.SemaphoreType.DMA((1,)),
        ],
        compiler_params=pltpu.CompilerParams(vmem_limit_bytes=24 << 20),
        cost_estimate=pl.CostEstimate(
            flops=2 * 4 * count * 3 * 256 * 512, bytes_accessed=12 * rows * width, transcendentals=count * 3 * 512
        ),
        name="attend",
    )(idx, bias, queries, keys_values)


def attend_back(idx, live, queries, grads, keys_values):
    rows, width = keys_values.shape[0] // 6, keys_values.shape[1]
    count = queries.shape[0]
    kv_shape = jax.ShapeDtypeStruct((6 * rows, width), jnp.bfloat16)
    return pl.pallas_call(
        backward_kernel,
        out_shape=[jax.ShapeDtypeStruct((count, WIN), jnp.bfloat16)] + [kv_shape],
        in_specs=[SMEM, SMEM, VMEM, VMEM] + [ANY],
        out_specs=[VMEM] * 2,
        scratch_shapes=[
            pltpu.VMEM((6 * rows, width), jnp.bfloat16),
            pltpu.VMEM((6 * rows, width), jnp.float32),
            pltpu.SemaphoreType.DMA((1,)),
        ],
        compiler_params=pltpu.CompilerParams(vmem_limit_bytes=56 << 20),
        cost_estimate=pl.CostEstimate(
            flops=2 * 10 * count * 3 * 256 * 512, bytes_accessed=24 * rows * width, transcendentals=count * 3 * 512
        ),
        name="attend_back",
    )(idx, live, queries, grads, keys_values)


JORDER = (3, 1, 2, 0)


def reduce_kernel(planes, n_own, *refs):
    (dkv_in, dq_ref, x_ref, wq_ref, wkv_ref, up_a, up_b, out_a, out_b, down_a, down_b) = refs[:11]
    attn_out, proj_out, up_out, down_out, side_out = refs[11:16]
    (own, core_in, z_out, z_in, g_all, dx_out, dx_in, acc) = refs[16:24]
    (p_slab, p_core, p_z, p_zin, p_fin) = refs[24:29]
    w_sum, w_got, w_two, w_zin = refs[29:32], refs[32:35], refs[35:38], refs[38:41]
    (l_sem, c_s, c_r, u_s, u_r, d_s, d_r, x_s, x_r) = refs[41:50]
    (pk_s, pk_r, pz_s, pz_r, pf_s, pf_r) = refs[50:56]
    (w2_s, w2_r, w3_s, w3_r, w4_s, w4_r) = refs[56:62]
    plane, y_at, core, x_at = place()
    piece = attn_out.shape[0]
    part = 4 * piece
    rest = planes - 1

    def there(j):
        return device_at(plane, y_at ^ (j >> 1), core, x_at ^ (j & 1))

    by_x, by_y, by_xy = there(1), there(2), there(3)
    by_core = device_at(plane, y_at, 1 - core, x_at)
    others = [device_at(lax.rem(plane + g, planes), y_at, core, x_at) for g in range(1, planes)]

    greet([by_x, by_y, by_xy, by_core] + others)

    has_above, has_below = plane < planes - 1, plane > 0
    above = device_at(plane + 1, y_at, core, x_at)
    below = device_at(plane - 1, y_at, core, x_at)

    def rows(r, j):
        return pl.ds(r * part + j * piece, piece)

    def in_rows(r, kk, j):
        return pl.ds((2 * r + kk) * part + j * piece, piece)

    turns = [(r, j) for j in JORDER for r in (0, 2)] + [(1, j) for j in JORDER]
    loads, to_core = {}, {}
    for n, (r, j) in enumerate(turns):
        loads[r, j] = pltpu.make_async_copy(
            dkv_in.at[in_rows(r, 0, j)], own.at[rows(r, j)], l_sem.at[n]
        )
        to_core[r, j] = remote(
            dkv_in.at[in_rows(r, 1, j)], core_in.at[rows(r, j)], c_s, c_r, n, by_core
        )
    for key in turns:
        to_core[key].start()
        loads[key].start()

    halves = [up_a.shape[2] // 2, out_a.shape[2] // 2]
    pairs = [(up_a, up_b), (out_a, out_b)]
    w2 = []
    for n in range(2):
        a, b = pairs[n]
        for p in range(planes):
            w_sum[n][p] = (a[p].astype(jnp.float32) + b[p].astype(jnp.float32)).astype(jnp.bfloat16)
        give = pl.ds(pl.multiple_of((1 - x_at) * halves[n], 128), halves[n])
        w2.append(remote(w_sum[n].at[:, :, give], w_got[n], w2_s, w2_r, n, by_x))
        w2[n].start()
    for p in range(planes):
        for y in range(2):
            w_sum[2][p, y] = (
                down_a[p, y].astype(jnp.float32) + down_b[p, y].astype(jnp.float32)
            ).astype(jnp.bfloat16)
    w2.append(remote(w_sum[2].at[:, 1 - y_at], w_got[2], w2_s, w2_r, 2, by_y))
    w2[2].start()

    to_below, to_above = {}, {}
    for n, j in enumerate(JORDER):
        to_below[j] = remote(
            z_out.at[rows(0, j)], z_in.at[rows(0, j)], d_s, d_r, n, below
        )
        to_above[j] = remote(
            z_out.at[rows(1, j)], z_in.at[rows(1, j)], u_s, u_r, n, above
        )

    def both(r, j):
        to_core[r, j].wait_recv()
        loads[r, j].wait()
        at = rows(r, j)
        return own[at, :].astype(jnp.float32) + core_in[at, :].astype(jnp.float32)

    for j in JORDER:
        z_out[rows(0, j), :] = both(0, j).astype(jnp.bfloat16)

        @pl.when(has_below)
        def _(j=j):
            to_below[j].start()

        z_out[rows(1, j), :] = both(2, j).astype(jnp.bfloat16)

        @pl.when(has_above)
        def _(j=j):
            to_above[j].start()

    w3 = []
    for n in range(3):
        w2[n].wait_recv()
        for p in range(planes):
            if n < 2:
                keep = w_sum[n][p, :, pl.ds(pl.multiple_of(x_at * halves[n], 128), halves[n])]
            else:
                keep = w_sum[n][p, y_at]
            w_two[n][p] = (
                keep.astype(jnp.float32) + w_got[n][p].astype(jnp.float32)
            ).astype(jnp.bfloat16)
        for g in range(1, planes):
            w3.append(
                remote(
                    w_two[n].at[lax.rem(plane + g, planes)],
                    w_zin[n].at[g - 1],
                    w3_s,
                    w3_r,
                    n * rest + g - 1,
                    others[g - 1],
                )
            )
            w3[-1].start()

    to_owner = {
        j: remote(
            dx_out.at[pl.ds((j - 1) * piece, piece)],
            dx_in.at[pl.ds((j - 1) * piece, piece)],
            x_s,
            x_r,
            j - 1,
            there(j),
        )
        for j in (1, 2, 3)
    }
    first = True
    for j in JORDER:
        g_all[:, 2 * WQ :] = dq_ref[pl.ds(j * piece, piece), :]
        g_all[:, : 2 * WQ] = both(1, j).astype(jnp.bfloat16)

        @pl.when(has_above)
        def _(j=j):
            to_below[j].wait_recv()
            g_all[:, : 2 * WQ] = (
                g_all[:, : 2 * WQ].astype(jnp.float32) + z_in[rows(0, j), :].astype(jnp.float32)
            ).astype(jnp.bfloat16)

        @pl.when(has_below)
        def _(j=j):
            to_above[j].wait_recv()
            g_all[:, : 2 * WQ] = (
                g_all[:, : 2 * WQ].astype(jnp.float32) + z_in[rows(1, j), :].astype(jnp.float32)
            ).astype(jnp.bfloat16)

        grads = g_all[...]
        dx = nt(grads[:, 2 * WQ :], wq_ref[...]) + nt(grads[:, : 2 * WQ], wkv_ref[...])
        if j:
            dx_out[pl.ds((j - 1) * piece, piece), :] = dx.astype(jnp.bfloat16)
            to_owner[j].start()
        else:
            attn_out[...] = dx
        step = tn(x_ref[pl.ds(j * piece, piece), :], grads)
        acc[...] = step if first else acc[...] + step
        first = False

    share = p_slab.shape[3]
    for p in range(planes):
        for y in range(2):
            for k in range(2):
                at = ((p * 2 + y) * 2 + k) * share
                p_slab[k, p, y] = acc[at : at + share, :].astype(jnp.bfloat16)
    pk = remote(p_slab.at[1 - core], p_core, pk_s, pk_r, 0, by_core)
    pk.start()

    outs = [up_out, side_out, down_out]
    w4 = []
    for n in range(3):
        total = w_two[n][plane].astype(jnp.float32)
        for g in range(1, planes):
            w3[n * rest + g - 1].wait_recv()
            total = total + w_zin[n][g - 1].astype(jnp.float32)
        outs[n][x_at] = total.astype(jnp.bfloat16)
        w4.append(remote(outs[n].at[x_at], outs[n].at[x_at], w4_s, w4_r, n, by_x))
        w4[n].start()

    pk.wait_recv()
    for p in range(planes):
        p_z[p] = (
            p_slab[core, p].astype(jnp.float32) + p_core[p].astype(jnp.float32)
        ).astype(jnp.bfloat16)
    pz = []
    for g in range(1, planes):
        pz.append(
            remote(
                p_z.at[lax.rem(plane + g, planes)], p_zin.at[g - 1], pz_s, pz_r, g - 1, others[g - 1]
            )
        )
        pz[-1].start()

    total = attn_out[...]
    for j in (3, 1, 2):
        to_owner[j].wait_recv()
        total = total + dx_in[pl.ds((j - 1) * piece, piece), :].astype(jnp.float32)
    attn_out[...] = total

    total = p_z[plane].astype(jnp.float32)
    for g in range(1, planes):
        pz[g - 1].wait_recv()
        total = total + p_zin[g - 1].astype(jnp.float32)
    p_fin[...] = total.astype(jnp.bfloat16)
    pf = []
    for j in (1, 2, 3):
        pf.append(
            remote(p_fin.at[y_at ^ (j >> 1)], proj_out.at[j], pf_s, pf_r, j - 1, there(j))
        )
        pf[-1].start()
    proj_out[0] = p_fin[y_at]
    for copy in pf:
        copy.wait()
    for copy in w4:
        copy.wait()
    for copy in w2 + w3 + pz + [pk]:
        copy.wait_send()
    for key in turns:
        to_core[key].wait_send()
    for j in (1, 2, 3):
        to_owner[j].wait_send()
    for j in JORDER:

        @pl.when(has_below)
        def _(j=j):
            to_below[j].wait_send()

        @pl.when(has_above)
        def _(j=j):
            to_above[j].wait_send()


def reduce_all(dkv, dq, stretch, wq, wkv, up, out, down, planes):
    low = jnp.bfloat16
    piece = dq.shape[0] // 4
    width = stretch.shape[1]
    share = up[0].shape[1]
    rest = planes - 1
    dma = pltpu.SemaphoreType.DMA
    vm = pltpu.VMEM
    side = out[0].shape[1]
    kinds = [(share, up[0].shape[2] // 2), (side, width // 2), (down[0].shape[2], down[0].shape[3])]
    cols = 2 * WQ + WIN
    sds = jax.ShapeDtypeStruct
    return pl.pallas_call(
        functools.partial(reduce_kernel, planes, 0),
        out_shape=[
            sds((piece, width), jnp.float32),
            sds((4, share, cols), low),
            sds((2,) + kinds[0], low),
            sds((2,) + kinds[2], low),
            sds((2,) + kinds[1], low),
        ],
        in_specs=[ANY] + [VMEM] * 10,
        out_specs=[VMEM] * 5,
        scratch_shapes=[
            vm((12 * piece, 2 * WQ), low),
            vm((12 * piece, 2 * WQ), low),
            vm((8 * piece, 2 * WQ), low),
            vm((8 * piece, 2 * WQ), low),
            vm((piece, cols), low),
            vm((3 * piece, width), low),
            vm((3 * piece, width), low),
            vm((width, cols), jnp.float32),
            vm((2, planes, 2, share, cols), low),
            vm((planes, 2, share, cols), low),
            vm((planes, 2, share, cols), low),
            vm((rest, 2, share, cols), low),
            vm((2, share, cols), low),
            vm(up[0].shape, low),
            vm(out[0].shape, low),
            vm(down[0].shape, low),
        ]
        + [vm((planes,) + k, low) for k in kinds] * 2
        + [vm((rest,) + k, low) for k in kinds]
        + [dma((12,))] * 3
        + [dma((4,))] * 4
        + [dma((3,))] * 2
        + [dma((1,))] * 2
        + [dma((rest,))] * 2
        + [dma((3,))] * 2
        + [dma((3,))] * 2
        + [dma((3 * rest,))] * 2
        + [dma((3,))] * 2,
        compiler_params=pltpu.CompilerParams(
            collective_id=1, has_side_effects=True, vmem_limit_bytes=58 << 20
        ),
        cost_estimate=pl.CostEstimate(
            flops=4 * 4 * piece * width * cols, bytes_accessed=40 << 20, transcendentals=0
        ),
        name="reduce_all",
    )(dkv, dq, stretch, wq, wkv, up[0], up[1], out[0], out[1], down[0], down[1])


def gradient_kernel(
    planes, ga_ref, ctx_ref, nl_ref, gp_ref, hid_ref, gm_ref, wout_ref, side_ref, *refs
):
    do_out, up_keep, up_give, out_keep, out_give, down_keep, down_give = refs[:7]
    dctx, up_loc, out_loc, down_loc, up_got, out_got, down_got = refs[7:14]
    do_s, do_r, up_s, up_r, out_s, out_r, down_s, down_r = refs[14:22]
    plane, y_at, core, x_at = place()
    piece, width = ga_ref.shape
    share = up_loc.shape[2]
    slab = down_loc.shape[2]
    pairs = 2 * planes
    group = y_at * 2 + x_at

    def there(j):
        return device_at(plane, y_at ^ (j >> 1), core, x_at ^ (j & 1))

    by_core = device_at(plane, y_at, 1 - core, x_at)
    greet([there(1), there(2), there(3), by_core])

    low = jnp.bfloat16
    trades = []
    for j in (3, 1, 2, 0):
        part = nt(ga_ref[...], wout_ref[pl.ds(j * WIN, WIN), :]).astype(low)
        if j:
            dctx[j - 1] = part
            trades.append(
                remote(
                    dctx.at[j - 1], do_out.at[pl.ds(j * piece, piece)], do_s, do_r, j - 1, there(j)
                )
            )
            trades[-1].start()
        else:
            do_out[pl.ds(0, piece), :] = part

    to_core = []
    tile = 2 * WQ
    per = tile // (2 * slab)
    for t in range(hid_ref.shape[1] // tile):
        cell = tn(hid_ref[:, t * tile : (t + 1) * tile], gm_ref[...])
        for n in range(per):
            for k in range(2):
                at = (n * 2 + k) * slab
                down_loc[k, t * per + n] = cell[at : at + slab].astype(low)
        span = pl.ds(t * per, per)
        to_core.append(
            remote(down_loc.at[1 - core, span], down_got.at[span], down_s, down_r, t, by_core)
        )
        to_core[-1].start()
    ups = []
    for t in range(gp_ref.shape[1] // tile):
        span = pl.ds(t * tile, tile)
        cell = tn(nl_ref[...], gp_ref[:, t * tile : (t + 1) * tile])
        for q in range(pairs):
            for k in range(2):
                at = (q * 2 + k) * share
                up_loc[k, q, :, t * tile : (t + 1) * tile] = cell[at : at + share].astype(low)
        ups.append(
            remote(
                up_loc.at[1 - core, :, :, span], up_got.at[:, :, span], up_s, up_r, t, by_core
            )
        )
        ups[-1].start()
    per_group = pairs // 4
    for j in range(4):
        cell = tn(ctx_ref[:, j * WIN : (j + 1) * WIN], ga_ref[...])
        for n in range(per_group):
            for k in range(2):
                at = WIN - WQ + (n * 2 + k) * share
                out_loc[k, (group ^ j) * per_group + n, :share, :] = cell[at : at + share].astype(low)
    for q in range(pairs):
        for k in range(2):
            out_loc[k, q, share:, :] = side_ref[q, k]
    outs = remote(out_loc.at[1 - core], out_got, out_s, out_r, 0, by_core)
    outs.start()

    half = width // 2
    for n, copy in enumerate(to_core):
        copy.wait_recv()
        for q in range(n * per, (n + 1) * per):
            total = (
                down_loc[core, q].astype(jnp.float32) + down_got[q].astype(jnp.float32)
            ).astype(low)
            low_half, high_half = total[:, :half], total[:, half:]
            first = x_at == 0
            down_keep[q] = jnp.where(first, low_half, high_half)
            down_give[q] = jnp.where(first, high_half, low_half)
    for copy in ups:
        copy.wait_recv()
    for p in range(planes):
        for at, dest in ((y_at, up_keep), (1 - y_at, up_give)):
            q = p * 2 + at
            dest[p] = (up_loc[core, q].astype(jnp.float32) + up_got[q].astype(jnp.float32)).astype(low)
    outs.wait_recv()
    for p in range(planes):
        for at, dest in ((y_at, out_keep), (1 - y_at, out_give)):
            q = p * 2 + at
            dest[p] = (out_loc[core, q].astype(jnp.float32) + out_got[q].astype(jnp.float32)).astype(
                low
            )
    for copy in trades:
        copy.wait()
    for copy in to_core + ups + [outs]:
        copy.wait_send()


def weight_gradients(ga, ctx, nl, gp, hid, gm, wout, side, planes):
    low = jnp.bfloat16
    piece, width = ga.shape
    pairs = 2 * planes
    wide = gp.shape[1]
    share, slab, tall = width // (2 * pairs), wide // (2 * pairs), side.shape[2]
    sds, vm, dma = jax.ShapeDtypeStruct, pltpu.VMEM, pltpu.SemaphoreType.DMA
    up, out = (planes, share, wide), (planes, share + tall, width)
    down = (pairs, slab, width // 2)
    tiles = wide // (2 * WQ)
    return pl.pallas_call(
        functools.partial(gradient_kernel, planes),
        out_shape=[sds((4 * piece, WIN), low)]
        + [sds(up, low)] * 2
        + [sds(out, low)] * 2
        + [sds(down, low)] * 2,
        in_specs=[VMEM] * 8,
        out_specs=[VMEM] * 7,
        scratch_shapes=[
            vm((3, piece, WIN), low),
            vm((2, pairs, share, wide), low),
            vm((2, pairs, share + tall, width), low),
            vm((2, pairs, slab, width), low),
            vm((pairs, share, wide), low),
            vm((pairs, share + tall, width), low),
            vm((pairs, slab, width), low),
        ]
        + [dma((3,))] * 2
        + [dma((tiles,))] * 2
        + [dma((1,))] * 2
        + [dma((tiles,))] * 2,
        compiler_params=pltpu.CompilerParams(
            collective_id=2, has_side_effects=True, vmem_limit_bytes=50 << 20
        ),
        cost_estimate=pl.CostEstimate(
            flops=2 * piece * width * (2 * wide + 2048), bytes_accessed=30 << 20, transcendentals=0
        ),
        name="weight_gradients",
    )(ga, ctx, nl, gp, hid, gm, wout, side)


def add_low(*terms):
    total = terms[0].astype(jnp.float32)
    for term in terms[1:]:
        total = total + term.astype(jnp.float32)
    return total


def pick(array, at, axis):
    return lax.dynamic_index_in_dim(array, at, axis, keepdims=False)


def plane_sum(slabs, plane, count):
    terms = [pick(slabs, plane, 0)]
    for gap in range(1, count):
        up = pick(slabs, jnp.minimum(plane + gap, count - 1), 0)
        down = pick(slabs, jnp.maximum(plane - gap, 0), 0)
        terms.append(plane_shift(up, gap))
        terms.append(plane_shift(down, -gap))
    return add_low(*terms)


def core_half(slabs, core, axis):
    got = xor_swap(pick(slabs, 1 - core, axis), 2)
    return add_low(pick(slabs, core, axis), got).astype(jnp.bfloat16)


def body(
    tokens,
    w_query,
    w_key,
    w_value,
    w_out,
    gain_attn,
    shift_attn,
    w_up,
    w_down,
    gain_mlp,
    shift_mlp,
    cotangent,
    lengths,
    seq_order,
    rand_blocks,
):
    piece, width = tokens.shape
    seqs, heads = lax.axis_size("seq"), lax.axis_size("head")
    planes = seqs // 4
    piece_blocks = piece // BLK
    assert heads == 2 and 8 * piece == MAXB * BLK and width == 4 * WQ
    seq_at, x_at = lax.axis_index("seq"), lax.axis_index("head")
    plane, y_at, core = seq_at // 4, (seq_at // 2) % 2, seq_at % 2
    group = y_at * 2 + x_at

    rand_y = lax.ppermute(rand_blocks, "seq", [(s, s ^ 2) for s in range(seqs)])

    def columns(weights):
        return lax.dynamic_slice_in_dim(weights, group * WQ, WQ, 1)

    wq_own = jnp.pad(columns(w_query) * jnp.bfloat16(DH ** (-0.5)), ((0, 0), (0, WIN - WQ)))
    wkv_own = jnp.concatenate([columns(w_key), columns(w_value)], axis=1)
    order = [group ^ j for j in range(4)]
    wout_own = jnp.concatenate(
        [
            jnp.pad(lax.dynamic_slice_in_dim(w_out, g * WQ, WQ, 0), ((WIN - WQ, 0), (0, 0)))
            for g in order
        ],
        axis=0,
    )

    local = jnp.arange(4 * piece_blocks, dtype=jnp.int32)
    far, near = local // piece_blocks, local % piece_blocks
    half = 4 * piece_blocks
    blocks = (
        plane * MAXB
        + (y_at ^ (far >> 1)) * half
        + core * (2 * piece_blocks)
        + (x_at ^ (far & 1)) * piece_blocks
        + near
    )
    here = rand_blocks.reshape(2, piece_blocks, -1)
    there = rand_y.reshape(2, piece_blocks, -1)
    rand_rows = jnp.concatenate(
        [pick(here, x_at, 0), pick(here, 1 - x_at, 0), pick(there, x_at, 0), pick(there, 1 - x_at, 0)],
        axis=0,
    )
    key_blocks, is_live = block_slots(blocks, rand_rows, lengths, seq_order)
    rel = key_blocks // MAXB - plane + 1
    in_plane = key_blocks % MAXB
    y_of, rest = in_plane // half, in_plane % half
    core_of, rest = rest // (2 * piece_blocks), rest % (2 * piece_blocks)
    x_of, near_of = rest // piece_blocks, rest % piece_blocks
    idx = (
        ((rel * 2 + (core_of ^ core)) * 4 + ((y_of ^ y_at) * 2 + (x_of ^ x_at))) * piece_blocks
        + near_of
    ).reshape(-1)
    live = is_live.astype(jnp.int32).reshape(-1)
    bias = jnp.repeat(jnp.where(is_live, 0.0, NEG).astype(jnp.float32), BLK, axis=1)

    def low_dot(a, b):
        return jnp.dot(a, b, preferred_element_type=jnp.float32).astype(jnp.bfloat16)

    keys_values, queries, stretch = gather_project(tokens, wq_own, wkv_own, planes)
    context = attend(idx, bias, queries, keys_values)

    def to_owners(array):
        parts = array.reshape(4, piece, -1)
        return [parts[0], xor_swap(parts[1], 1), xor_swap(parts[2], 4), xor_swap(parts[3], 5)]

    context_tok = jnp.concatenate(to_owners(context), axis=1)
    attn_out = jnp.dot(context_tok, wout_own, preferred_element_type=jnp.float32)
    normed, hat_one, dev_one = norm_forward(
        tokens.astype(jnp.float32) + attn_out, gain_attn, shift_attn
    )
    normed_low = normed.astype(jnp.bfloat16)
    hidden_pre = jnp.dot(normed_low, w_up, preferred_element_type=jnp.float32)
    hidden = gelu_tanh(hidden_pre).astype(jnp.bfloat16)
    mlp_out = jnp.dot(hidden, w_down, preferred_element_type=jnp.float32)
    output, hat_two, dev_two = norm_forward(normed + mlp_out, gain_mlp, shift_mlp)
    grad_two, grad_gain_mlp, grad_shift_mlp = norm_backward(
        cotangent.astype(jnp.float32), hat_two, dev_two, gain_mlp
    )
    grad_mlp = grad_two.astype(jnp.bfloat16)
    grad_hidden = jnp.dot(grad_mlp, w_down.T, preferred_element_type=jnp.float32)
    gelu_out, gelu_pull = jax.vjp(gelu_tanh, hidden_pre)
    grad_pre = gelu_pull(grad_hidden)[0].astype(jnp.bfloat16)
    grad_normed = grad_two + jnp.dot(grad_pre, w_up.T, preferred_element_type=jnp.float32)
    grad_one, grad_gain_attn, grad_shift_attn = norm_backward(
        grad_normed, hat_one, dev_one, gain_attn
    )
    grad_attn = grad_one.astype(jnp.bfloat16)

    norm_rows = jnp.stack([grad_gain_attn, grad_shift_attn, grad_gain_mlp, grad_shift_mlp])
    share = width // seqs
    norm_rows = norm_rows.reshape(4, seqs, share).transpose(1, 0, 2).reshape(seqs, 1, 4 * share)
    norm_rows = jnp.pad(norm_rows, ((0, 0), (0, 15), (0, width - 4 * share))).astype(jnp.bfloat16)
    grad_ctx, up_keep, up_give, out_keep, out_give, down_keep, down_give = weight_gradients(
        grad_attn,
        context_tok,
        normed_low,
        grad_pre,
        hidden,
        grad_mlp,
        wout_own,
        norm_rows.reshape(2 * planes, 2, 16, width),
        planes,
    )
    up_pair = (up_keep, xor_swap(up_give, 4))
    out_pair = (out_keep, xor_swap(out_give, 4))
    two_y = (planes, 2) + down_keep.shape[1:]
    down_pair = (down_keep.reshape(two_y), xor_swap(down_give, 1).reshape(two_y))

    grad_q, grad_kv = attend_back(idx, live, queries, grad_ctx, keys_values)
    wq_plain = jnp.pad(columns(w_query), ((0, 0), (0, WIN - WQ)))
    grad_attend, quarters, up_two, down_two, out_two = reduce_all(
        grad_kv, grad_q, stretch, wq_plain, wkv_own, up_pair, out_pair, down_pair, planes
    )
    grad_tokens = grad_one + grad_attend

    def joined(two):
        return jnp.concatenate([two[0], two[1]], axis=1).astype(jnp.float32)

    up_total, down_total, out_total = joined(up_two), joined(down_two), joined(out_two)
    quarters = [pick(quarters, g, 0) for g in order]

    def whole(at):
        return jnp.concatenate([q[:, at : at + WQ] for q in quarters], axis=1).astype(jnp.float32)

    norm_row = out_total[share]

    def norm_grad(n):
        return norm_row[n * share : (n + 1) * share]

    return (
        output.astype(jnp.bfloat16),
        grad_tokens,
        whole(2 * WQ),
        whole(0),
        whole(WQ),
        out_total[:share],
        norm_grad(0),
        norm_grad(1),
        up_total,
        down_total,
        norm_grad(2),
        norm_grad(3),
    )


def solution(mesh):
    rows = P(("seq", "head"), None)
    seq_rows, seq_only = P("seq", None), P("seq")
    return jax.shard_map(
        body,
        mesh=mesh,
        in_specs=(rows,) + (P(),) * 10 + (rows, P(), P(), seq_rows),
        out_specs=(
            rows,
            rows,
            seq_rows,
            seq_rows,
            seq_rows,
            seq_rows,
            seq_only,
            seq_only,
            seq_rows,
            seq_rows,
            seq_only,
            seq_only,
        ),
        check_vma=False,
    )
```

```python
import functools

import jax
import jax.numpy as jnp
from jax import lax
from jax.experimental import pallas as pl
from jax.experimental.pallas import tpu as pltpu
from jax.sharding import PartitionSpec as P

DH = 64
BLK = 64
MAXB = 64
SLOTS = 8
HG = 3
WQ = HG * DH
WIN = 256
AXES = ("seq", "head")
NEG = -1e30

eps_norm = 1e-06


def xor_swap(value, bits):
    count = lax.axis_size("seq") * lax.axis_size("head")
    return lax.ppermute(value, AXES, [(d, d ^ bits) for d in range(count)])


def plane_shift(value, steps):
    count = lax.axis_size("seq") * lax.axis_size("head")
    gap = 8 * steps
    return lax.ppermute(
        value, AXES, [(d, d + gap) for d in range(count) if 0 <= d + gap < count]
    )


def norm_forward(values, gain_vec, shift_vec):
    center = values - jnp.mean(values, axis=-1, keepdims=True)
    spread = jnp.mean(center * center, axis=-1, keepdims=True)
    inv_dev = lax.rsqrt(spread + eps_norm)
    x_hat = center * inv_dev
    return (x_hat * gain_vec + shift_vec, x_hat, inv_dev)


def norm_backward(grad_in, x_hat, inv_dev, gain_vec):
    grad_gain = jnp.sum(grad_in * x_hat, axis=0)
    grad_shift = jnp.sum(grad_in, axis=0)
    grad_hat = grad_in * gain_vec
    grad_mean = jnp.mean(grad_hat, axis=-1, keepdims=True)
    grad_proj = jnp.mean(grad_hat * x_hat, axis=-1, keepdims=True)
    return (inv_dev * (grad_hat - grad_mean - x_hat * grad_proj), grad_gain, grad_shift)


def gelu_tanh(values):
    return jax.nn.gelu(values, approximate=True)


def lane_groups(rows, offset):
    lane = lax.broadcasted_iota(jnp.int32, (rows, WIN), 1) - offset
    return [jnp.logical_and(lane >= h * DH, lane < (h + 1) * DH) for h in range(HG)]


def spread_heads(block, offset):
    zero = jnp.zeros_like(block)
    return jnp.concatenate([jnp.where(m, block, zero) for m in lane_groups(BLK, offset)], axis=0)


def fold_heads(stacked, offset):
    masks = lane_groups(BLK, offset)
    total = jnp.where(masks[0], stacked[:BLK], 0.0)
    for h in range(1, HG):
        total = total + jnp.where(masks[h], stacked[h * BLK : (h + 1) * BLK], 0.0)
    return total


def nt(a, b):
    return lax.dot_general(a, b, (((1,), (1,)), ((), ())), preferred_element_type=jnp.float32)


def tn(a, b):
    return lax.dot_general(a, b, (((0,), (0,)), ((), ())), preferred_element_type=jnp.float32)


def backward_kernel(idx_ref, live_ref, q_ref, do_ref, lse_ref, *refs):
    kv_ref, dq_ref, dkv_ref, kv, acc, sems = refs

    def clear(n, carry):
        acc[pl.ds(pl.multiple_of(n * 256, 256), 256), :] = jnp.zeros((256, 2 * WQ), jnp.float32)
        return carry

    copy = pltpu.make_async_copy(kv_ref, kv, sems.at[0])
    copy.start()
    lax.fori_loop(0, acc.shape[0] // 256, clear, 0)
    copy.wait()

    def step(i, carry):
        q_rows = pl.multiple_of(i * BLK, BLK)
        qexp = spread_heads(q_ref[pl.ds(q_rows, BLK), :], 0)
        doexp = spread_heads(do_ref[pl.ds(q_rows, BLK), :], 64)
        rows = [
            pl.multiple_of(idx_ref[i * SLOTS + s] * BLK, BLK) for s in range(SLOTS)
        ]
        keys = jnp.concatenate([kv[pl.ds(r, BLK), 0:WIN] for r in rows], axis=0)
        values = jnp.concatenate([kv[pl.ds(r, BLK), 128 : 128 + WIN] for r in rows], axis=0)
        raw = nt(keys, qexp)
        level = lse_ref[pl.ds(i, 1), :]
        probs = jnp.concatenate(
            [
                jnp.exp(
                    raw[s * BLK : (s + 1) * BLK]
                    - (level + jnp.where(live_ref[i * SLOTS + s] > 0, 0.0, -NEG))
                )
                for s in range(SLOTS)
            ],
            axis=0,
        )
        grad_probs = nt(values, doexp)
        inner = jnp.sum(probs * grad_probs, axis=0, keepdims=True)
        grad_scores = (probs * (grad_probs - inner)).astype(jnp.bfloat16)
        dk = jnp.dot(grad_scores, qexp, preferred_element_type=jnp.float32)
        dv = jnp.dot(probs.astype(jnp.bfloat16), doexp, preferred_element_type=jnp.float32)
        dq = tn(grad_scores, keys)
        dq_ref[pl.ds(q_rows, BLK), :] = (fold_heads(dq, 0) * DH ** (-0.5)).astype(jnp.bfloat16)
        for s in range(SLOTS):
            k_s, v_s = dk[s * BLK : (s + 1) * BLK], dv[s * BLK : (s + 1) * BLK]
            at = pl.ds(rows[s], BLK)
            acc[at, 0:128] += k_s[:, :128]
            acc[at, 128:256] += k_s[:, 128:] + v_s[:, :128]
            acc[at, 256:384] += v_s[:, 128:]
        return carry

    lax.fori_loop(0, q_ref.shape[0] // BLK, step, 0, unroll=4)

    def emit(n, carry):
        at = pl.ds(pl.multiple_of(n * 256, 256), 256)
        dkv_ref[at, :] = acc[at, :].astype(jnp.bfloat16)
        return carry

    lax.fori_loop(0, acc.shape[0] // 256, emit, 0)


VMEM = pl.BlockSpec(memory_space=pltpu.VMEM)
SMEM = pl.BlockSpec(memory_space=pltpu.SMEM)
ANY = pl.BlockSpec(memory_space=pl.ANY)


def device_at(plane, y_at, core, x_at):
    return (plane * 4 + y_at * 2 + core, x_at)


def place():
    seq_at, x_at = lax.axis_index("seq"), lax.axis_index("head")
    return seq_at // 4, (seq_at // 2) % 2, seq_at % 2, x_at


def remote(src, dst, sems, recvs, at, device):
    return pltpu.make_async_remote_copy(
        src_ref=src,
        dst_ref=dst,
        send_sem=sems.at[at],
        recv_sem=recvs.at[at],
        device_id=device,
        device_id_type=pl.DeviceIdType.MESH,
    )


def greet(partners):
    barrier = pltpu.get_barrier_semaphore()
    for device in partners:
        pl.semaphore_signal(
            barrier, inc=1, device_id=device, device_id_type=pl.DeviceIdType.MESH
        )
    pl.semaphore_wait(barrier, len(partners))


CHUNK_ORDER = (0, 1, 2, 4, 3, 5, 6, 7)
JORDER = (3, 1, 2, 0)


def slot_tables(plane, y_at, core, x_at, at, lengths, order, rand_own, rand_got, idx_ref, live_ref):
    per = at["piece_blocks"]

    def one(i, carry):
        far, near = i // per, i % per
        y_of, x_of = y_at ^ (far >> 1), x_at ^ (far & 1)
        block = plane * MAXB + y_of * (4 * per) + core * (2 * per) + x_of * per + near
        begin, first, span = jnp.int32(0), jnp.int32(0), jnp.int32(1)
        for m in range(at["seqs"]):
            size = lengths[order[m]]
            inside = begin <= block
            first = jnp.where(inside, begin, first)
            span = jnp.where(inside, size, span)
            begin = begin + size
        row = x_of * per + near
        draws = []
        for n in range(SLOTS - 5):
            spot = row * (SLOTS - 5) + n
            draw = jnp.where(far >= 2, rand_got[0, spot], rand_own[0, spot])
            for power in range(16, -1, -1):
                multiple = span * (1 << power)
                draw = jnp.where(draw >= multiple, draw - multiple, draw)
            draws.append(first + draw)
        candidates = [block - 1, block, block + 1, first, first + span - 1] + draws
        kept = []
        for s in range(SLOTS):
            alive = jnp.int32(1)
            if s == 0:
                alive = (block > first).astype(jnp.int32)
            if s == 2:
                alive = (block < first + span - 1).astype(jnp.int32)
            for e in range(s):
                same = (candidates[e] == candidates[s]).astype(jnp.int32)
                alive = alive * (1 - kept[e] * same)
            kept.append(alive)
            key = jnp.where(alive > 0, candidates[s], block)
            rel = key // MAXB - plane + 1
            inner = key % MAXB
            y_key, rest = inner // (4 * per), inner % (4 * per)
            core_key, rest = rest // (2 * per), rest % (2 * per)
            x_key, near_key = rest // per, rest % per
            spot = (rel * 2 + (core_key ^ core)) * 4 + ((y_key ^ y_at) * 2 + (x_key ^ x_at))
            idx_ref[i * SLOTS + s] = spot * per + near_key
            live_ref[i * SLOTS + s] = alive
        return carry

    lax.fori_loop(0, 4 * per, one, 0)


def attend_block(i, idx_ref, live_ref, q_ref, kv, lse_ref):
    qexp = spread_heads(q_ref[pl.ds(pl.multiple_of(i * BLK, BLK), BLK), :], 0)
    at = [idx_ref[i * SLOTS + s] for s in range(SLOTS)]
    off = [jnp.where(live_ref[i * SLOTS + s] > 0, 0.0, -NEG) for s in range(SLOTS)]
    keys = jnp.concatenate([kv[r, :, 0:WIN] for r in at], axis=0)
    values = jnp.concatenate([kv[r, :, 128 : 128 + WIN] for r in at], axis=0)
    raw = nt(keys, qexp)
    parts = [raw[s * BLK : (s + 1) * BLK] for s in range(SLOTS)]
    top = jnp.max(parts[1], axis=0, keepdims=True)
    for s in range(SLOTS):
        top = jnp.maximum(top, jnp.max(parts[s], axis=0, keepdims=True) - off[s])
    e = [jnp.exp(parts[s] - (top + off[s])) for s in range(SLOTS)]
    total = jnp.sum(e[0], axis=0, keepdims=True)
    for s in range(1, SLOTS):
        total = total + jnp.sum(e[s], axis=0, keepdims=True)
    lse_ref[pl.ds(i, 1), :] = top + jnp.log(total)
    scale = 1.0 / total
    probs = jnp.concatenate([(v * scale).astype(jnp.bfloat16) for v in e], axis=0)
    return fold_heads(tn(probs, values), 64).astype(jnp.bfloat16)


def gather_kernel(planes, tok_ref, wq_ref, wkv_ref, len_ref, ord_ref, rand_vm, rand_sm, *refs):
    kv, q_ref, x_out, idx_ref, live_ref = refs[:5]
    xs, kvs, rand_got, rand_two = refs[5:9]
    x_send, x_recv, k_send, k_recv, up_send, up_recv, dn_send, dn_recv = refs[9:17]
    f_send, f_recv, g_send, g_recv, s_sem, st_sem, r_send, r_recv, l_sem = refs[17:26]
    plane, y_at, core, x_at = place()
    piece = tok_ref.shape[0]
    rows = piece // 2
    part = 4 * piece
    by_x = device_at(plane, y_at, core, 1 - x_at)
    by_y = device_at(plane, 1 - y_at, core, x_at)
    by_core = device_at(plane, y_at, 1 - core, x_at)
    above = device_at(plane + 1, y_at, core, x_at)
    below = device_at(plane - 1, y_at, core, x_at)
    has_above, has_below = plane < planes - 1, plane > 0
    ring = [device_at(lax.rem(plane + g, planes), y_at, core, x_at) for g in (1, planes - 1)]
    greet([by_x, by_y, by_core] + ring)

    def x_rows(c):
        return xs.at[pl.ds((c - 2) * rows, rows)]

    def tok_rows(c):
        return tok_ref.at[pl.ds(c * rows, rows)]

    hops = {
        2: remote(tok_rows(0), x_rows(2), x_send, x_recv, 0, by_x),
        4: remote(tok_rows(0), x_rows(4), x_send, x_recv, 2, by_y),
        3: remote(tok_rows(1), x_rows(3), x_send, x_recv, 1, by_x),
        5: remote(tok_rows(1), x_rows(5), x_send, x_recv, 3, by_y),
        6: remote(x_rows(2), x_rows(6), x_send, x_recv, 4, by_y),
        7: remote(x_rows(5), x_rows(7), x_send, x_recv, 5, by_x),
    }
    rand_trade = remote(rand_vm, rand_got, r_send, r_recv, 0, by_y)
    rand_trade.start()
    for c in (2, 4, 3, 5):
        hops[c].start()

    def kv_rows(part_at, c):
        return kv.at[pl.ds(part_at * part + c * rows, rows)]

    to_core, to_above, to_below, pass_up, pass_down, stores = {}, {}, {}, {}, {}, {}
    for c in range(8):
        mine = kvs.at[pl.ds(c * rows, rows)]
        stores[c] = pltpu.make_async_copy(mine, kv_rows(2, c), st_sem.at[c])
        to_core[c] = remote(mine, kv_rows(3, c), k_send, k_recv, c, by_core)
        to_above[c] = remote(mine, kv_rows(0, c), up_send, up_recv, c, above)
        to_below[c] = remote(mine, kv_rows(4, c), dn_send, dn_recv, c, below)
        pass_up[c] = remote(kv_rows(0, c), kv_rows(1, c), f_send, f_recv, c, by_core)
        pass_down[c] = remote(kv_rows(4, c), kv_rows(5, c), g_send, g_recv, c, by_core)
    keeps = {
        c: pltpu.make_async_copy(
            tok_rows(c) if c < 2 else x_rows(c), x_out.at[pl.ds(c * rows, rows)], s_sem.at[c]
        )
        for c in range(8)
    }

    def relay(c):
        @pl.when(has_below)
        def _():
            to_above[c].wait_recv()
            pass_up[c].start()

        @pl.when(has_above)
        def _():
            to_below[c].wait_recv()
            pass_down[c].start()

    for n, c in enumerate(CHUNK_ORDER):
        if n == 2:
            rand_trade.wait()
            to_scalar = pltpu.make_async_copy(rand_got, rand_two, l_sem.at[0])
            to_scalar.start()
            to_scalar.wait()
            slot_tables(
                plane,
                y_at,
                core,
                x_at,
                dict(piece_blocks=piece // BLK, seqs=len_ref.shape[0]),
                len_ref,
                ord_ref,
                rand_sm,
                rand_two,
                idx_ref,
                live_ref,
            )
        if c >= 2:
            hops[c].wait_recv()
        if c == 2:
            hops[6].start()
        if c == 5:
            hops[7].start()
        keeps[c].start()
        block = tok_ref[pl.ds(c * rows, rows), :] if c < 2 else xs[pl.ds((c - 2) * rows, rows), :]
        kvs[pl.ds(c * rows, rows), :] = jnp.dot(
            block, wkv_ref[...], preferred_element_type=jnp.float32
        ).astype(jnp.bfloat16)

        @pl.when(has_above)
        def _(c=c):
            to_above[c].start()

        @pl.when(has_below)
        def _(c=c):
            to_below[c].start()

        to_core[c].start()
        stores[c].start()
        q_ref[pl.ds(c * rows, rows), :] = jnp.dot(
            block, wq_ref[...], preferred_element_type=jnp.float32
        ).astype(jnp.bfloat16)
        if n >= 3:
            relay(CHUNK_ORDER[n - 3])
    for c in CHUNK_ORDER[5:]:
        relay(c)
    for c in range(8):
        to_core[c].wait_recv()

        @pl.when(has_above)
        def _(c=c):
            pass_down[c].wait_recv()

        @pl.when(has_below)
        def _(c=c):
            pass_up[c].wait_recv()

    for c in (2, 4, 3, 5, 6, 7):
        hops[c].wait_send()
    for c in range(8):
        to_core[c].wait_send()
        stores[c].wait()
        keeps[c].wait()

        @pl.when(has_above)
        def _(c=c):
            to_above[c].wait_send()
            pass_down[c].wait_send()

        @pl.when(has_below)
        def _(c=c):
            to_below[c].wait_send()
            pass_up[c].wait_send()


def gather_project(tokens, wq_own, wkv_own, lengths, seq_order, rand_row, planes):
    piece, width = tokens.shape
    dma, low = pltpu.SemaphoreType.DMA, jnp.bfloat16
    sds = jax.ShapeDtypeStruct
    blocks = 4 * piece // BLK
    return pl.pallas_call(
        functools.partial(gather_kernel, planes),
        out_shape=[
            sds((24 * piece, 2 * WQ), low),
            sds((4 * piece, WIN), low),
            sds((4 * piece, width), low),
            sds((blocks * SLOTS,), jnp.int32),
            sds((blocks * SLOTS,), jnp.int32),
        ],
        in_specs=[VMEM] * 3 + [SMEM] * 2 + [VMEM, SMEM],
        out_specs=[ANY, VMEM, ANY, SMEM, SMEM],
        scratch_shapes=[
            pltpu.VMEM((3 * piece, width), low),
            pltpu.VMEM((4 * piece, 2 * WQ), low),
            pltpu.VMEM(rand_row.shape, jnp.int32),
            pltpu.SMEM(rand_row.shape, jnp.int32),
            dma((6,)),
            dma((6,)),
        ]
        + [dma((8,))] * 12
        + [dma((1,))] * 3,
        compiler_params=pltpu.CompilerParams(
            collective_id=0, has_side_effects=True, vmem_limit_bytes=24 << 20
        ),
        cost_estimate=pl.CostEstimate(
            flops=2 * 4 * piece * width * 640, bytes_accessed=40 << 20, transcendentals=0
        ),
        name="gather_project",
    )(tokens, wq_own, wkv_own, lengths, seq_order, rand_row, rand_row)


def attend_kernel(planes, idx_ref, live_ref, q_ref, kv_in, ctx_out, lse_ref, *refs):
    kv, ctx, o_send, o_recv, l_sem = refs
    plane, y_at, core, x_at = place()
    piece = ctx_out.shape[0]
    fetch = pltpu.make_async_copy(kv_in, kv, l_sem.at[0])
    fetch.start()
    greet([device_at(plane, y_at ^ (j >> 1), core, x_at ^ (j & 1)) for j in (1, 2, 3)])
    fetch.wait()
    per = piece // BLK
    trades = {}
    for j in JORDER:

        def step(n, carry, j=j):
            done = attend_block(j * per + n, idx_ref, live_ref, q_ref, kv, lse_ref)
            at = pl.ds(pl.multiple_of(n * BLK, BLK), BLK)
            if j:
                ctx[j - 1, at, :] = done
            else:
                ctx_out[at, 0:WIN] = done
            return carry

        lax.fori_loop(0, per, step, 0, unroll=2)
        if j:
            trades[j] = remote(
                ctx.at[j - 1],
                ctx_out.at[:, pl.ds(j * WIN, WIN)],
                o_send,
                o_recv,
                j - 1,
                device_at(plane, y_at ^ (j >> 1), core, x_at ^ (j & 1)),
            )
            trades[j].start()
    for j in (3, 1, 2):
        trades[j].wait()


def attend(idx, live, queries, keys_values, planes):
    piece = queries.shape[0] // 4
    dma, low, sds = pltpu.SemaphoreType.DMA, jnp.bfloat16, jax.ShapeDtypeStruct
    return pl.pallas_call(
        functools.partial(attend_kernel, planes),
        out_shape=[sds((piece, 4 * WIN), low), sds((4 * piece // BLK, WQ), jnp.float32)],
        in_specs=[SMEM, SMEM, VMEM, ANY],
        out_specs=[VMEM, VMEM],
        scratch_shapes=[
            pltpu.VMEM((keys_values.shape[0] // BLK, BLK, keys_values.shape[1]), low),
            pltpu.VMEM((3, piece, WIN), low),
            dma((3,)),
            dma((3,)),
            dma((1,)),
        ],
        compiler_params=pltpu.CompilerParams(
            collective_id=3, has_side_effects=True, vmem_limit_bytes=24 << 20
        ),
        name="attend",
    )(idx, live, queries, keys_values.reshape(-1, BLK, keys_values.shape[1]))


def attend_back(idx, live, queries, grads, level, keys_values):
    rows, width = keys_values.shape[0] // 6, keys_values.shape[1]
    count = queries.shape[0]
    kv_shape = jax.ShapeDtypeStruct((6 * rows, width), jnp.bfloat16)
    return pl.pallas_call(
        backward_kernel,
        out_shape=[jax.ShapeDtypeStruct((count, WIN), jnp.bfloat16)] + [kv_shape],
        in_specs=[SMEM, SMEM, VMEM, VMEM, VMEM, ANY],
        out_specs=[VMEM] * 2,
        scratch_shapes=[
            pltpu.VMEM((6 * rows, width), jnp.bfloat16),
            pltpu.VMEM((6 * rows, width), jnp.float32),
            pltpu.SemaphoreType.DMA((1,)),
        ],
        compiler_params=pltpu.CompilerParams(vmem_limit_bytes=56 << 20),
        cost_estimate=pl.CostEstimate(
            flops=2 * 10 * count * 3 * 256 * 512, bytes_accessed=24 * rows * width, transcendentals=count * 3 * 512
        ),
        name="attend_back",
    )(idx, live, queries, grads, level, keys_values)


def reduce_kernel(planes, n_own, *refs):
    (dkv_in, dq_ref, x_ref, wq_ref, wkv_ref, up_a, up_b, out_a, out_b, down_a, down_b) = refs[:11]
    attn_out, proj_out, up_out, down_out, side_out = refs[11:16]
    (own, core_in, z_out, z_in, g_all, dx_out, dx_in, acc) = refs[16:24]
    (p_slab, p_core, p_z, p_zin, p_fin) = refs[24:29]
    w_sum, w_got, w_two, w_zin = refs[29:32], refs[32:35], refs[35:38], refs[38:41]
    (l_sem, c_s, c_r, u_s, u_r, d_s, d_r, x_s, x_r) = refs[41:50]
    (pk_s, pk_r, pz_s, pz_r, pf_s, pf_r) = refs[50:56]
    (w2_s, w2_r, w3_s, w3_r, w4_s, w4_r) = refs[56:62]
    plane, y_at, core, x_at = place()
    piece = attn_out.shape[0]
    part = 4 * piece
    rest = planes - 1

    def there(j):
        return device_at(plane, y_at ^ (j >> 1), core, x_at ^ (j & 1))

    by_x, by_y, by_xy = there(1), there(2), there(3)
    by_core = device_at(plane, y_at, 1 - core, x_at)
    others = [device_at(lax.rem(plane + g, planes), y_at, core, x_at) for g in range(1, planes)]

    greet([by_x, by_y, by_xy, by_core] + others)

    has_above, has_below = plane < planes - 1, plane > 0
    above = device_at(plane + 1, y_at, core, x_at)
    below = device_at(plane - 1, y_at, core, x_at)

    def rows(r, j):
        return pl.ds(r * part + j * piece, piece)

    def in_rows(r, kk, j):
        return pl.ds((2 * r + kk) * part + j * piece, piece)

    turns = [(r, j) for j in JORDER for r in (0, 2)] + [(1, j) for j in JORDER]
    loads, to_core = {}, {}
    for n, (r, j) in enumerate(turns):
        loads[r, j] = pltpu.make_async_copy(
            dkv_in.at[in_rows(r, 0, j)], own.at[rows(r, j)], l_sem.at[n]
        )
        to_core[r, j] = remote(
            dkv_in.at[in_rows(r, 1, j)], core_in.at[rows(r, j)], c_s, c_r, n, by_core
        )
    for key in turns:
        to_core[key].start()
        loads[key].start()

    halves = [up_a.shape[2] // 2, out_a.shape[2] // 2]
    pairs = [(up_a, up_b), (out_a, out_b)]
    w2 = []
    for n in range(2):
        a, b = pairs[n]
        for p in range(planes):
            w_sum[n][p] = (a[p].astype(jnp.float32) + b[p].astype(jnp.float32)).astype(jnp.bfloat16)
        give = pl.ds(pl.multiple_of((1 - x_at) * halves[n], 128), halves[n])
        w2.append(remote(w_sum[n].at[:, :, give], w_got[n], w2_s, w2_r, n, by_x))
        w2[n].start()
    for p in range(planes):
        for y in range(2):
            w_sum[2][p, y] = (
                down_a[p, y].astype(jnp.float32) + down_b[p, y].astype(jnp.float32)
            ).astype(jnp.bfloat16)
    w2.append(remote(w_sum[2].at[:, 1 - y_at], w_got[2], w2_s, w2_r, 2, by_y))
    w2[2].start()

    to_below, to_above = {}, {}
    for n, j in enumerate(JORDER):
        to_below[j] = remote(
            z_out.at[rows(0, j)], z_in.at[rows(0, j)], d_s, d_r, n, below
        )
        to_above[j] = remote(
            z_out.at[rows(1, j)], z_in.at[rows(1, j)], u_s, u_r, n, above
        )

    def both(r, j):
        to_core[r, j].wait_recv()
        loads[r, j].wait()
        at = rows(r, j)
        return own[at, :].astype(jnp.float32) + core_in[at, :].astype(jnp.float32)

    for j in JORDER:
        z_out[rows(0, j), :] = both(0, j).astype(jnp.bfloat16)

        @pl.when(has_below)
        def _(j=j):
            to_below[j].start()

        z_out[rows(1, j), :] = both(2, j).astype(jnp.bfloat16)

        @pl.when(has_above)
        def _(j=j):
            to_above[j].start()

    w3 = []
    for n in range(3):
        w2[n].wait_recv()
        for p in range(planes):
            if n < 2:
                keep = w_sum[n][p, :, pl.ds(pl.multiple_of(x_at * halves[n], 128), halves[n])]
            else:
                keep = w_sum[n][p, y_at]
            w_two[n][p] = (
                keep.astype(jnp.float32) + w_got[n][p].astype(jnp.float32)
            ).astype(jnp.bfloat16)
        for g in range(1, planes):
            w3.append(
                remote(
                    w_two[n].at[lax.rem(plane + g, planes)],
                    w_zin[n].at[g - 1],
                    w3_s,
                    w3_r,
                    n * rest + g - 1,
                    others[g - 1],
                )
            )
            w3[-1].start()

    to_owner = {
        j: remote(
            dx_out.at[pl.ds((j - 1) * piece, piece)],
            dx_in.at[pl.ds((j - 1) * piece, piece)],
            x_s,
            x_r,
            j - 1,
            there(j),
        )
        for j in (1, 2, 3)
    }
    first = True
    for j in JORDER:
        g_all[:, 2 * WQ :] = dq_ref[pl.ds(j * piece, piece), :]
        g_all[:, : 2 * WQ] = both(1, j).astype(jnp.bfloat16)

        @pl.when(has_above)
        def _(j=j):
            to_below[j].wait_recv()
            g_all[:, : 2 * WQ] = (
                g_all[:, : 2 * WQ].astype(jnp.float32) + z_in[rows(0, j), :].astype(jnp.float32)
            ).astype(jnp.bfloat16)

        @pl.when(has_below)
        def _(j=j):
            to_above[j].wait_recv()
            g_all[:, : 2 * WQ] = (
                g_all[:, : 2 * WQ].astype(jnp.float32) + z_in[rows(1, j), :].astype(jnp.float32)
            ).astype(jnp.bfloat16)

        grads = g_all[...]
        dx = nt(grads[:, 2 * WQ :], wq_ref[...]) + nt(grads[:, : 2 * WQ], wkv_ref[...])
        if j:
            dx_out[pl.ds((j - 1) * piece, piece), :] = dx.astype(jnp.bfloat16)
            to_owner[j].start()
        else:
            attn_out[...] = dx
        step = tn(x_ref[pl.ds(j * piece, piece), :], grads)
        acc[...] = step if first else acc[...] + step
        first = False

    share = p_slab.shape[3]
    for p in range(planes):
        for y in range(2):
            for k in range(2):
                at = ((p * 2 + y) * 2 + k) * share
                p_slab[k, p, y] = acc[at : at + share, :].astype(jnp.bfloat16)
    pk = remote(p_slab.at[1 - core], p_core, pk_s, pk_r, 0, by_core)
    pk.start()

    outs = [up_out, side_out, down_out]
    w4 = []
    for n in range(3):
        total = w_two[n][plane].astype(jnp.float32)
        for g in range(1, planes):
            w3[n * rest + g - 1].wait_recv()
            total = total + w_zin[n][g - 1].astype(jnp.float32)
        outs[n][x_at] = total.astype(jnp.bfloat16)
        w4.append(remote(outs[n].at[x_at], outs[n].at[x_at], w4_s, w4_r, n, by_x))
        w4[n].start()

    pk.wait_recv()
    for p in range(planes):
        p_z[p] = (
            p_slab[core, p].astype(jnp.float32) + p_core[p].astype(jnp.float32)
        ).astype(jnp.bfloat16)
    pz = []
    for g in range(1, planes):
        pz.append(
            remote(
                p_z.at[lax.rem(plane + g, planes)], p_zin.at[g - 1], pz_s, pz_r, g - 1, others[g - 1]
            )
        )
        pz[-1].start()

    total = attn_out[...]
    for j in (3, 1, 2):
        to_owner[j].wait_recv()
        total = total + dx_in[pl.ds((j - 1) * piece, piece), :].astype(jnp.float32)
    attn_out[...] = total

    total = p_z[plane].astype(jnp.float32)
    for g in range(1, planes):
        pz[g - 1].wait_recv()
        total = total + p_zin[g - 1].astype(jnp.float32)
    p_fin[...] = total.astype(jnp.bfloat16)
    pf = []
    for j in (1, 2, 3):
        pf.append(
            remote(p_fin.at[y_at ^ (j >> 1)], proj_out.at[j], pf_s, pf_r, j - 1, there(j))
        )
        pf[-1].start()
    proj_out[0] = p_fin[y_at]
    for copy in pf:
        copy.wait()
    for copy in w4:
        copy.wait()
    for copy in w2 + w3 + pz + [pk]:
        copy.wait_send()
    for key in turns:
        to_core[key].wait_send()
    for j in (1, 2, 3):
        to_owner[j].wait_send()
    for j in JORDER:

        @pl.when(has_below)
        def _(j=j):
            to_below[j].wait_send()

        @pl.when(has_above)
        def _(j=j):
            to_above[j].wait_send()


def reduce_all(dkv, dq, stretch, wq, wkv, up, out, down, planes):
    low = jnp.bfloat16
    piece = dq.shape[0] // 4
    width = stretch.shape[1]
    share = up[0].shape[1]
    rest = planes - 1
    dma = pltpu.SemaphoreType.DMA
    vm = pltpu.VMEM
    side = out[0].shape[1]
    kinds = [(share, up[0].shape[2] // 2), (side, width // 2), (down[0].shape[2], down[0].shape[3])]
    cols = 2 * WQ + WIN
    sds = jax.ShapeDtypeStruct
    return pl.pallas_call(
        functools.partial(reduce_kernel, planes, 0),
        out_shape=[
            sds((piece, width), jnp.float32),
            sds((4, share, cols), low),
            sds((2,) + kinds[0], low),
            sds((2,) + kinds[2], low),
            sds((2,) + kinds[1], low),
        ],
        in_specs=[ANY] + [VMEM] * 10,
        out_specs=[VMEM] * 5,
        scratch_shapes=[
            vm((12 * piece, 2 * WQ), low),
            vm((12 * piece, 2 * WQ), low),
            vm((8 * piece, 2 * WQ), low),
            vm((8 * piece, 2 * WQ), low),
            vm((piece, cols), low),
            vm((3 * piece, width), low),
            vm((3 * piece, width), low),
            vm((width, cols), jnp.float32),
            vm((2, planes, 2, share, cols), low),
            vm((planes, 2, share, cols), low),
            vm((planes, 2, share, cols), low),
            vm((rest, 2, share, cols), low),
            vm((2, share, cols), low),
            vm(up[0].shape, low),
            vm(out[0].shape, low),
            vm(down[0].shape, low),
        ]
        + [vm((planes,) + k, low) for k in kinds] * 2
        + [vm((rest,) + k, low) for k in kinds]
        + [dma((12,))] * 3
        + [dma((4,))] * 4
        + [dma((3,))] * 2
        + [dma((1,))] * 2
        + [dma((rest,))] * 2
        + [dma((3,))] * 2
        + [dma((3,))] * 2
        + [dma((3 * rest,))] * 2
        + [dma((3,))] * 2,
        compiler_params=pltpu.CompilerParams(
            collective_id=1, has_side_effects=True, vmem_limit_bytes=58 << 20
        ),
        cost_estimate=pl.CostEstimate(
            flops=4 * 4 * piece * width * cols, bytes_accessed=40 << 20, transcendentals=0
        ),
        name="reduce_all",
    )(dkv, dq, stretch, wq, wkv, up[0], up[1], out[0], out[1], down[0], down[1])


def gradient_kernel(
    planes, ga_ref, ctx_ref, nl_ref, gp_ref, hid_ref, gm_ref, wout_ref, side_ref, *refs
):
    do_out, up_keep, up_give, out_keep, out_give, down_keep, down_give = refs[:7]
    dctx, up_loc, out_loc, down_loc, up_got, out_got, down_got = refs[7:14]
    do_s, do_r, up_s, up_r, out_s, out_r, down_s, down_r = refs[14:22]
    plane, y_at, core, x_at = place()
    piece, width = ga_ref.shape
    share = up_loc.shape[2]
    slab = down_loc.shape[2]
    pairs = 2 * planes
    group = y_at * 2 + x_at

    def there(j):
        return device_at(plane, y_at ^ (j >> 1), core, x_at ^ (j & 1))

    by_core = device_at(plane, y_at, 1 - core, x_at)
    greet([there(1), there(2), there(3), by_core])

    low = jnp.bfloat16
    trades = []
    for j in (3, 1, 2, 0):
        part = nt(ga_ref[...], wout_ref[pl.ds(j * WIN, WIN), :]).astype(low)
        if j:
            dctx[j - 1] = part
            trades.append(
                remote(
                    dctx.at[j - 1], do_out.at[pl.ds(j * piece, piece)], do_s, do_r, j - 1, there(j)
                )
            )
            trades[-1].start()
        else:
            do_out[pl.ds(0, piece), :] = part

    to_core = []
    tile = 2 * WQ
    per = tile // (2 * slab)
    for t in range(hid_ref.shape[1] // tile):
        cell = tn(hid_ref[:, t * tile : (t + 1) * tile], gm_ref[...])
        for n in range(per):
            for k in range(2):
                at = (n * 2 + k) * slab
                down_loc[k, t * per + n] = cell[at : at + slab].astype(low)
        span = pl.ds(t * per, per)
        to_core.append(
            remote(down_loc.at[1 - core, span], down_got.at[span], down_s, down_r, t, by_core)
        )
        to_core[-1].start()
    ups = []
    for t in range(gp_ref.shape[1] // tile):
        span = pl.ds(t * tile, tile)
        cell = tn(nl_ref[...], gp_ref[:, t * tile : (t + 1) * tile])
        for q in range(pairs):
            for k in range(2):
                at = (q * 2 + k) * share
                up_loc[k, q, :, t * tile : (t + 1) * tile] = cell[at : at + share].astype(low)
        ups.append(
            remote(
                up_loc.at[1 - core, :, :, span], up_got.at[:, :, span], up_s, up_r, t, by_core
            )
        )
        ups[-1].start()
    per_group = pairs // 4
    for j in range(4):
        cell = tn(ctx_ref[:, j * WIN : (j + 1) * WIN], ga_ref[...])
        for n in range(per_group):
            for k in range(2):
                at = WIN - WQ + (n * 2 + k) * share
                out_loc[k, (group ^ j) * per_group + n, :share, :] = cell[at : at + share].astype(low)
    for q in range(pairs):
        for k in range(2):
            out_loc[k, q, share:, :] = side_ref[q, k]
    outs = remote(out_loc.at[1 - core], out_got, out_s, out_r, 0, by_core)
    outs.start()

    half = width // 2
    for n, copy in enumerate(to_core):
        copy.wait_recv()
        for q in range(n * per, (n + 1) * per):
            total = (
                down_loc[core, q].astype(jnp.float32) + down_got[q].astype(jnp.float32)
            ).astype(low)
            low_half, high_half = total[:, :half], total[:, half:]
            first = x_at == 0
            down_keep[q] = jnp.where(first, low_half, high_half)
            down_give[q] = jnp.where(first, high_half, low_half)
    for copy in ups:
        copy.wait_recv()
    for p in range(planes):
        for at, dest in ((y_at, up_keep), (1 - y_at, up_give)):
            q = p * 2 + at
            dest[p] = (up_loc[core, q].astype(jnp.float32) + up_got[q].astype(jnp.float32)).astype(low)
    outs.wait_recv()
    for p in range(planes):
        for at, dest in ((y_at, out_keep), (1 - y_at, out_give)):
            q = p * 2 + at
            dest[p] = (out_loc[core, q].astype(jnp.float32) + out_got[q].astype(jnp.float32)).astype(
                low
            )
    for copy in trades:
        copy.wait()
    for copy in to_core + ups + [outs]:
        copy.wait_send()


def weight_gradients(ga, ctx, nl, gp, hid, gm, wout, side, planes):
    low = jnp.bfloat16
    piece, width = ga.shape
    pairs = 2 * planes
    wide = gp.shape[1]
    share, slab, tall = width // (2 * pairs), wide // (2 * pairs), side.shape[2]
    sds, vm, dma = jax.ShapeDtypeStruct, pltpu.VMEM, pltpu.SemaphoreType.DMA
    up, out = (planes, share, wide), (planes, share + tall, width)
    down = (pairs, slab, width // 2)
    tiles = wide // (2 * WQ)
    return pl.pallas_call(
        functools.partial(gradient_kernel, planes),
        out_shape=[sds((4 * piece, WIN), low)]
        + [sds(up, low)] * 2
        + [sds(out, low)] * 2
        + [sds(down, low)] * 2,
        in_specs=[VMEM] * 8,
        out_specs=[VMEM] * 7,
        scratch_shapes=[
            vm((3, piece, WIN), low),
            vm((2, pairs, share, wide), low),
            vm((2, pairs, share + tall, width), low),
            vm((2, pairs, slab, width), low),
            vm((pairs, share, wide), low),
            vm((pairs, share + tall, width), low),
            vm((pairs, slab, width), low),
        ]
        + [dma((3,))] * 2
        + [dma((tiles,))] * 2
        + [dma((1,))] * 2
        + [dma((tiles,))] * 2,
        compiler_params=pltpu.CompilerParams(
            collective_id=2, has_side_effects=True, vmem_limit_bytes=50 << 20
        ),
        cost_estimate=pl.CostEstimate(
            flops=2 * piece * width * (2 * wide + 2048), bytes_accessed=30 << 20, transcendentals=0
        ),
        name="weight_gradients",
    )(ga, ctx, nl, gp, hid, gm, wout, side)


def add_low(*terms):
    total = terms[0].astype(jnp.float32)
    for term in terms[1:]:
        total = total + term.astype(jnp.float32)
    return total


def pick(array, at, axis):
    return lax.dynamic_index_in_dim(array, at, axis, keepdims=False)


def plane_sum(slabs, plane, count):
    terms = [pick(slabs, plane, 0)]
    for gap in range(1, count):
        up = pick(slabs, jnp.minimum(plane + gap, count - 1), 0)
        down = pick(slabs, jnp.maximum(plane - gap, 0), 0)
        terms.append(plane_shift(up, gap))
        terms.append(plane_shift(down, -gap))
    return add_low(*terms)


def core_half(slabs, core, axis):
    got = xor_swap(pick(slabs, 1 - core, axis), 2)
    return add_low(pick(slabs, core, axis), got).astype(jnp.bfloat16)


def body(
    tokens,
    w_query,
    w_key,
    w_value,
    w_out,
    gain_attn,
    shift_attn,
    w_up,
    w_down,
    gain_mlp,
    shift_mlp,
    cotangent,
    lengths,
    seq_order,
    rand_blocks,
):
    piece, width = tokens.shape
    seqs, heads = lax.axis_size("seq"), lax.axis_size("head")
    planes = seqs // 4
    assert heads == 2 and 8 * piece == MAXB * BLK and width == 4 * WQ
    seq_at, x_at = lax.axis_index("seq"), lax.axis_index("head")
    plane, y_at, core = seq_at // 4, (seq_at // 2) % 2, seq_at % 2
    group = y_at * 2 + x_at

    def columns(weights):
        return lax.dynamic_slice_in_dim(weights, group * WQ, WQ, 1)

    wq_own = jnp.pad(columns(w_query) * jnp.bfloat16(DH ** (-0.5)), ((0, 0), (0, WIN - WQ)))
    wkv_own = jnp.concatenate([columns(w_key), columns(w_value)], axis=1)
    order = [group ^ j for j in range(4)]
    wout_own = jnp.concatenate(
        [
            jnp.pad(lax.dynamic_slice_in_dim(w_out, g * WQ, WQ, 0), ((WIN - WQ, 0), (0, 0)))
            for g in order
        ],
        axis=0,
    )

    def low_dot(a, b):
        return jnp.dot(a, b, preferred_element_type=jnp.float32).astype(jnp.bfloat16)

    flat = rand_blocks.reshape(1, -1)
    rand_row = jnp.pad(flat, ((0, 0), (0, 128 - flat.shape[1])))
    keys_values, queries, stretch, idx, live = gather_project(
        tokens, wq_own, wkv_own, lengths, seq_order, rand_row, planes
    )
    context_tok, level = attend(idx, live, queries, keys_values, planes)
    attn_out = jnp.dot(context_tok, wout_own, preferred_element_type=jnp.float32)
    normed, hat_one, dev_one = norm_forward(
        tokens.astype(jnp.float32) + attn_out, gain_attn, shift_attn
    )
    normed_low = normed.astype(jnp.bfloat16)
    hidden_pre = jnp.dot(normed_low, w_up, preferred_element_type=jnp.float32)
    hidden = gelu_tanh(hidden_pre).astype(jnp.bfloat16)
    mlp_out = jnp.dot(hidden, w_down, preferred_element_type=jnp.float32)
    output, hat_two, dev_two = norm_forward(normed + mlp_out, gain_mlp, shift_mlp)
    grad_two, grad_gain_mlp, grad_shift_mlp = norm_backward(
        cotangent.astype(jnp.float32), hat_two, dev_two, gain_mlp
    )
    grad_mlp = grad_two.astype(jnp.bfloat16)
    grad_hidden = jnp.dot(grad_mlp, w_down.T, preferred_element_type=jnp.float32)
    gelu_out, gelu_pull = jax.vjp(gelu_tanh, hidden_pre)
    grad_pre = gelu_pull(grad_hidden)[0].astype(jnp.bfloat16)
    grad_normed = grad_two + jnp.dot(grad_pre, w_up.T, preferred_element_type=jnp.float32)
    grad_one, grad_gain_attn, grad_shift_attn = norm_backward(
        grad_normed, hat_one, dev_one, gain_attn
    )
    grad_attn = grad_one.astype(jnp.bfloat16)

    norm_rows = jnp.stack([grad_gain_attn, grad_shift_attn, grad_gain_mlp, grad_shift_mlp])
    share = width // seqs
    norm_rows = norm_rows.reshape(4, seqs, share).transpose(1, 0, 2).reshape(seqs, 1, 4 * share)
    norm_rows = jnp.pad(norm_rows, ((0, 0), (0, 15), (0, width - 4 * share))).astype(jnp.bfloat16)
    grad_ctx, up_keep, up_give, out_keep, out_give, down_keep, down_give = weight_gradients(
        grad_attn,
        context_tok,
        normed_low,
        grad_pre,
        hidden,
        grad_mlp,
        wout_own,
        norm_rows.reshape(2 * planes, 2, 16, width),
        planes,
    )
    up_pair = (up_keep, xor_swap(up_give, 4))
    out_pair = (out_keep, xor_swap(out_give, 4))
    two_y = (planes, 2) + down_keep.shape[1:]
    down_pair = (down_keep.reshape(two_y), xor_swap(down_give, 1).reshape(two_y))

    grad_q, grad_kv = attend_back(idx, live, queries, grad_ctx, level, keys_values)
    wq_plain = jnp.pad(columns(w_query), ((0, 0), (0, WIN - WQ)))
    grad_attend, quarters, up_two, down_two, out_two = reduce_all(
        grad_kv, grad_q, stretch, wq_plain, wkv_own, up_pair, out_pair, down_pair, planes
    )
    grad_tokens = grad_one + grad_attend

    def joined(two):
        return jnp.concatenate([two[0], two[1]], axis=1).astype(jnp.float32)

    up_total, down_total, out_total = joined(up_two), joined(down_two), joined(out_two)
    quarters = [pick(quarters, g, 0) for g in order]

    def whole(at):
        return jnp.concatenate([q[:, at : at + WQ] for q in quarters], axis=1).astype(jnp.float32)

    norm_row = out_total[share]

    def norm_grad(n):
        return norm_row[n * share : (n + 1) * share]

    return (
        output.astype(jnp.bfloat16),
        grad_tokens,
        whole(2 * WQ),
        whole(0),
        whole(WQ),
        out_total[:share],
        norm_grad(0),
        norm_grad(1),
        up_total,
        down_total,
        norm_grad(2),
        norm_grad(3),
    )


def solution(mesh):
    rows = P(("seq", "head"), None)
    seq_rows, seq_only = P("seq", None), P("seq")
    return jax.shard_map(
        body,
        mesh=mesh,
        in_specs=(rows,) + (P(),) * 10 + (rows, P(), P(), seq_rows),
        out_specs=(
            rows,
            rows,
            seq_rows,
            seq_rows,
            seq_rows,
            seq_rows,
            seq_only,
            seq_only,
            seq_rows,
            seq_rows,
            seq_only,
            seq_only,
        ),
        check_vma=False,
    )
```

```python
import functools

import jax
import jax.numpy as jnp
from jax import lax
from jax.experimental import pallas as pl
from jax.experimental.pallas import tpu as pltpu
from jax.sharding import PartitionSpec as P

DH = 64
BLK = 64
MAXB = 64
SLOTS = 8
HG = 3
WQ = HG * DH
WIN = 256
AXES = ("seq", "head")
NEG = -1e30

eps_norm = 1e-06


def xor_swap(value, bits):
    count = lax.axis_size("seq") * lax.axis_size("head")
    return lax.ppermute(value, AXES, [(d, d ^ bits) for d in range(count)])


def lane_groups(rows, offset):
    lane = lax.broadcasted_iota(jnp.int32, (rows, WIN), 1) - offset
    return [jnp.logical_and(lane >= h * DH, lane < (h + 1) * DH) for h in range(HG)]


def spread_heads(block, offset):
    zero = jnp.zeros_like(block)
    return jnp.concatenate([jnp.where(m, block, zero) for m in lane_groups(BLK, offset)], axis=0)


def fold_heads(stacked, offset):
    masks = lane_groups(BLK, offset)
    total = jnp.where(masks[0], stacked[:BLK], 0.0)
    for h in range(1, HG):
        total = total + jnp.where(masks[h], stacked[h * BLK : (h + 1) * BLK], 0.0)
    return total


def nt(a, b):
    return lax.dot_general(a, b, (((1,), (1,)), ((), ())), preferred_element_type=jnp.float32)


def tn(a, b):
    return lax.dot_general(a, b, (((0,), (0,)), ((), ())), preferred_element_type=jnp.float32)


def backward_kernel(idx_ref, live_ref, q_ref, do_ref, lse_ref, *refs):
    kv_ref, dq_ref, dkv_ref, kv, acc, sems = refs

    def clear(n, carry):
        acc[pl.ds(pl.multiple_of(n * 256, 256), 256), :] = jnp.zeros((256, 2 * WQ), jnp.float32)
        return carry

    copy = pltpu.make_async_copy(kv_ref, kv, sems.at[0])
    copy.start()
    lax.fori_loop(0, acc.shape[0] // 256, clear, 0)
    copy.wait()

    def step(i, carry):
        q_rows = pl.multiple_of(i * BLK, BLK)
        qexp = spread_heads(q_ref[pl.ds(q_rows, BLK), :], 0)
        doexp = spread_heads(do_ref[pl.ds(q_rows, BLK), :], 64)
        rows = [
            pl.multiple_of(idx_ref[i * SLOTS + s] * BLK, BLK) for s in range(SLOTS)
        ]
        keys = jnp.concatenate([kv[pl.ds(r, BLK), 0:WIN] for r in rows], axis=0)
        values = jnp.concatenate([kv[pl.ds(r, BLK), 128 : 128 + WIN] for r in rows], axis=0)
        raw = nt(keys, qexp)
        level = lse_ref[pl.ds(i, 1), :]
        probs = jnp.concatenate(
            [
                jnp.exp(
                    raw[s * BLK : (s + 1) * BLK]
                    - (level + jnp.where(live_ref[i * SLOTS + s] > 0, 0.0, -NEG))
                )
                for s in range(SLOTS)
            ],
            axis=0,
        )
        grad_probs = nt(values, doexp)
        inner = jnp.sum(probs * grad_probs, axis=0, keepdims=True)
        grad_scores = (probs * (grad_probs - inner)).astype(jnp.bfloat16)
        dk = jnp.dot(grad_scores, qexp, preferred_element_type=jnp.float32)
        dv = jnp.dot(probs.astype(jnp.bfloat16), doexp, preferred_element_type=jnp.float32)
        dq = tn(grad_scores, keys)
        dq_ref[pl.ds(q_rows, BLK), :] = (fold_heads(dq, 0) * DH ** (-0.5)).astype(jnp.bfloat16)
        for s in range(SLOTS):
            k_s, v_s = dk[s * BLK : (s + 1) * BLK], dv[s * BLK : (s + 1) * BLK]
            at = pl.ds(rows[s], BLK)
            acc[at, 0:128] += k_s[:, :128]
            acc[at, 128:256] += k_s[:, 128:] + v_s[:, :128]
            acc[at, 256:384] += v_s[:, 128:]
        return carry

    lax.fori_loop(0, q_ref.shape[0] // BLK, step, 0, unroll=4)

    def emit(n, carry):
        at = pl.ds(pl.multiple_of(n * 256, 256), 256)
        dkv_ref[at, :] = acc[at, :].astype(jnp.bfloat16)
        return carry

    lax.fori_loop(0, acc.shape[0] // 256, emit, 0)


VMEM = pl.BlockSpec(memory_space=pltpu.VMEM)
SMEM = pl.BlockSpec(memory_space=pltpu.SMEM)
ANY = pl.BlockSpec(memory_space=pl.ANY)


def device_at(plane, y_at, core, x_at):
    return (plane * 4 + y_at * 2 + core, x_at)


def place():
    seq_at, x_at = lax.axis_index("seq"), lax.axis_index("head")
    return seq_at // 4, (seq_at // 2) % 2, seq_at % 2, x_at


def remote(src, dst, sems, recvs, at, device):
    return pltpu.make_async_remote_copy(
        src_ref=src,
        dst_ref=dst,
        send_sem=sems.at[at],
        recv_sem=recvs.at[at],
        device_id=device,
        device_id_type=pl.DeviceIdType.MESH,
    )


def greet(partners):
    barrier = pltpu.get_barrier_semaphore()
    for device in partners:
        pl.semaphore_signal(
            barrier, inc=1, device_id=device, device_id_type=pl.DeviceIdType.MESH
        )
    pl.semaphore_wait(barrier, len(partners))


CHUNK_ORDER = (0, 1, 2, 4, 3, 5, 6, 7)
JORDER = (3, 1, 2, 0)


def slot_tables(plane, y_at, core, x_at, at, lengths, order, rand_own, rand_got, idx_ref, live_ref):
    per = at["piece_blocks"]

    def one(i, carry):
        far, near = i // per, i % per
        y_of, x_of = y_at ^ (far >> 1), x_at ^ (far & 1)
        block = plane * MAXB + y_of * (4 * per) + core * (2 * per) + x_of * per + near
        begin, first, span = jnp.int32(0), jnp.int32(0), jnp.int32(1)
        for m in range(at["seqs"]):
            size = lengths[order[m]]
            inside = begin <= block
            first = jnp.where(inside, begin, first)
            span = jnp.where(inside, size, span)
            begin = begin + size
        row = x_of * per + near
        draws = []
        for n in range(SLOTS - 5):
            spot = row * (SLOTS - 5) + n
            draw = jnp.where(far >= 2, rand_got[0, spot], rand_own[0, spot])
            for power in range(16, -1, -1):
                multiple = span * (1 << power)
                draw = jnp.where(draw >= multiple, draw - multiple, draw)
            draws.append(first + draw)
        candidates = [block - 1, block, block + 1, first, first + span - 1] + draws
        kept = []
        for s in range(SLOTS):
            alive = jnp.int32(1)
            if s == 0:
                alive = (block > first).astype(jnp.int32)
            if s == 2:
                alive = (block < first + span - 1).astype(jnp.int32)
            for e in range(s):
                same = (candidates[e] == candidates[s]).astype(jnp.int32)
                alive = alive * (1 - kept[e] * same)
            kept.append(alive)
            key = jnp.where(alive > 0, candidates[s], block)
            rel = key // MAXB - plane + 1
            inner = key % MAXB
            y_key, rest = inner // (4 * per), inner % (4 * per)
            core_key, rest = rest // (2 * per), rest % (2 * per)
            x_key, near_key = rest // per, rest % per
            spot = (rel * 2 + (core_key ^ core)) * 4 + ((y_key ^ y_at) * 2 + (x_key ^ x_at))
            idx_ref[i * SLOTS + s] = jnp.clip(spot * per + near_key, 0, 24 * per - 1)
            live_ref[i * SLOTS + s] = alive
        return carry

    lax.fori_loop(0, 4 * per, one, 0)


def attend_block(i, idx_ref, live_ref, q_ref, kv, lse_ref):
    qexp = spread_heads(q_ref[pl.ds(pl.multiple_of(i * BLK, BLK), BLK), :], 0)
    at = [idx_ref[i * SLOTS + s] for s in range(SLOTS)]
    off = [jnp.where(live_ref[i * SLOTS + s] > 0, 0.0, -NEG) for s in range(SLOTS)]
    keys = jnp.concatenate([kv[r, :, 0:WIN] for r in at], axis=0)
    values = jnp.concatenate([kv[r, :, 128 : 128 + WIN] for r in at], axis=0)
    raw = nt(keys, qexp)
    parts = [raw[s * BLK : (s + 1) * BLK] for s in range(SLOTS)]
    top = jnp.max(parts[1], axis=0, keepdims=True)
    for s in range(SLOTS):
        top = jnp.maximum(top, jnp.max(parts[s], axis=0, keepdims=True) - off[s])
    e = [jnp.exp(parts[s] - (top + off[s])) for s in range(SLOTS)]
    total = jnp.sum(e[0], axis=0, keepdims=True)
    for s in range(1, SLOTS):
        total = total + jnp.sum(e[s], axis=0, keepdims=True)
    lse_ref[pl.ds(i, 1), :] = top + jnp.log(total)
    scale = 1.0 / total
    probs = jnp.concatenate([(v * scale).astype(jnp.bfloat16) for v in e], axis=0)
    return fold_heads(tn(probs, values), 64).astype(jnp.bfloat16)


def forward_kernel(planes, tok_ref, wq_ref, wkv_ref, len_ref, ord_ref, rand_vm, rand_sm, *refs):
    kv_out, q_ref, x_out, ctx_out, lse_ref, idx_ref, live_ref = refs[:7]
    xs, kv, ctx, rand_got, rand_two = refs[7:12]
    x_send, x_recv, k_send, k_recv, up_send, up_recv, dn_send, dn_recv = refs[12:20]
    f_send, f_recv, g_send, g_recv, s_sem, o_send, o_recv, r_send, r_recv, l_sem = refs[20:30]
    plane, y_at, core, x_at = place()
    piece = tok_ref.shape[0]
    rows = piece // 2
    part = 4 * piece
    by_x = device_at(plane, y_at, core, 1 - x_at)
    by_y = device_at(plane, 1 - y_at, core, x_at)
    by_xy = device_at(plane, 1 - y_at, core, 1 - x_at)
    by_core = device_at(plane, y_at, 1 - core, x_at)
    above = device_at(plane + 1, y_at, core, x_at)
    below = device_at(plane - 1, y_at, core, x_at)
    has_above, has_below = plane < planes - 1, plane > 0
    ring = [device_at(lax.rem(plane + g, planes), y_at, core, x_at) for g in (1, planes - 1)]
    greet([by_x, by_y, by_xy, by_core] + ring)

    def x_rows(c):
        return xs.at[pl.ds((c - 2) * rows, rows)]

    def tok_rows(c):
        return tok_ref.at[pl.ds(c * rows, rows)]

    hops = {
        2: remote(tok_rows(0), x_rows(2), x_send, x_recv, 0, by_x),
        4: remote(tok_rows(0), x_rows(4), x_send, x_recv, 2, by_y),
        3: remote(tok_rows(1), x_rows(3), x_send, x_recv, 1, by_x),
        5: remote(tok_rows(1), x_rows(5), x_send, x_recv, 3, by_y),
        6: remote(x_rows(2), x_rows(6), x_send, x_recv, 4, by_y),
        7: remote(x_rows(5), x_rows(7), x_send, x_recv, 5, by_x),
    }
    rand_trade = remote(rand_vm, rand_got, r_send, r_recv, 0, by_y)
    rand_trade.start()
    for c in (2, 4, 3, 5):
        hops[c].start()

    def kv_rows(part_at, c):
        return kv.at[pl.ds((part_at * part + c * rows) // BLK, rows // BLK)]

    to_core, to_above, to_below, pass_up, pass_down = {}, {}, {}, {}, {}
    for c in range(8):
        mine = kv_rows(2, c)
        to_core[c] = remote(mine, kv_rows(3, c), k_send, k_recv, c, by_core)
        to_above[c] = remote(mine, kv_rows(0, c), up_send, up_recv, c, above)
        to_below[c] = remote(mine, kv_rows(4, c), dn_send, dn_recv, c, below)
        pass_up[c] = remote(kv_rows(0, c), kv_rows(1, c), f_send, f_recv, c, by_core)
        pass_down[c] = remote(kv_rows(4, c), kv_rows(5, c), g_send, g_recv, c, by_core)
    keeps = {
        c: pltpu.make_async_copy(
            tok_rows(c) if c < 2 else x_rows(c), x_out.at[pl.ds(c * rows, rows)], s_sem.at[c]
        )
        for c in range(8)
    }

    def relay(c):
        @pl.when(has_below)
        def _():
            to_above[c].wait_recv()
            pass_up[c].start()

        @pl.when(has_above)
        def _():
            to_below[c].wait_recv()
            pass_down[c].start()

    for n, c in enumerate(CHUNK_ORDER):
        if n == 2:
            rand_trade.wait()
            to_scalar = pltpu.make_async_copy(rand_got, rand_two, l_sem.at[0])
            to_scalar.start()
            to_scalar.wait()
            slot_tables(
                plane,
                y_at,
                core,
                x_at,
                dict(piece_blocks=piece // BLK, seqs=len_ref.shape[0]),
                len_ref,
                ord_ref,
                rand_sm,
                rand_two,
                idx_ref,
                live_ref,
            )
        if c >= 2:
            hops[c].wait_recv()
        if c == 2:
            hops[6].start()
        if c == 5:
            hops[7].start()
        keeps[c].start()
        block = tok_ref[pl.ds(c * rows, rows), :] if c < 2 else xs[pl.ds((c - 2) * rows, rows), :]
        made = jnp.dot(block, wkv_ref[...], preferred_element_type=jnp.float32).astype(jnp.bfloat16)
        kv[pl.ds((2 * part + c * rows) // BLK, rows // BLK)] = made.reshape(rows // BLK, BLK, -1)

        @pl.when(has_above)
        def _(c=c):
            to_above[c].start()

        @pl.when(has_below)
        def _(c=c):
            to_below[c].start()

        to_core[c].start()
        q_ref[pl.ds(c * rows, rows), :] = jnp.dot(
            block, wq_ref[...], preferred_element_type=jnp.float32
        ).astype(jnp.bfloat16)
        if n >= 3:
            relay(CHUNK_ORDER[n - 3])
    for c in CHUNK_ORDER[5:]:
        relay(c)
    for c in range(8):
        to_core[c].wait_recv()

        @pl.when(has_above)
        def _(c=c):
            pass_down[c].wait_recv()

        @pl.when(has_below)
        def _(c=c):
            pass_up[c].wait_recv()

    saved = pltpu.make_async_copy(kv, kv_out, l_sem.at[1])
    saved.start()
    per = piece // BLK
    trades = {}
    for j in JORDER:

        def step(n, carry, j=j):
            done = attend_block(j * per + n, idx_ref, live_ref, q_ref, kv, lse_ref)
            at = pl.ds(pl.multiple_of(n * BLK, BLK), BLK)
            if j:
                ctx[j - 1, at, :] = done
            else:
                ctx_out[at, 0:WIN] = done
            return carry

        lax.fori_loop(0, per, step, 0, unroll=2)
        if j:
            trades[j] = remote(
                ctx.at[j - 1],
                ctx_out.at[:, pl.ds(j * WIN, WIN)],
                o_send,
                o_recv,
                j - 1,
                device_at(plane, y_at ^ (j >> 1), core, x_at ^ (j & 1)),
            )
            trades[j].start()
    for c in (2, 4, 3, 5, 6, 7):
        hops[c].wait_send()
    for c in range(8):
        to_core[c].wait_send()
        keeps[c].wait()

        @pl.when(has_above)
        def _(c=c):
            to_above[c].wait_send()
            pass_down[c].wait_send()

        @pl.when(has_below)
        def _(c=c):
            to_below[c].wait_send()
            pass_up[c].wait_send()

    saved.wait()
    for j in (3, 1, 2):
        trades[j].wait()


def forward_attention(tokens, wq_own, wkv_own, lengths, seq_order, rand_row, planes):
    piece, width = tokens.shape
    dma, low = pltpu.SemaphoreType.DMA, jnp.bfloat16
    sds = jax.ShapeDtypeStruct
    blocks = 4 * piece // BLK
    return pl.pallas_call(
        functools.partial(forward_kernel, planes),
        out_shape=[
            sds((24 * piece // BLK, BLK, 2 * WQ), low),
            sds((4 * piece, WIN), low),
            sds((4 * piece, width), low),
            sds((piece, 4 * WIN), low),
            sds((blocks, WQ), jnp.float32),
            sds((blocks * SLOTS,), jnp.int32),
            sds((blocks * SLOTS,), jnp.int32),
        ],
        in_specs=[VMEM] * 3 + [SMEM] * 2 + [VMEM, SMEM],
        out_specs=[ANY, VMEM, ANY, VMEM, VMEM, SMEM, SMEM],
        scratch_shapes=[
            pltpu.VMEM((3 * piece, width), low),
            pltpu.VMEM((24 * piece // BLK, BLK, 2 * WQ), low),
            pltpu.VMEM((3, piece, WIN), low),
            pltpu.VMEM(rand_row.shape, jnp.int32),
            pltpu.SMEM(rand_row.shape, jnp.int32),
            dma((6,)),
            dma((6,)),
        ]
        + [dma((8,))] * 11
        + [dma((3,))] * 2
        + [dma((1,))] * 2
        + [dma((2,))],
        compiler_params=pltpu.CompilerParams(
            collective_id=0, has_side_effects=True, vmem_limit_bytes=62 << 20
        ),
        cost_estimate=pl.CostEstimate(
            flops=2 * 4 * piece * width * 640, bytes_accessed=40 << 20, transcendentals=0
        ),
        name="forward_attention",
    )(tokens, wq_own, wkv_own, lengths, seq_order, rand_row, rand_row)


def attend_back(idx, live, queries, grads, level, keys_values):
    rows, width = keys_values.shape[0] // 6, keys_values.shape[1]
    count = queries.shape[0]
    kv_shape = jax.ShapeDtypeStruct((6 * rows, width), jnp.bfloat16)
    return pl.pallas_call(
        backward_kernel,
        out_shape=[jax.ShapeDtypeStruct((count, WIN), jnp.bfloat16)] + [kv_shape],
        in_specs=[SMEM, SMEM, VMEM, VMEM, VMEM, ANY],
        out_specs=[VMEM] * 2,
        scratch_shapes=[
            pltpu.VMEM((6 * rows, width), jnp.bfloat16),
            pltpu.VMEM((6 * rows, width), jnp.float32),
            pltpu.SemaphoreType.DMA((1,)),
        ],
        compiler_params=pltpu.CompilerParams(vmem_limit_bytes=56 << 20),
        cost_estimate=pl.CostEstimate(
            flops=2 * 10 * count * 3 * 256 * 512, bytes_accessed=24 * rows * width, transcendentals=count * 3 * 512
        ),
        name="attend_back",
    )(idx, live, queries, grads, level, keys_values)


def reduce_kernel(planes, *refs):
    dkv_in, dq_in, x_in, wq_in, wkv_in, one_in = refs[:6]
    pair_in = refs[6:12]
    tok_out, q_out, k_out, v_out, up_out, side_out, norm_out, down_out = refs[12:20]
    own, core_in, z_out, z_in, g_all, dx_out, dx_in, acc = refs[20:28]
    dq, xs, wq, wkv, one = refs[28:33]
    p_slab, p_core, p_z, p_zin, p_fin, p_all = refs[33:39]
    keep, give = refs[39:42], refs[42:45]
    got, two, fin = refs[45:48], refs[48:51], refs[51:54]
    line_out, line_in = refs[54:57], refs[57:60]
    l_sem, i_sem, c_s, c_r, u_s, u_r, d_s, d_r, x_s, x_r = refs[60:70]
    pk_s, pk_r, pz_s, pz_r, pf_s, pf_r = refs[70:76]
    w2_s, w2_r, w3_s, w3_r, w4_s, w4_r = refs[76:82]
    plane, y_at, core, x_at = place()
    piece = tok_out.shape[0]
    part = 4 * piece
    rest = planes - 1
    group = y_at * 2 + x_at
    low, f32 = jnp.bfloat16, jnp.float32

    def there(j):
        return device_at(plane, y_at ^ (j >> 1), core, x_at ^ (j & 1))

    by_x, by_y = there(1), there(2)
    by_core = device_at(plane, y_at, 1 - core, x_at)
    others = [device_at(lax.rem(plane + g, planes), y_at, core, x_at) for g in range(1, planes)]
    has_above, has_below = plane < planes - 1, plane > 0
    above = device_at(plane + 1, y_at, core, x_at)
    below = device_at(plane - 1, y_at, core, x_at)

    def chunk(base, j):
        return pl.ds(pl.multiple_of(base + j * piece, piece), piece)

    def load_own(turn, r, j):
        return pltpu.make_async_copy(
            dkv_in.at[chunk(2 * r * part, j)], own.at[chunk(r * part, j)], l_sem.at[turn]
        )

    def to_core(turn, r, j):
        return remote(
            dkv_in.at[chunk((2 * r + 1) * part, j)],
            core_in.at[chunk(r * part, j)],
            c_s,
            c_r,
            turn,
            by_core,
        )

    def to_below(j):
        return remote(z_out.at[chunk(0, j)], z_in.at[chunk(0, j)], d_s, d_r, j, below)

    def to_above(j):
        return remote(z_out.at[chunk(part, j)], z_in.at[chunk(part, j)], u_s, u_r, j, above)

    def to_owner(j):
        return remote(dx_out.at[j - 1], dx_in.at[j - 1], x_s, x_r, j - 1, there(j))

    def every(n, action):
        j = 3 - n
        for turn, r in ((n * 2, 0), (n * 2 + 1, 2)):
            action(turn, r, j)

    greet([by_x, by_y, there(3), by_core] + others)

    def begin(n, carry):
        def go(turn, r, j):
            to_core(turn, r, j).start()
            load_own(turn, r, j).start()

        every(n, go)
        return carry

    lax.fori_loop(0, 4, begin, 0)

    def begin_mid(n, carry):
        to_core(8 + n, 1, 3 - n).start()
        load_own(8 + n, 1, 3 - n).start()
        return carry

    lax.fori_loop(0, 4, begin_mid, 0)
    inputs = [(pair_in[2 * n], keep[n]) for n in range(3)]
    inputs += [(pair_in[2 * n + 1], give[n]) for n in range(3)]
    inputs += [(wq_in, wq), (wkv_in, wkv), (dq_in, dq), (x_in, xs), (one_in, one)]
    inputs = [pltpu.make_async_copy(src, dst, i_sem.at[n]) for n, (src, dst) in enumerate(inputs)]
    for copy in inputs:
        copy.start()

    def both(turn, r, j):
        to_core(turn, r, j).wait_recv()
        load_own(turn, r, j).wait()
        at = chunk(r * part, j)
        return own[at, :].astype(f32) + core_in[at, :].astype(f32)

    def spread(n, carry):
        j = 3 - n
        z_out[chunk(0, j), :] = both(2 * n, 0, j).astype(low)

        @pl.when(has_below)
        def _():
            to_below(j).start()

        z_out[chunk(part, j), :] = both(2 * n + 1, 2, j).astype(low)

        @pl.when(has_above)
        def _():
            to_above(j).start()

        return carry

    lax.fori_loop(0, 4, spread, 0)

    for copy in inputs[:6]:
        copy.wait()
    halves = [keep[0].shape[2] // 2, keep[1].shape[2] // 2]
    w2 = []
    for n in range(3):

        def merge(p, carry, n=n):
            keep[n][p] = (keep[n][p].astype(f32) + give[n][p].astype(f32)).astype(low)
            return carry

        lax.fori_loop(0, planes, merge, 0)
        if n < 2:
            cols = pl.ds(pl.multiple_of((1 - x_at) * halves[n], 128), halves[n])
            w2.append(remote(keep[n].at[:, :, cols], got[n], w2_s, w2_r, n, by_x))
        else:
            w2.append(remote(keep[n].at[:, 1 - y_at], got[n], w2_s, w2_r, n, by_y))
        w2[n].start()
    for copy in inputs[6:]:
        copy.wait()
    acc[...] = jnp.zeros_like(acc)

    def arrive(n):
        j = 3 - n
        g_all[:, 2 * WQ :] = dq[chunk(0, j), :]
        g_all[:, : 2 * WQ] = both(8 + n, 1, j).astype(low)

        @pl.when(has_above)
        def _():
            to_below(j).wait_recv()
            g_all[:, : 2 * WQ] = (
                g_all[:, : 2 * WQ].astype(f32) + z_in[chunk(0, j), :].astype(f32)
            ).astype(low)

        @pl.when(has_below)
        def _():
            to_above(j).wait_recv()
            g_all[:, : 2 * WQ] = (
                g_all[:, : 2 * WQ].astype(f32) + z_in[chunk(part, j), :].astype(f32)
            ).astype(low)

    def back(j):
        grads = g_all[...]
        return nt(grads[:, 2 * WQ :], wq[...]) + nt(grads[:, : 2 * WQ], wkv[...])

    def outer(j):
        acc[...] += tn(xs[chunk(0, j), :], g_all[...])

    def send_back(n, carry):
        arrive(n)
        dx_out[2 - n] = back(3 - n).astype(low)
        to_owner(3 - n).start()
        outer(3 - n)
        return carry

    lax.fori_loop(0, 3, send_back, 0)

    for n in range(3):
        w2[n].wait_recv()

        def halve(p, carry, n=n):
            if n < 2:
                cols = pl.ds(pl.multiple_of(x_at * halves[n], 128), halves[n])
                mine = keep[n][p, :, cols]
            else:
                mine = keep[n][p, y_at]
            two[n][p] = (mine.astype(f32) + got[n][p].astype(f32)).astype(low)
            return carry

        lax.fori_loop(0, planes, halve, 0)

    def line_copy(n, way, t):
        return remote(
            line_out[n].at[way, t],
            line_in[n].at[way, t],
            w3_s,
            w3_r,
            (n * 2 + way) * rest + t,
            below if way else above,
        )

    def line_step(t):
        for n in range(3):
            for way in range(2):
                spot = (planes - 1 - plane) if way else plane
                gap = planes - 1 - t
                slab = (plane - gap) if way else (plane + gap)
                sends = jnp.logical_and(t >= spot, spot < planes - 1)

                @pl.when(jnp.logical_and(sends, spot == 0))
                def _():
                    line_out[n][way, t] = two[n][slab]
                    line_copy(n, way, t).start()

                @pl.when(jnp.logical_and(sends, spot > 0))
                def _():
                    line_copy(n, way, t - 1).wait_recv()
                    line_out[n][way, t] = (
                        two[n][slab].astype(f32) + line_in[n][way, t - 1].astype(f32)
                    ).astype(low)
                    line_copy(n, way, t).start()

    arrive(3)
    line_step(0)
    tok_out[...] = one[...] + back(0)
    outer(0)

    share = p_slab.shape[3]
    for p in range(planes):
        for y in range(2):
            for k in range(2):
                at = ((p * 2 + y) * 2 + k) * share
                p_slab[k, p, y] = acc[at : at + share, :].astype(low)
    pk = remote(p_slab.at[1 - core], p_core, pk_s, pk_r, 0, by_core)
    pk.start()
    if planes > 2:
        line_step(1)
    pk.wait_recv()

    def merge_core(p, carry):
        p_z[p] = (p_slab[core, p].astype(f32) + p_core[p].astype(f32)).astype(low)
        return carry

    lax.fori_loop(0, planes, merge_core, 0)
    pz = [
        remote(
            p_z.at[lax.rem(plane + g, planes)], p_zin.at[g - 1], pz_s, pz_r, g - 1, others[g - 1]
        )
        for g in range(1, planes)
    ]
    for copy in pz:
        copy.start()

    def next_step(t, carry):
        line_step(t)
        return carry

    lax.fori_loop(2, planes - 1, next_step, 0)
    for j in (3, 2, 1):
        to_owner(j).wait_recv()
        tok_out[...] += dx_in[j - 1].astype(f32)

    total = p_z[plane].astype(f32)
    for g in range(1, planes):
        pz[g - 1].wait_recv()
        total = total + p_zin[g - 1].astype(f32)
    p_fin[...] = total.astype(low)
    pf = [
        remote(p_fin.at[y_at ^ (j >> 1)], p_all.at[j], pf_s, pf_r, j - 1, there(j))
        for j in (1, 2, 3)
    ]
    for copy in pf:
        copy.start()
    p_all[0] = p_fin[y_at]

    w4 = []
    for n in range(3):
        fin[n][x_at] = two[n][plane]

        @pl.when(has_below)
        def _(n=n):
            line_copy(n, 0, rest - 1).wait_recv()
            fin[n][x_at] = (
                fin[n][x_at].astype(f32) + line_in[n][0, rest - 1].astype(f32)
            ).astype(low)

        @pl.when(has_above)
        def _(n=n):
            line_copy(n, 1, rest - 1).wait_recv()
            fin[n][x_at] = (
                fin[n][x_at].astype(f32) + line_in[n][1, rest - 1].astype(f32)
            ).astype(low)

        w4.append(remote(fin[n].at[x_at], fin[n].at[x_at], w4_s, w4_r, n, by_x))
        w4[n].start()

    for copy in pf:
        copy.wait()
    for a in range(4):
        grads = p_all[a ^ group].astype(f32)
        for n, dest in enumerate((k_out, v_out, q_out)):
            dest[:, a * WQ : (a + 1) * WQ] = grads[:, n * WQ : (n + 1) * WQ]
    for n, dest in ((0, up_out), (2, down_out)):
        w4[n].wait()
        width = dest.shape[1] // 2
        for side in range(2):
            dest[:, side * width : (side + 1) * width] = fin[n][side].astype(f32)
    w4[1].wait()
    width = side_out.shape[1] // 2
    for side in range(2):
        done = fin[1][side].astype(f32)
        side_out[:, side * width : (side + 1) * width] = done[:share]
        norm_out[:, side * width : (side + 1) * width] = done[share : share + 8]

    for copy in w2 + pz + [pk]:
        copy.wait_send()

    def settle(n, carry):
        every(n, lambda turn, r, j: to_core(turn, r, j).wait_send())
        to_core(8 + n, 1, 3 - n).wait_send()

        @pl.when(has_below)
        def _():
            to_below(3 - n).wait_send()

        @pl.when(has_above)
        def _():
            to_above(3 - n).wait_send()

        return carry

    lax.fori_loop(0, 4, settle, 0)
    for j in (1, 2, 3):
        to_owner(j).wait_send()

    def settle_line(t, carry):
        for n in range(3):
            for way in range(2):
                spot = (planes - 1 - plane) if way else plane

                @pl.when(jnp.logical_and(t >= spot, spot < planes - 1))
                def _():
                    line_copy(n, way, t).wait_send()

        return carry

    lax.fori_loop(0, planes - 1, settle_line, 0)


def reduce_all(dkv, dq, stretch, wq, wkv, one, up, out, down, planes):
    low, f32 = jnp.bfloat16, jnp.float32
    piece = dq.shape[0] // 4
    width = stretch.shape[1]
    share = up[0].shape[1]
    rest = planes - 1
    dma, vm, sds = pltpu.SemaphoreType.DMA, pltpu.VMEM, jax.ShapeDtypeStruct
    cols = 2 * WQ + WIN
    tall = out[0].shape[1]
    wide = up[0].shape[2]
    kinds = [(share, wide // 2), (tall, width // 2), down[0].shape[2:]]
    pairs = [up[0].shape, out[0].shape, down[0].shape]
    return pl.pallas_call(
        functools.partial(reduce_kernel, planes),
        out_shape=[sds((piece, width), f32)]
        + [sds((share, width), f32)] * 3
        + [
            sds((share, wide), f32),
            sds((share, width), f32),
            sds((8, width), f32),
            sds((kinds[2][0], width), f32),
        ],
        in_specs=[ANY] * 12,
        out_specs=[VMEM] * 8,
        scratch_shapes=[
            vm((12 * piece, 2 * WQ), low),
            vm((12 * piece, 2 * WQ), low),
            vm((8 * piece, 2 * WQ), low),
            vm((8 * piece, 2 * WQ), low),
            vm((piece, cols), low),
            vm((3, piece, width), low),
            vm((3, piece, width), low),
            vm((width, cols), f32),
            vm(dq.shape, low),
            vm(stretch.shape, low),
            vm(wq.shape, low),
            vm(wkv.shape, low),
            vm(one.shape, f32),
            vm((2, planes, 2, share, cols), low),
            vm((planes, 2, share, cols), low),
            vm((planes, 2, share, cols), low),
            vm((rest, 2, share, cols), low),
            vm((2, share, cols), low),
            vm((4, share, cols), low),
        ]
        + [vm(p, low) for p in pairs] * 2
        + [vm((planes,) + k, low) for k in kinds] * 2
        + [vm((2,) + k, low) for k in kinds]
        + [vm((2, rest) + k, low) for k in kinds] * 2
        + [dma((12,)), dma((11,))]
        + [dma((12,))] * 2
        + [dma((4,))] * 4
        + [dma((3,))] * 2
        + [dma((1,))] * 2
        + [dma((rest,))] * 2
        + [dma((3,))] * 2
        + [dma((3,))] * 2
        + [dma((6 * rest,))] * 2
        + [dma((3,))] * 2,
        compiler_params=pltpu.CompilerParams(
            collective_id=1, has_side_effects=True, vmem_limit_bytes=60 << 20
        ),
        cost_estimate=pl.CostEstimate(
            flops=4 * 4 * piece * width * cols, bytes_accessed=40 << 20, transcendentals=0
        ),
        name="reduce_all",
    )(dkv, dq, stretch, wq, wkv, one, up[0], up[1], out[0], out[1], down[0], down[1])


def dense_kernel(
    planes,
    tok_ref,
    ctx_ref,
    cot_ref,
    g1_ref,
    b1_ref,
    g2_ref,
    b2_ref,
    wout_ref,
    wup_in,
    wdown_in,
    *refs,
):
    out_ref, one_ref, do_out, up_keep, up_give, out_keep, out_give, down_keep, down_give = refs[:9]
    wup, wdown, acc, x1, s1, g_two, nl, hid, slope, gp, gm, ga = refs[9:21]
    dctx, up_loc, out_loc, down_loc, up_got, out_got, down_got, down_sum = refs[21:29]
    w_sem, mv_sem, do_s, do_r, up_s, up_r, out_s, out_r, down_s, down_r = refs[29:39]
    plane, y_at, core, x_at = place()
    piece, width = tok_ref.shape
    share = up_loc.shape[2]
    slab = down_loc.shape[2]
    pairs = 2 * planes
    group = y_at * 2 + x_at
    f32 = jnp.float32
    bring = [
        pltpu.make_async_copy(wup_in, wup, w_sem.at[0]),
        pltpu.make_async_copy(wdown_in, wdown, w_sem.at[1]),
    ]
    for copy in bring:
        copy.start()

    def there(j):
        return device_at(plane, y_at ^ (j >> 1), core, x_at ^ (j & 1))

    by_core = device_at(plane, y_at, 1 - core, x_at)
    greet([there(1), there(2), there(3), by_core])

    height, tile = 32, 2 * WQ
    wide = wup.shape[1]

    def rows_of(n):
        return pl.ds(pl.multiple_of(n * height, height), height)

    def cols_of(n):
        return pl.ds(pl.multiple_of(n * tile, tile), tile)

    def mean(v):
        return jnp.mean(v, axis=1, keepdims=True)

    def fold(v):
        return v[:8] + v[8:16] + v[16:24] + v[24:]

    acc[...] = jnp.dot(ctx_ref[...], wout_ref[...], preferred_element_type=f32)
    g1, b1, g2, b2 = (r[...].reshape(1, width) for r in (g1_ref, b1_ref, g2_ref, b2_ref))

    def norm_one(n, carry):
        at = rows_of(n)
        value = tok_ref[at, :].astype(f32) + acc[at, :]
        center = value - mean(value)
        inverse = lax.rsqrt(mean(center * center) + eps_norm)
        hat = center * inverse
        x1[at, :] = hat
        s1[at, :] = jnp.broadcast_to(inverse, (height, 128))
        nl[at, :] = (hat * g1 + b1).astype(jnp.bfloat16)
        return carry

    lax.fori_loop(0, piece // height, norm_one, 0, unroll=2)
    bring[0].wait()

    def expand(n, carry):
        at = cols_of(n)
        pre = jnp.dot(nl[...], wup[:, at], preferred_element_type=f32)
        square = pre * pre
        inner = 0.7978845608028654 * pre * (1.0 + 0.044715 * square)
        bend = jnp.tanh(inner)
        half_up = 0.5 + 0.5 * bend
        hid[:, at] = (pre * half_up).astype(jnp.bfloat16)
        slope[:, at] = half_up + 0.5 * pre * (1.0 - bend * bend) * (
            0.7978845608028654 + 0.1070322243 * square
        )
        return carry

    lax.fori_loop(0, wide // tile, expand, 0)
    bring[1].wait()
    acc[...] = jnp.dot(hid[...], wdown[...], preferred_element_type=f32)
    nothing = jnp.zeros((8, width), f32)

    def norm_two(n, carry):
        gain_sum, shift_sum = carry
        at = rows_of(n)
        value = x1[at, :] * g1 + b1 + acc[at, :]
        center = value - mean(value)
        inverse = lax.rsqrt(mean(center * center) + eps_norm)
        hat = center * inverse
        out_ref[at, :] = (hat * g2 + b2).astype(jnp.bfloat16)
        cot = cot_ref[at, :].astype(f32)
        gain_sum, shift_sum = gain_sum + fold(cot * hat), shift_sum + fold(cot)
        up = cot * g2
        grad = inverse * (up - mean(up) - hat * mean(up * hat))
        g_two[at, :] = grad
        gm[at, :] = grad.astype(jnp.bfloat16)
        return gain_sum, shift_sum

    gain_two, shift_two = lax.fori_loop(0, piece // height, norm_two, (nothing, nothing), unroll=2)

    def shrink(n, carry):
        at = cols_of(n)
        back = nt(gm[...], wdown[at, :])
        gp[:, at] = (back * slope[:, at]).astype(jnp.bfloat16)
        return carry

    lax.fori_loop(0, wide // tile, shrink, 0)
    acc[...] = nt(gp[...], wup[...])

    def norm_three(n, carry):
        gain_sum, shift_sum = carry
        at = rows_of(n)
        grad_in, hat = g_two[at, :] + acc[at, :], x1[at, :]
        gain_sum, shift_sum = gain_sum + fold(grad_in * hat), shift_sum + fold(grad_in)
        up = grad_in * g1
        grad = s1[at, 0:1] * (up - mean(up) - hat * mean(up * hat))
        one_ref[at, :] = grad
        ga[at, :] = grad.astype(jnp.bfloat16)
        return gain_sum, shift_sum

    gain_one, shift_one = lax.fori_loop(
        0, piece // height, norm_three, (nothing, nothing), unroll=2
    )
    side = jnp.concatenate(
        [jnp.sum(v, axis=0, keepdims=True) for v in (gain_one, shift_one, gain_two, shift_two)]
        + [jnp.zeros((12, width), f32)],
        axis=0,
    ).astype(jnp.bfloat16)

    low = jnp.bfloat16
    trades = []
    for j in (3, 1, 2, 0):
        part = nt(ga[...], wout_ref[pl.ds(j * WIN, WIN), :]).astype(low)
        if j:
            dctx[j - 1] = part
            trades.append(
                remote(
                    dctx.at[j - 1], do_out.at[pl.ds(j * piece, piece)], do_s, do_r, j - 1, there(j)
                )
            )
            trades[-1].start()
        else:
            do_out[pl.ds(0, piece), :] = part

    to_core = []
    tile = 2 * WQ
    per = tile // (2 * slab)
    for t in range(hid.shape[1] // tile):
        cell = tn(hid[:, t * tile : (t + 1) * tile], gm[...])
        for n in range(per):
            for k in range(2):
                at = (n * 2 + k) * slab
                down_loc[k, t * per + n] = cell[at : at + slab].astype(low)
        span = pl.ds(t * per, per)
        to_core.append(
            remote(down_loc.at[1 - core, span], down_got.at[span], down_s, down_r, t, by_core)
        )
        to_core[-1].start()
    ups = []
    for t in range(gp.shape[1] // tile):
        span = pl.ds(t * tile, tile)
        cell = tn(nl[...], gp[:, t * tile : (t + 1) * tile])
        for q in range(pairs):
            for k in range(2):
                at = (q * 2 + k) * share
                up_loc[k, q, :, t * tile : (t + 1) * tile] = cell[at : at + share].astype(low)
        ups.append(
            remote(
                up_loc.at[1 - core, :, :, span], up_got.at[:, :, span], up_s, up_r, t, by_core
            )
        )
        ups[-1].start()
    per_group = pairs // 4
    for j in range(4):
        cell = tn(ctx_ref[:, j * WIN : (j + 1) * WIN], ga[...])
        for n in range(per_group):
            for k in range(2):
                at = WIN - WQ + (n * 2 + k) * share
                out_loc[k, (group ^ j) * per_group + n, :share, :] = cell[at : at + share].astype(low)
    for q in range(pairs):
        for k in range(2):
            out_loc[k, q, share:, :] = side
    outs = remote(out_loc.at[1 - core], out_got, out_s, out_r, 0, by_core)
    outs.start()

    moved = []

    def move(source, dest):
        moved.append(pltpu.make_async_copy(source, dest, mv_sem.at[len(moved)]))
        moved[-1].start()

    half = width // 2
    for n, copy in enumerate(to_core):
        copy.wait_recv()
        for q in range(n * per, (n + 1) * per):
            total = (
                down_loc[core, q].astype(jnp.float32) + down_got[q].astype(jnp.float32)
            ).astype(low)
            down_sum[0, q] = total[:, :half]
            down_sum[1, q] = total[:, half:]
    move(down_sum.at[x_at], down_keep)
    move(down_sum.at[1 - x_at], down_give)
    for copy in ups:
        copy.wait_recv()
    for p in range(planes):
        for y in range(2):
            q = p * 2 + y
            up_got[q] = (up_loc[core, q].astype(jnp.float32) + up_got[q].astype(jnp.float32)).astype(low)
    outs.wait_recv()
    for p in range(planes):
        for y in range(2):
            q = p * 2 + y
            out_got[q] = (
                out_loc[core, q].astype(jnp.float32) + out_got[q].astype(jnp.float32)
            ).astype(low)
        for got, keep, give in ((up_got, up_keep, up_give), (out_got, out_keep, out_give)):
            move(got.at[p * 2 + y_at], keep.at[p])
            move(got.at[p * 2 + 1 - y_at], give.at[p])
    for copy in trades:
        copy.wait()
    for copy in to_core + ups + [outs]:
        copy.wait_send()
    for copy in moved:
        copy.wait()


def dense_layers(tokens, ctx, cotangent, norms, wout, w_up, w_down, planes):
    low = jnp.bfloat16
    piece, width = tokens.shape
    pairs = 2 * planes
    wide = w_up.shape[1]
    share, slab, tall = width // (2 * pairs), wide // (2 * pairs), 16
    sds, vm, dma = jax.ShapeDtypeStruct, pltpu.VMEM, pltpu.SemaphoreType.DMA
    up, out = (planes, share, wide), (planes, share + tall, width)
    down = (pairs, slab, width // 2)
    tiles = wide // (2 * WQ)
    f32 = jnp.float32
    return pl.pallas_call(
        functools.partial(dense_kernel, planes),
        out_shape=[sds((piece, width), low), sds((piece, width), f32), sds((4 * piece, WIN), low)]
        + [sds(up, low)] * 2
        + [sds(out, low)] * 2
        + [sds(down, low)] * 2,
        in_specs=[VMEM] * 8 + [ANY] * 2,
        out_specs=[VMEM] * 3 + [ANY] * 6,
        scratch_shapes=[
            vm(w_up.shape, low),
            vm(w_down.shape, low),
            vm((piece, width), f32),
            vm((piece, width), f32),
            vm((piece, 128), f32),
            vm((piece, width), f32),
            vm((piece, width), low),
            vm((piece, wide), low),
            vm((piece, wide), f32),
            vm((piece, wide), low),
            vm((piece, width), low),
            vm((piece, width), low),
            vm((3, piece, WIN), low),
            vm((2, pairs, share, wide), low),
            vm((2, pairs, share + tall, width), low),
            vm((2, pairs, slab, width), low),
            vm((pairs, share, wide), low),
            vm((pairs, share + tall, width), low),
            vm((pairs, slab, width), low),
            vm((2, pairs, slab, width // 2), low),
            dma((2,)),
            dma((2 + 4 * planes,)),
        ]
        + [dma((3,))] * 2
        + [dma((tiles,))] * 2
        + [dma((1,))] * 2
        + [dma((tiles,))] * 2,
        compiler_params=pltpu.CompilerParams(
            collective_id=2, has_side_effects=True, vmem_limit_bytes=62 << 20
        ),
        cost_estimate=pl.CostEstimate(
            flops=2 * piece * width * (6 * wide + 3072), bytes_accessed=30 << 20, transcendentals=0
        ),
        name="dense_layers",
    )(tokens, ctx, cotangent, *norms, wout, w_up, w_down)


def pick(array, at, axis):
    return lax.dynamic_index_in_dim(array, at, axis, keepdims=False)


def body(
    tokens,
    w_query,
    w_key,
    w_value,
    w_out,
    gain_attn,
    shift_attn,
    w_up,
    w_down,
    gain_mlp,
    shift_mlp,
    cotangent,
    lengths,
    seq_order,
    rand_blocks,
):
    piece, width = tokens.shape
    seqs, heads = lax.axis_size("seq"), lax.axis_size("head")
    planes = seqs // 4
    assert heads == 2 and 8 * piece == MAXB * BLK and width == 4 * WQ
    seq_at, x_at = lax.axis_index("seq"), lax.axis_index("head")
    plane, y_at, core = seq_at // 4, (seq_at // 2) % 2, seq_at % 2
    group = y_at * 2 + x_at

    def columns(weights):
        return lax.dynamic_slice_in_dim(weights, group * WQ, WQ, 1)

    wq_own = jnp.pad(columns(w_query) * jnp.bfloat16(DH ** (-0.5)), ((0, 0), (0, WIN - WQ)))
    wkv_own = jnp.concatenate([columns(w_key), columns(w_value)], axis=1)
    order = [group ^ j for j in range(4)]
    wout_own = jnp.concatenate(
        [
            jnp.pad(lax.dynamic_slice_in_dim(w_out, g * WQ, WQ, 0), ((WIN - WQ, 0), (0, 0)))
            for g in order
        ],
        axis=0,
    )

    flat = rand_blocks.reshape(1, -1)
    rand_row = jnp.pad(flat, ((0, 0), (0, 128 - flat.shape[1])))
    keys_values, queries, stretch, context_tok, level, idx, live = forward_attention(
        tokens, wq_own, wkv_own, lengths, seq_order, rand_row, planes
    )
    share = width // seqs
    norms = [gain_attn, shift_attn, gain_mlp, shift_mlp]
    output, grad_one, grad_ctx, up_keep, up_give, out_keep, out_give, down_keep, down_give = (
        dense_layers(tokens, context_tok, cotangent, norms, wout_own, w_up, w_down, planes)
    )
    up_pair = (up_keep, xor_swap(up_give, 4))
    out_pair = (out_keep, xor_swap(out_give, 4))
    two_y = (planes, 2) + down_keep.shape[1:]
    down_pair = (down_keep.reshape(two_y), xor_swap(down_give, 1).reshape(two_y))

    grad_q, grad_kv = attend_back(
        idx, live, queries, grad_ctx, level, keys_values.reshape(-1, 2 * WQ)
    )
    wq_plain = jnp.pad(columns(w_query), ((0, 0), (0, WIN - WQ)))
    grad_tokens, grad_wq, grad_wk, grad_wv, up_total, out_total, norm_rows, down_total = reduce_all(
        grad_kv,
        grad_q,
        stretch,
        wq_plain,
        wkv_own,
        grad_one,
        up_pair,
        out_pair,
        down_pair,
        planes,
    )

    def norm_grad(n):
        return lax.dynamic_slice_in_dim(norm_rows[n], seq_at * share, share, 0)

    return (
        output,
        grad_tokens,
        grad_wq,
        grad_wk,
        grad_wv,
        out_total,
        norm_grad(0),
        norm_grad(1),
        up_total,
        down_total,
        norm_grad(2),
        norm_grad(3),
    )


def solution(mesh):
    rows = P(("seq", "head"), None)
    seq_rows, seq_only = P("seq", None), P("seq")
    return jax.shard_map(
        body,
        mesh=mesh,
        in_specs=(rows,) + (P(),) * 10 + (rows, P(), P(), seq_rows),
        out_specs=(
            rows,
            rows,
            seq_rows,
            seq_rows,
            seq_rows,
            seq_rows,
            seq_only,
            seq_only,
            seq_rows,
            seq_rows,
            seq_only,
            seq_only,
        ),
        check_vma=False,
    )
```

```python
import functools

import jax
import jax.numpy as jnp
from jax import lax
from jax.experimental import pallas as pl
from jax.experimental.pallas import tpu as pltpu
from jax.sharding import PartitionSpec as P

DH = 64
BLK = 64
MAXB = 64
SLOTS = 8
HG = 3
WQ = HG * DH
WIN = 256
AXES = ("seq", "head")
NEG = -1e30

eps_norm = 1e-06


def xor_swap(value, bits):
    count = lax.axis_size("seq") * lax.axis_size("head")
    return lax.ppermute(value, AXES, [(d, d ^ bits) for d in range(count)])


def lane_groups(rows, offset):
    lane = lax.broadcasted_iota(jnp.int32, (rows, WIN), 1) - offset
    return [jnp.logical_and(lane >= h * DH, lane < (h + 1) * DH) for h in range(HG)]


def spread_heads(block, offset):
    zero = jnp.zeros_like(block)
    return jnp.concatenate([jnp.where(m, block, zero) for m in lane_groups(BLK, offset)], axis=0)


def fold_heads(stacked, offset):
    masks = lane_groups(BLK, offset)
    total = jnp.where(masks[0], stacked[:BLK], 0.0)
    for h in range(1, HG):
        total = total + jnp.where(masks[h], stacked[h * BLK : (h + 1) * BLK], 0.0)
    return total


def nt(a, b):
    return lax.dot_general(a, b, (((1,), (1,)), ((), ())), preferred_element_type=jnp.float32)


def tn(a, b):
    return lax.dot_general(a, b, (((0,), (0,)), ((), ())), preferred_element_type=jnp.float32)


def backward_kernel(idx_ref, live_ref, q_ref, do_ref, lse_ref, *refs):
    kv_ref, dq_ref, dkv_ref, kv, acc, sems = refs

    def clear(n, carry):
        acc[pl.ds(pl.multiple_of(n * 256, 256), 256), :] = jnp.zeros((256, 2 * WQ), jnp.float32)
        return carry

    copy = pltpu.make_async_copy(kv_ref, kv, sems.at[0])
    copy.start()
    lax.fori_loop(0, acc.shape[0] // 256, clear, 0)
    copy.wait()

    def step(i, carry):
        q_rows = pl.multiple_of(i * BLK, BLK)
        qexp = spread_heads(q_ref[pl.ds(q_rows, BLK), :], 0)
        doexp = spread_heads(do_ref[pl.ds(q_rows, BLK), :], 64)
        rows = [
            pl.multiple_of(idx_ref[i * SLOTS + s] * BLK, BLK) for s in range(SLOTS)
        ]
        keys = jnp.concatenate([kv[pl.ds(r, BLK), 0:WIN] for r in rows], axis=0)
        values = jnp.concatenate([kv[pl.ds(r, BLK), 128 : 128 + WIN] for r in rows], axis=0)
        raw = nt(keys, qexp)
        level = lse_ref[pl.ds(i, 1), :]
        probs = jnp.concatenate(
            [
                jnp.exp(
                    raw[s * BLK : (s + 1) * BLK]
                    - (level + jnp.where(live_ref[i * SLOTS + s] > 0, 0.0, -NEG))
                )
                for s in range(SLOTS)
            ],
            axis=0,
        )
        grad_probs = nt(values, doexp)
        inner = jnp.sum(probs * grad_probs, axis=0, keepdims=True)
        grad_scores = (probs * (grad_probs - inner)).astype(jnp.bfloat16)
        dk = jnp.dot(grad_scores, qexp, preferred_element_type=jnp.float32)
        dv = jnp.dot(probs.astype(jnp.bfloat16), doexp, preferred_element_type=jnp.float32)
        dq = tn(grad_scores, keys)
        dq_ref[pl.ds(q_rows, BLK), :] = fold_heads(dq, 0).astype(jnp.bfloat16)
        for s in range(SLOTS):
            k_s, v_s = dk[s * BLK : (s + 1) * BLK], dv[s * BLK : (s + 1) * BLK]
            at = pl.ds(rows[s], BLK)
            acc[at, 0:128] += k_s[:, :128]
            acc[at, 128:256] += k_s[:, 128:] + v_s[:, :128]
            acc[at, 256:384] += v_s[:, 128:]
        return carry

    lax.fori_loop(0, q_ref.shape[0] // BLK, step, 0, unroll=4)

    def emit(n, carry):
        at = pl.ds(pl.multiple_of(n * 256, 256), 256)
        dkv_ref[at, :] = acc[at, :].astype(jnp.bfloat16)
        return carry

    lax.fori_loop(0, acc.shape[0] // 256, emit, 0)


VMEM = pl.BlockSpec(memory_space=pltpu.VMEM)
SMEM = pl.BlockSpec(memory_space=pltpu.SMEM)
ANY = pl.BlockSpec(memory_space=pl.ANY)


def device_at(plane, y_at, core, x_at):
    return (plane * 4 + y_at * 2 + core, x_at)


def place():
    seq_at, x_at = lax.axis_index("seq"), lax.axis_index("head")
    return seq_at // 4, (seq_at // 2) % 2, seq_at % 2, x_at


def remote(src, dst, sems, recvs, at, device):
    return pltpu.make_async_remote_copy(
        src_ref=src,
        dst_ref=dst,
        send_sem=sems.at[at],
        recv_sem=recvs.at[at],
        device_id=device,
        device_id_type=pl.DeviceIdType.MESH,
    )


def greet(partners):
    barrier = pltpu.get_barrier_semaphore()
    for device in partners:
        pl.semaphore_signal(
            barrier, inc=1, device_id=device, device_id_type=pl.DeviceIdType.MESH
        )
    pl.semaphore_wait(barrier, len(partners))


CHUNK_ORDER = (0, 1, 2, 4, 3, 5, 6, 7)


def slot_tables(plane, y_at, core, x_at, at, lengths, order, rand_own, rand_got, idx_ref, live_ref):
    per = at["piece_blocks"]

    def one(i, carry):
        far, near = i // per, i % per
        y_of, x_of = y_at ^ (far >> 1), x_at ^ (far & 1)
        block = plane * MAXB + y_of * (4 * per) + core * (2 * per) + x_of * per + near
        begin, first, span = jnp.int32(0), jnp.int32(0), jnp.int32(1)
        for m in range(at["seqs"]):
            size = lengths[order[m]]
            inside = begin <= block
            first = jnp.where(inside, begin, first)
            span = jnp.where(inside, size, span)
            begin = begin + size
        row = x_of * per + near
        draws = []
        for n in range(SLOTS - 5):
            spot = row * (SLOTS - 5) + n
            draw = jnp.where(far >= 2, rand_got[0, spot], rand_own[0, spot])
            for power in range(16, -1, -1):
                multiple = span * (1 << power)
                draw = jnp.where(draw >= multiple, draw - multiple, draw)
            draws.append(first + draw)
        candidates = [block - 1, block, block + 1, first, first + span - 1] + draws
        kept = []
        for s in range(SLOTS):
            alive = jnp.int32(1)
            if s == 0:
                alive = (block > first).astype(jnp.int32)
            if s == 2:
                alive = (block < first + span - 1).astype(jnp.int32)
            for e in range(s):
                same = (candidates[e] == candidates[s]).astype(jnp.int32)
                alive = alive * (1 - kept[e] * same)
            kept.append(alive)
            key = jnp.where(alive > 0, candidates[s], block)
            rel = key // MAXB - plane + 1
            inner = key % MAXB
            y_key, rest = inner // (4 * per), inner % (4 * per)
            core_key, rest = rest // (2 * per), rest % (2 * per)
            x_key, near_key = rest // per, rest % per
            spot = (rel * 2 + (core_key ^ core)) * 4 + ((y_key ^ y_at) * 2 + (x_key ^ x_at))
            idx_ref[i * SLOTS + s] = jnp.clip(spot * per + near_key, 0, 24 * per - 1)
            live_ref[i * SLOTS + s] = alive
        return carry

    lax.fori_loop(0, 4 * per, one, 0)


def attend_block(i, idx_ref, live_ref, q_ref, kv, lse_ref):
    qexp = spread_heads(q_ref[pl.ds(pl.multiple_of(i * BLK, BLK), BLK), :], 0)
    at = [idx_ref[i * SLOTS + s] for s in range(SLOTS)]
    off = [jnp.where(live_ref[i * SLOTS + s] > 0, 0.0, -NEG) for s in range(SLOTS)]
    keys = jnp.concatenate([kv[r, :, 0:WIN] for r in at], axis=0)
    values = jnp.concatenate([kv[r, :, 128 : 128 + WIN] for r in at], axis=0)
    raw = nt(keys, qexp)
    parts = [raw[s * BLK : (s + 1) * BLK] for s in range(SLOTS)]
    top = jnp.max(parts[1], axis=0, keepdims=True)
    for s in range(SLOTS):
        top = jnp.maximum(top, jnp.max(parts[s], axis=0, keepdims=True) - off[s])
    e = [jnp.exp(parts[s] - (top + off[s])) for s in range(SLOTS)]
    total = jnp.sum(e[0], axis=0, keepdims=True)
    for s in range(1, SLOTS):
        total = total + jnp.sum(e[s], axis=0, keepdims=True)
    lse_ref[pl.ds(i, 1), :] = top + jnp.log(total)
    scale = 1.0 / total
    probs = jnp.concatenate([(v * scale).astype(jnp.bfloat16) for v in e], axis=0)
    return fold_heads(tn(probs, values), 64).astype(jnp.bfloat16)


def forward_kernel(planes, tok_ref, wq_in, wk_in, wv_in, len_ref, ord_ref, rand_vm, rand_sm, *refs):
    kv_out, q_ref, x_out, ctx_out, lse_ref, idx_ref, live_ref, wq_out, wkv_out = refs[:9]
    xs, kv, ctx, rand_got, rand_two, w_full, wq_ref, wkv_ref = refs[9:17]
    x_send, x_recv, k_send, k_recv, up_send, up_recv, dn_send, dn_recv = refs[17:25]
    f_send, f_recv, g_send, g_recv, s_sem, o_send, o_recv, r_send, r_recv, l_sem = refs[25:35]
    weights = [
        pltpu.make_async_copy(w, w_full.at[n], l_sem.at[2 + n])
        for n, w in enumerate((wk_in, wv_in, wq_in))
    ]
    for copy in weights:
        copy.start()
    plane, y_at, core, x_at = place()
    piece = tok_ref.shape[0]
    rows = piece // 2
    part = 4 * piece
    by_x = device_at(plane, y_at, core, 1 - x_at)
    by_y = device_at(plane, 1 - y_at, core, x_at)
    by_xy = device_at(plane, 1 - y_at, core, 1 - x_at)
    by_core = device_at(plane, y_at, 1 - core, x_at)
    above = device_at(plane + 1, y_at, core, x_at)
    below = device_at(plane - 1, y_at, core, x_at)
    has_above, has_below = plane < planes - 1, plane > 0
    ring = [device_at(lax.rem(plane + g, planes), y_at, core, x_at) for g in (1, planes - 1)]
    greet([by_x, by_y, by_xy, by_core] + ring)

    def x_rows(c):
        return xs.at[pl.ds((c - 2) * rows, rows)]

    def tok_rows(c):
        return tok_ref.at[pl.ds(c * rows, rows)]

    hops = {
        2: remote(tok_rows(0), x_rows(2), x_send, x_recv, 0, by_x),
        4: remote(tok_rows(0), x_rows(4), x_send, x_recv, 2, by_y),
        3: remote(tok_rows(1), x_rows(3), x_send, x_recv, 1, by_x),
        5: remote(tok_rows(1), x_rows(5), x_send, x_recv, 3, by_y),
        6: remote(x_rows(2), x_rows(6), x_send, x_recv, 4, by_y),
        7: remote(x_rows(5), x_rows(7), x_send, x_recv, 5, by_x),
    }
    rand_trade = remote(rand_vm, rand_got, r_send, r_recv, 0, by_y)
    rand_trade.start()
    for c in (2, 4, 3, 5):
        hops[c].start()

    wq_ref[:, WQ:] = jnp.zeros((wq_ref.shape[0], WIN - WQ), jnp.bfloat16)
    for copy in weights:
        copy.wait()
    for g in range(4):

        @pl.when(y_at * 2 + x_at == g)
        def _(g=g):
            cols = slice(g * WQ, (g + 1) * WQ)
            wkv_ref[:, :WQ] = w_full[0, :, cols]
            wkv_ref[:, WQ:] = w_full[1, :, cols]
            wq_ref[:, :WQ] = w_full[2, :, cols] * jnp.bfloat16(DH ** (-0.5))

    hand_on = [
        pltpu.make_async_copy(wq_ref, wq_out, l_sem.at[5]),
        pltpu.make_async_copy(wkv_ref, wkv_out, l_sem.at[6]),
    ]
    for copy in hand_on:
        copy.start()

    def kv_rows(part_at, c):
        return kv.at[pl.ds((part_at * part + c * rows) // BLK, rows // BLK)]

    to_core, to_above, to_below, pass_up, pass_down = {}, {}, {}, {}, {}
    for c in range(8):
        mine = kv_rows(2, c)
        to_core[c] = remote(mine, kv_rows(3, c), k_send, k_recv, c, by_core)
        to_above[c] = remote(mine, kv_rows(0, c), up_send, up_recv, c, above)
        to_below[c] = remote(mine, kv_rows(4, c), dn_send, dn_recv, c, below)
        pass_up[c] = remote(kv_rows(0, c), kv_rows(1, c), f_send, f_recv, c, by_core)
        pass_down[c] = remote(kv_rows(4, c), kv_rows(5, c), g_send, g_recv, c, by_core)
    keeps = {
        c: pltpu.make_async_copy(
            tok_rows(c) if c < 2 else x_rows(c), x_out.at[pl.ds(c * rows, rows)], s_sem.at[c]
        )
        for c in range(8)
    }

    def relay(c):
        @pl.when(has_below)
        def _():
            to_above[c].wait_recv()
            pass_up[c].start()

        @pl.when(has_above)
        def _():
            to_below[c].wait_recv()
            pass_down[c].start()

    for n, c in enumerate(CHUNK_ORDER):
        if c >= 2:
            hops[c].wait_recv()
        if c == 2:
            hops[6].start()
        if c == 5:
            hops[7].start()
        keeps[c].start()
        block = tok_ref[pl.ds(c * rows, rows), :] if c < 2 else xs[pl.ds((c - 2) * rows, rows), :]
        made = jnp.dot(block, wkv_ref[...], preferred_element_type=jnp.float32).astype(jnp.bfloat16)
        kv[pl.ds((2 * part + c * rows) // BLK, rows // BLK)] = made.reshape(rows // BLK, BLK, -1)

        @pl.when(has_above)
        def _(c=c):
            to_above[c].start()

        @pl.when(has_below)
        def _(c=c):
            to_below[c].start()

        to_core[c].start()
        q_ref[pl.ds(c * rows, rows), :] = jnp.dot(
            block, wq_ref[...], preferred_element_type=jnp.float32
        ).astype(jnp.bfloat16)
        if n >= 3:
            relay(CHUNK_ORDER[n - 3])
    relay(CHUNK_ORDER[5])
    rand_trade.wait()
    to_scalar = pltpu.make_async_copy(rand_got, rand_two, l_sem.at[0])
    to_scalar.start()
    to_scalar.wait()
    slot_tables(
        plane,
        y_at,
        core,
        x_at,
        dict(piece_blocks=piece // BLK, seqs=len_ref.shape[0]),
        len_ref,
        ord_ref,
        rand_sm,
        rand_two,
        idx_ref,
        live_ref,
    )
    for c in CHUNK_ORDER[6:]:
        relay(c)
    for c in range(8):
        to_core[c].wait_recv()

        @pl.when(has_above)
        def _(c=c):
            pass_down[c].wait_recv()

        @pl.when(has_below)
        def _(c=c):
            pass_up[c].wait_recv()

    saved = pltpu.make_async_copy(kv, kv_out, l_sem.at[1])
    saved.start()
    per = piece // BLK

    def part_of(turn):
        middle = turn - 2
        j = jnp.where(turn < 2, 3, jnp.where(turn < 6, 1 + lax.rem(turn, 2), 0))
        half = jnp.where(turn < 2, turn, jnp.where(turn < 6, middle // 2, turn - 6))
        return j, half

    def trade(turn):
        j, half = part_of(turn)
        span = pl.ds(pl.multiple_of(half * rows, rows), rows)
        return remote(
            ctx.at[j, span],
            ctx_out.at[span, pl.ds(pl.multiple_of(j * WIN, WIN), WIN)],
            o_send,
            o_recv,
            turn,
            device_at(plane, y_at ^ (j >> 1), core, x_at ^ (j & 1)),
        )

    def attend_part(turn, carry):
        j, half = part_of(turn)

        def step(n, carry):
            at = pl.ds(pl.multiple_of(n * BLK, BLK), BLK)
            ctx[j, at, :] = attend_block(j * per + n, idx_ref, live_ref, q_ref, kv, lse_ref)
            return carry

        first = half * (per // 2)
        for n in range(per // 2):
            step(first + n, 0)

        @pl.when(turn < 6)
        def _():
            trade(turn).start()

        return carry

    lax.fori_loop(0, 8, attend_part, 0)
    ctx_out[:, 0:WIN] = ctx[0]
    for c in (2, 4, 3, 5, 6, 7):
        hops[c].wait_send()
    for c in range(8):
        to_core[c].wait_send()
        keeps[c].wait()

        @pl.when(has_above)
        def _(c=c):
            to_above[c].wait_send()
            pass_down[c].wait_send()

        @pl.when(has_below)
        def _(c=c):
            to_below[c].wait_send()
            pass_up[c].wait_send()

    saved.wait()
    for copy in hand_on:
        copy.wait()

    def settle(turn, carry):
        trade(turn).wait()
        return carry

    lax.fori_loop(0, 6, settle, 0)


def forward_attention(tokens, w_query, w_key, w_value, lengths, seq_order, rand_row, planes):
    piece, width = tokens.shape
    dma, low = pltpu.SemaphoreType.DMA, jnp.bfloat16
    sds = jax.ShapeDtypeStruct
    blocks = 4 * piece // BLK
    return pl.pallas_call(
        functools.partial(forward_kernel, planes),
        out_shape=[
            sds((24 * piece // BLK, BLK, 2 * WQ), low),
            sds((4 * piece, WIN), low),
            sds((4 * piece, width), low),
            sds((piece, 4 * WIN), low),
            sds((blocks, WQ), jnp.float32),
            sds((blocks * SLOTS,), jnp.int32),
            sds((blocks * SLOTS,), jnp.int32),
            sds((width, WIN), low),
            sds((width, 2 * WQ), low),
        ],
        in_specs=[VMEM] + [ANY] * 3 + [SMEM] * 2 + [VMEM, SMEM],
        out_specs=[ANY, VMEM, ANY, VMEM, VMEM, SMEM, SMEM, ANY, ANY],
        scratch_shapes=[
            pltpu.VMEM((3 * piece, width), low),
            pltpu.VMEM((24 * piece // BLK, BLK, 2 * WQ), low),
            pltpu.VMEM((4, piece, WIN), low),
            pltpu.VMEM(rand_row.shape, jnp.int32),
            pltpu.SMEM(rand_row.shape, jnp.int32),
            pltpu.VMEM((3, width, width), low),
            pltpu.VMEM((width, WIN), low),
            pltpu.VMEM((width, 2 * WQ), low),
            dma((6,)),
            dma((6,)),
        ]
        + [dma((8,))] * 11
        + [dma((6,))] * 2
        + [dma((1,))] * 2
        + [dma((7,))],
        compiler_params=pltpu.CompilerParams(
            collective_id=0, has_side_effects=True, vmem_limit_bytes=62 << 20
        ),
        cost_estimate=pl.CostEstimate(
            flops=2 * 4 * piece * width * 640, bytes_accessed=40 << 20, transcendentals=0
        ),
        name="forward_attention",
    )(tokens, w_query, w_key, w_value, lengths, seq_order, rand_row, rand_row)


def attend_back(idx, live, queries, grads, level, keys_values):
    rows, width = keys_values.shape[0] // 6, keys_values.shape[1]
    count = queries.shape[0]
    kv_shape = jax.ShapeDtypeStruct((6 * rows, width), jnp.bfloat16)
    return pl.pallas_call(
        backward_kernel,
        out_shape=[jax.ShapeDtypeStruct((count, WIN), jnp.bfloat16)] + [kv_shape],
        in_specs=[SMEM, SMEM, VMEM, VMEM, VMEM, ANY],
        out_specs=[VMEM] * 2,
        scratch_shapes=[
            pltpu.VMEM((6 * rows, width), jnp.bfloat16),
            pltpu.VMEM((6 * rows, width), jnp.float32),
            pltpu.SemaphoreType.DMA((1,)),
        ],
        compiler_params=pltpu.CompilerParams(vmem_limit_bytes=56 << 20),
        cost_estimate=pl.CostEstimate(
            flops=2 * 10 * count * 3 * 256 * 512, bytes_accessed=24 * rows * width, transcendentals=count * 3 * 512
        ),
        name="attend_back",
    )(idx, live, queries, grads, level, keys_values)


def reduce_kernel(planes, *refs):
    dkv_in, dq_in, x_in, wq_in, wkv_in, one_in = refs[:6]
    pair_in = refs[6:12]
    tok_out, q_out, k_out, v_out, up_out, side_out, norm_out, down_out = refs[12:20]
    own, core_in, z_out, z_in, g_all, dx_out, dx_in, acc = refs[20:28]
    dq, xs, wq, wkv, one = refs[28:33]
    p_slab, p_core, p_z, p_zin, p_fin, p_all = refs[33:39]
    keep, give = refs[39:42], refs[42:45]
    got, two, fin = refs[45:48], refs[48:51], refs[51:54]
    line_out, line_in = refs[54:57], refs[57:60]
    l_sem, i_sem, c_s, c_r, u_s, u_r, d_s, d_r, x_s, x_r = refs[60:70]
    pk_s, pk_r, pz_s, pz_r, pf_s, pf_r = refs[70:76]
    w2_s, w2_r, w3_s, w3_r, w4_s, w4_r, w1_s, w1_r = refs[76:84]
    plane, y_at, core, x_at = place()
    piece = tok_out.shape[0]
    part = 4 * piece
    rest = planes - 1
    group = y_at * 2 + x_at
    low, f32 = jnp.bfloat16, jnp.float32

    def there(j):
        return device_at(plane, y_at ^ (j >> 1), core, x_at ^ (j & 1))

    by_x, by_y = there(1), there(2)
    by_core = device_at(plane, y_at, 1 - core, x_at)
    others = [device_at(lax.rem(plane + g, planes), y_at, core, x_at) for g in range(1, planes)]
    has_above, has_below = plane < planes - 1, plane > 0
    above = device_at(plane + 1, y_at, core, x_at)
    below = device_at(plane - 1, y_at, core, x_at)

    def chunk(base, j):
        return pl.ds(pl.multiple_of(base + j * piece, piece), piece)

    def load_own(turn, r, j):
        return pltpu.make_async_copy(
            dkv_in.at[chunk(2 * r * part, j)], own.at[chunk(r * part, j)], l_sem.at[turn]
        )

    def to_core(turn, r, j):
        return remote(
            dkv_in.at[chunk((2 * r + 1) * part, j)],
            core_in.at[chunk(r * part, j)],
            c_s,
            c_r,
            turn,
            by_core,
        )

    def to_below(j):
        return remote(z_out.at[chunk(0, j)], z_in.at[chunk(0, j)], d_s, d_r, j, below)

    def to_above(j):
        return remote(z_out.at[chunk(part, j)], z_in.at[chunk(part, j)], u_s, u_r, j, above)

    def to_owner(j):
        return remote(dx_out.at[j - 1], dx_in.at[j - 1], x_s, x_r, j - 1, there(j))

    def every(n, action):
        j = 3 - n
        for turn, r in ((n * 2, 0), (n * 2 + 1, 2)):
            action(turn, r, j)

    greet([by_x, by_y, there(3), by_core] + others)

    def begin(n, carry):
        def go(turn, r, j):
            to_core(turn, r, j).start()
            load_own(turn, r, j).start()

        every(n, go)
        return carry

    lax.fori_loop(0, 4, begin, 0)

    def begin_mid(n, carry):
        to_core(8 + n, 1, 3 - n).start()
        load_own(8 + n, 1, 3 - n).start()
        return carry

    lax.fori_loop(0, 4, begin_mid, 0)
    inputs = [(pair_in[2 * n], keep[n]) for n in range(3)]
    inputs += [(pair_in[2 * n + 1], give[n]) for n in (0, 2)]
    inputs += [(wq_in, wq), (wkv_in, wkv), (dq_in, dq), (x_in, xs), (one_in, one)]
    inputs = [pltpu.make_async_copy(src, dst, i_sem.at[n]) for n, (src, dst) in enumerate(inputs)]
    for copy in inputs:
        copy.start()
    w1 = remote(pair_in[3], give[1], w1_s, w1_r, 0, by_y)
    w1.start()

    def both(turn, r, j):
        to_core(turn, r, j).wait_recv()
        load_own(turn, r, j).wait()
        at = chunk(r * part, j)
        return own[at, :].astype(f32) + core_in[at, :].astype(f32)

    def spread(n, carry):
        j = 3 - n
        z_out[chunk(0, j), :] = both(2 * n, 0, j).astype(low)

        @pl.when(has_below)
        def _():
            to_below(j).start()

        z_out[chunk(part, j), :] = both(2 * n + 1, 2, j).astype(low)

        @pl.when(has_above)
        def _():
            to_above(j).start()

        return carry

    lax.fori_loop(0, 4, spread, 0)

    for copy in inputs[:5]:
        copy.wait()
    halves = [keep[0].shape[2] // 2, keep[1].shape[2] // 2]
    w2 = {}
    for n in (0, 2, 1):
        if n == 1:
            w1.wait()

        def merge(p, carry, n=n):
            keep[n][p] = (keep[n][p].astype(f32) + give[n][p].astype(f32)).astype(low)
            return carry

        lax.fori_loop(0, planes, merge, 0)
        if n < 2:
            cols = pl.ds(pl.multiple_of((1 - x_at) * halves[n], 128), halves[n])
            w2[n] = remote(keep[n].at[:, :, cols], got[n], w2_s, w2_r, n, by_x)
        else:
            w2[n] = remote(keep[n].at[:, 1 - y_at], got[n], w2_s, w2_r, n, by_y)
        w2[n].start()
    for copy in inputs[5:]:
        copy.wait()
    acc[...] = jnp.zeros_like(acc)

    def arrive(n):
        j = 3 - n
        g_all[:, 2 * WQ :] = dq[chunk(0, j), :]
        g_all[:, : 2 * WQ] = both(8 + n, 1, j).astype(low)

        @pl.when(has_above)
        def _():
            to_below(j).wait_recv()
            g_all[:, : 2 * WQ] = (
                g_all[:, : 2 * WQ].astype(f32) + z_in[chunk(0, j), :].astype(f32)
            ).astype(low)

        @pl.when(has_below)
        def _():
            to_above(j).wait_recv()
            g_all[:, : 2 * WQ] = (
                g_all[:, : 2 * WQ].astype(f32) + z_in[chunk(part, j), :].astype(f32)
            ).astype(low)

    def back(j):
        grads = g_all[...]
        return nt(grads[:, 2 * WQ :], wq[...]) + nt(grads[:, : 2 * WQ], wkv[...])

    def outer(j):
        acc[...] += tn(xs[chunk(0, j), :], g_all[...])

    def send_back(n, carry):
        arrive(n)
        dx_out[2 - n] = back(3 - n).astype(low)
        to_owner(3 - n).start()
        outer(3 - n)
        return carry

    lax.fori_loop(0, 3, send_back, 0)

    for n in range(3):
        w2[n].wait_recv()

        def halve(p, carry, n=n):
            if n < 2:
                cols = pl.ds(pl.multiple_of(x_at * halves[n], 128), halves[n])
                mine = keep[n][p, :, cols]
            else:
                mine = keep[n][p, y_at]
            two[n][p] = (mine.astype(f32) + got[n][p].astype(f32)).astype(low)
            return carry

        lax.fori_loop(0, planes, halve, 0)

    def line_copy(n, way, t):
        return remote(
            line_out[n].at[way, t],
            line_in[n].at[way, t],
            w3_s,
            w3_r,
            (n * 2 + way) * rest + t,
            below if way else above,
        )

    def line_step(t):
        for n in range(3):
            for way in range(2):
                spot = (planes - 1 - plane) if way else plane
                gap = planes - 1 - t
                slab = (plane - gap) if way else (plane + gap)
                sends = jnp.logical_and(t >= spot, spot < planes - 1)

                @pl.when(jnp.logical_and(sends, spot == 0))
                def _():
                    line_out[n][way, t] = two[n][slab]
                    line_copy(n, way, t).start()

                @pl.when(jnp.logical_and(sends, spot > 0))
                def _():
                    line_copy(n, way, t - 1).wait_recv()
                    line_out[n][way, t] = (
                        two[n][slab].astype(f32) + line_in[n][way, t - 1].astype(f32)
                    ).astype(low)
                    line_copy(n, way, t).start()

    arrive(3)
    line_step(0)
    tok_out[...] = one[...] + back(0)
    outer(0)

    share = p_slab.shape[3]
    acc[:, 2 * WQ :] *= DH ** (-0.5)
    for p in range(planes):
        for y in range(2):
            for k in range(2):
                at = ((p * 2 + y) * 2 + k) * share
                p_slab[k, p, y] = acc[at : at + share, :].astype(low)
    pk = remote(p_slab.at[1 - core], p_core, pk_s, pk_r, 0, by_core)
    pk.start()
    if planes > 2:
        line_step(1)
    pk.wait_recv()

    def merge_core(p, carry):
        p_z[p] = (p_slab[core, p].astype(f32) + p_core[p].astype(f32)).astype(low)
        return carry

    lax.fori_loop(0, planes, merge_core, 0)
    pz = [
        remote(
            p_z.at[lax.rem(plane + g, planes)], p_zin.at[g - 1], pz_s, pz_r, g - 1, others[g - 1]
        )
        for g in range(1, planes)
    ]
    for copy in pz:
        copy.start()

    def next_step(t, carry):
        line_step(t)
        return carry

    lax.fori_loop(2, planes - 1, next_step, 0)
    for j in (3, 2, 1):
        to_owner(j).wait_recv()
        tok_out[...] += dx_in[j - 1].astype(f32)

    total = p_z[plane].astype(f32)
    for g in range(1, planes):
        pz[g - 1].wait_recv()
        total = total + p_zin[g - 1].astype(f32)
    p_fin[...] = total.astype(low)
    pf = [
        remote(p_fin.at[y_at ^ (j >> 1)], p_all.at[j], pf_s, pf_r, j - 1, there(j))
        for j in (1, 2, 3)
    ]
    for copy in pf:
        copy.start()
    p_all[0] = p_fin[y_at]

    w4 = []
    for n in range(3):
        fin[n][x_at] = two[n][plane]

        @pl.when(has_below)
        def _(n=n):
            line_copy(n, 0, rest - 1).wait_recv()
            fin[n][x_at] = (
                fin[n][x_at].astype(f32) + line_in[n][0, rest - 1].astype(f32)
            ).astype(low)

        @pl.when(has_above)
        def _(n=n):
            line_copy(n, 1, rest - 1).wait_recv()
            fin[n][x_at] = (
                fin[n][x_at].astype(f32) + line_in[n][1, rest - 1].astype(f32)
            ).astype(low)

        w4.append(remote(fin[n].at[x_at], fin[n].at[x_at], w4_s, w4_r, n, by_x))
        w4[n].start()

    for copy in pf:
        copy.wait()
    for a in range(4):
        grads = p_all[a ^ group].astype(f32)
        for n, dest in enumerate((k_out, v_out, q_out)):
            dest[:, a * WQ : (a + 1) * WQ] = grads[:, n * WQ : (n + 1) * WQ]
    for n, dest in ((0, up_out), (2, down_out)):
        w4[n].wait()
        width = dest.shape[1] // 2
        for side in range(2):
            dest[:, side * width : (side + 1) * width] = fin[n][side].astype(f32)
    w4[1].wait()
    width = side_out.shape[1] // 2
    for side in range(2):
        done = fin[1][side].astype(f32)
        side_out[:, side * width : (side + 1) * width] = done[:share]
        norm_out[:, side * width : (side + 1) * width] = done[share : share + 8]

    for copy in list(w2.values()) + pz + [pk]:
        copy.wait_send()

    def settle(n, carry):
        every(n, lambda turn, r, j: to_core(turn, r, j).wait_send())
        to_core(8 + n, 1, 3 - n).wait_send()

        @pl.when(has_below)
        def _():
            to_below(3 - n).wait_send()

        @pl.when(has_above)
        def _():
            to_above(3 - n).wait_send()

        return carry

    lax.fori_loop(0, 4, settle, 0)
    for j in (1, 2, 3):
        to_owner(j).wait_send()

    def settle_line(t, carry):
        for n in range(3):
            for way in range(2):
                spot = (planes - 1 - plane) if way else plane

                @pl.when(jnp.logical_and(t >= spot, spot < planes - 1))
                def _():
                    line_copy(n, way, t).wait_send()

        return carry

    lax.fori_loop(0, planes - 1, settle_line, 0)


def reduce_all(dkv, dq, stretch, wq, wkv, one, up, out, down, planes):
    low, f32 = jnp.bfloat16, jnp.float32
    piece = dq.shape[0] // 4
    width = stretch.shape[1]
    share = up[0].shape[1]
    rest = planes - 1
    dma, vm, sds = pltpu.SemaphoreType.DMA, pltpu.VMEM, jax.ShapeDtypeStruct
    cols = 2 * WQ + WIN
    tall = out[0].shape[1]
    wide = up[0].shape[2]
    kinds = [(share, wide // 2), (tall, width // 2), down[0].shape[2:]]
    pairs = [up[0].shape, out[0].shape, down[0].shape]
    return pl.pallas_call(
        functools.partial(reduce_kernel, planes),
        out_shape=[sds((piece, width), f32)]
        + [sds((share, width), f32)] * 3
        + [
            sds((share, wide), f32),
            sds((share, width), f32),
            sds((8, width), f32),
            sds((kinds[2][0], width), f32),
        ],
        in_specs=[ANY] * 12,
        out_specs=[VMEM] * 8,
        scratch_shapes=[
            vm((12 * piece, 2 * WQ), low),
            vm((12 * piece, 2 * WQ), low),
            vm((8 * piece, 2 * WQ), low),
            vm((8 * piece, 2 * WQ), low),
            vm((piece, cols), low),
            vm((3, piece, width), low),
            vm((3, piece, width), low),
            vm((width, cols), f32),
            vm(dq.shape, low),
            vm(stretch.shape, low),
            vm(wq.shape, low),
            vm(wkv.shape, low),
            vm(one.shape, f32),
            vm((2, planes, 2, share, cols), low),
            vm((planes, 2, share, cols), low),
            vm((planes, 2, share, cols), low),
            vm((rest, 2, share, cols), low),
            vm((2, share, cols), low),
            vm((4, share, cols), low),
        ]
        + [vm(p, low) for p in pairs] * 2
        + [vm((planes,) + k, low) for k in kinds] * 2
        + [vm((2,) + k, low) for k in kinds]
        + [vm((2, rest) + k, low) for k in kinds] * 2
        + [dma((12,)), dma((11,))]
        + [dma((12,))] * 2
        + [dma((4,))] * 4
        + [dma((3,))] * 2
        + [dma((1,))] * 2
        + [dma((rest,))] * 2
        + [dma((3,))] * 2
        + [dma((3,))] * 2
        + [dma((6 * rest,))] * 2
        + [dma((3,))] * 2
        + [dma((1,))] * 2,
        compiler_params=pltpu.CompilerParams(
            collective_id=1, has_side_effects=True, vmem_limit_bytes=60 << 20
        ),
        cost_estimate=pl.CostEstimate(
            flops=4 * 4 * piece * width * cols, bytes_accessed=40 << 20, transcendentals=0
        ),
        name="reduce_all",
    )(dkv, dq, stretch, wq, wkv, one, up[0], up[1], out[0], out[1], down[0], down[1])


def dense_kernel(
    planes,
    tok_ref,
    ctx_ref,
    cot_ref,
    g1_ref,
    b1_ref,
    g2_ref,
    b2_ref,
    wout_in,
    wup_in,
    wdown_in,
    *refs,
):
    out_ref, one_ref, do_out, up_keep, up_give, out_keep, out_give, down_keep, down_give = refs[:9]
    wup, wdown, acc, x1, s1, g_two, nl, hid, slope, gp, gm, ga = refs[9:21]
    dctx, up_loc, out_loc, down_loc, up_got, out_got, down_got, down_sum = refs[21:29]
    w_sem, mv_sem, do_s, do_r, up_s, up_r, out_s, out_r, down_s, down_r = refs[29:39]
    wout_ref = refs[39]
    plane, y_at, core, x_at = place()
    piece, width = tok_ref.shape
    share = up_loc.shape[2]
    slab = down_loc.shape[2]
    pairs = 2 * planes
    group = y_at * 2 + x_at
    f32 = jnp.float32
    fetch = [
        pltpu.make_async_copy(
            wout_in.at[pl.ds(pl.multiple_of((group ^ j) * WQ, WQ), WQ)],
            wout_ref.at[pl.ds(j * WIN + WIN - WQ, WQ)],
            w_sem.at[2 + j],
        )
        for j in range(4)
    ]
    for copy in fetch:
        copy.start()
    bring = [
        pltpu.make_async_copy(wup_in, wup, w_sem.at[0]),
        pltpu.make_async_copy(wdown_in, wdown, w_sem.at[1]),
    ]
    for copy in bring:
        copy.start()

    def there(j):
        return device_at(plane, y_at ^ (j >> 1), core, x_at ^ (j & 1))

    by_core = device_at(plane, y_at, 1 - core, x_at)
    greet([there(1), there(2), there(3), by_core])

    height, tile = 32, 2 * WQ
    wide = wup.shape[1]

    def rows_of(n):
        return pl.ds(pl.multiple_of(n * height, height), height)

    def cols_of(n):
        return pl.ds(pl.multiple_of(n * tile, tile), tile)

    def mean(v):
        return jnp.mean(v, axis=1, keepdims=True)

    def fold(v):
        return v[:8] + v[8:16] + v[16:24] + v[24:]

    for j in range(4):
        wout_ref[j * WIN : j * WIN + WIN - WQ, :] = jnp.zeros((WIN - WQ, width), jnp.bfloat16)
    for copy in fetch:
        copy.wait()
    acc[...] = jnp.dot(ctx_ref[...], wout_ref[...], preferred_element_type=f32)
    g1, b1, g2, b2 = (r[...].reshape(1, width) for r in (g1_ref, b1_ref, g2_ref, b2_ref))

    def norm_one(n, carry):
        at = rows_of(n)
        value = tok_ref[at, :].astype(f32) + acc[at, :]
        center = value - mean(value)
        inverse = lax.rsqrt(mean(center * center) + eps_norm)
        hat = center * inverse
        x1[at, :] = hat
        s1[at, :] = jnp.broadcast_to(inverse, (height, 128))
        nl[at, :] = (hat * g1 + b1).astype(jnp.bfloat16)
        return carry

    lax.fori_loop(0, piece // height, norm_one, 0, unroll=2)
    bring[0].wait()

    def expand(n, carry):
        at = cols_of(n)
        pre = jnp.dot(nl[...], wup[:, at], preferred_element_type=f32)
        square = pre * pre
        inner = 0.7978845608028654 * pre * (1.0 + 0.044715 * square)
        bend = jnp.tanh(inner)
        half_up = 0.5 + 0.5 * bend
        hid[:, at] = (pre * half_up).astype(jnp.bfloat16)
        slope[:, at] = half_up + 0.5 * pre * (1.0 - bend * bend) * (
            0.7978845608028654 + 0.1070322243 * square
        )
        return carry

    lax.fori_loop(0, wide // tile, expand, 0)
    bring[1].wait()
    acc[...] = jnp.dot(hid[...], wdown[...], preferred_element_type=f32)
    nothing = jnp.zeros((8, width), f32)

    def norm_two(n, carry):
        gain_sum, shift_sum = carry
        at = rows_of(n)
        value = x1[at, :] * g1 + b1 + acc[at, :]
        center = value - mean(value)
        inverse = lax.rsqrt(mean(center * center) + eps_norm)
        hat = center * inverse
        out_ref[at, :] = (hat * g2 + b2).astype(jnp.bfloat16)
        cot = cot_ref[at, :].astype(f32)
        gain_sum, shift_sum = gain_sum + fold(cot * hat), shift_sum + fold(cot)
        up = cot * g2
        grad = inverse * (up - mean(up) - hat * mean(up * hat))
        g_two[at, :] = grad
        gm[at, :] = grad.astype(jnp.bfloat16)
        return gain_sum, shift_sum

    gain_two, shift_two = lax.fori_loop(0, piece // height, norm_two, (nothing, nothing), unroll=2)

    def shrink(n, carry):
        at = cols_of(n)
        back = nt(gm[...], wdown[at, :])
        gp[:, at] = (back * slope[:, at]).astype(jnp.bfloat16)
        return carry

    lax.fori_loop(0, wide // tile, shrink, 0)
    acc[...] = nt(gp[...], wup[...])

    def norm_three(n, carry):
        gain_sum, shift_sum = carry
        at = rows_of(n)
        grad_in, hat = g_two[at, :] + acc[at, :], x1[at, :]
        gain_sum, shift_sum = gain_sum + fold(grad_in * hat), shift_sum + fold(grad_in)
        up = grad_in * g1
        grad = s1[at, 0:1] * (up - mean(up) - hat * mean(up * hat))
        one_ref[at, :] = grad
        ga[at, :] = grad.astype(jnp.bfloat16)
        return gain_sum, shift_sum

    gain_one, shift_one = lax.fori_loop(
        0, piece // height, norm_three, (nothing, nothing), unroll=2
    )
    side = jnp.concatenate(
        [jnp.sum(v, axis=0, keepdims=True) for v in (gain_one, shift_one, gain_two, shift_two)]
        + [jnp.zeros((12, width), f32)],
        axis=0,
    ).astype(jnp.bfloat16)

    low = jnp.bfloat16
    trades = []
    for j in (3, 1, 2, 0):
        part = nt(ga[...], wout_ref[pl.ds(j * WIN, WIN), :]).astype(low)
        if j:
            dctx[j - 1] = part
            trades.append(
                remote(
                    dctx.at[j - 1], do_out.at[pl.ds(j * piece, piece)], do_s, do_r, j - 1, there(j)
                )
            )
            trades[-1].start()
        else:
            do_out[pl.ds(0, piece), :] = part

    tile = 2 * WQ
    per = tile // (2 * slab)
    tiles = wide // tile

    def down_copy(t):
        span = pl.ds(t * per, per)
        return remote(down_loc.at[1 - core, span], down_got.at[span], down_s, down_r, t, by_core)

    def up_copy(t):
        span = cols_of(t)
        return remote(
            up_loc.at[1 - core, :, :, span], up_got.at[:, :, span], up_s, up_r, t, by_core
        )

    def make_down(t, carry):
        cell = tn(hid[:, cols_of(t)], gm[...])
        for n in range(per):
            for k in range(2):
                at = (n * 2 + k) * slab
                down_loc[k, t * per + n] = cell[at : at + slab].astype(low)
        down_copy(t).start()
        return carry

    lax.fori_loop(0, tiles, make_down, 0)

    def make_up(t, carry):
        cell = tn(nl[...], gp[:, cols_of(t)])
        for q in range(pairs):
            for k in range(2):
                at = (q * 2 + k) * share
                up_loc[k, q, :, cols_of(t)] = cell[at : at + share].astype(low)
        up_copy(t).start()
        return carry

    lax.fori_loop(0, tiles, make_up, 0)
    per_group = pairs // 4
    for j in range(4):
        cell = tn(ctx_ref[:, j * WIN : (j + 1) * WIN], ga[...])
        for n in range(per_group):
            for k in range(2):
                at = WIN - WQ + (n * 2 + k) * share
                out_loc[k, (group ^ j) * per_group + n, :share, :] = cell[at : at + share].astype(low)
    for q in range(pairs):
        for k in range(2):
            out_loc[k, q, share:, :] = side
    outs = remote(out_loc.at[1 - core], out_got, out_s, out_r, 0, by_core)
    outs.start()

    moved = []

    def move(source, dest):
        moved.append(pltpu.make_async_copy(source, dest, mv_sem.at[len(moved)]))
        moved[-1].start()

    half = width // 2

    def sum_down(t, carry):
        down_copy(t).wait_recv()
        for n in range(per):
            q = t * per + n
            total = (
                down_loc[core, q].astype(jnp.float32) + down_got[q].astype(jnp.float32)
            ).astype(low)
            down_sum[0, q] = total[:, :half]
            down_sum[1, q] = total[:, half:]
        return carry

    lax.fori_loop(0, tiles, sum_down, 0)
    move(down_sum.at[x_at], down_keep)
    move(down_sum.at[1 - x_at], down_give)

    def sum_up(q, carry):
        up_got[q] = (up_loc[core, q].astype(jnp.float32) + up_got[q].astype(jnp.float32)).astype(low)
        return carry

    for t in range(tiles):
        up_copy(t).wait_recv()
    lax.fori_loop(0, pairs, sum_up, 0)
    outs.wait_recv()
    for p in range(planes):
        for y in range(2):
            q = p * 2 + y
            out_got[q] = (
                out_loc[core, q].astype(jnp.float32) + out_got[q].astype(jnp.float32)
            ).astype(low)
        for got, keep, give in ((up_got, up_keep, up_give), (out_got, out_keep, out_give)):
            move(got.at[p * 2 + y_at], keep.at[p])
            move(got.at[p * 2 + 1 - y_at], give.at[p])
    for copy in trades:
        copy.wait()
    for t in range(tiles):
        down_copy(t).wait_send()
        up_copy(t).wait_send()
    outs.wait_send()
    for copy in moved:
        copy.wait()


def dense_layers(tokens, ctx, cotangent, norms, wout, w_up, w_down, planes):
    low = jnp.bfloat16
    piece, width = tokens.shape
    pairs = 2 * planes
    wide = w_up.shape[1]
    share, slab, tall = width // (2 * pairs), wide // (2 * pairs), 16
    sds, vm, dma = jax.ShapeDtypeStruct, pltpu.VMEM, pltpu.SemaphoreType.DMA
    up, out = (planes, share, wide), (planes, share + tall, width)
    down = (pairs, slab, width // 2)
    tiles = wide // (2 * WQ)
    f32 = jnp.float32
    return pl.pallas_call(
        functools.partial(dense_kernel, planes),
        out_shape=[sds((piece, width), low), sds((piece, width), f32), sds((4 * piece, WIN), low)]
        + [sds(up, low)] * 2
        + [sds(out, low)] * 2
        + [sds(down, low)] * 2,
        in_specs=[VMEM] * 7 + [ANY] * 3,
        out_specs=[VMEM] * 3 + [ANY] * 6,
        scratch_shapes=[
            vm(w_up.shape, low),
            vm(w_down.shape, low),
            vm((piece, width), f32),
            vm((piece, width), f32),
            vm((piece, 128), f32),
            vm((piece, width), f32),
            vm((piece, width), low),
            vm((piece, wide), low),
            vm((piece, wide), f32),
            vm((piece, wide), low),
            vm((piece, width), low),
            vm((piece, width), low),
            vm((3, piece, WIN), low),
            vm((2, pairs, share, wide), low),
            vm((2, pairs, share + tall, width), low),
            vm((2, pairs, slab, width), low),
            vm((pairs, share, wide), low),
            vm((pairs, share + tall, width), low),
            vm((pairs, slab, width), low),
            vm((2, pairs, slab, width // 2), low),
            dma((6,)),
            dma((2 + 4 * planes,)),
        ]
        + [dma((3,))] * 2
        + [dma((tiles,))] * 2
        + [dma((1,))] * 2
        + [dma((tiles,))] * 2
        + [vm((4 * WIN, width), low)],
        compiler_params=pltpu.CompilerParams(
            collective_id=2, has_side_effects=True, vmem_limit_bytes=62 << 20
        ),
        cost_estimate=pl.CostEstimate(
            flops=2 * piece * width * (6 * wide + 3072), bytes_accessed=30 << 20, transcendentals=0
        ),
        name="dense_layers",
    )(tokens, ctx, cotangent, *norms, wout, w_up, w_down)


def finish_kernel(share, *refs):
    count = (len(refs) - 5) // 2
    for n in range(count):
        refs[count + 1 + n][...] = refs[n][...]
    seq_at = lax.axis_index("seq")
    rows = refs[count][...]
    width = rows.shape[1]
    spot = lax.broadcasted_iota(jnp.int32, (width, 128), 0) - seq_at * share
    chosen = (spot == lax.broadcasted_iota(jnp.int32, (width, 128), 1)).astype(jnp.float32)
    picked = jnp.dot(
        rows, chosen, preferred_element_type=jnp.float32, precision=lax.Precision.HIGHEST
    )
    for n in range(4):
        refs[2 * count + 1 + n][...] = picked[n, :share]


def finish(arrays, norm_rows, share):
    sds = jax.ShapeDtypeStruct
    return pl.pallas_call(
        functools.partial(finish_kernel, share),
        out_shape=[sds(v.shape, v.dtype) for v in arrays] + [sds((share,), jnp.float32)] * 4,
        in_specs=[VMEM] * (len(arrays) + 1),
        out_specs=[VMEM] * (len(arrays) + 4),
        compiler_params=pltpu.CompilerParams(vmem_limit_bytes=62 << 20),
        name="finish",
    )(*arrays, norm_rows)


def body(
    tokens,
    w_query,
    w_key,
    w_value,
    w_out,
    gain_attn,
    shift_attn,
    w_up,
    w_down,
    gain_mlp,
    shift_mlp,
    cotangent,
    lengths,
    seq_order,
    rand_blocks,
):
    piece, width = tokens.shape
    seqs, heads = lax.axis_size("seq"), lax.axis_size("head")
    planes = seqs // 4
    assert heads == 2 and 8 * piece == MAXB * BLK and width == 4 * WQ
    seq_at, x_at = lax.axis_index("seq"), lax.axis_index("head")
    plane, y_at, core = seq_at // 4, (seq_at // 2) % 2, seq_at % 2
    group = y_at * 2 + x_at

    flat = rand_blocks.reshape(1, -1)
    rand_row = jnp.pad(flat, ((0, 0), (0, 128 - flat.shape[1])))
    keys_values, queries, stretch, context_tok, level, idx, live, wq_own, wkv_own = (
        forward_attention(
            tokens, w_query, w_key, w_value, lengths, seq_order, rand_row, planes
        )
    )
    share = width // seqs
    norms = [gain_attn, shift_attn, gain_mlp, shift_mlp]
    output, grad_one, grad_ctx, up_keep, up_give, out_keep, out_give, down_keep, down_give = (
        dense_layers(tokens, context_tok, cotangent, norms, w_out, w_up, w_down, planes)
    )
    up_pair = (up_keep, xor_swap(up_give, 4))
    out_pair = (out_keep, out_give)
    two_y = (planes, 2) + down_keep.shape[1:]
    down_pair = (down_keep.reshape(two_y), xor_swap(down_give, 1).reshape(two_y))

    grad_q, grad_kv = attend_back(
        idx, live, queries, grad_ctx, level, keys_values.reshape(-1, 2 * WQ)
    )
    grad_tokens, grad_wq, grad_wk, grad_wv, up_total, out_total, norm_rows, down_total = reduce_all(
        grad_kv,
        grad_q,
        stretch,
        wq_own,
        wkv_own,
        grad_one,
        up_pair,
        out_pair,
        down_pair,
        planes,
    )

    finals = finish(
        (grad_tokens, grad_wq, grad_wk, grad_wv, out_total, up_total, down_total), norm_rows, share
    )

    grad_tokens, grad_wq, grad_wk, grad_wv, grad_out, grad_up, grad_down = finals[:7]
    gain_one, shift_one, gain_two, shift_two = finals[7:]
    return (
        output,
        grad_tokens,
        grad_wq,
        grad_wk,
        grad_wv,
        grad_out,
        gain_one,
        shift_one,
        grad_up,
        grad_down,
        gain_two,
        shift_two,
    )


def solution(mesh):
    rows = P(("seq", "head"), None)
    seq_rows, seq_only = P("seq", None), P("seq")
    return jax.shard_map(
        body,
        mesh=mesh,
        in_specs=(rows,) + (P(),) * 10 + (rows, P(), P(), seq_rows),
        out_specs=(
            rows,
            rows,
            seq_rows,
            seq_rows,
            seq_rows,
            seq_rows,
            seq_only,
            seq_only,
            seq_rows,
            seq_rows,
            seq_only,
            seq_only,
        ),
        check_vma=False,
    )
```

```python
import functools

import jax
import jax.numpy as jnp
from jax import lax
from jax.experimental import pallas as pl
from jax.experimental.pallas import tpu as pltpu
from jax.sharding import PartitionSpec as P

DH = 64
BLK = 64
MAXB = 64
SLOTS = 8
HG = 3
WQ = HG * DH
WIN = 256
AXES = ("seq", "head")
NEG = -1e30

eps_norm = 1e-06


def xor_swap(value, bits):
    count = lax.axis_size("seq") * lax.axis_size("head")
    return lax.ppermute(value, AXES, [(d, d ^ bits) for d in range(count)])


def lane_groups(rows, offset):
    lane = lax.broadcasted_iota(jnp.int32, (rows, WIN), 1) - offset
    return [jnp.logical_and(lane >= h * DH, lane < (h + 1) * DH) for h in range(HG)]


def spread_heads(block, offset):
    zero = jnp.zeros_like(block)
    return jnp.concatenate([jnp.where(m, block, zero) for m in lane_groups(BLK, offset)], axis=0)


def fold_heads(stacked, offset):
    masks = lane_groups(BLK, offset)
    total = jnp.where(masks[0], stacked[:BLK], 0.0)
    for h in range(1, HG):
        total = total + jnp.where(masks[h], stacked[h * BLK : (h + 1) * BLK], 0.0)
    return total


def nt(a, b):
    return lax.dot_general(a, b, (((1,), (1,)), ((), ())), preferred_element_type=jnp.float32)


def tn(a, b):
    return lax.dot_general(a, b, (((0,), (0,)), ((), ())), preferred_element_type=jnp.float32)


def backward_kernel(idx_ref, live_ref, q_ref, do_ref, o_ref, lse_ref, *refs):
    kv_ref, dq_ref, dkv_ref, kv, acc, sems = refs

    def clear(n, carry):
        acc[pl.ds(pl.multiple_of(n * 256, 256), 256), :] = jnp.zeros((256, 2 * WQ), jnp.float32)
        return carry

    copy = pltpu.make_async_copy(kv_ref, kv, sems.at[0])
    copy.start()
    lax.fori_loop(0, acc.shape[0] // 256, clear, 0)
    copy.wait()

    def step(i, carry):
        q_rows = pl.multiple_of(i * BLK, BLK)
        qexp = spread_heads(q_ref[pl.ds(q_rows, BLK), :], 0)
        doexp = spread_heads(do_ref[pl.ds(q_rows, BLK), :], 64)
        rows = [
            pl.multiple_of(idx_ref[i * SLOTS + s] * BLK, BLK) for s in range(SLOTS)
        ]
        keys = jnp.concatenate([kv[pl.ds(r, BLK), 0:WIN] for r in rows], axis=0)
        values = jnp.concatenate([kv[pl.ds(r, BLK), 128 : 128 + WIN] for r in rows], axis=0)
        product = do_ref[pl.ds(q_rows, BLK), :].astype(jnp.float32) * o_ref[
            pl.ds(q_rows, BLK), :
        ].astype(jnp.float32)
        high = product.astype(jnp.bfloat16)
        ones = jnp.ones((8, WIN), jnp.bfloat16)
        inner = nt(ones, spread_heads(high, 64)) + nt(
            ones, spread_heads((product - high.astype(jnp.float32)).astype(jnp.bfloat16), 64)
        )
        inner = inner[0:1]
        level = lse_ref[pl.ds(i, 1), :]
        raw = nt(keys, qexp)
        grad_probs = nt(values, doexp)
        probs, grad_scores = [], []
        for s in range(SLOTS):
            at = slice(s * BLK, (s + 1) * BLK)
            off = level + jnp.where(live_ref[i * SLOTS + s] > 0, 0.0, -NEG)
            p = jnp.exp(raw[at] - off)
            probs.append(p.astype(jnp.bfloat16))
            grad_scores.append((p * (grad_probs[at] - inner)).astype(jnp.bfloat16))
        probs = jnp.concatenate(probs, axis=0)
        grad_scores = jnp.concatenate(grad_scores, axis=0)
        dk = jnp.dot(grad_scores, qexp, preferred_element_type=jnp.float32)
        dv = jnp.dot(probs, doexp, preferred_element_type=jnp.float32)
        dq = tn(grad_scores, keys)
        dq_ref[pl.ds(q_rows, BLK), :] = fold_heads(dq, 0).astype(jnp.bfloat16)
        for s in range(SLOTS):
            k_s, v_s = dk[s * BLK : (s + 1) * BLK], dv[s * BLK : (s + 1) * BLK]
            at = pl.ds(rows[s], BLK)
            acc[at, 0:128] += k_s[:, :128]
            acc[at, 128:256] += k_s[:, 128:] + v_s[:, :128]
            acc[at, 256:384] += v_s[:, 128:]
        return carry

    lax.fori_loop(0, q_ref.shape[0] // BLK, step, 0, unroll=4)

    def emit(n, carry):
        at = pl.ds(pl.multiple_of(n * 256, 256), 256)
        dkv_ref[at, :] = acc[at, :].astype(jnp.bfloat16)
        return carry

    lax.fori_loop(0, acc.shape[0] // 256, emit, 0)


VMEM = pl.BlockSpec(memory_space=pltpu.VMEM)
SMEM = pl.BlockSpec(memory_space=pltpu.SMEM)
ANY = pl.BlockSpec(memory_space=pl.ANY)


def device_at(plane, y_at, core, x_at):
    return (plane * 4 + y_at * 2 + core, x_at)


def place():
    seq_at, x_at = lax.axis_index("seq"), lax.axis_index("head")
    return seq_at // 4, (seq_at // 2) % 2, seq_at % 2, x_at


def remote(src, dst, sems, recvs, at, device):
    return pltpu.make_async_remote_copy(
        src_ref=src,
        dst_ref=dst,
        send_sem=sems.at[at],
        recv_sem=recvs.at[at],
        device_id=device,
        device_id_type=pl.DeviceIdType.MESH,
    )


def greet(partners):
    barrier = pltpu.get_barrier_semaphore()
    for device in partners:
        pl.semaphore_signal(
            barrier, inc=1, device_id=device, device_id_type=pl.DeviceIdType.MESH
        )
    pl.semaphore_wait(barrier, len(partners))


CHUNK_ORDER = (0, 1, 2, 4, 3, 5, 6, 7)


def slot_tables(plane, y_at, core, x_at, at, lengths, order, rand_own, rand_got, idx_ref, live_ref):
    per = at["piece_blocks"]

    def one(i, carry):
        far, near = i // per, i % per
        y_of, x_of = y_at ^ (far >> 1), x_at ^ (far & 1)
        block = plane * MAXB + y_of * (4 * per) + core * (2 * per) + x_of * per + near
        begin, first, span = jnp.int32(0), jnp.int32(0), jnp.int32(1)
        for m in range(at["seqs"]):
            size = lengths[order[m]]
            inside = begin <= block
            first = jnp.where(inside, begin, first)
            span = jnp.where(inside, size, span)
            begin = begin + size
        row = x_of * per + near
        draws = []
        for n in range(SLOTS - 5):
            spot = row * (SLOTS - 5) + n
            draw = jnp.where(far >= 2, rand_got[0, spot], rand_own[0, spot])
            for power in range(16, -1, -1):
                multiple = span * (1 << power)
                draw = jnp.where(draw >= multiple, draw - multiple, draw)
            draws.append(first + draw)
        candidates = [block - 1, block, block + 1, first, first + span - 1] + draws
        kept = []
        for s in range(SLOTS):
            alive = jnp.int32(1)
            if s == 0:
                alive = (block > first).astype(jnp.int32)
            if s == 2:
                alive = (block < first + span - 1).astype(jnp.int32)
            for e in range(s):
                same = (candidates[e] == candidates[s]).astype(jnp.int32)
                alive = alive * (1 - kept[e] * same)
            kept.append(alive)
            key = jnp.where(alive > 0, candidates[s], block)
            rel = key // MAXB - plane + 1
            inner = key % MAXB
            y_key, rest = inner // (4 * per), inner % (4 * per)
            core_key, rest = rest // (2 * per), rest % (2 * per)
            x_key, near_key = rest // per, rest % per
            spot = (rel * 2 + (core_key ^ core)) * 4 + ((y_key ^ y_at) * 2 + (x_key ^ x_at))
            idx_ref[i * SLOTS + s] = jnp.clip(spot * per + near_key, 0, 24 * per - 1)
            live_ref[i * SLOTS + s] = alive
        return carry

    lax.fori_loop(at["begin"], at["end"], one, 0)


def attend_block(i, idx_ref, live_ref, q_ref, kv, lse_ref):
    qexp = spread_heads(q_ref[pl.ds(pl.multiple_of(i * BLK, BLK), BLK), :], 0)
    at = [idx_ref[i * SLOTS + s] for s in range(SLOTS)]
    off = [jnp.where(live_ref[i * SLOTS + s] > 0, 0.0, -NEG) for s in range(SLOTS)]
    keys = jnp.concatenate([kv[r, :, 0:WIN] for r in at], axis=0)
    values = jnp.concatenate([kv[r, :, 128 : 128 + WIN] for r in at], axis=0)
    raw = nt(keys, qexp)
    parts = [raw[s * BLK : (s + 1) * BLK] for s in range(SLOTS)]
    top = jnp.max(parts[1], axis=0, keepdims=True)
    for s in range(SLOTS):
        top = jnp.maximum(top, jnp.max(parts[s], axis=0, keepdims=True) - off[s])
    e = [jnp.exp(parts[s] - (top + off[s])) for s in range(SLOTS)]
    total = jnp.sum(e[0], axis=0, keepdims=True)
    for s in range(1, SLOTS):
        total = total + jnp.sum(e[s], axis=0, keepdims=True)
    lse_ref[pl.ds(i, 1), :] = top + jnp.log(total)
    scale = 1.0 / total
    probs = jnp.concatenate([(v * scale).astype(jnp.bfloat16) for v in e], axis=0)
    return fold_heads(tn(probs, values), 64).astype(jnp.bfloat16)


def forward_kernel(planes, tok_ref, wq_in, wk_in, wv_in, len_ref, ord_ref, rand_vm, rand_sm, *refs):
    kv_out, q_ref, x_out, ctx_out, lse_ref, idx_ref, live_ref, wq_out, wkv_out, ctx_keep = refs[:10]
    xs, kv, ctx, rand_got, rand_two, w_full, wq_ref, wkv_ref = refs[10:18]
    x_send, x_recv, k_send, k_recv, up_send, up_recv, dn_send, dn_recv = refs[18:26]
    f_send, f_recv, g_send, g_recv, s_sem, o_send, o_recv, r_send, r_recv, l_sem = refs[26:36]
    weights = [
        pltpu.make_async_copy(w, w_full.at[n], l_sem.at[2 + n])
        for n, w in enumerate((wk_in, wv_in, wq_in))
    ]
    for copy in weights:
        copy.start()
    plane, y_at, core, x_at = place()
    piece = tok_ref.shape[0]
    rows = piece // 2
    part = 4 * piece
    by_x = device_at(plane, y_at, core, 1 - x_at)
    by_y = device_at(plane, 1 - y_at, core, x_at)
    by_xy = device_at(plane, 1 - y_at, core, 1 - x_at)
    by_core = device_at(plane, y_at, 1 - core, x_at)
    above = device_at(plane + 1, y_at, core, x_at)
    below = device_at(plane - 1, y_at, core, x_at)
    has_above, has_below = plane < planes - 1, plane > 0
    ring = [device_at(lax.rem(plane + g, planes), y_at, core, x_at) for g in (1, planes - 1)]
    greet([by_x, by_y, by_xy, by_core] + ring)

    def x_rows(c):
        return xs.at[pl.ds((c - 2) * rows, rows)]

    def tok_rows(c):
        return tok_ref.at[pl.ds(c * rows, rows)]

    hops = {
        2: remote(tok_rows(0), x_rows(2), x_send, x_recv, 0, by_x),
        4: remote(tok_rows(0), x_rows(4), x_send, x_recv, 2, by_y),
        3: remote(tok_rows(1), x_rows(3), x_send, x_recv, 1, by_x),
        5: remote(tok_rows(1), x_rows(5), x_send, x_recv, 3, by_y),
        6: remote(x_rows(2), x_rows(6), x_send, x_recv, 4, by_y),
        7: remote(x_rows(5), x_rows(7), x_send, x_recv, 5, by_x),
    }
    rand_trade = remote(rand_vm, rand_got, r_send, r_recv, 0, by_y)
    rand_trade.start()
    for c in (2, 4, 3, 5):
        hops[c].start()

    wq_ref[:, WQ:] = jnp.zeros((wq_ref.shape[0], WIN - WQ), jnp.bfloat16)
    for copy in weights:
        copy.wait()
    for g in range(4):

        @pl.when(y_at * 2 + x_at == g)
        def _(g=g):
            cols = slice(g * WQ, (g + 1) * WQ)
            wkv_ref[:, :WQ] = w_full[0, :, cols]
            wkv_ref[:, WQ:] = w_full[1, :, cols]
            wq_ref[:, :WQ] = w_full[2, :, cols] * jnp.bfloat16(DH ** (-0.5))

    hand_on = [
        pltpu.make_async_copy(wq_ref, wq_out, l_sem.at[5]),
        pltpu.make_async_copy(wkv_ref, wkv_out, l_sem.at[6]),
    ]
    for copy in hand_on:
        copy.start()

    def kv_rows(part_at, c):
        return kv.at[pl.ds((part_at * part + c * rows) // BLK, rows // BLK)]

    to_core, to_above, to_below, pass_up, pass_down = {}, {}, {}, {}, {}
    for c in range(8):
        mine = kv_rows(2, c)
        to_core[c] = remote(mine, kv_rows(3, c), k_send, k_recv, c, by_core)
        to_above[c] = remote(mine, kv_rows(0, c), up_send, up_recv, c, above)
        to_below[c] = remote(mine, kv_rows(4, c), dn_send, dn_recv, c, below)
        pass_up[c] = remote(kv_rows(0, c), kv_rows(1, c), f_send, f_recv, c, by_core)
        pass_down[c] = remote(kv_rows(4, c), kv_rows(5, c), g_send, g_recv, c, by_core)
    keeps = {
        c: pltpu.make_async_copy(
            tok_rows(c) if c < 2 else x_rows(c), x_out.at[pl.ds(c * rows, rows)], s_sem.at[c]
        )
        for c in range(8)
    }

    def relay(c):
        @pl.when(has_below)
        def _():
            to_above[c].wait_recv()
            pass_up[c].start()

        @pl.when(has_above)
        def _():
            to_below[c].wait_recv()
            pass_down[c].start()

    def tables(begin, end):
        slot_tables(
            plane,
            y_at,
            core,
            x_at,
            dict(piece_blocks=piece // BLK, seqs=len_ref.shape[0], begin=begin, end=end),
            len_ref,
            ord_ref,
            rand_sm,
            rand_two,
            idx_ref,
            live_ref,
        )

    query_blocks = part // BLK
    for n, c in enumerate(CHUNK_ORDER):
        if n == 2:
            rand_trade.wait()
            to_scalar = pltpu.make_async_copy(rand_got, rand_two, l_sem.at[0])
            to_scalar.start()
            to_scalar.wait()
            tables(0, query_blocks // 3)
        if n == 4:
            tables(query_blocks // 3, 2 * query_blocks // 3)
        if n == 6:
            tables(2 * query_blocks // 3, query_blocks)
        if c >= 2:
            hops[c].wait_recv()
        if c == 2:
            hops[6].start()
        if c == 5:
            hops[7].start()
        keeps[c].start()
        block = tok_ref[pl.ds(c * rows, rows), :] if c < 2 else xs[pl.ds((c - 2) * rows, rows), :]
        made = jnp.dot(block, wkv_ref[...], preferred_element_type=jnp.float32).astype(jnp.bfloat16)
        kv[pl.ds((2 * part + c * rows) // BLK, rows // BLK)] = made.reshape(rows // BLK, BLK, -1)

        @pl.when(has_above)
        def _(c=c):
            to_above[c].start()

        @pl.when(has_below)
        def _(c=c):
            to_below[c].start()

        to_core[c].start()
        q_ref[pl.ds(c * rows, rows), :] = jnp.dot(
            block, wq_ref[...], preferred_element_type=jnp.float32
        ).astype(jnp.bfloat16)
        if n >= 3:
            relay(CHUNK_ORDER[n - 3])
    for c in CHUNK_ORDER[5:]:
        relay(c)
    for c in range(8):
        to_core[c].wait_recv()

        @pl.when(has_above)
        def _(c=c):
            pass_down[c].wait_recv()

        @pl.when(has_below)
        def _(c=c):
            pass_up[c].wait_recv()

    saved = pltpu.make_async_copy(kv, kv_out, l_sem.at[1])
    saved.start()
    per = piece // BLK

    def part_of(turn):
        middle = turn - 2
        j = jnp.where(turn < 2, 3, jnp.where(turn < 6, 1 + lax.rem(turn, 2), 0))
        half = jnp.where(turn < 2, turn, jnp.where(turn < 6, middle // 2, turn - 6))
        return j, half

    def trade(turn):
        j, half = part_of(turn)
        span = pl.ds(pl.multiple_of(half * rows, rows), rows)
        return remote(
            ctx.at[j, span],
            ctx_out.at[span, pl.ds(pl.multiple_of(j * WIN, WIN), WIN)],
            o_send,
            o_recv,
            turn,
            device_at(plane, y_at ^ (j >> 1), core, x_at ^ (j & 1)),
        )

    def attend_part(turn, carry):
        j, half = part_of(turn)

        def step(n, carry):
            at = pl.ds(pl.multiple_of(n * BLK, BLK), BLK)
            ctx[j, at, :] = attend_block(j * per + n, idx_ref, live_ref, q_ref, kv, lse_ref)
            return carry

        first = half * (per // 2)
        for n in range(per // 2):
            step(first + n, 0)

        @pl.when(turn < 6)
        def _():
            trade(turn).start()

        return carry

    lax.fori_loop(0, 8, attend_part, 0)
    ctx_out[:, 0:WIN] = ctx[0]
    hand_on.append(pltpu.make_async_copy(ctx, ctx_keep, l_sem.at[7]))
    hand_on[-1].start()
    for c in (2, 4, 3, 5, 6, 7):
        hops[c].wait_send()
    for c in range(8):
        to_core[c].wait_send()
        keeps[c].wait()

        @pl.when(has_above)
        def _(c=c):
            to_above[c].wait_send()
            pass_down[c].wait_send()

        @pl.when(has_below)
        def _(c=c):
            to_below[c].wait_send()
            pass_up[c].wait_send()

    saved.wait()
    for copy in hand_on:
        copy.wait()

    def settle(turn, carry):
        trade(turn).wait()
        return carry

    lax.fori_loop(0, 6, settle, 0)


def forward_attention(tokens, w_query, w_key, w_value, lengths, seq_order, rand_row, planes):
    piece, width = tokens.shape
    dma, low = pltpu.SemaphoreType.DMA, jnp.bfloat16
    sds = jax.ShapeDtypeStruct
    blocks = 4 * piece // BLK
    return pl.pallas_call(
        functools.partial(forward_kernel, planes),
        out_shape=[
            sds((24 * piece // BLK, BLK, 2 * WQ), low),
            sds((4 * piece, WIN), low),
            sds((4 * piece, width), low),
            sds((piece, 4 * WIN), low),
            sds((blocks, WQ), jnp.float32),
            sds((blocks * SLOTS,), jnp.int32),
            sds((blocks * SLOTS,), jnp.int32),
            sds((width, WIN), low),
            sds((width, 2 * WQ), low),
            sds((4, piece, WIN), low),
        ],
        in_specs=[VMEM] + [ANY] * 3 + [SMEM] * 2 + [VMEM, SMEM],
        out_specs=[ANY, VMEM, ANY, VMEM, VMEM, SMEM, SMEM, ANY, ANY, ANY],
        scratch_shapes=[
            pltpu.VMEM((3 * piece, width), low),
            pltpu.VMEM((24 * piece // BLK, BLK, 2 * WQ), low),
            pltpu.VMEM((4, piece, WIN), low),
            pltpu.VMEM(rand_row.shape, jnp.int32),
            pltpu.SMEM(rand_row.shape, jnp.int32),
            pltpu.VMEM((3, width, width), low),
            pltpu.VMEM((width, WIN), low),
            pltpu.VMEM((width, 2 * WQ), low),
            dma((6,)),
            dma((6,)),
        ]
        + [dma((8,))] * 11
        + [dma((6,))] * 2
        + [dma((1,))] * 2
        + [dma((8,))],
        compiler_params=pltpu.CompilerParams(
            collective_id=0, has_side_effects=True, vmem_limit_bytes=62 << 20
        ),
        cost_estimate=pl.CostEstimate(
            flops=2 * 4 * piece * width * 640, bytes_accessed=40 << 20, transcendentals=0
        ),
        name="forward_attention",
    )(tokens, w_query, w_key, w_value, lengths, seq_order, rand_row, rand_row)


def attend_back(idx, live, queries, grads, context, level, keys_values):
    rows, width = keys_values.shape[0] // 6, keys_values.shape[1]
    count = queries.shape[0]
    kv_shape = jax.ShapeDtypeStruct((6 * rows, width), jnp.bfloat16)
    return pl.pallas_call(
        backward_kernel,
        out_shape=[jax.ShapeDtypeStruct((count, WIN), jnp.bfloat16)] + [kv_shape],
        in_specs=[SMEM, SMEM, VMEM, VMEM, VMEM, VMEM, ANY],
        out_specs=[VMEM] * 2,
        scratch_shapes=[
            pltpu.VMEM((6 * rows, width), jnp.bfloat16),
            pltpu.VMEM((6 * rows, width), jnp.float32),
            pltpu.SemaphoreType.DMA((1,)),
        ],
        compiler_params=pltpu.CompilerParams(vmem_limit_bytes=56 << 20),
        cost_estimate=pl.CostEstimate(
            flops=2 * 10 * count * 3 * 256 * 512, bytes_accessed=24 * rows * width, transcendentals=count * 3 * 512
        ),
        name="attend_back",
    )(idx, live, queries, grads, context, level, keys_values)


def reduce_kernel(planes, *refs):
    dkv_in, dq_in, x_in, wq_in, wkv_in, one_in = refs[:6]
    pair_in = refs[6:12]
    tok_out, q_out, k_out, v_out, up_out, side_out, norm_out, down_out = refs[12:20]
    own, core_in, z_out, z_in, g_all, dx_out, dx_in, acc = refs[20:28]
    dq, xs, wq, wkv, one = refs[28:33]
    p_slab, p_core, p_z, p_zin, p_fin, p_all = refs[33:39]
    keep, give = refs[39:42], refs[42:45]
    got, two, fin = refs[45:48], refs[48:51], refs[51:54]
    line_out, line_in = refs[54:57], refs[57:60]
    l_sem, i_sem, c_s, c_r, u_s, u_r, d_s, d_r, x_s, x_r = refs[60:70]
    pk_s, pk_r, pz_s, pz_r, pf_s, pf_r = refs[70:76]
    w2_s, w2_r, w3_s, w3_r, w4_s, w4_r, w1_s, w1_r = refs[76:84]
    plane, y_at, core, x_at = place()
    piece = tok_out.shape[0]
    part = 4 * piece
    rest = planes - 1
    group = y_at * 2 + x_at
    low, f32 = jnp.bfloat16, jnp.float32

    def there(j):
        return device_at(plane, y_at ^ (j >> 1), core, x_at ^ (j & 1))

    by_x, by_y = there(1), there(2)
    by_core = device_at(plane, y_at, 1 - core, x_at)
    others = [device_at(lax.rem(plane + g, planes), y_at, core, x_at) for g in range(1, planes)]
    has_above, has_below = plane < planes - 1, plane > 0
    above = device_at(plane + 1, y_at, core, x_at)
    below = device_at(plane - 1, y_at, core, x_at)

    def chunk(base, j):
        return pl.ds(pl.multiple_of(base + j * piece, piece), piece)

    def load_own(turn, r, j):
        return pltpu.make_async_copy(
            dkv_in.at[chunk(2 * r * part, j)], own.at[chunk(r * part, j)], l_sem.at[turn]
        )

    def to_core(turn, r, j):
        return remote(
            dkv_in.at[chunk((2 * r + 1) * part, j)],
            core_in.at[chunk(r * part, j)],
            c_s,
            c_r,
            turn,
            by_core,
        )

    def to_below(j):
        return remote(z_out.at[chunk(0, j)], z_in.at[chunk(0, j)], d_s, d_r, j, below)

    def to_above(j):
        return remote(z_out.at[chunk(part, j)], z_in.at[chunk(part, j)], u_s, u_r, j, above)

    def to_owner(j):
        return remote(dx_out.at[j - 1], dx_in.at[j - 1], x_s, x_r, j - 1, there(j))

    def every(n, action):
        j = 3 - n
        for turn, r in ((n * 2, 0), (n * 2 + 1, 2)):
            action(turn, r, j)

    greet([by_x, by_y, there(3), by_core] + others)

    def begin(n, carry):
        def go(turn, r, j):
            to_core(turn, r, j).start()
            load_own(turn, r, j).start()

        every(n, go)
        return carry

    lax.fori_loop(0, 4, begin, 0)

    def begin_mid(n, carry):
        to_core(8 + n, 1, 3 - n).start()
        load_own(8 + n, 1, 3 - n).start()
        return carry

    lax.fori_loop(0, 4, begin_mid, 0)
    inputs = [(pair_in[2 * n], keep[n]) for n in range(3)]
    inputs += [(pair_in[2 * n + 1], give[n]) for n in (0, 2)]
    inputs += [(wq_in, wq), (wkv_in, wkv), (dq_in, dq), (x_in, xs), (one_in, one)]
    inputs = [pltpu.make_async_copy(src, dst, i_sem.at[n]) for n, (src, dst) in enumerate(inputs)]
    for copy in inputs:
        copy.start()
    w1 = remote(pair_in[3], give[1], w1_s, w1_r, 0, by_y)
    w1.start()

    def both(turn, r, j):
        to_core(turn, r, j).wait_recv()
        load_own(turn, r, j).wait()
        at = chunk(r * part, j)
        return own[at, :].astype(f32) + core_in[at, :].astype(f32)

    def spread(n, carry):
        j = 3 - n
        z_out[chunk(0, j), :] = both(2 * n, 0, j).astype(low)

        @pl.when(has_below)
        def _():
            to_below(j).start()

        z_out[chunk(part, j), :] = both(2 * n + 1, 2, j).astype(low)

        @pl.when(has_above)
        def _():
            to_above(j).start()

        return carry

    lax.fori_loop(0, 4, spread, 0)

    for copy in inputs[:5]:
        copy.wait()
    halves = [keep[0].shape[2] // 2, keep[1].shape[2] // 2]
    w2 = {}
    for n in (0, 2, 1):
        if n == 1:
            w1.wait()

        def merge(p, carry, n=n):
            keep[n][p] = (keep[n][p].astype(f32) + give[n][p].astype(f32)).astype(low)
            return carry

        lax.fori_loop(0, planes, merge, 0)
        if n < 2:
            cols = pl.ds(pl.multiple_of((1 - x_at) * halves[n], 128), halves[n])
            w2[n] = remote(keep[n].at[:, :, cols], got[n], w2_s, w2_r, n, by_x)
        else:
            w2[n] = remote(keep[n].at[:, 1 - y_at], got[n], w2_s, w2_r, n, by_y)
        w2[n].start()
    for copy in inputs[5:]:
        copy.wait()
    acc[...] = jnp.zeros_like(acc)

    def arrive(n):
        j = 3 - n
        g_all[:, 2 * WQ :] = dq[chunk(0, j), :]
        g_all[:, : 2 * WQ] = both(8 + n, 1, j).astype(low)

        @pl.when(has_above)
        def _():
            to_below(j).wait_recv()
            g_all[:, : 2 * WQ] = (
                g_all[:, : 2 * WQ].astype(f32) + z_in[chunk(0, j), :].astype(f32)
            ).astype(low)

        @pl.when(has_below)
        def _():
            to_above(j).wait_recv()
            g_all[:, : 2 * WQ] = (
                g_all[:, : 2 * WQ].astype(f32) + z_in[chunk(part, j), :].astype(f32)
            ).astype(low)

    def back(j):
        grads = g_all[...]
        return nt(grads[:, 2 * WQ :], wq[...]) + nt(grads[:, : 2 * WQ], wkv[...])

    def outer(j):
        acc[...] += tn(xs[chunk(0, j), :], g_all[...])

    def send_back(n, carry):
        arrive(n)
        dx_out[2 - n] = back(3 - n).astype(low)
        to_owner(3 - n).start()
        outer(3 - n)
        return carry

    lax.fori_loop(0, 3, send_back, 0)

    for n in range(3):
        w2[n].wait_recv()

        def halve(p, carry, n=n):
            if n < 2:
                cols = pl.ds(pl.multiple_of(x_at * halves[n], 128), halves[n])
                mine = keep[n][p, :, cols]
            else:
                mine = keep[n][p, y_at]
            two[n][p] = (mine.astype(f32) + got[n][p].astype(f32)).astype(low)
            return carry

        lax.fori_loop(0, planes, halve, 0)

    def line_copy(n, way, t):
        return remote(
            line_out[n].at[way, t],
            line_in[n].at[way, t],
            w3_s,
            w3_r,
            (n * 2 + way) * rest + t,
            below if way else above,
        )

    def line_step(t):
        for n in range(3):
            for way in range(2):
                spot = (planes - 1 - plane) if way else plane
                gap = planes - 1 - t
                slab = (plane - gap) if way else (plane + gap)
                sends = jnp.logical_and(t >= spot, spot < planes - 1)

                @pl.when(jnp.logical_and(sends, spot == 0))
                def _():
                    line_out[n][way, t] = two[n][slab]
                    line_copy(n, way, t).start()

                @pl.when(jnp.logical_and(sends, spot > 0))
                def _():
                    line_copy(n, way, t - 1).wait_recv()
                    line_out[n][way, t] = (
                        two[n][slab].astype(f32) + line_in[n][way, t - 1].astype(f32)
                    ).astype(low)
                    line_copy(n, way, t).start()

    arrive(3)
    line_step(0)
    tok_out[...] = one[...] + back(0)
    outer(0)

    share = p_slab.shape[3]
    acc[:, 2 * WQ :] *= DH ** (-0.5)
    for p in range(planes):
        for y in range(2):
            for k in range(2):
                at = ((p * 2 + y) * 2 + k) * share
                p_slab[k, p, y] = acc[at : at + share, :].astype(low)
    pk = remote(p_slab.at[1 - core], p_core, pk_s, pk_r, 0, by_core)
    pk.start()
    if planes > 2:
        line_step(1)
    pk.wait_recv()

    def merge_core(p, carry):
        p_z[p] = (p_slab[core, p].astype(f32) + p_core[p].astype(f32)).astype(low)
        return carry

    lax.fori_loop(0, planes, merge_core, 0)
    pz = [
        remote(
            p_z.at[lax.rem(plane + g, planes)], p_zin.at[g - 1], pz_s, pz_r, g - 1, others[g - 1]
        )
        for g in range(1, planes)
    ]

    def next_step(t, carry):
        line_step(t)
        return carry

    lax.fori_loop(2, planes - 1, next_step, 0)
    for copy in pz:
        copy.start()
    w4 = []
    for n in range(3):
        fin[n][x_at] = two[n][plane]

        @pl.when(has_below)
        def _(n=n):
            line_copy(n, 0, rest - 1).wait_recv()
            fin[n][x_at] = (
                fin[n][x_at].astype(f32) + line_in[n][0, rest - 1].astype(f32)
            ).astype(low)

        @pl.when(has_above)
        def _(n=n):
            line_copy(n, 1, rest - 1).wait_recv()
            fin[n][x_at] = (
                fin[n][x_at].astype(f32) + line_in[n][1, rest - 1].astype(f32)
            ).astype(low)

        w4.append(remote(fin[n].at[x_at], fin[n].at[x_at], w4_s, w4_r, n, by_x))
        w4[n].start()

    for j in (3, 2, 1):
        to_owner(j).wait_recv()
        tok_out[...] += dx_in[j - 1].astype(f32)

    total = p_z[plane].astype(f32)
    for g in range(1, planes):
        pz[g - 1].wait_recv()
        total = total + p_zin[g - 1].astype(f32)
    p_fin[...] = total.astype(low)
    pf = [
        remote(p_fin.at[y_at ^ (j >> 1)], p_all.at[j], pf_s, pf_r, j - 1, there(j))
        for j in (1, 2, 3)
    ]
    for copy in pf:
        copy.start()
    p_all[0] = p_fin[y_at]

    for copy in pf:
        copy.wait()
    for a in range(4):
        grads = p_all[a ^ group].astype(f32)
        for n, dest in enumerate((k_out, v_out, q_out)):
            dest[:, a * WQ : (a + 1) * WQ] = grads[:, n * WQ : (n + 1) * WQ]
    for n, dest in ((0, up_out), (2, down_out)):
        w4[n].wait()
        width = dest.shape[1] // 2
        for side in range(2):
            dest[:, side * width : (side + 1) * width] = fin[n][side].astype(f32)
    w4[1].wait()
    width = side_out.shape[1] // 2
    for side in range(2):
        done = fin[1][side].astype(f32)
        side_out[:, side * width : (side + 1) * width] = done[:share]
        norm_out[:, side * width : (side + 1) * width] = done[share : share + 8]

    for copy in list(w2.values()) + pz + [pk]:
        copy.wait_send()

    def settle(n, carry):
        every(n, lambda turn, r, j: to_core(turn, r, j).wait_send())
        to_core(8 + n, 1, 3 - n).wait_send()

        @pl.when(has_below)
        def _():
            to_below(3 - n).wait_send()

        @pl.when(has_above)
        def _():
            to_above(3 - n).wait_send()

        return carry

    lax.fori_loop(0, 4, settle, 0)
    for j in (1, 2, 3):
        to_owner(j).wait_send()

    def settle_line(t, carry):
        for n in range(3):
            for way in range(2):
                spot = (planes - 1 - plane) if way else plane

                @pl.when(jnp.logical_and(t >= spot, spot < planes - 1))
                def _():
                    line_copy(n, way, t).wait_send()

        return carry

    lax.fori_loop(0, planes - 1, settle_line, 0)


def reduce_all(dkv, dq, stretch, wq, wkv, one, up, out, down, planes):
    low, f32 = jnp.bfloat16, jnp.float32
    piece = dq.shape[0] // 4
    width = stretch.shape[1]
    share = up[0].shape[1]
    rest = planes - 1
    dma, vm, sds = pltpu.SemaphoreType.DMA, pltpu.VMEM, jax.ShapeDtypeStruct
    cols = 2 * WQ + WIN
    tall = out[0].shape[1]
    wide = up[0].shape[2]
    kinds = [(share, wide // 2), (tall, width // 2), down[0].shape[2:]]
    pairs = [up[0].shape, out[0].shape, down[0].shape]
    return pl.pallas_call(
        functools.partial(reduce_kernel, planes),
        out_shape=[sds((piece, width), f32)]
        + [sds((share, width), f32)] * 3
        + [
            sds((share, wide), f32),
            sds((share, width), f32),
            sds((8, width), f32),
            sds((kinds[2][0], width), f32),
        ],
        in_specs=[ANY] * 12,
        out_specs=[VMEM] * 8,
        scratch_shapes=[
            vm((12 * piece, 2 * WQ), low),
            vm((12 * piece, 2 * WQ), low),
            vm((8 * piece, 2 * WQ), low),
            vm((8 * piece, 2 * WQ), low),
            vm((piece, cols), low),
            vm((3, piece, width), low),
            vm((3, piece, width), low),
            vm((width, cols), f32),
            vm(dq.shape, low),
            vm(stretch.shape, low),
            vm(wq.shape, low),
            vm(wkv.shape, low),
            vm(one.shape, f32),
            vm((2, planes, 2, share, cols), low),
            vm((planes, 2, share, cols), low),
            vm((planes, 2, share, cols), low),
            vm((rest, 2, share, cols), low),
            vm((2, share, cols), low),
            vm((4, share, cols), low),
        ]
        + [vm(p, low) for p in pairs] * 2
        + [vm((planes,) + k, low) for k in kinds] * 2
        + [vm((2,) + k, low) for k in kinds]
        + [vm((2, rest) + k, low) for k in kinds] * 2
        + [dma((12,)), dma((11,))]
        + [dma((12,))] * 2
        + [dma((4,))] * 4
        + [dma((3,))] * 2
        + [dma((1,))] * 2
        + [dma((rest,))] * 2
        + [dma((3,))] * 2
        + [dma((3,))] * 2
        + [dma((6 * rest,))] * 2
        + [dma((3,))] * 2
        + [dma((1,))] * 2,
        compiler_params=pltpu.CompilerParams(
            collective_id=1, has_side_effects=True, vmem_limit_bytes=60 << 20
        ),
        cost_estimate=pl.CostEstimate(
            flops=4 * 4 * piece * width * cols, bytes_accessed=40 << 20, transcendentals=0
        ),
        name="reduce_all",
    )(dkv, dq, stretch, wq, wkv, one, up[0], up[1], out[0], out[1], down[0], down[1])


def dense_kernel(
    planes,
    tok_ref,
    ctx_ref,
    cot_ref,
    g1_ref,
    b1_ref,
    g2_ref,
    b2_ref,
    wout_in,
    wup_in,
    wdown_in,
    *refs,
):
    out_ref, one_ref, do_out, up_keep, up_give, out_keep, out_give, down_keep, down_give = refs[:9]
    wup, wdown, acc, x1, s1, g_two, nl, hid, slope, gp, gm, ga = refs[9:21]
    dctx, up_loc, out_loc, down_loc, up_got, out_got, down_got, down_sum = refs[21:29]
    w_sem, mv_sem, do_s, do_r, up_s, up_r, out_s, out_r, down_s, down_r = refs[29:39]
    wout_ref = refs[39]
    plane, y_at, core, x_at = place()
    piece, width = tok_ref.shape
    share = up_loc.shape[2]
    slab = down_loc.shape[2]
    pairs = 2 * planes
    group = y_at * 2 + x_at
    f32 = jnp.float32
    fetch = [
        pltpu.make_async_copy(
            wout_in.at[pl.ds(pl.multiple_of((group ^ j) * WQ, WQ), WQ)],
            wout_ref.at[pl.ds(j * WIN + WIN - WQ, WQ)],
            w_sem.at[2 + j],
        )
        for j in range(4)
    ]
    for copy in fetch:
        copy.start()
    bring = [
        pltpu.make_async_copy(wup_in, wup, w_sem.at[0]),
        pltpu.make_async_copy(wdown_in, wdown, w_sem.at[1]),
    ]
    for copy in bring:
        copy.start()

    def there(j):
        return device_at(plane, y_at ^ (j >> 1), core, x_at ^ (j & 1))

    by_core = device_at(plane, y_at, 1 - core, x_at)
    height, tile = 32, 2 * WQ
    wide = wup.shape[1]

    def rows_of(n):
        return pl.ds(pl.multiple_of(n * height, height), height)

    def cols_of(n):
        return pl.ds(pl.multiple_of(n * tile, tile), tile)

    def mean(v):
        return jnp.mean(v, axis=1, keepdims=True)

    def fold(v):
        return v[:8] + v[8:16] + v[16:24] + v[24:]

    for j in range(4):
        wout_ref[j * WIN : j * WIN + WIN - WQ, :] = jnp.zeros((WIN - WQ, width), jnp.bfloat16)
    for copy in fetch:
        copy.wait()
    acc[...] = jnp.dot(ctx_ref[...], wout_ref[...], preferred_element_type=f32)
    g1, b1, g2, b2 = (r[...].reshape(1, width) for r in (g1_ref, b1_ref, g2_ref, b2_ref))

    def norm_one(n, carry):
        at = rows_of(n)
        value = tok_ref[at, :].astype(f32) + acc[at, :]
        center = value - mean(value)
        inverse = lax.rsqrt(mean(center * center) + eps_norm)
        hat = center * inverse
        x1[at, :] = hat
        s1[at, :] = jnp.broadcast_to(inverse, (height, 128))
        nl[at, :] = (hat * g1 + b1).astype(jnp.bfloat16)
        return carry

    lax.fori_loop(0, piece // height, norm_one, 0, unroll=4)
    bring[0].wait()

    def expand(n, carry):
        at = cols_of(n)
        pre = jnp.dot(nl[...], wup[:, at], preferred_element_type=f32)
        square = pre * pre
        inner = 0.7978845608028654 * pre * (1.0 + 0.044715 * square)
        bend = jnp.tanh(inner)
        half_up = 0.5 + 0.5 * bend
        hid[:, at] = (pre * half_up).astype(jnp.bfloat16)
        slope[:, at] = half_up + 0.5 * pre * (1.0 - bend * bend) * (
            0.7978845608028654 + 0.1070322243 * square
        )
        return carry

    lax.fori_loop(0, wide // tile, expand, 0, unroll=2)
    bring[1].wait()
    acc[...] = jnp.dot(hid[...], wdown[...], preferred_element_type=f32)
    nothing = jnp.zeros((8, width), f32)

    def norm_two(n, carry):
        gain_sum, shift_sum = carry
        at = rows_of(n)
        value = x1[at, :] * g1 + b1 + acc[at, :]
        center = value - mean(value)
        inverse = lax.rsqrt(mean(center * center) + eps_norm)
        hat = center * inverse
        out_ref[at, :] = (hat * g2 + b2).astype(jnp.bfloat16)
        cot = cot_ref[at, :].astype(f32)
        gain_sum, shift_sum = gain_sum + fold(cot * hat), shift_sum + fold(cot)
        up = cot * g2
        grad = inverse * (up - mean(up) - hat * mean(up * hat))
        g_two[at, :] = grad
        gm[at, :] = grad.astype(jnp.bfloat16)
        return gain_sum, shift_sum

    gain_two, shift_two = lax.fori_loop(0, piece // height, norm_two, (nothing, nothing), unroll=4)

    def shrink(n, carry):
        at = cols_of(n)
        back = nt(gm[...], wdown[at, :])
        gp[:, at] = (back * slope[:, at]).astype(jnp.bfloat16)
        return carry

    lax.fori_loop(0, wide // tile, shrink, 0, unroll=2)
    acc[...] = nt(gp[...], wup[...])

    def norm_three(n, carry):
        gain_sum, shift_sum = carry
        at = rows_of(n)
        grad_in, hat = g_two[at, :] + acc[at, :], x1[at, :]
        gain_sum, shift_sum = gain_sum + fold(grad_in * hat), shift_sum + fold(grad_in)
        up = grad_in * g1
        grad = s1[at, 0:1] * (up - mean(up) - hat * mean(up * hat))
        one_ref[at, :] = grad
        ga[at, :] = grad.astype(jnp.bfloat16)
        return gain_sum, shift_sum

    gain_one, shift_one = lax.fori_loop(
        0, piece // height, norm_three, (nothing, nothing), unroll=4
    )
    side = jnp.concatenate(
        [jnp.sum(v, axis=0, keepdims=True) for v in (gain_one, shift_one, gain_two, shift_two)]
        + [jnp.zeros((12, width), f32)],
        axis=0,
    ).astype(jnp.bfloat16)

    low = jnp.bfloat16
    greet([there(1), there(2), there(3), by_core])
    trades = []
    for j in (3, 1, 2, 0):
        part = nt(ga[...], wout_ref[pl.ds(j * WIN, WIN), :]).astype(low)
        if j:
            dctx[j - 1] = part
            trades.append(
                remote(
                    dctx.at[j - 1], do_out.at[pl.ds(j * piece, piece)], do_s, do_r, j - 1, there(j)
                )
            )
            trades[-1].start()
        else:
            do_out[pl.ds(0, piece), :] = part

    tile = 2 * WQ
    per = tile // (2 * slab)
    tiles = wide // tile

    def down_copy(t):
        span = pl.ds(t * per, per)
        return remote(down_loc.at[1 - core, span], down_got.at[span], down_s, down_r, t, by_core)

    def up_copy(t):
        span = cols_of(t)
        return remote(
            up_loc.at[1 - core, :, :, span], up_got.at[:, :, span], up_s, up_r, t, by_core
        )

    def make_down(t, carry):
        cell = tn(hid[:, cols_of(t)], gm[...])
        for n in range(per):
            for k in range(2):
                at = (n * 2 + k) * slab
                down_loc[k, t * per + n] = cell[at : at + slab].astype(low)
        down_copy(t).start()
        return carry

    lax.fori_loop(0, tiles, make_down, 0)

    def make_up(t, carry):
        cell = tn(nl[...], gp[:, cols_of(t)])
        for q in range(pairs):
            for k in range(2):
                at = (q * 2 + k) * share
                up_loc[k, q, :, cols_of(t)] = cell[at : at + share].astype(low)
        up_copy(t).start()
        return carry

    lax.fori_loop(0, tiles, make_up, 0)
    per_group = pairs // 4
    for j in range(4):
        cell = tn(ctx_ref[:, j * WIN : (j + 1) * WIN], ga[...])
        for n in range(per_group):
            for k in range(2):
                at = WIN - WQ + (n * 2 + k) * share
                out_loc[k, (group ^ j) * per_group + n, :share, :] = cell[at : at + share].astype(low)
    for q in range(pairs):
        for k in range(2):
            out_loc[k, q, share:, :] = side
    outs = remote(out_loc.at[1 - core], out_got, out_s, out_r, 0, by_core)
    outs.start()

    moved = []

    def move(source, dest):
        moved.append(pltpu.make_async_copy(source, dest, mv_sem.at[len(moved)]))
        moved[-1].start()

    half = width // 2

    def sum_down(t, carry):
        down_copy(t).wait_recv()
        for n in range(per):
            q = t * per + n
            total = (
                down_loc[core, q].astype(jnp.float32) + down_got[q].astype(jnp.float32)
            ).astype(low)
            down_sum[0, q] = total[:, :half]
            down_sum[1, q] = total[:, half:]
        return carry

    lax.fori_loop(0, tiles, sum_down, 0)
    move(down_sum.at[x_at], down_keep)
    move(down_sum.at[1 - x_at], down_give)

    def sum_up(q, carry):
        up_got[q] = (up_loc[core, q].astype(jnp.float32) + up_got[q].astype(jnp.float32)).astype(low)
        return carry

    for t in range(tiles):
        up_copy(t).wait_recv()
    lax.fori_loop(0, pairs, sum_up, 0)
    outs.wait_recv()
    for p in range(planes):
        for y in range(2):
            q = p * 2 + y
            out_got[q] = (
                out_loc[core, q].astype(jnp.float32) + out_got[q].astype(jnp.float32)
            ).astype(low)
        for got, keep, give in ((up_got, up_keep, up_give), (out_got, out_keep, out_give)):
            move(got.at[p * 2 + y_at], keep.at[p])
            move(got.at[p * 2 + 1 - y_at], give.at[p])
    for copy in trades:
        copy.wait()
    for t in range(tiles):
        down_copy(t).wait_send()
        up_copy(t).wait_send()
    outs.wait_send()
    for copy in moved:
        copy.wait()


def dense_layers(tokens, ctx, cotangent, norms, wout, w_up, w_down, planes):
    low = jnp.bfloat16
    piece, width = tokens.shape
    pairs = 2 * planes
    wide = w_up.shape[1]
    share, slab, tall = width // (2 * pairs), wide // (2 * pairs), 16
    sds, vm, dma = jax.ShapeDtypeStruct, pltpu.VMEM, pltpu.SemaphoreType.DMA
    up, out = (planes, share, wide), (planes, share + tall, width)
    down = (pairs, slab, width // 2)
    tiles = wide // (2 * WQ)
    f32 = jnp.float32
    return pl.pallas_call(
        functools.partial(dense_kernel, planes),
        out_shape=[sds((piece, width), low), sds((piece, width), f32), sds((4 * piece, WIN), low)]
        + [sds(up, low)] * 2
        + [sds(out, low)] * 2
        + [sds(down, low)] * 2,
        in_specs=[VMEM] * 7 + [ANY] * 3,
        out_specs=[VMEM] * 3 + [ANY] * 6,
        scratch_shapes=[
            vm(w_up.shape, low),
            vm(w_down.shape, low),
            vm((piece, width), f32),
            vm((piece, width), f32),
            vm((piece, 128), f32),
            vm((piece, width), f32),
            vm((piece, width), low),
            vm((piece, wide), low),
            vm((piece, wide), f32),
            vm((piece, wide), low),
            vm((piece, width), low),
            vm((piece, width), low),
            vm((3, piece, WIN), low),
            vm((2, pairs, share, wide), low),
            vm((2, pairs, share + tall, width), low),
            vm((2, pairs, slab, width), low),
            vm((pairs, share, wide), low),
            vm((pairs, share + tall, width), low),
            vm((pairs, slab, width), low),
            vm((2, pairs, slab, width // 2), low),
            dma((6,)),
            dma((2 + 4 * planes,)),
        ]
        + [dma((3,))] * 2
        + [dma((tiles,))] * 2
        + [dma((1,))] * 2
        + [dma((tiles,))] * 2
        + [vm((4 * WIN, width), low)],
        compiler_params=pltpu.CompilerParams(
            collective_id=2, has_side_effects=True, vmem_limit_bytes=63 << 20
        ),
        cost_estimate=pl.CostEstimate(
            flops=2 * piece * width * (6 * wide + 3072), bytes_accessed=30 << 20, transcendentals=0
        ),
        name="dense_layers",
    )(tokens, ctx, cotangent, *norms, wout, w_up, w_down)


def finish_kernel(share, count, *refs):
    sources, rows_ref, dests = refs[:count], refs[count], refs[count + 1 : 2 * count + 1]
    parts = refs[2 * count + 1 : 2 * count + 5]
    for source, dest in zip(sources, dests):
        dest[...] = source[...]
    seq_at = lax.axis_index("seq")
    rows = rows_ref[...]
    width = rows.shape[1]
    spot = lax.broadcasted_iota(jnp.int32, (width, 128), 0) - seq_at * share
    chosen = (spot == lax.broadcasted_iota(jnp.int32, (width, 128), 1)).astype(jnp.float32)
    picked = jnp.dot(
        rows, chosen, preferred_element_type=jnp.float32, precision=lax.Precision.HIGHEST
    )
    for n in range(4):
        parts[n][...] = picked[n, :share]


def finish(arrays, norm_rows, share):
    sds, count = jax.ShapeDtypeStruct, len(arrays)
    return pl.pallas_call(
        functools.partial(finish_kernel, share, count),
        out_shape=[sds(v.shape, v.dtype) for v in arrays] + [sds((share,), jnp.float32)] * 4,
        in_specs=[VMEM] * (count + 1),
        out_specs=[VMEM] * (count + 4),
        compiler_params=pltpu.CompilerParams(vmem_limit_bytes=62 << 20),
        name="finish",
    )(*arrays, norm_rows)


def body(
    tokens,
    w_query,
    w_key,
    w_value,
    w_out,
    gain_attn,
    shift_attn,
    w_up,
    w_down,
    gain_mlp,
    shift_mlp,
    cotangent,
    lengths,
    seq_order,
    rand_blocks,
):
    piece, width = tokens.shape
    seqs, heads = lax.axis_size("seq"), lax.axis_size("head")
    planes = seqs // 4
    assert heads == 2 and 8 * piece == MAXB * BLK and width == 4 * WQ
    seq_at, x_at = lax.axis_index("seq"), lax.axis_index("head")
    plane, y_at, core = seq_at // 4, (seq_at // 2) % 2, seq_at % 2
    group = y_at * 2 + x_at

    flat = rand_blocks.reshape(1, -1)
    rand_row = jnp.pad(flat, ((0, 0), (0, 128 - flat.shape[1])))
    keys_values, queries, stretch, context_tok, level, idx, live, wq_own, wkv_own, ctx_own = (
        forward_attention(
            tokens, w_query, w_key, w_value, lengths, seq_order, rand_row, planes
        )
    )
    share = width // seqs
    norms = [gain_attn, shift_attn, gain_mlp, shift_mlp]
    output, grad_one, grad_ctx, up_keep, up_give, out_keep, out_give, down_keep, down_give = (
        dense_layers(tokens, context_tok, cotangent, norms, w_out, w_up, w_down, planes)
    )
    up_pair = (up_keep, xor_swap(up_give, 4))
    out_pair = (out_keep, out_give)
    two_y = (planes, 2) + down_keep.shape[1:]
    down_pair = (down_keep.reshape(two_y), xor_swap(down_give, 1).reshape(two_y))

    grad_q, grad_kv = attend_back(
        idx,
        live,
        queries,
        grad_ctx,
        ctx_own.reshape(-1, WIN),
        level,
        keys_values.reshape(-1, 2 * WQ),
    )
    grad_tokens, grad_wq, grad_wk, grad_wv, up_total, out_total, norm_rows, down_total = reduce_all(
        grad_kv,
        grad_q,
        stretch,
        wq_own,
        wkv_own,
        grad_one,
        up_pair,
        out_pair,
        down_pair,
        planes,
    )

    finals = finish(
        (output, grad_tokens, grad_wq, grad_wk, grad_wv, out_total, up_total, down_total),
        norm_rows,
        share,
    )

    output, grad_tokens, grad_wq, grad_wk, grad_wv, grad_out, grad_up, grad_down = finals[:8]
    gain_one, shift_one, gain_two, shift_two = finals[8:]
    return (
        output,
        grad_tokens,
        grad_wq,
        grad_wk,
        grad_wv,
        grad_out,
        gain_one,
        shift_one,
        grad_up,
        grad_down,
        gain_two,
        shift_two,
    )


def solution(mesh):
    rows = P(("seq", "head"), None)
    seq_rows, seq_only = P("seq", None), P("seq")
    return jax.shard_map(
        body,
        mesh=mesh,
        in_specs=(rows,) + (P(),) * 10 + (rows, P(), P(), seq_rows),
        out_specs=(
            rows,
            rows,
            seq_rows,
            seq_rows,
            seq_rows,
            seq_rows,
            seq_only,
            seq_only,
            seq_rows,
            seq_rows,
            seq_only,
            seq_only,
        ),
        check_vma=False,
    )
```

```python
import functools

import jax
import jax.numpy as jnp
from jax import lax
from jax.experimental import pallas as pl
from jax.experimental.pallas import tpu as pltpu
from jax.sharding import PartitionSpec as P

DH = 64
BLK = 64
MAXB = 64
SLOTS = 8
HG = 3
WQ = HG * DH
WIN = 256
AXES = ("seq", "head")
NEG = -1e30

eps_norm = 1e-06


def xor_swap(value, bits):
    count = lax.axis_size("seq") * lax.axis_size("head")
    return lax.ppermute(value, AXES, [(d, d ^ bits) for d in range(count)])


def lane_groups(rows, offset):
    lane = lax.broadcasted_iota(jnp.int32, (rows, WIN), 1) - offset
    return [jnp.logical_and(lane >= h * DH, lane < (h + 1) * DH) for h in range(HG)]


def spread_heads(block, offset):
    zero = jnp.zeros_like(block)
    return jnp.concatenate([jnp.where(m, block, zero) for m in lane_groups(BLK, offset)], axis=0)


def fold_heads(stacked, offset):
    masks = lane_groups(BLK, offset)
    total = jnp.where(masks[0], stacked[:BLK], 0.0)
    for h in range(1, HG):
        total = total + jnp.where(masks[h], stacked[h * BLK : (h + 1) * BLK], 0.0)
    return total


def nt(a, b):
    return lax.dot_general(a, b, (((1,), (1,)), ((), ())), preferred_element_type=jnp.float32)


def tn(a, b):
    return lax.dot_general(a, b, (((0,), (0,)), ((), ())), preferred_element_type=jnp.float32)


def backward_kernel(idx_ref, live_ref, q_ref, do_ref, o_ref, lse_ref, *refs):
    kv_ref, dq_ref, dkv_ref, kv, acc, sems = refs

    def clear(n, carry):
        acc[pl.ds(pl.multiple_of(n * 256, 256), 256), :] = jnp.zeros((256, 2 * WQ), jnp.float32)
        return carry

    copy = pltpu.make_async_copy(kv_ref, kv, sems.at[0])
    copy.start()
    lax.fori_loop(0, acc.shape[0] // 256, clear, 0)
    copy.wait()

    def step(i, carry):
        q_rows = pl.multiple_of(i * BLK, BLK)
        qexp = spread_heads(q_ref[pl.ds(q_rows, BLK), :], 0)
        doexp = spread_heads(do_ref[pl.ds(q_rows, BLK), :], 64)
        rows = [
            pl.multiple_of(idx_ref[i * SLOTS + s] * BLK, BLK) for s in range(SLOTS)
        ]
        keys = jnp.concatenate([kv[pl.ds(r, BLK), 0:WIN] for r in rows], axis=0)
        values = jnp.concatenate([kv[pl.ds(r, BLK), 128 : 128 + WIN] for r in rows], axis=0)
        product = do_ref[pl.ds(q_rows, BLK), :].astype(jnp.float32) * o_ref[
            pl.ds(q_rows, BLK), :
        ].astype(jnp.float32)
        high = product.astype(jnp.bfloat16)
        ones = jnp.ones((8, WIN), jnp.bfloat16)
        inner = nt(ones, spread_heads(high, 64)) + nt(
            ones, spread_heads((product - high.astype(jnp.float32)).astype(jnp.bfloat16), 64)
        )
        inner = inner[0:1]
        level = lse_ref[pl.ds(i, 1), :]
        raw = nt(keys, qexp)
        grad_probs = nt(values, doexp)
        probs, grad_scores = [], []
        for s in range(SLOTS):
            at = slice(s * BLK, (s + 1) * BLK)
            off = level + jnp.where(live_ref[i * SLOTS + s] > 0, 0.0, -NEG)
            p = jnp.exp(raw[at] - off)
            probs.append(p.astype(jnp.bfloat16))
            grad_scores.append((p * (grad_probs[at] - inner)).astype(jnp.bfloat16))
        probs = jnp.concatenate(probs, axis=0)
        grad_scores = jnp.concatenate(grad_scores, axis=0)
        dk = jnp.dot(grad_scores, qexp, preferred_element_type=jnp.float32)
        dv = jnp.dot(probs, doexp, preferred_element_type=jnp.float32)
        dq = tn(grad_scores, keys)
        dq_ref[pl.ds(q_rows, BLK), :] = fold_heads(dq, 0).astype(jnp.bfloat16)
        for s in range(SLOTS):
            k_s, v_s = dk[s * BLK : (s + 1) * BLK], dv[s * BLK : (s + 1) * BLK]
            at = pl.ds(rows[s], BLK)
            acc[at, 0:128] += k_s[:, :128]
            acc[at, 128:256] += k_s[:, 128:] + v_s[:, :128]
            acc[at, 256:384] += v_s[:, 128:]
        return carry

    lax.fori_loop(0, q_ref.shape[0] // BLK, step, 0, unroll=8)

    def emit(n, carry):
        at = pl.ds(pl.multiple_of(n * 256, 256), 256)
        dkv_ref[at, :] = acc[at, :].astype(jnp.bfloat16)
        return carry

    lax.fori_loop(0, acc.shape[0] // 256, emit, 0)


VMEM = pl.BlockSpec(memory_space=pltpu.VMEM)
SMEM = pl.BlockSpec(memory_space=pltpu.SMEM)
ANY = pl.BlockSpec(memory_space=pl.ANY)


def device_at(plane, y_at, core, x_at):
    return (plane * 4 + y_at * 2 + core, x_at)


def place():
    seq_at, x_at = lax.axis_index("seq"), lax.axis_index("head")
    return seq_at // 4, (seq_at // 2) % 2, seq_at % 2, x_at


def remote(src, dst, sems, recvs, at, device):
    return pltpu.make_async_remote_copy(
        src_ref=src,
        dst_ref=dst,
        send_sem=sems.at[at],
        recv_sem=recvs.at[at],
        device_id=device,
        device_id_type=pl.DeviceIdType.MESH,
    )


def greet(partners):
    barrier = pltpu.get_barrier_semaphore()
    for device in partners:
        pl.semaphore_signal(
            barrier, inc=1, device_id=device, device_id_type=pl.DeviceIdType.MESH
        )
    pl.semaphore_wait(barrier, len(partners))


CHUNK_ORDER = (0, 1, 2, 4, 3, 5, 6, 7)


def slot_tables(plane, y_at, core, x_at, at, lengths, order, rand_own, rand_got, idx_ref, live_ref):
    per = at["piece_blocks"]

    def one(i, carry):
        far, near = i // per, i % per
        y_of, x_of = y_at ^ (far >> 1), x_at ^ (far & 1)
        block = plane * MAXB + y_of * (4 * per) + core * (2 * per) + x_of * per + near
        begin, first, span = jnp.int32(0), jnp.int32(0), jnp.int32(1)
        for m in range(at["seqs"]):
            size = lengths[order[m]]
            inside = begin <= block
            first = jnp.where(inside, begin, first)
            span = jnp.where(inside, size, span)
            begin = begin + size
        row = x_of * per + near
        draws = []
        for n in range(SLOTS - 5):
            draw = jnp.where(far >= 2, rand_got[row, n], rand_own[row, n])
            for power in range(16, -1, -1):
                multiple = span * (1 << power)
                draw = jnp.where(draw >= multiple, draw - multiple, draw)
            draws.append(first + draw)
        candidates = [block - 1, block, block + 1, first, first + span - 1] + draws
        kept = []
        for s in range(SLOTS):
            alive = jnp.int32(1)
            if s == 0:
                alive = (block > first).astype(jnp.int32)
            if s == 2:
                alive = (block < first + span - 1).astype(jnp.int32)
            for e in range(s):
                same = (candidates[e] == candidates[s]).astype(jnp.int32)
                alive = alive * (1 - kept[e] * same)
            kept.append(alive)
            key = jnp.where(alive > 0, candidates[s], block)
            rel = key // MAXB - plane + 1
            inner = key % MAXB
            y_key, rest = inner // (4 * per), inner % (4 * per)
            core_key, rest = rest // (2 * per), rest % (2 * per)
            x_key, near_key = rest // per, rest % per
            spot = (rel * 2 + (core_key ^ core)) * 4 + ((y_key ^ y_at) * 2 + (x_key ^ x_at))
            idx_ref[i * SLOTS + s] = jnp.clip(spot * per + near_key, 0, 24 * per - 1)
            live_ref[i * SLOTS + s] = alive
        return carry

    lax.fori_loop(at["begin"], at["end"], one, 0)


def attend_block(i, idx_ref, live_ref, q_ref, kv, lse_ref):
    qexp = spread_heads(q_ref[pl.ds(pl.multiple_of(i * BLK, BLK), BLK), :], 0)
    at = [idx_ref[i * SLOTS + s] for s in range(SLOTS)]
    off = [jnp.where(live_ref[i * SLOTS + s] > 0, 0.0, -NEG) for s in range(SLOTS)]
    keys = jnp.concatenate([kv[r, :, 0:WIN] for r in at], axis=0)
    values = jnp.concatenate([kv[r, :, 128 : 128 + WIN] for r in at], axis=0)
    raw = nt(keys, qexp)
    parts = [raw[s * BLK : (s + 1) * BLK] for s in range(SLOTS)]
    top = jnp.max(parts[1], axis=0, keepdims=True)
    for s in range(SLOTS):
        top = jnp.maximum(top, jnp.max(parts[s], axis=0, keepdims=True) - off[s])
    e = [jnp.exp(parts[s] - (top + off[s])) for s in range(SLOTS)]
    total = jnp.sum(e[0], axis=0, keepdims=True)
    for s in range(1, SLOTS):
        total = total + jnp.sum(e[s], axis=0, keepdims=True)
    lse_ref[pl.ds(i, 1), :] = top + jnp.log(total)
    scale = 1.0 / total
    probs = jnp.concatenate([(v * scale).astype(jnp.bfloat16) for v in e], axis=0)
    return fold_heads(tn(probs, values), 64).astype(jnp.bfloat16)


def forward_kernel(planes, tok_ref, wq_in, wk_in, wv_in, len_ref, ord_ref, rand_vm, rand_sm, *refs):
    kv_out, q_ref, x_out, ctx_out, lse_ref, idx_ref, live_ref, wq_out, wkv_out, ctx_keep = refs[:10]
    xs, kv, ctx, rand_got, rand_two, w_full, wq_ref, wkv_ref = refs[10:18]
    x_send, x_recv, k_send, k_recv, up_send, up_recv, dn_send, dn_recv = refs[18:26]
    f_send, f_recv, g_send, g_recv, s_sem, o_send, o_recv, r_send, r_recv, l_sem = refs[26:36]
    weights = [
        pltpu.make_async_copy(w, w_full.at[n], l_sem.at[2 + n])
        for n, w in enumerate((wk_in, wv_in, wq_in))
    ]
    for copy in weights:
        copy.start()
    plane, y_at, core, x_at = place()
    piece = tok_ref.shape[0]
    rows = piece // 2
    part = 4 * piece
    by_x = device_at(plane, y_at, core, 1 - x_at)
    by_y = device_at(plane, 1 - y_at, core, x_at)
    by_xy = device_at(plane, 1 - y_at, core, 1 - x_at)
    by_core = device_at(plane, y_at, 1 - core, x_at)
    above = device_at(plane + 1, y_at, core, x_at)
    below = device_at(plane - 1, y_at, core, x_at)
    has_above, has_below = plane < planes - 1, plane > 0
    ring = [device_at(lax.rem(plane + g, planes), y_at, core, x_at) for g in (1, planes - 1)]
    greet([by_x, by_y, by_xy, by_core] + ring)

    def x_rows(c):
        return xs.at[pl.ds((c - 2) * rows, rows)]

    def tok_rows(c):
        return tok_ref.at[pl.ds(c * rows, rows)]

    hops = {
        2: remote(tok_rows(0), x_rows(2), x_send, x_recv, 0, by_x),
        4: remote(tok_rows(0), x_rows(4), x_send, x_recv, 2, by_y),
        3: remote(tok_rows(1), x_rows(3), x_send, x_recv, 1, by_x),
        5: remote(tok_rows(1), x_rows(5), x_send, x_recv, 3, by_y),
        6: remote(x_rows(2), x_rows(6), x_send, x_recv, 4, by_y),
        7: remote(x_rows(5), x_rows(7), x_send, x_recv, 5, by_x),
    }
    rand_trade = remote(rand_vm, rand_got, r_send, r_recv, 0, by_y)
    rand_trade.start()
    for c in (2, 4, 3, 5):
        hops[c].start()

    wq_ref[:, WQ:] = jnp.zeros((wq_ref.shape[0], WIN - WQ), jnp.bfloat16)
    for copy in weights:
        copy.wait()
    for g in range(4):

        @pl.when(y_at * 2 + x_at == g)
        def _(g=g):
            cols = slice(g * WQ, (g + 1) * WQ)
            wkv_ref[:, :WQ] = w_full[0, :, cols]
            wkv_ref[:, WQ:] = w_full[1, :, cols]
            wq_ref[:, :WQ] = w_full[2, :, cols] * jnp.bfloat16(DH ** (-0.5))

    hand_on = [
        pltpu.make_async_copy(wq_ref, wq_out, l_sem.at[5]),
        pltpu.make_async_copy(wkv_ref, wkv_out, l_sem.at[6]),
    ]
    for copy in hand_on:
        copy.start()

    def kv_rows(part_at, c):
        return kv.at[pl.ds((part_at * part + c * rows) // BLK, rows // BLK)]

    to_core, to_above, to_below, pass_up, pass_down = {}, {}, {}, {}, {}
    for c in range(8):
        mine = kv_rows(2, c)
        to_core[c] = remote(mine, kv_rows(3, c), k_send, k_recv, c, by_core)
        to_above[c] = remote(mine, kv_rows(0, c), up_send, up_recv, c, above)
        to_below[c] = remote(mine, kv_rows(4, c), dn_send, dn_recv, c, below)
        pass_up[c] = remote(kv_rows(0, c), kv_rows(1, c), f_send, f_recv, c, by_core)
        pass_down[c] = remote(kv_rows(4, c), kv_rows(5, c), g_send, g_recv, c, by_core)
    keeps = {
        c: pltpu.make_async_copy(
            tok_rows(c) if c < 2 else x_rows(c), x_out.at[pl.ds(c * rows, rows)], s_sem.at[c]
        )
        for c in range(8)
    }

    def relay(c):
        @pl.when(has_below)
        def _():
            to_above[c].wait_recv()
            pass_up[c].start()

        @pl.when(has_above)
        def _():
            to_below[c].wait_recv()
            pass_down[c].start()

    def tables(begin, end):
        slot_tables(
            plane,
            y_at,
            core,
            x_at,
            dict(piece_blocks=piece // BLK, seqs=len_ref.shape[0], begin=begin, end=end),
            len_ref,
            ord_ref,
            rand_sm,
            rand_two,
            idx_ref,
            live_ref,
        )

    query_blocks = part // BLK
    for n, c in enumerate(CHUNK_ORDER):
        if n == 2:
            rand_trade.wait()
            to_scalar = pltpu.make_async_copy(rand_got, rand_two, l_sem.at[0])
            to_scalar.start()
            to_scalar.wait()
            tables(0, query_blocks // 3)
        if n == 4:
            tables(query_blocks // 3, 2 * query_blocks // 3)
        if n == 6:
            tables(2 * query_blocks // 3, query_blocks)
        if c >= 2:
            hops[c].wait_recv()
        if c == 2:
            hops[6].start()
        if c == 5:
            hops[7].start()
        keeps[c].start()
        block = tok_ref[pl.ds(c * rows, rows), :] if c < 2 else xs[pl.ds((c - 2) * rows, rows), :]
        made = jnp.dot(block, wkv_ref[...], preferred_element_type=jnp.float32).astype(jnp.bfloat16)
        kv[pl.ds((2 * part + c * rows) // BLK, rows // BLK)] = made.reshape(rows // BLK, BLK, -1)

        @pl.when(has_above)
        def _(c=c):
            to_above[c].start()

        @pl.when(has_below)
        def _(c=c):
            to_below[c].start()

        to_core[c].start()
        q_ref[pl.ds(c * rows, rows), :] = jnp.dot(
            block, wq_ref[...], preferred_element_type=jnp.float32
        ).astype(jnp.bfloat16)
        if n >= 3:
            relay(CHUNK_ORDER[n - 3])
    for c in CHUNK_ORDER[5:]:
        relay(c)
    for c in range(8):
        to_core[c].wait_recv()

        @pl.when(has_above)
        def _(c=c):
            pass_down[c].wait_recv()

        @pl.when(has_below)
        def _(c=c):
            pass_up[c].wait_recv()

    saved = pltpu.make_async_copy(kv, kv_out, l_sem.at[1])
    saved.start()
    per = piece // BLK

    def part_of(turn):
        middle = turn - 2
        j = jnp.where(turn < 2, 3, jnp.where(turn < 6, 1 + lax.rem(turn, 2), 0))
        half = jnp.where(turn < 2, turn, jnp.where(turn < 6, middle // 2, turn - 6))
        return j, half

    def trade(turn):
        j, half = part_of(turn)
        span = pl.ds(pl.multiple_of(half * rows, rows), rows)
        return remote(
            ctx.at[j, span],
            ctx_out.at[span, pl.ds(pl.multiple_of(j * WIN, WIN), WIN)],
            o_send,
            o_recv,
            turn,
            device_at(plane, y_at ^ (j >> 1), core, x_at ^ (j & 1)),
        )

    def attend_part(turn, carry):
        j, half = part_of(turn)

        def step(n, carry):
            at = pl.ds(pl.multiple_of(n * BLK, BLK), BLK)
            ctx[j, at, :] = attend_block(j * per + n, idx_ref, live_ref, q_ref, kv, lse_ref)
            return carry

        first = half * (per // 2)
        for n in range(per // 2):
            step(first + n, 0)

        @pl.when(turn < 6)
        def _():
            trade(turn).start()

        return carry

    lax.fori_loop(0, 8, attend_part, 0)
    ctx_out[:, 0:WIN] = ctx[0]
    hand_on.append(pltpu.make_async_copy(ctx, ctx_keep, l_sem.at[7]))
    hand_on[-1].start()
    for c in (2, 4, 3, 5, 6, 7):
        hops[c].wait_send()
    for c in range(8):
        to_core[c].wait_send()
        keeps[c].wait()

        @pl.when(has_above)
        def _(c=c):
            to_above[c].wait_send()
            pass_down[c].wait_send()

        @pl.when(has_below)
        def _(c=c):
            to_below[c].wait_send()
            pass_up[c].wait_send()

    saved.wait()
    for copy in hand_on:
        copy.wait()

    def settle(turn, carry):
        trade(turn).wait()
        return carry

    lax.fori_loop(0, 6, settle, 0)


def forward_attention(tokens, w_query, w_key, w_value, lengths, seq_order, rand_row, planes):
    piece, width = tokens.shape
    dma, low = pltpu.SemaphoreType.DMA, jnp.bfloat16
    sds = jax.ShapeDtypeStruct
    blocks = 4 * piece // BLK
    return pl.pallas_call(
        functools.partial(forward_kernel, planes),
        out_shape=[
            sds((24 * piece // BLK, BLK, 2 * WQ), low),
            sds((4 * piece, WIN), low),
            sds((4 * piece, width), low),
            sds((piece, 4 * WIN), low),
            sds((blocks, WQ), jnp.float32),
            sds((blocks * SLOTS,), jnp.int32),
            sds((blocks * SLOTS,), jnp.int32),
            sds((width, WIN), low),
            sds((width, 2 * WQ), low),
            sds((4, piece, WIN), low),
        ],
        in_specs=[VMEM] + [ANY] * 3 + [SMEM] * 2 + [VMEM, SMEM],
        out_specs=[ANY, VMEM, ANY, VMEM, VMEM, SMEM, SMEM, ANY, ANY, ANY],
        scratch_shapes=[
            pltpu.VMEM((3 * piece, width), low),
            pltpu.VMEM((24 * piece // BLK, BLK, 2 * WQ), low),
            pltpu.VMEM((4, piece, WIN), low),
            pltpu.VMEM(rand_row.shape, jnp.int32),
            pltpu.SMEM(rand_row.shape, jnp.int32),
            pltpu.VMEM((3, width, width), low),
            pltpu.VMEM((width, WIN), low),
            pltpu.VMEM((width, 2 * WQ), low),
            dma((6,)),
            dma((6,)),
        ]
        + [dma((8,))] * 11
        + [dma((6,))] * 2
        + [dma((1,))] * 2
        + [dma((8,))],
        compiler_params=pltpu.CompilerParams(
            collective_id=0, has_side_effects=True, vmem_limit_bytes=62 << 20
        ),
        cost_estimate=pl.CostEstimate(
            flops=2 * 4 * piece * width * 640, bytes_accessed=40 << 20, transcendentals=0
        ),
        name="forward_attention",
    )(tokens, w_query, w_key, w_value, lengths, seq_order, rand_row, rand_row)


def attend_back(idx, live, queries, grads, context, level, keys_values):
    rows, width = keys_values.shape[0] // 6, keys_values.shape[1]
    count = queries.shape[0]
    kv_shape = jax.ShapeDtypeStruct((6 * rows, width), jnp.bfloat16)
    return pl.pallas_call(
        backward_kernel,
        out_shape=[jax.ShapeDtypeStruct((count, WIN), jnp.bfloat16)] + [kv_shape],
        in_specs=[SMEM, SMEM, VMEM, VMEM, VMEM, VMEM, ANY],
        out_specs=[VMEM] * 2,
        scratch_shapes=[
            pltpu.VMEM((6 * rows, width), jnp.bfloat16),
            pltpu.VMEM((6 * rows, width), jnp.float32),
            pltpu.SemaphoreType.DMA((1,)),
        ],
        compiler_params=pltpu.CompilerParams(vmem_limit_bytes=56 << 20),
        cost_estimate=pl.CostEstimate(
            flops=2 * 10 * count * 3 * 256 * 512, bytes_accessed=24 * rows * width, transcendentals=count * 3 * 512
        ),
        name="attend_back",
    )(idx, live, queries, grads, context, level, keys_values)


def reduce_kernel(planes, *refs):
    dkv_in, dq_in, x_in, wq_in, wkv_in, one_in = refs[:6]
    pair_in = refs[6:12]
    tok_out, q_out, k_out, v_out, up_out, side_out, norm_out, down_out = refs[12:20]
    own, core_in, z_out, z_in, g_all, dx_out, dx_in, acc = refs[20:28]
    dq, xs, wq, wkv, one = refs[28:33]
    p_slab, p_core, p_z, p_zin, p_fin, p_all = refs[33:39]
    keep, give = refs[39:42], refs[42:45]
    got, two, fin = refs[45:48], refs[48:51], refs[51:54]
    line_out, line_in = refs[54:57], refs[57:60]
    l_sem, i_sem, c_s, c_r, u_s, u_r, d_s, d_r, x_s, x_r = refs[60:70]
    pk_s, pk_r, pz_s, pz_r, pf_s, pf_r = refs[70:76]
    w2_s, w2_r, w3_s, w3_r, w4_s, w4_r, w1_s, w1_r = refs[76:84]
    plane, y_at, core, x_at = place()
    piece = tok_out.shape[0]
    part = 4 * piece
    rest = planes - 1
    group = y_at * 2 + x_at
    low, f32 = jnp.bfloat16, jnp.float32

    def there(j):
        return device_at(plane, y_at ^ (j >> 1), core, x_at ^ (j & 1))

    by_x, by_y = there(1), there(2)
    by_core = device_at(plane, y_at, 1 - core, x_at)
    others = [device_at(lax.rem(plane + g, planes), y_at, core, x_at) for g in range(1, planes)]
    has_above, has_below = plane < planes - 1, plane > 0
    above = device_at(plane + 1, y_at, core, x_at)
    below = device_at(plane - 1, y_at, core, x_at)

    def chunk(base, j):
        return pl.ds(pl.multiple_of(base + j * piece, piece), piece)

    def load_own(turn, r, j):
        return pltpu.make_async_copy(
            dkv_in.at[chunk(2 * r * part, j)], own.at[chunk(r * part, j)], l_sem.at[turn]
        )

    def to_core(turn, r, j):
        return remote(
            dkv_in.at[chunk((2 * r + 1) * part, j)],
            core_in.at[chunk(r * part, j)],
            c_s,
            c_r,
            turn,
            by_core,
        )

    def to_below(j):
        return remote(z_out.at[chunk(0, j)], z_in.at[chunk(0, j)], d_s, d_r, j, below)

    def to_above(j):
        return remote(z_out.at[chunk(part, j)], z_in.at[chunk(part, j)], u_s, u_r, j, above)

    def to_owner(j):
        return remote(dx_out.at[j - 1], dx_in.at[j - 1], x_s, x_r, j - 1, there(j))

    half_piece = piece // 2

    def pass_on(j):
        span = pl.ds((j - 1) * half_piece, half_piece)
        return remote(dx_out.at[2, span], dx_in.at[2, span], x_s, x_r, 1 + j, there(j))

    def take_in(j):
        span = pl.ds((j - 1) * half_piece, half_piece)
        pass_on(j).wait_recv()
        spot = 2 - j
        dx_out[spot, span, :] = (
            dx_out[spot, span, :].astype(f32) + dx_in[2, span, :].astype(f32)
        ).astype(low)
        to_owner(3 - j).start()

    def every(n, action):
        j = 3 - n
        for turn, r in ((n * 2, 0), (n * 2 + 1, 2)):
            action(turn, r, j)

    greet([by_x, by_y, there(3), by_core] + others)

    def begin(n, carry):
        def go(turn, r, j):
            to_core(turn, r, j).start()
            load_own(turn, r, j).start()

        every(n, go)
        return carry

    lax.fori_loop(0, 4, begin, 0)

    def begin_mid(n, carry):
        to_core(8 + n, 1, 3 - n).start()
        load_own(8 + n, 1, 3 - n).start()
        return carry

    lax.fori_loop(0, 4, begin_mid, 0)
    inputs = [(pair_in[2 * n], keep[n]) for n in range(3)]
    inputs += [(pair_in[2 * n + 1], give[n]) for n in (0, 2)]
    inputs += [(wq_in, wq), (wkv_in, wkv), (dq_in, dq), (x_in, xs), (one_in, one)]
    inputs = [pltpu.make_async_copy(src, dst, i_sem.at[n]) for n, (src, dst) in enumerate(inputs)]
    for copy in inputs:
        copy.start()
    w1 = remote(pair_in[3], give[1], w1_s, w1_r, 0, by_y)
    w1.start()

    def both(turn, r, j):
        to_core(turn, r, j).wait_recv()
        load_own(turn, r, j).wait()
        at = chunk(r * part, j)
        return own[at, :].astype(f32) + core_in[at, :].astype(f32)

    def spread(n, carry):
        j = 3 - n
        z_out[chunk(0, j), :] = both(2 * n, 0, j).astype(low)

        @pl.when(jnp.logical_and(has_below, n < 3))
        def _():
            to_below(j).start()

        z_out[chunk(part, j), :] = both(2 * n + 1, 2, j).astype(low)

        @pl.when(jnp.logical_and(has_above, n < 3))
        def _():
            to_above(j).start()

        return carry

    lax.fori_loop(0, 4, spread, 0)

    for copy in inputs[:5]:
        copy.wait()
    halves = [keep[0].shape[2] // 2, keep[1].shape[2] // 2]
    w2 = {}
    for n in (0, 2, 1):
        if n == 1:
            w1.wait()

        def merge(p, carry, n=n):
            keep[n][p] = (keep[n][p].astype(f32) + give[n][p].astype(f32)).astype(low)
            return carry

        lax.fori_loop(0, planes, merge, 0)
        if n < 2:
            cols = pl.ds(pl.multiple_of((1 - x_at) * halves[n], 128), halves[n])
            w2[n] = remote(keep[n].at[:, :, cols], got[n], w2_s, w2_r, n, by_x)
        else:
            w2[n] = remote(keep[n].at[:, 1 - y_at], got[n], w2_s, w2_r, n, by_y)
        w2[n].start()
    for copy in inputs[5:]:
        copy.wait()
    acc[...] = jnp.zeros_like(acc)

    def arrive(n):
        j = 3 - n
        g_all[:, 2 * WQ :] = dq[chunk(0, j), :]
        g_all[:, : 2 * WQ] = both(8 + n, 1, j).astype(low)

        @pl.when(has_above)
        def _():
            to_below(j).wait_recv()
            g_all[:, : 2 * WQ] = (
                g_all[:, : 2 * WQ].astype(f32) + z_in[chunk(0, j), :].astype(f32)
            ).astype(low)

        @pl.when(has_below)
        def _():
            to_above(j).wait_recv()
            g_all[:, : 2 * WQ] = (
                g_all[:, : 2 * WQ].astype(f32) + z_in[chunk(part, j), :].astype(f32)
            ).astype(low)

    def back(j):
        grads = g_all[...]
        return nt(grads[:, 2 * WQ :], wq[...]) + nt(grads[:, : 2 * WQ], wkv[...])

    def outer(j):
        acc[...] += tn(xs[chunk(0, j), :], g_all[...])

    def turn_back(n, carry):
        arrive(n)
        dx_out[2 - n] = back(3 - n).astype(low)
        outer(3 - n)
        return carry

    turn_back(0, 0)
    pass_on(1).start()
    pass_on(2).start()
    turn_back(1, 0)

    for n in range(3):
        w2[n].wait_recv()

        def halve(p, carry, n=n):
            if n < 2:
                cols = pl.ds(pl.multiple_of(x_at * halves[n], 128), halves[n])
                mine = keep[n][p, :, cols]
            else:
                mine = keep[n][p, y_at]
            two[n][p] = (mine.astype(f32) + got[n][p].astype(f32)).astype(low)
            return carry

        lax.fori_loop(0, planes, halve, 0)

    def line_copy(n, way, t):
        return remote(
            line_out[n].at[way, t],
            line_in[n].at[way, t],
            w3_s,
            w3_r,
            (n * 2 + way) * rest + t,
            below if way else above,
        )

    def line_step(t):
        for n in range(3):
            for way in range(2):
                spot = (planes - 1 - plane) if way else plane
                gap = planes - 1 - t
                slab = (plane - gap) if way else (plane + gap)
                sends = jnp.logical_and(t >= spot, spot < planes - 1)

                @pl.when(jnp.logical_and(sends, spot == 0))
                def _():
                    line_out[n][way, t] = two[n][slab]
                    line_copy(n, way, t).start()

                @pl.when(jnp.logical_and(sends, spot > 0))
                def _():
                    line_copy(n, way, t - 1).wait_recv()
                    line_out[n][way, t] = (
                        two[n][slab].astype(f32) + line_in[n][way, t - 1].astype(f32)
                    ).astype(low)
                    line_copy(n, way, t).start()

    line_step(0)

    @pl.when(has_below)
    def _():
        to_below(0).start()

    @pl.when(has_above)
    def _():
        to_above(0).start()

    take_in(1)
    turn_back(2, 0)
    take_in(2)
    if planes > 2:
        line_step(1)
    arrive(3)
    tok_out[...] = one[...] + back(0)
    outer(0)

    share = p_slab.shape[3]
    acc[:, 2 * WQ :] *= DH ** (-0.5)
    for p in range(planes):
        for y in range(2):
            for k in range(2):
                at = ((p * 2 + y) * 2 + k) * share
                p_slab[k, p, y] = acc[at : at + share, :].astype(low)
    pk = remote(p_slab.at[1 - core], p_core, pk_s, pk_r, 0, by_core)
    pk.start()
    pk.wait_recv()

    def merge_core(p, carry):
        p_z[p] = (p_slab[core, p].astype(f32) + p_core[p].astype(f32)).astype(low)
        return carry

    lax.fori_loop(0, planes, merge_core, 0)
    pz = [
        remote(
            p_z.at[lax.rem(plane + g, planes)], p_zin.at[g - 1], pz_s, pz_r, g - 1, others[g - 1]
        )
        for g in range(1, planes)
    ]

    def next_step(t, carry):
        line_step(t)
        return carry

    lax.fori_loop(2, planes - 1, next_step, 0)
    for copy in pz:
        copy.start()
    w4 = []
    for n in range(3):
        fin[n][x_at] = two[n][plane]

        @pl.when(has_below)
        def _(n=n):
            line_copy(n, 0, rest - 1).wait_recv()
            fin[n][x_at] = (
                fin[n][x_at].astype(f32) + line_in[n][0, rest - 1].astype(f32)
            ).astype(low)

        @pl.when(has_above)
        def _(n=n):
            line_copy(n, 1, rest - 1).wait_recv()
            fin[n][x_at] = (
                fin[n][x_at].astype(f32) + line_in[n][1, rest - 1].astype(f32)
            ).astype(low)

        w4.append(remote(fin[n].at[x_at], fin[n].at[x_at], w4_s, w4_r, n, by_x))
        w4[n].start()

    for j in (2, 1):
        to_owner(j).wait_recv()
        tok_out[...] += dx_in[j - 1].astype(f32)

    total = p_z[plane].astype(f32)
    for g in range(1, planes):
        pz[g - 1].wait_recv()
        total = total + p_zin[g - 1].astype(f32)
    p_fin[...] = total.astype(low)
    pf = [
        remote(p_fin.at[y_at ^ (j >> 1)], p_all.at[j], pf_s, pf_r, j - 1, there(j))
        for j in (1, 2, 3)
    ]
    for copy in pf:
        copy.start()
    p_all[0] = p_fin[y_at]

    for copy in pf:
        copy.wait()
    for a in range(4):
        grads = p_all[a ^ group].astype(f32)
        for n, dest in enumerate((k_out, v_out, q_out)):
            dest[:, a * WQ : (a + 1) * WQ] = grads[:, n * WQ : (n + 1) * WQ]
    for n, dest in ((0, up_out), (2, down_out)):
        w4[n].wait()
        width = dest.shape[1] // 2
        for side in range(2):
            dest[:, side * width : (side + 1) * width] = fin[n][side].astype(f32)
    w4[1].wait()
    width = side_out.shape[1] // 2
    for side in range(2):
        done = fin[1][side].astype(f32)
        side_out[:, side * width : (side + 1) * width] = done[:share]
        norm_out[:, side * width : (side + 1) * width] = done[share : share + 8]

    for copy in list(w2.values()) + pz + [pk]:
        copy.wait_send()

    def settle(n, carry):
        every(n, lambda turn, r, j: to_core(turn, r, j).wait_send())
        to_core(8 + n, 1, 3 - n).wait_send()

        @pl.when(has_below)
        def _():
            to_below(3 - n).wait_send()

        @pl.when(has_above)
        def _():
            to_above(3 - n).wait_send()

        return carry

    lax.fori_loop(0, 4, settle, 0)
    for j in (1, 2):
        to_owner(j).wait_send()
        pass_on(j).wait_send()

    def settle_line(t, carry):
        for n in range(3):
            for way in range(2):
                spot = (planes - 1 - plane) if way else plane

                @pl.when(jnp.logical_and(t >= spot, spot < planes - 1))
                def _():
                    line_copy(n, way, t).wait_send()

        return carry

    lax.fori_loop(0, planes - 1, settle_line, 0)


def reduce_all(dkv, dq, stretch, wq, wkv, one, up, out, down, planes):
    low, f32 = jnp.bfloat16, jnp.float32
    piece = dq.shape[0] // 4
    width = stretch.shape[1]
    share = up[0].shape[1]
    rest = planes - 1
    dma, vm, sds = pltpu.SemaphoreType.DMA, pltpu.VMEM, jax.ShapeDtypeStruct
    cols = 2 * WQ + WIN
    tall = out[0].shape[1]
    wide = up[0].shape[2]
    kinds = [(share, wide // 2), (tall, width // 2), down[0].shape[2:]]
    pairs = [up[0].shape, out[0].shape, down[0].shape]
    return pl.pallas_call(
        functools.partial(reduce_kernel, planes),
        out_shape=[sds((piece, width), f32)]
        + [sds((share, width), f32)] * 3
        + [
            sds((share, wide), f32),
            sds((share, width), f32),
            sds((8, width), f32),
            sds((kinds[2][0], width), f32),
        ],
        in_specs=[ANY] * 12,
        out_specs=[VMEM] * 8,
        scratch_shapes=[
            vm((12 * piece, 2 * WQ), low),
            vm((12 * piece, 2 * WQ), low),
            vm((8 * piece, 2 * WQ), low),
            vm((8 * piece, 2 * WQ), low),
            vm((piece, cols), low),
            vm((3, piece, width), low),
            vm((3, piece, width), low),
            vm((width, cols), f32),
            vm(dq.shape, low),
            vm(stretch.shape, low),
            vm(wq.shape, low),
            vm(wkv.shape, low),
            vm(one.shape, f32),
            vm((2, planes, 2, share, cols), low),
            vm((planes, 2, share, cols), low),
            vm((planes, 2, share, cols), low),
            vm((rest, 2, share, cols), low),
            vm((2, share, cols), low),
            vm((4, share, cols), low),
        ]
        + [vm(p, low) for p in pairs] * 2
        + [vm((planes,) + k, low) for k in kinds] * 2
        + [vm((2,) + k, low) for k in kinds]
        + [vm((2, rest) + k, low) for k in kinds] * 2
        + [dma((12,)), dma((11,))]
        + [dma((12,))] * 2
        + [dma((4,))] * 6
        + [dma((1,))] * 2
        + [dma((rest,))] * 2
        + [dma((3,))] * 2
        + [dma((3,))] * 2
        + [dma((6 * rest,))] * 2
        + [dma((3,))] * 2
        + [dma((1,))] * 2,
        compiler_params=pltpu.CompilerParams(
            collective_id=1, has_side_effects=True, vmem_limit_bytes=60 << 20
        ),
        cost_estimate=pl.CostEstimate(
            flops=4 * 4 * piece * width * cols, bytes_accessed=40 << 20, transcendentals=0
        ),
        name="reduce_all",
    )(dkv, dq, stretch, wq, wkv, one, up[0], up[1], out[0], out[1], down[0], down[1])


def dense_kernel(
    planes,
    tok_ref,
    ctx_ref,
    cot_ref,
    g1_ref,
    b1_ref,
    g2_ref,
    b2_ref,
    wout_in,
    wup_in,
    wdown_in,
    *refs,
):
    out_ref, one_ref, do_out, up_keep, up_give, out_keep, out_give, down_keep, down_give = refs[:9]
    wup, wdown, acc, x1, s1, g_two, nl, hid, slope, gp, gm, ga = refs[9:21]
    dctx, up_loc, out_loc, down_loc, up_got, out_got, down_got, down_sum = refs[21:29]
    w_sem, mv_sem, do_s, do_r, up_s, up_r, out_s, out_r, down_s, down_r = refs[29:39]
    wout_ref = refs[39]
    plane, y_at, core, x_at = place()
    piece, width = tok_ref.shape
    share = up_loc.shape[2]
    slab = down_loc.shape[2]
    pairs = 2 * planes
    group = y_at * 2 + x_at
    f32 = jnp.float32
    fetch = [
        pltpu.make_async_copy(
            wout_in.at[pl.ds(pl.multiple_of((group ^ j) * WQ, WQ), WQ)],
            wout_ref.at[pl.ds(j * WIN + WIN - WQ, WQ)],
            w_sem.at[2 + j],
        )
        for j in range(4)
    ]
    for copy in fetch:
        copy.start()
    bring = [
        pltpu.make_async_copy(wup_in, wup, w_sem.at[0]),
        pltpu.make_async_copy(wdown_in, wdown, w_sem.at[1]),
    ]
    for copy in bring:
        copy.start()

    def there(j):
        return device_at(plane, y_at ^ (j >> 1), core, x_at ^ (j & 1))

    by_core = device_at(plane, y_at, 1 - core, x_at)
    height, tile = 32, 2 * WQ
    wide = wup.shape[1]

    def rows_of(n):
        return pl.ds(pl.multiple_of(n * height, height), height)

    def cols_of(n):
        return pl.ds(pl.multiple_of(n * tile, tile), tile)

    def mean(v):
        return jnp.mean(v, axis=1, keepdims=True)

    def fold(v):
        return v[:8] + v[8:16] + v[16:24] + v[24:]

    for j in range(4):
        wout_ref[j * WIN : j * WIN + WIN - WQ, :] = jnp.zeros((WIN - WQ, width), jnp.bfloat16)
    for copy in fetch:
        copy.wait()
    acc[...] = jnp.dot(ctx_ref[...], wout_ref[...], preferred_element_type=f32)
    g1, b1, g2, b2 = (r[...].reshape(1, width) for r in (g1_ref, b1_ref, g2_ref, b2_ref))

    def norm_one(n, carry):
        at = rows_of(n)
        value = tok_ref[at, :].astype(f32) + acc[at, :]
        center = value - mean(value)
        inverse = lax.rsqrt(mean(center * center) + eps_norm)
        hat = center * inverse
        x1[at, :] = hat
        s1[at, :] = jnp.broadcast_to(inverse, (height, 128))
        nl[at, :] = (hat * g1 + b1).astype(jnp.bfloat16)
        return carry

    lax.fori_loop(0, piece // height, norm_one, 0, unroll=4)
    bring[0].wait()

    def expand(n, carry):
        at = cols_of(n)
        pre = jnp.dot(nl[...], wup[:, at], preferred_element_type=f32)
        square = pre * pre
        bend = jnp.tanh(pre * (0.7978845608028654 + 0.035677408136300125 * square))
        half_up = 0.5 + 0.5 * bend
        value = pre * half_up
        hid[:, at] = value.astype(jnp.bfloat16)
        slope[:, at] = half_up + value * (1.0 - bend) * (
            0.7978845608028654 + 0.10703222440890037 * square
        )
        return carry

    lax.fori_loop(0, wide // tile, expand, 0, unroll=2)
    bring[1].wait()
    acc[...] = jnp.dot(hid[...], wdown[...], preferred_element_type=f32)
    nothing = jnp.zeros((8, width), f32)

    def norm_two(n, carry):
        gain_sum, shift_sum = carry
        at = rows_of(n)
        value = x1[at, :] * g1 + b1 + acc[at, :]
        center = value - mean(value)
        inverse = lax.rsqrt(mean(center * center) + eps_norm)
        hat = center * inverse
        out_ref[at, :] = (hat * g2 + b2).astype(jnp.bfloat16)
        cot = cot_ref[at, :].astype(f32)
        gain_sum, shift_sum = gain_sum + fold(cot * hat), shift_sum + fold(cot)
        up = cot * g2
        grad = inverse * (up - mean(up) - hat * mean(up * hat))
        g_two[at, :] = grad
        gm[at, :] = grad.astype(jnp.bfloat16)
        return gain_sum, shift_sum

    gain_two, shift_two = lax.fori_loop(0, piece // height, norm_two, (nothing, nothing), unroll=4)

    def shrink(n, carry):
        at = cols_of(n)
        back = nt(gm[...], wdown[at, :])
        gp[:, at] = (back * slope[:, at]).astype(jnp.bfloat16)
        return carry

    lax.fori_loop(0, wide // tile, shrink, 0, unroll=2)
    acc[...] = nt(gp[...], wup[...])

    def norm_three(n, carry):
        gain_sum, shift_sum = carry
        at = rows_of(n)
        grad_in, hat = g_two[at, :] + acc[at, :], x1[at, :]
        gain_sum, shift_sum = gain_sum + fold(grad_in * hat), shift_sum + fold(grad_in)
        up = grad_in * g1
        grad = s1[at, 0:1] * (up - mean(up) - hat * mean(up * hat))
        one_ref[at, :] = grad
        ga[at, :] = grad.astype(jnp.bfloat16)
        return gain_sum, shift_sum

    gain_one, shift_one = lax.fori_loop(
        0, piece // height, norm_three, (nothing, nothing), unroll=4
    )
    side = jnp.concatenate(
        [jnp.sum(v, axis=0, keepdims=True) for v in (gain_one, shift_one, gain_two, shift_two)]
        + [jnp.zeros((12, width), f32)],
        axis=0,
    ).astype(jnp.bfloat16)

    low = jnp.bfloat16
    greet([there(1), there(2), there(3), by_core])
    trades = []
    for j in (3, 1, 2, 0):
        part = nt(ga[...], wout_ref[pl.ds(j * WIN, WIN), :]).astype(low)
        if j:
            dctx[j - 1] = part
            trades.append(
                remote(
                    dctx.at[j - 1], do_out.at[pl.ds(j * piece, piece)], do_s, do_r, j - 1, there(j)
                )
            )
            trades[-1].start()
        else:
            do_out[pl.ds(0, piece), :] = part

    tile = 2 * WQ
    per = tile // (2 * slab)
    tiles = wide // tile

    def down_copy(t):
        span = pl.ds(t * per, per)
        return remote(down_loc.at[1 - core, span], down_got.at[span], down_s, down_r, t, by_core)

    def up_copy(t):
        span = cols_of(t)
        return remote(
            up_loc.at[1 - core, :, :, span], up_got.at[:, :, span], up_s, up_r, t, by_core
        )

    def make_down(t, carry):
        cell = tn(hid[:, cols_of(t)], gm[...])
        for n in range(per):
            for k in range(2):
                at = (n * 2 + k) * slab
                down_loc[k, t * per + n] = cell[at : at + slab].astype(low)
        down_copy(t).start()
        return carry

    lax.fori_loop(0, tiles, make_down, 0)

    def make_up(t, carry):
        cell = tn(nl[...], gp[:, cols_of(t)])
        for q in range(pairs):
            for k in range(2):
                at = (q * 2 + k) * share
                up_loc[k, q, :, cols_of(t)] = cell[at : at + share].astype(low)
        up_copy(t).start()
        return carry

    lax.fori_loop(0, tiles, make_up, 0)
    moved = []

    def move(source, dest):
        moved.append(pltpu.make_async_copy(source, dest, mv_sem.at[len(moved)]))
        moved[-1].start()

    half = width // 2

    def sum_down(t, carry):
        down_copy(t).wait_recv()
        for n in range(per):
            q = t * per + n
            total = (
                down_loc[core, q].astype(jnp.float32) + down_got[q].astype(jnp.float32)
            ).astype(low)
            down_sum[0, q] = total[:, :half]
            down_sum[1, q] = total[:, half:]
        return carry

    lax.fori_loop(0, tiles, sum_down, 0)
    move(down_sum.at[x_at], down_keep)
    move(down_sum.at[1 - x_at], down_give)

    per_group = pairs // 4
    for j in range(4):
        cell = tn(ctx_ref[:, j * WIN : (j + 1) * WIN], ga[...])
        for n in range(per_group):
            for k in range(2):
                at = WIN - WQ + (n * 2 + k) * share
                out_loc[k, (group ^ j) * per_group + n, :share, :] = cell[at : at + share].astype(low)
    for q in range(pairs):
        for k in range(2):
            out_loc[k, q, share:, :] = side
    outs = remote(out_loc.at[1 - core], out_got, out_s, out_r, 0, by_core)
    outs.start()

    def sum_up(q, carry):
        up_got[q] = (up_loc[core, q].astype(jnp.float32) + up_got[q].astype(jnp.float32)).astype(low)
        return carry

    for t in range(tiles):
        up_copy(t).wait_recv()
    lax.fori_loop(0, pairs, sum_up, 0)
    outs.wait_recv()
    for p in range(planes):
        for y in range(2):
            q = p * 2 + y
            out_got[q] = (
                out_loc[core, q].astype(jnp.float32) + out_got[q].astype(jnp.float32)
            ).astype(low)
        for got, keep, give in ((up_got, up_keep, up_give), (out_got, out_keep, out_give)):
            move(got.at[p * 2 + y_at], keep.at[p])
            move(got.at[p * 2 + 1 - y_at], give.at[p])
    for copy in trades:
        copy.wait()
    for t in range(tiles):
        down_copy(t).wait_send()
        up_copy(t).wait_send()
    outs.wait_send()
    for copy in moved:
        copy.wait()


def dense_layers(tokens, ctx, cotangent, norms, wout, w_up, w_down, planes):
    low = jnp.bfloat16
    piece, width = tokens.shape
    pairs = 2 * planes
    wide = w_up.shape[1]
    share, slab, tall = width // (2 * pairs), wide // (2 * pairs), 16
    sds, vm, dma = jax.ShapeDtypeStruct, pltpu.VMEM, pltpu.SemaphoreType.DMA
    up, out = (planes, share, wide), (planes, share + tall, width)
    down = (pairs, slab, width // 2)
    tiles = wide // (2 * WQ)
    f32 = jnp.float32
    return pl.pallas_call(
        functools.partial(dense_kernel, planes),
        out_shape=[sds((piece, width), low), sds((piece, width), f32), sds((4 * piece, WIN), low)]
        + [sds(up, low)] * 2
        + [sds(out, low)] * 2
        + [sds(down, low)] * 2,
        in_specs=[VMEM] * 7 + [ANY] * 3,
        out_specs=[VMEM] * 3 + [ANY] * 6,
        scratch_shapes=[
            vm(w_up.shape, low),
            vm(w_down.shape, low),
            vm((piece, width), f32),
            vm((piece, width), f32),
            vm((piece, 128), f32),
            vm((piece, width), f32),
            vm((piece, width), low),
            vm((piece, wide), low),
            vm((piece, wide), f32),
            vm((piece, wide), low),
            vm((piece, width), low),
            vm((piece, width), low),
            vm((3, piece, WIN), low),
            vm((2, pairs, share, wide), low),
            vm((2, pairs, share + tall, width), low),
            vm((2, pairs, slab, width), low),
            vm((pairs, share, wide), low),
            vm((pairs, share + tall, width), low),
            vm((pairs, slab, width), low),
            vm((2, pairs, slab, width // 2), low),
            dma((6,)),
            dma((2 + 4 * planes,)),
        ]
        + [dma((3,))] * 2
        + [dma((tiles,))] * 2
        + [dma((1,))] * 2
        + [dma((tiles,))] * 2
        + [vm((4 * WIN, width), low)],
        compiler_params=pltpu.CompilerParams(
            collective_id=2, has_side_effects=True, vmem_limit_bytes=63 << 20
        ),
        cost_estimate=pl.CostEstimate(
            flops=2 * piece * width * (6 * wide + 3072), bytes_accessed=30 << 20, transcendentals=0
        ),
        name="dense_layers",
    )(tokens, ctx, cotangent, *norms, wout, w_up, w_down)


def finish_kernel(share, count, *refs):
    sources, rows_ref, dests = refs[:count], refs[count], refs[count + 1 : 2 * count + 1]
    parts = refs[2 * count + 1 : 2 * count + 5]
    for source, dest in zip(sources, dests):
        dest[...] = source[...]
    seq_at = lax.axis_index("seq")
    rows = rows_ref[...]
    width = rows.shape[1]
    spot = lax.broadcasted_iota(jnp.int32, (width, 128), 0) - seq_at * share
    chosen = (spot == lax.broadcasted_iota(jnp.int32, (width, 128), 1)).astype(jnp.float32)
    picked = jnp.dot(
        rows, chosen, preferred_element_type=jnp.float32, precision=lax.Precision.HIGHEST
    )
    for n in range(4):
        parts[n][...] = picked[n, :share]


def finish(arrays, norm_rows, share):
    sds, count = jax.ShapeDtypeStruct, len(arrays)
    return pl.pallas_call(
        functools.partial(finish_kernel, share, count),
        out_shape=[sds(v.shape, v.dtype) for v in arrays] + [sds((share,), jnp.float32)] * 4,
        in_specs=[VMEM] * (count + 1),
        out_specs=[VMEM] * (count + 4),
        compiler_params=pltpu.CompilerParams(vmem_limit_bytes=62 << 20),
        name="finish",
    )(*arrays, norm_rows)


def body(
    tokens,
    w_query,
    w_key,
    w_value,
    w_out,
    gain_attn,
    shift_attn,
    w_up,
    w_down,
    gain_mlp,
    shift_mlp,
    cotangent,
    lengths,
    seq_order,
    rand_blocks,
):
    piece, width = tokens.shape
    seqs, heads = lax.axis_size("seq"), lax.axis_size("head")
    planes = seqs // 4
    assert heads == 2 and 8 * piece == MAXB * BLK and width == 4 * WQ
    seq_at, x_at = lax.axis_index("seq"), lax.axis_index("head")
    plane, y_at, core = seq_at // 4, (seq_at // 2) % 2, seq_at % 2
    group = y_at * 2 + x_at

    keys_values, queries, stretch, context_tok, level, idx, live, wq_own, wkv_own, ctx_own = (
        forward_attention(
            tokens, w_query, w_key, w_value, lengths, seq_order, rand_blocks, planes
        )
    )
    share = width // seqs
    norms = [gain_attn, shift_attn, gain_mlp, shift_mlp]
    output, grad_one, grad_ctx, up_keep, up_give, out_keep, out_give, down_keep, down_give = (
        dense_layers(tokens, context_tok, cotangent, norms, w_out, w_up, w_down, planes)
    )
    up_pair = (up_keep, xor_swap(up_give, 4))
    out_pair = (out_keep, out_give)
    two_y = (planes, 2) + down_keep.shape[1:]
    down_pair = (down_keep.reshape(two_y), xor_swap(down_give, 1).reshape(two_y))

    grad_q, grad_kv = attend_back(
        idx,
        live,
        queries,
        grad_ctx,
        ctx_own.reshape(-1, WIN),
        level,
        keys_values.reshape(-1, 2 * WQ),
    )
    grad_tokens, grad_wq, grad_wk, grad_wv, up_total, out_total, norm_rows, down_total = reduce_all(
        grad_kv,
        grad_q,
        stretch,
        wq_own,
        wkv_own,
        grad_one,
        up_pair,
        out_pair,
        down_pair,
        planes,
    )

    finals = finish(
        (output, grad_tokens, grad_wq, grad_wk, grad_wv, out_total, up_total, down_total),
        norm_rows,
        share,
    )

    output, grad_tokens, grad_wq, grad_wk, grad_wv, grad_out, grad_up, grad_down = finals[:8]
    gain_one, shift_one, gain_two, shift_two = finals[8:]
    return (
        output,
        grad_tokens,
        grad_wq,
        grad_wk,
        grad_wv,
        grad_out,
        gain_one,
        shift_one,
        grad_up,
        grad_down,
        gain_two,
        shift_two,
    )


def solution(mesh):
    rows = P(("seq", "head"), None)
    seq_rows, seq_only = P("seq", None), P("seq")
    return jax.shard_map(
        body,
        mesh=mesh,
        in_specs=(rows,) + (P(),) * 10 + (rows, P(), P(), seq_rows),
        out_specs=(
            rows,
            rows,
            seq_rows,
            seq_rows,
            seq_rows,
            seq_rows,
            seq_only,
            seq_only,
            seq_rows,
            seq_rows,
            seq_only,
            seq_only,
        ),
        check_vma=False,
    )
```

```python
import functools

import jax
import jax.numpy as jnp
from jax import lax
from jax.experimental import pallas as pl
from jax.experimental.pallas import tpu as pltpu
from jax.sharding import PartitionSpec as P

DH = 64
BLK = 64
MAXB = 64
SLOTS = 8
HG = 3
WQ = HG * DH
WIN = 256
AXES = ("seq", "head")
NEG = -1e30

eps_norm = 1e-06


def xor_swap(value, bits):
    count = lax.axis_size("seq") * lax.axis_size("head")
    return lax.ppermute(value, AXES, [(d, d ^ bits) for d in range(count)])


def lane_groups(rows, offset):
    lane = lax.broadcasted_iota(jnp.int32, (rows, WIN), 1) - offset
    return [jnp.logical_and(lane >= h * DH, lane < (h + 1) * DH) for h in range(HG)]


def spread_heads(block, offset):
    zero = jnp.zeros_like(block)
    return jnp.concatenate([jnp.where(m, block, zero) for m in lane_groups(BLK, offset)], axis=0)


def fold_heads(stacked, offset):
    masks = lane_groups(BLK, offset)
    total = jnp.where(masks[0], stacked[:BLK], 0.0)
    for h in range(1, HG):
        total = total + jnp.where(masks[h], stacked[h * BLK : (h + 1) * BLK], 0.0)
    return total


def nt(a, b):
    return lax.dot_general(a, b, (((1,), (1,)), ((), ())), preferred_element_type=jnp.float32)


def tn(a, b):
    return lax.dot_general(a, b, (((0,), (0,)), ((), ())), preferred_element_type=jnp.float32)


def backward_kernel(idx_ref, live_ref, q_ref, do_ref, o_ref, lse_ref, *refs):
    kv_ref, dq_ref, dkv_ref, kv, acc, sems = refs

    def clear(n, carry):
        acc[pl.ds(pl.multiple_of(n * 256, 256), 256), :] = jnp.zeros((256, 2 * WQ), jnp.float32)
        return carry

    copy = pltpu.make_async_copy(kv_ref, kv, sems.at[0])
    copy.start()
    lax.fori_loop(0, acc.shape[0] // 256, clear, 0)
    copy.wait()

    def step(i, carry):
        q_rows = pl.multiple_of(i * BLK, BLK)
        qexp = spread_heads(q_ref[pl.ds(q_rows, BLK), :], 0)
        doexp = spread_heads(do_ref[pl.ds(q_rows, BLK), :], 64)
        rows = [
            pl.multiple_of(idx_ref[i * SLOTS + s] * BLK, BLK) for s in range(SLOTS)
        ]
        keys = jnp.concatenate([kv[pl.ds(r, BLK), 0:WIN] for r in rows], axis=0)
        values = jnp.concatenate([kv[pl.ds(r, BLK), 128 : 128 + WIN] for r in rows], axis=0)
        product = do_ref[pl.ds(q_rows, BLK), :].astype(jnp.float32) * o_ref[
            pl.ds(q_rows, BLK), :
        ].astype(jnp.float32)
        high = product.astype(jnp.bfloat16)
        ones = jnp.ones((8, WIN), jnp.bfloat16)
        inner = nt(ones, spread_heads(high, 64)) + nt(
            ones, spread_heads((product - high.astype(jnp.float32)).astype(jnp.bfloat16), 64)
        )
        inner = inner[0:1]
        level = lse_ref[pl.ds(i, 1), :]
        raw = nt(keys, qexp)
        grad_probs = nt(values, doexp)
        probs, grad_scores = [], []
        for s in range(SLOTS):
            at = slice(s * BLK, (s + 1) * BLK)
            off = level + jnp.where(live_ref[i * SLOTS + s] > 0, 0.0, -NEG)
            p = jnp.exp(raw[at] - off)
            probs.append(p.astype(jnp.bfloat16))
            grad_scores.append((p * (grad_probs[at] - inner)).astype(jnp.bfloat16))
        probs = jnp.concatenate(probs, axis=0)
        grad_scores = jnp.concatenate(grad_scores, axis=0)
        dk = jnp.dot(grad_scores, qexp, preferred_element_type=jnp.float32)
        dv = jnp.dot(probs, doexp, preferred_element_type=jnp.float32)
        dq = tn(grad_scores, keys)
        dq_ref[pl.ds(q_rows, BLK), :] = fold_heads(dq, 0).astype(jnp.bfloat16)
        for s in range(SLOTS):
            k_s, v_s = dk[s * BLK : (s + 1) * BLK], dv[s * BLK : (s + 1) * BLK]
            at = pl.ds(rows[s], BLK)
            acc[at, 0:128] += k_s[:, :128]
            acc[at, 128:256] += k_s[:, 128:] + v_s[:, :128]
            acc[at, 256:384] += v_s[:, 128:]
        return carry

    lax.fori_loop(0, q_ref.shape[0] // BLK, step, 0, unroll=8)

    def emit(n, carry):
        at = pl.ds(pl.multiple_of(n * 256, 256), 256)
        dkv_ref[at, :] = acc[at, :].astype(jnp.bfloat16)
        return carry

    lax.fori_loop(0, acc.shape[0] // 256, emit, 0)


VMEM = pl.BlockSpec(memory_space=pltpu.VMEM)
SMEM = pl.BlockSpec(memory_space=pltpu.SMEM)
ANY = pl.BlockSpec(memory_space=pl.ANY)


def device_at(plane, y_at, core, x_at):
    return (plane * 4 + y_at * 2 + core, x_at)


def place():
    seq_at, x_at = lax.axis_index("seq"), lax.axis_index("head")
    return seq_at // 4, (seq_at // 2) % 2, seq_at % 2, x_at


def remote(src, dst, sems, recvs, at, device):
    return pltpu.make_async_remote_copy(
        src_ref=src,
        dst_ref=dst,
        send_sem=sems.at[at],
        recv_sem=recvs.at[at],
        device_id=device,
        device_id_type=pl.DeviceIdType.MESH,
    )


def greet(partners):
    barrier = pltpu.get_barrier_semaphore()
    for device in partners:
        pl.semaphore_signal(
            barrier, inc=1, device_id=device, device_id_type=pl.DeviceIdType.MESH
        )
    pl.semaphore_wait(barrier, len(partners))


CHUNK_ORDER = (0, 1, 2, 4, 3, 5, 6, 7)


def slot_tables(plane, y_at, core, x_at, at, lengths, order, rand_own, rand_got, idx_ref, live_ref):
    per = at["piece_blocks"]

    def one(i, carry):
        far, near = i // per, i % per
        y_of, x_of = y_at ^ (far >> 1), x_at ^ (far & 1)
        block = plane * MAXB + y_of * (4 * per) + core * (2 * per) + x_of * per + near
        begin, first, span = jnp.int32(0), jnp.int32(0), jnp.int32(1)
        for m in range(at["seqs"]):
            size = lengths[order[m]]
            inside = begin <= block
            first = jnp.where(inside, begin, first)
            span = jnp.where(inside, size, span)
            begin = begin + size
        row = x_of * per + near
        draws = []
        for n in range(SLOTS - 5):
            draw = jnp.where(far >= 2, rand_got[n, row], rand_own[n, row])
            for power in range(16, -1, -1):
                multiple = span * (1 << power)
                draw = jnp.where(draw >= multiple, draw - multiple, draw)
            draws.append(first + draw)
        candidates = [block - 1, block, block + 1, first, first + span - 1] + draws
        kept = []
        for s in range(SLOTS):
            alive = jnp.int32(1)
            if s == 0:
                alive = (block > first).astype(jnp.int32)
            if s == 2:
                alive = (block < first + span - 1).astype(jnp.int32)
            for e in range(s):
                same = (candidates[e] == candidates[s]).astype(jnp.int32)
                alive = alive * (1 - kept[e] * same)
            kept.append(alive)
            key = jnp.where(alive > 0, candidates[s], block)
            rel = key // MAXB - plane + 1
            inner = key % MAXB
            y_key, rest = inner // (4 * per), inner % (4 * per)
            core_key, rest = rest // (2 * per), rest % (2 * per)
            x_key, near_key = rest // per, rest % per
            spot = (rel * 2 + (core_key ^ core)) * 4 + ((y_key ^ y_at) * 2 + (x_key ^ x_at))
            idx_ref[i * SLOTS + s] = jnp.clip(spot * per + near_key, 0, 24 * per - 1)
            live_ref[i * SLOTS + s] = alive
        return carry

    lax.fori_loop(at["begin"], at["end"], one, 0)


def attend_block(i, idx_ref, live_ref, q_ref, kv, lse_ref):
    qexp = spread_heads(q_ref[pl.ds(pl.multiple_of(i * BLK, BLK), BLK), :], 0)
    at = [idx_ref[i * SLOTS + s] for s in range(SLOTS)]
    off = [jnp.where(live_ref[i * SLOTS + s] > 0, 0.0, -NEG) for s in range(SLOTS)]
    keys = jnp.concatenate([kv[r, :, 0:WIN] for r in at], axis=0)
    values = jnp.concatenate([kv[r, :, 128 : 128 + WIN] for r in at], axis=0)
    raw = nt(keys, qexp)
    parts = [raw[s * BLK : (s + 1) * BLK] for s in range(SLOTS)]
    top = jnp.max(parts[1], axis=0, keepdims=True)
    for s in range(SLOTS):
        top = jnp.maximum(top, jnp.max(parts[s], axis=0, keepdims=True) - off[s])
    e = [jnp.exp(parts[s] - (top + off[s])) for s in range(SLOTS)]
    total = jnp.sum(e[0], axis=0, keepdims=True)
    for s in range(1, SLOTS):
        total = total + jnp.sum(e[s], axis=0, keepdims=True)
    lse_ref[pl.ds(i, 1), :] = top + jnp.log(total)
    scale = 1.0 / total
    probs = jnp.concatenate([(v * scale).astype(jnp.bfloat16) for v in e], axis=0)
    return fold_heads(tn(probs, values), 64).astype(jnp.bfloat16)


def forward_kernel(planes, tok_ref, wq_in, wk_in, wv_in, len_ref, ord_ref, rand_vm, rand_sm, *refs):
    kv_out, q_ref, x_out, ctx_out, lse_ref, idx_ref, live_ref, wq_out, wkv_out, ctx_keep = refs[:10]
    xs, kv, ctx, rand_got, rand_two, w_full, wq_ref, wkv_ref = refs[10:18]
    x_send, x_recv, k_send, k_recv, up_send, up_recv, dn_send, dn_recv = refs[18:26]
    f_send, f_recv, g_send, g_recv, s_sem, o_send, o_recv, r_send, r_recv, l_sem = refs[26:36]
    weights = [
        pltpu.make_async_copy(w, w_full.at[n], l_sem.at[2 + n])
        for n, w in enumerate((wk_in, wv_in, wq_in))
    ]
    for copy in weights:
        copy.start()
    plane, y_at, core, x_at = place()
    piece = tok_ref.shape[0]
    rows = piece // 2
    part = 4 * piece
    by_x = device_at(plane, y_at, core, 1 - x_at)
    by_y = device_at(plane, 1 - y_at, core, x_at)
    by_xy = device_at(plane, 1 - y_at, core, 1 - x_at)
    by_core = device_at(plane, y_at, 1 - core, x_at)
    above = device_at(plane + 1, y_at, core, x_at)
    below = device_at(plane - 1, y_at, core, x_at)
    has_above, has_below = plane < planes - 1, plane > 0
    ring = [device_at(lax.rem(plane + g, planes), y_at, core, x_at) for g in (1, planes - 1)]
    greet([by_x, by_y, by_xy, by_core] + ring)

    def x_rows(c):
        return xs.at[pl.ds((c - 2) * rows, rows)]

    def tok_rows(c):
        return tok_ref.at[pl.ds(c * rows, rows)]

    hops = {
        2: remote(tok_rows(0), x_rows(2), x_send, x_recv, 0, by_x),
        4: remote(tok_rows(0), x_rows(4), x_send, x_recv, 2, by_y),
        3: remote(tok_rows(1), x_rows(3), x_send, x_recv, 1, by_x),
        5: remote(tok_rows(1), x_rows(5), x_send, x_recv, 3, by_y),
        6: remote(x_rows(2), x_rows(6), x_send, x_recv, 4, by_y),
        7: remote(x_rows(5), x_rows(7), x_send, x_recv, 5, by_x),
    }
    rand_trade = remote(rand_vm, rand_got, r_send, r_recv, 0, by_y)
    rand_trade.start()
    for c in (2, 4, 3, 5):
        hops[c].start()

    wq_ref[:, WQ:] = jnp.zeros((wq_ref.shape[0], WIN - WQ), jnp.bfloat16)
    for copy in weights:
        copy.wait()
    for g in range(4):

        @pl.when(y_at * 2 + x_at == g)
        def _(g=g):
            cols = slice(g * WQ, (g + 1) * WQ)
            wkv_ref[:, :WQ] = w_full[0, :, cols]
            wkv_ref[:, WQ:] = w_full[1, :, cols]
            wq_ref[:, :WQ] = w_full[2, :, cols] * jnp.bfloat16(DH ** (-0.5))

    hand_on = [
        pltpu.make_async_copy(wq_ref, wq_out, l_sem.at[5]),
        pltpu.make_async_copy(wkv_ref, wkv_out, l_sem.at[6]),
    ]
    for copy in hand_on:
        copy.start()

    def kv_rows(part_at, c):
        return kv.at[pl.ds((part_at * part + c * rows) // BLK, rows // BLK)]

    to_core, to_above, to_below, pass_up, pass_down = {}, {}, {}, {}, {}
    for c in range(8):
        mine = kv_rows(2, c)
        to_core[c] = remote(mine, kv_rows(3, c), k_send, k_recv, c, by_core)
        to_above[c] = remote(mine, kv_rows(0, c), up_send, up_recv, c, above)
        to_below[c] = remote(mine, kv_rows(4, c), dn_send, dn_recv, c, below)
        pass_up[c] = remote(kv_rows(0, c), kv_rows(1, c), f_send, f_recv, c, by_core)
        pass_down[c] = remote(kv_rows(4, c), kv_rows(5, c), g_send, g_recv, c, by_core)
    keeps = {
        c: pltpu.make_async_copy(
            tok_rows(c) if c < 2 else x_rows(c), x_out.at[pl.ds(c * rows, rows)], s_sem.at[c]
        )
        for c in range(8)
    }

    def relay(c):
        @pl.when(has_below)
        def _():
            to_above[c].wait_recv()
            pass_up[c].start()

        @pl.when(has_above)
        def _():
            to_below[c].wait_recv()
            pass_down[c].start()

    def tables(begin, end):
        slot_tables(
            plane,
            y_at,
            core,
            x_at,
            dict(piece_blocks=piece // BLK, seqs=len_ref.shape[0], begin=begin, end=end),
            len_ref,
            ord_ref,
            rand_sm,
            rand_two,
            idx_ref,
            live_ref,
        )

    query_blocks = part // BLK
    for n, c in enumerate(CHUNK_ORDER):
        if n == 2:
            rand_trade.wait()
            to_scalar = pltpu.make_async_copy(rand_got, rand_two, l_sem.at[0])
            to_scalar.start()
            to_scalar.wait()
            tables(0, query_blocks // 3)
        if n == 4:
            tables(query_blocks // 3, 2 * query_blocks // 3)
        if n == 6:
            tables(2 * query_blocks // 3, query_blocks)
        if c >= 2:
            hops[c].wait_recv()
        if c == 2:
            hops[6].start()
        if c == 5:
            hops[7].start()
        keeps[c].start()
        block = tok_ref[pl.ds(c * rows, rows), :] if c < 2 else xs[pl.ds((c - 2) * rows, rows), :]
        made = jnp.dot(block, wkv_ref[...], preferred_element_type=jnp.float32).astype(jnp.bfloat16)
        kv[pl.ds((2 * part + c * rows) // BLK, rows // BLK)] = made.reshape(rows // BLK, BLK, -1)

        @pl.when(has_above)
        def _(c=c):
            to_above[c].start()

        @pl.when(has_below)
        def _(c=c):
            to_below[c].start()

        to_core[c].start()
        q_ref[pl.ds(c * rows, rows), :] = jnp.dot(
            block, wq_ref[...], preferred_element_type=jnp.float32
        ).astype(jnp.bfloat16)
        if n >= 3:
            relay(CHUNK_ORDER[n - 3])
    for c in CHUNK_ORDER[5:]:
        relay(c)
    for c in range(8):
        to_core[c].wait_recv()

        @pl.when(has_above)
        def _(c=c):
            pass_down[c].wait_recv()

        @pl.when(has_below)
        def _(c=c):
            pass_up[c].wait_recv()

    saved = pltpu.make_async_copy(kv, kv_out, l_sem.at[1])
    saved.start()
    per = piece // BLK

    def part_of(turn):
        middle = turn - 2
        j = jnp.where(turn < 2, 3, jnp.where(turn < 6, 1 + lax.rem(turn, 2), 0))
        half = jnp.where(turn < 2, turn, jnp.where(turn < 6, middle // 2, turn - 6))
        return j, half

    def trade(turn):
        j, half = part_of(turn)
        span = pl.ds(pl.multiple_of(half * rows, rows), rows)
        return remote(
            ctx.at[j, span],
            ctx_out.at[span, pl.ds(pl.multiple_of(j * WIN, WIN), WIN)],
            o_send,
            o_recv,
            turn,
            device_at(plane, y_at ^ (j >> 1), core, x_at ^ (j & 1)),
        )

    def attend_part(turn, carry):
        j, half = part_of(turn)

        def step(n, carry):
            at = pl.ds(pl.multiple_of(n * BLK, BLK), BLK)
            ctx[j, at, :] = attend_block(j * per + n, idx_ref, live_ref, q_ref, kv, lse_ref)
            return carry

        first = half * (per // 2)
        for n in range(per // 2):
            step(first + n, 0)

        @pl.when(turn < 6)
        def _():
            trade(turn).start()

        return carry

    lax.fori_loop(0, 8, attend_part, 0)
    ctx_out[:, 0:WIN] = ctx[0]
    hand_on.append(pltpu.make_async_copy(ctx, ctx_keep, l_sem.at[7]))
    hand_on[-1].start()
    for c in (2, 4, 3, 5, 6, 7):
        hops[c].wait_send()
    for c in range(8):
        to_core[c].wait_send()
        keeps[c].wait()

        @pl.when(has_above)
        def _(c=c):
            to_above[c].wait_send()
            pass_down[c].wait_send()

        @pl.when(has_below)
        def _(c=c):
            to_below[c].wait_send()
            pass_up[c].wait_send()

    saved.wait()
    for copy in hand_on:
        copy.wait()

    def settle(turn, carry):
        trade(turn).wait()
        return carry

    lax.fori_loop(0, 6, settle, 0)


def forward_attention(tokens, w_query, w_key, w_value, lengths, seq_order, rand_row, planes):
    piece, width = tokens.shape
    dma, low = pltpu.SemaphoreType.DMA, jnp.bfloat16
    sds = jax.ShapeDtypeStruct
    blocks = 4 * piece // BLK
    return pl.pallas_call(
        functools.partial(forward_kernel, planes),
        out_shape=[
            sds((24 * piece // BLK, BLK, 2 * WQ), low),
            sds((4 * piece, WIN), low),
            sds((4 * piece, width), low),
            sds((piece, 4 * WIN), low),
            sds((blocks, WQ), jnp.float32),
            sds((blocks * SLOTS,), jnp.int32),
            sds((blocks * SLOTS,), jnp.int32),
            sds((width, WIN), low),
            sds((width, 2 * WQ), low),
            sds((4, piece, WIN), low),
        ],
        in_specs=[VMEM] + [ANY] * 3 + [SMEM] * 2 + [VMEM, SMEM],
        out_specs=[ANY, VMEM, ANY, VMEM, VMEM, SMEM, SMEM, ANY, ANY, ANY],
        scratch_shapes=[
            pltpu.VMEM((3 * piece, width), low),
            pltpu.VMEM((24 * piece // BLK, BLK, 2 * WQ), low),
            pltpu.VMEM((4, piece, WIN), low),
            pltpu.VMEM(rand_row.shape, jnp.int32),
            pltpu.SMEM(rand_row.shape, jnp.int32),
            pltpu.VMEM((3, width, width), low),
            pltpu.VMEM((width, WIN), low),
            pltpu.VMEM((width, 2 * WQ), low),
            dma((6,)),
            dma((6,)),
        ]
        + [dma((8,))] * 11
        + [dma((6,))] * 2
        + [dma((1,))] * 2
        + [dma((8,))],
        compiler_params=pltpu.CompilerParams(
            collective_id=0, has_side_effects=True, vmem_limit_bytes=62 << 20
        ),
        cost_estimate=pl.CostEstimate(
            flops=2 * 4 * piece * width * 640, bytes_accessed=40 << 20, transcendentals=0
        ),
        name="forward_attention",
    )(tokens, w_query, w_key, w_value, lengths, seq_order, rand_row, rand_row)


def attend_back(idx, live, queries, grads, context, level, keys_values):
    rows, width = keys_values.shape[0] // 6, keys_values.shape[1]
    count = queries.shape[0]
    kv_shape = jax.ShapeDtypeStruct((6 * rows, width), jnp.bfloat16)
    return pl.pallas_call(
        backward_kernel,
        out_shape=[jax.ShapeDtypeStruct((count, WIN), jnp.bfloat16)] + [kv_shape],
        in_specs=[SMEM, SMEM, VMEM, VMEM, VMEM, VMEM, ANY],
        out_specs=[VMEM] * 2,
        scratch_shapes=[
            pltpu.VMEM((6 * rows, width), jnp.bfloat16),
            pltpu.VMEM((6 * rows, width), jnp.float32),
            pltpu.SemaphoreType.DMA((1,)),
        ],
        compiler_params=pltpu.CompilerParams(vmem_limit_bytes=62 << 20),
        cost_estimate=pl.CostEstimate(
            flops=2 * 10 * count * 3 * 256 * 512, bytes_accessed=24 * rows * width, transcendentals=count * 3 * 512
        ),
        name="attend_back",
    )(idx, live, queries, grads, context, level, keys_values)


def reduce_kernel(planes, *refs):
    dkv_in, dq_in, x_in, wq_in, wkv_in, one_in = refs[:6]
    pair_in = refs[6:12]
    tok_out, q_out, k_out, v_out, up_out, side_out, norm_out, down_out = refs[12:20]
    own, core_in, z_out, z_in, g_all, dx_out, dx_in, acc = refs[20:28]
    dq, xs, wq, wkv, one = refs[28:33]
    p_slab, p_core, p_z, p_zin, p_fin, p_all = refs[33:39]
    keep, give = refs[39:42], refs[42:45]
    got, two, fin = refs[45:48], refs[48:51], refs[51:54]
    line_out, line_in = refs[54:57], refs[57:60]
    l_sem, i_sem, c_s, c_r, u_s, u_r, d_s, d_r, x_s, x_r = refs[60:70]
    pk_s, pk_r, pz_s, pz_r, pf_s, pf_r = refs[70:76]
    w2_s, w2_r, w3_s, w3_r, w4_s, w4_r, w1_s, w1_r = refs[76:84]
    plane, y_at, core, x_at = place()
    piece = tok_out.shape[0]
    part = 4 * piece
    rest = planes - 1
    group = y_at * 2 + x_at
    low, f32 = jnp.bfloat16, jnp.float32

    def there(j):
        return device_at(plane, y_at ^ (j >> 1), core, x_at ^ (j & 1))

    by_x, by_y = there(1), there(2)
    by_core = device_at(plane, y_at, 1 - core, x_at)
    others = [device_at(lax.rem(plane + g, planes), y_at, core, x_at) for g in range(1, planes)]
    has_above, has_below = plane < planes - 1, plane > 0
    above = device_at(plane + 1, y_at, core, x_at)
    below = device_at(plane - 1, y_at, core, x_at)

    def chunk(base, j):
        return pl.ds(pl.multiple_of(base + j * piece, piece), piece)

    def load_own(turn, r, j):
        return pltpu.make_async_copy(
            dkv_in.at[chunk(2 * r * part, j)], own.at[chunk(r * part, j)], l_sem.at[turn]
        )

    def to_core(turn, r, j):
        return remote(
            dkv_in.at[chunk((2 * r + 1) * part, j)],
            core_in.at[chunk(r * part, j)],
            c_s,
            c_r,
            turn,
            by_core,
        )

    def to_below(j):
        return remote(z_out.at[chunk(0, j)], z_in.at[chunk(0, j)], d_s, d_r, j, below)

    def to_above(j):
        return remote(z_out.at[chunk(part, j)], z_in.at[chunk(part, j)], u_s, u_r, j, above)

    def to_owner(j):
        return remote(dx_out.at[j - 1], dx_in.at[j - 1], x_s, x_r, j - 1, there(j))

    half_piece = piece // 2

    def pass_on(j):
        span = pl.ds((j - 1) * half_piece, half_piece)
        return remote(dx_out.at[2, span], dx_in.at[2, span], x_s, x_r, 1 + j, there(j))

    def take_in(j):
        span = pl.ds((j - 1) * half_piece, half_piece)
        pass_on(j).wait_recv()
        spot = 2 - j
        dx_out[spot, span, :] = (
            dx_out[spot, span, :].astype(f32) + dx_in[2, span, :].astype(f32)
        ).astype(low)
        to_owner(3 - j).start()

    def every(n, action):
        j = 3 - n
        for turn, r in ((n * 2, 0), (n * 2 + 1, 2)):
            action(turn, r, j)

    greet([by_x, by_y, there(3), by_core] + others)

    def begin(n, carry):
        def go(turn, r, j):
            to_core(turn, r, j).start()
            load_own(turn, r, j).start()

        every(n, go)
        return carry

    lax.fori_loop(0, 4, begin, 0)

    def begin_mid(n, carry):
        to_core(8 + n, 1, 3 - n).start()
        load_own(8 + n, 1, 3 - n).start()
        return carry

    lax.fori_loop(0, 4, begin_mid, 0)
    inputs = [(pair_in[2 * n], keep[n]) for n in range(3)]
    inputs += [(pair_in[2 * n + 1], give[n]) for n in (0, 2)]
    inputs += [(wq_in, wq), (wkv_in, wkv), (dq_in, dq), (x_in, xs), (one_in, one)]
    inputs = [pltpu.make_async_copy(src, dst, i_sem.at[n]) for n, (src, dst) in enumerate(inputs)]
    for copy in inputs:
        copy.start()
    w1 = remote(pair_in[3], give[1], w1_s, w1_r, 0, by_y)
    w1.start()

    def both(turn, r, j):
        to_core(turn, r, j).wait_recv()
        load_own(turn, r, j).wait()
        at = chunk(r * part, j)
        return own[at, :].astype(f32) + core_in[at, :].astype(f32)

    def spread(n, carry):
        j = 3 - n
        z_out[chunk(0, j), :] = both(2 * n, 0, j).astype(low)

        @pl.when(jnp.logical_and(has_below, n < 3))
        def _():
            to_below(j).start()

        z_out[chunk(part, j), :] = both(2 * n + 1, 2, j).astype(low)

        @pl.when(jnp.logical_and(has_above, n < 3))
        def _():
            to_above(j).start()

        return carry

    lax.fori_loop(0, 4, spread, 0)

    for copy in inputs[:5]:
        copy.wait()
    halves = [keep[0].shape[2] // 2, keep[1].shape[2] // 2]
    w2 = {}
    for n in (0, 2, 1):
        if n == 1:
            w1.wait()

        def merge(p, carry, n=n):
            keep[n][p] = (keep[n][p].astype(f32) + give[n][p].astype(f32)).astype(low)
            return carry

        lax.fori_loop(0, planes, merge, 0)
        if n < 2:
            cols = pl.ds(pl.multiple_of((1 - x_at) * halves[n], 128), halves[n])
            w2[n] = remote(keep[n].at[:, :, cols], got[n], w2_s, w2_r, n, by_x)
        else:
            w2[n] = remote(keep[n].at[:, 1 - y_at], got[n], w2_s, w2_r, n, by_y)
        w2[n].start()
    for copy in inputs[5:]:
        copy.wait()
    acc[...] = jnp.zeros_like(acc)

    def arrive(n):
        j = 3 - n
        g_all[:, 2 * WQ :] = dq[chunk(0, j), :]
        g_all[:, : 2 * WQ] = both(8 + n, 1, j).astype(low)

        @pl.when(has_above)
        def _():
            to_below(j).wait_recv()
            g_all[:, : 2 * WQ] = (
                g_all[:, : 2 * WQ].astype(f32) + z_in[chunk(0, j), :].astype(f32)
            ).astype(low)

        @pl.when(has_below)
        def _():
            to_above(j).wait_recv()
            g_all[:, : 2 * WQ] = (
                g_all[:, : 2 * WQ].astype(f32) + z_in[chunk(part, j), :].astype(f32)
            ).astype(low)

    def back(j):
        grads = g_all[...]
        return nt(grads[:, 2 * WQ :], wq[...]) + nt(grads[:, : 2 * WQ], wkv[...])

    def outer(j):
        acc[...] += tn(xs[chunk(0, j), :], g_all[...])

    def turn_back(n, carry):
        arrive(n)
        dx_out[2 - n] = back(3 - n).astype(low)
        outer(3 - n)
        return carry

    turn_back(0, 0)
    pass_on(1).start()
    pass_on(2).start()
    turn_back(1, 0)

    for n in range(3):
        w2[n].wait_recv()

        def halve(p, carry, n=n):
            if n < 2:
                cols = pl.ds(pl.multiple_of(x_at * halves[n], 128), halves[n])
                mine = keep[n][p, :, cols]
            else:
                mine = keep[n][p, y_at]
            two[n][p] = (mine.astype(f32) + got[n][p].astype(f32)).astype(low)
            return carry

        lax.fori_loop(0, planes, halve, 0)

    def line_copy(n, way, t):
        return remote(
            line_out[n].at[way, t],
            line_in[n].at[way, t],
            w3_s,
            w3_r,
            (n * 2 + way) * rest + t,
            below if way else above,
        )

    def line_step(t):
        for n in range(3):
            for way in range(2):
                spot = (planes - 1 - plane) if way else plane
                gap = planes - 1 - t
                slab = (plane - gap) if way else (plane + gap)
                sends = jnp.logical_and(t >= spot, spot < planes - 1)

                @pl.when(jnp.logical_and(sends, spot == 0))
                def _():
                    line_out[n][way, t] = two[n][slab]
                    line_copy(n, way, t).start()

                @pl.when(jnp.logical_and(sends, spot > 0))
                def _():
                    line_copy(n, way, t - 1).wait_recv()
                    line_out[n][way, t] = (
                        two[n][slab].astype(f32) + line_in[n][way, t - 1].astype(f32)
                    ).astype(low)
                    line_copy(n, way, t).start()

    line_step(0)

    @pl.when(has_below)
    def _():
        to_below(0).start()

    @pl.when(has_above)
    def _():
        to_above(0).start()

    take_in(1)
    turn_back(2, 0)
    take_in(2)
    if planes > 2:
        line_step(1)
    arrive(3)
    outer(0)

    share = p_slab.shape[3]
    acc[:, 2 * WQ :] *= DH ** (-0.5)
    for p in range(planes):
        for y in range(2):
            for k in range(2):
                at = ((p * 2 + y) * 2 + k) * share
                p_slab[k, p, y] = acc[at : at + share, :].astype(low)
    pk = remote(p_slab.at[1 - core], p_core, pk_s, pk_r, 0, by_core)
    pk.start()
    tok_out[...] = one[...] + back(0)
    pk.wait_recv()

    def merge_core(p, carry):
        p_z[p] = (p_slab[core, p].astype(f32) + p_core[p].astype(f32)).astype(low)
        return carry

    lax.fori_loop(0, planes, merge_core, 0)
    pz = [
        remote(
            p_z.at[lax.rem(plane + g, planes)], p_zin.at[g - 1], pz_s, pz_r, g - 1, others[g - 1]
        )
        for g in range(1, planes)
    ]

    def next_step(t, carry):
        line_step(t)
        return carry

    lax.fori_loop(2, planes - 1, next_step, 0)
    for copy in pz:
        copy.start()
    w4 = []
    for n in range(3):
        fin[n][x_at] = two[n][plane]

        @pl.when(has_below)
        def _(n=n):
            line_copy(n, 0, rest - 1).wait_recv()
            fin[n][x_at] = (
                fin[n][x_at].astype(f32) + line_in[n][0, rest - 1].astype(f32)
            ).astype(low)

        @pl.when(has_above)
        def _(n=n):
            line_copy(n, 1, rest - 1).wait_recv()
            fin[n][x_at] = (
                fin[n][x_at].astype(f32) + line_in[n][1, rest - 1].astype(f32)
            ).astype(low)

        w4.append(remote(fin[n].at[x_at], fin[n].at[x_at], w4_s, w4_r, n, by_x))
        w4[n].start()

    for j in (2, 1):
        to_owner(j).wait_recv()
        tok_out[...] += dx_in[j - 1].astype(f32)

    total = p_z[plane].astype(f32)
    for g in range(1, planes):
        pz[g - 1].wait_recv()
        total = total + p_zin[g - 1].astype(f32)
    p_fin[...] = total.astype(low)
    pf = [
        remote(p_fin.at[y_at ^ (j >> 1)], p_all.at[j], pf_s, pf_r, j - 1, there(j))
        for j in (1, 2, 3)
    ]
    for copy in pf:
        copy.start()
    p_all[0] = p_fin[y_at]

    for copy in pf:
        copy.wait()
    for a in range(4):
        grads = p_all[a ^ group].astype(f32)
        for n, dest in enumerate((k_out, v_out, q_out)):
            dest[:, a * WQ : (a + 1) * WQ] = grads[:, n * WQ : (n + 1) * WQ]
    for n, dest in ((0, up_out), (2, down_out)):
        w4[n].wait()
        width = dest.shape[1] // 2
        for side in range(2):
            dest[:, side * width : (side + 1) * width] = fin[n][side].astype(f32)
    w4[1].wait()
    width = side_out.shape[1] // 2
    for side in range(2):
        done = fin[1][side].astype(f32)
        side_out[:, side * width : (side + 1) * width] = done[:share]
        norm_out[:, side * width : (side + 1) * width] = done[share : share + 8]

    for copy in list(w2.values()) + pz + [pk]:
        copy.wait_send()

    def settle(n, carry):
        every(n, lambda turn, r, j: to_core(turn, r, j).wait_send())
        to_core(8 + n, 1, 3 - n).wait_send()

        @pl.when(has_below)
        def _():
            to_below(3 - n).wait_send()

        @pl.when(has_above)
        def _():
            to_above(3 - n).wait_send()

        return carry

    lax.fori_loop(0, 4, settle, 0)
    for j in (1, 2):
        to_owner(j).wait_send()
        pass_on(j).wait_send()

    def settle_line(t, carry):
        for n in range(3):
            for way in range(2):
                spot = (planes - 1 - plane) if way else plane

                @pl.when(jnp.logical_and(t >= spot, spot < planes - 1))
                def _():
                    line_copy(n, way, t).wait_send()

        return carry

    lax.fori_loop(0, planes - 1, settle_line, 0)


def reduce_all(dkv, dq, stretch, wq, wkv, one, up, out, down, planes):
    low, f32 = jnp.bfloat16, jnp.float32
    piece = dq.shape[0] // 4
    width = stretch.shape[1]
    share = up[0].shape[1]
    rest = planes - 1
    dma, vm, sds = pltpu.SemaphoreType.DMA, pltpu.VMEM, jax.ShapeDtypeStruct
    cols = 2 * WQ + WIN
    tall = out[0].shape[1]
    wide = up[0].shape[2]
    kinds = [(share, wide // 2), (tall, width // 2), down[0].shape[2:]]
    pairs = [up[0].shape, out[0].shape, down[0].shape]
    return pl.pallas_call(
        functools.partial(reduce_kernel, planes),
        out_shape=[sds((piece, width), f32)]
        + [sds((share, width), f32)] * 3
        + [
            sds((share, wide), f32),
            sds((share, width), f32),
            sds((8, width), f32),
            sds((kinds[2][0], width), f32),
        ],
        in_specs=[ANY] * 12,
        out_specs=[VMEM] * 8,
        scratch_shapes=[
            vm((12 * piece, 2 * WQ), low),
            vm((12 * piece, 2 * WQ), low),
            vm((8 * piece, 2 * WQ), low),
            vm((8 * piece, 2 * WQ), low),
            vm((piece, cols), low),
            vm((3, piece, width), low),
            vm((3, piece, width), low),
            vm((width, cols), f32),
            vm(dq.shape, low),
            vm(stretch.shape, low),
            vm(wq.shape, low),
            vm(wkv.shape, low),
            vm(one.shape, f32),
            vm((2, planes, 2, share, cols), low),
            vm((planes, 2, share, cols), low),
            vm((planes, 2, share, cols), low),
            vm((rest, 2, share, cols), low),
            vm((2, share, cols), low),
            vm((4, share, cols), low),
        ]
        + [vm(p, low) for p in pairs] * 2
        + [vm((planes,) + k, low) for k in kinds] * 2
        + [vm((2,) + k, low) for k in kinds]
        + [vm((2, rest) + k, low) for k in kinds] * 2
        + [dma((12,)), dma((11,))]
        + [dma((12,))] * 2
        + [dma((4,))] * 6
        + [dma((1,))] * 2
        + [dma((rest,))] * 2
        + [dma((3,))] * 2
        + [dma((3,))] * 2
        + [dma((6 * rest,))] * 2
        + [dma((3,))] * 2
        + [dma((1,))] * 2,
        compiler_params=pltpu.CompilerParams(
            collective_id=1, has_side_effects=True, vmem_limit_bytes=60 << 20
        ),
        cost_estimate=pl.CostEstimate(
            flops=4 * 4 * piece * width * cols, bytes_accessed=40 << 20, transcendentals=0
        ),
        name="reduce_all",
    )(dkv, dq, stretch, wq, wkv, one, up[0], up[1], out[0], out[1], down[0], down[1])


def dense_kernel(
    planes,
    tok_ref,
    ctx_ref,
    cot_ref,
    g1_ref,
    b1_ref,
    g2_ref,
    b2_ref,
    wout_in,
    wup_in,
    wdown_in,
    *refs,
):
    out_ref, one_ref, do_out, up_keep, up_give, out_keep, out_give, down_keep, down_give = refs[:9]
    wup, wdown, acc, x1, s1, g_two, nl, hid, slope, gp, gm, ga = refs[9:21]
    dctx, up_loc, out_loc, down_loc, up_got, out_got, down_got, down_sum = refs[21:29]
    w_sem, mv_sem, do_s, do_r, up_s, up_r, out_s, out_r, down_s, down_r = refs[29:39]
    wout_ref = refs[39]
    plane, y_at, core, x_at = place()
    piece, width = tok_ref.shape
    share = up_loc.shape[2]
    slab = down_loc.shape[2]
    pairs = 2 * planes
    group = y_at * 2 + x_at
    f32 = jnp.float32
    fetch = [
        pltpu.make_async_copy(
            wout_in.at[pl.ds(pl.multiple_of((group ^ j) * WQ, WQ), WQ)],
            wout_ref.at[pl.ds(j * WIN + WIN - WQ, WQ)],
            w_sem.at[2 + j],
        )
        for j in range(4)
    ]
    for copy in fetch:
        copy.start()
    bring = [
        pltpu.make_async_copy(wup_in, wup, w_sem.at[0]),
        pltpu.make_async_copy(wdown_in, wdown, w_sem.at[1]),
    ]
    for copy in bring:
        copy.start()

    def there(j):
        return device_at(plane, y_at ^ (j >> 1), core, x_at ^ (j & 1))

    by_core = device_at(plane, y_at, 1 - core, x_at)
    height, tile = 32, 2 * WQ
    wide = wup.shape[1]

    def rows_of(n):
        return pl.ds(pl.multiple_of(n * height, height), height)

    def cols_of(n):
        return pl.ds(pl.multiple_of(n * tile, tile), tile)

    def mean(v):
        return jnp.mean(v, axis=1, keepdims=True)

    def fold(v):
        return v[:8] + v[8:16] + v[16:24] + v[24:]

    for j in range(4):
        wout_ref[j * WIN : j * WIN + WIN - WQ, :] = jnp.zeros((WIN - WQ, width), jnp.bfloat16)
    for copy in fetch:
        copy.wait()
    acc[...] = jnp.dot(ctx_ref[...], wout_ref[...], preferred_element_type=f32)
    g1, b1, g2, b2 = (r[...].reshape(1, width) for r in (g1_ref, b1_ref, g2_ref, b2_ref))

    def norm_one(n, carry):
        at = rows_of(n)
        value = tok_ref[at, :].astype(f32) + acc[at, :]
        center = value - mean(value)
        inverse = lax.rsqrt(mean(center * center) + eps_norm)
        hat = center * inverse
        x1[at, :] = hat
        s1[at, :] = jnp.broadcast_to(inverse, (height, 128))
        nl[at, :] = (hat * g1 + b1).astype(jnp.bfloat16)
        return carry

    lax.fori_loop(0, piece // height, norm_one, 0, unroll=4)
    bring[0].wait()

    def expand(n, carry):
        at = cols_of(n)
        pre = jnp.dot(nl[...], wup[:, at], preferred_element_type=f32)
        square = pre * pre
        bend = jnp.tanh(pre * (0.7978845608028654 + 0.035677408136300125 * square))
        half_up = 0.5 + 0.5 * bend
        value = pre * half_up
        hid[:, at] = value.astype(jnp.bfloat16)
        slope[:, at] = half_up + value * (1.0 - bend) * (
            0.7978845608028654 + 0.10703222440890037 * square
        )
        return carry

    lax.fori_loop(0, wide // tile, expand, 0, unroll=2)
    bring[1].wait()
    acc[...] = jnp.dot(hid[...], wdown[...], preferred_element_type=f32)
    nothing = jnp.zeros((8, width), f32)

    def norm_two(n, carry):
        gain_sum, shift_sum = carry
        at = rows_of(n)
        value = x1[at, :] * g1 + b1 + acc[at, :]
        center = value - mean(value)
        inverse = lax.rsqrt(mean(center * center) + eps_norm)
        hat = center * inverse
        out_ref[at, :] = (hat * g2 + b2).astype(jnp.bfloat16)
        cot = cot_ref[at, :].astype(f32)
        gain_sum, shift_sum = gain_sum + fold(cot * hat), shift_sum + fold(cot)
        up = cot * g2
        grad = inverse * (up - mean(up) - hat * mean(up * hat))
        g_two[at, :] = grad
        gm[at, :] = grad.astype(jnp.bfloat16)
        return gain_sum, shift_sum

    gain_two, shift_two = lax.fori_loop(0, piece // height, norm_two, (nothing, nothing), unroll=4)

    def shrink(n, carry):
        at = cols_of(n)
        back = nt(gm[...], wdown[at, :])
        gp[:, at] = (back * slope[:, at]).astype(jnp.bfloat16)
        return carry

    lax.fori_loop(0, wide // tile, shrink, 0, unroll=2)
    acc[...] = nt(gp[...], wup[...])

    def norm_three(n, carry):
        gain_sum, shift_sum = carry
        at = rows_of(n)
        grad_in, hat = g_two[at, :] + acc[at, :], x1[at, :]
        gain_sum, shift_sum = gain_sum + fold(grad_in * hat), shift_sum + fold(grad_in)
        up = grad_in * g1
        grad = s1[at, 0:1] * (up - mean(up) - hat * mean(up * hat))
        one_ref[at, :] = grad
        ga[at, :] = grad.astype(jnp.bfloat16)
        return gain_sum, shift_sum

    gain_one, shift_one = lax.fori_loop(
        0, piece // height, norm_three, (nothing, nothing), unroll=4
    )
    side = jnp.concatenate(
        [jnp.sum(v, axis=0, keepdims=True) for v in (gain_one, shift_one, gain_two, shift_two)]
        + [jnp.zeros((12, width), f32)],
        axis=0,
    ).astype(jnp.bfloat16)

    low = jnp.bfloat16
    greet([there(1), there(2), there(3), by_core])
    trades = []
    for j in (3, 1, 2, 0):
        part = nt(ga[...], wout_ref[pl.ds(j * WIN, WIN), :]).astype(low)
        if j:
            dctx[j - 1] = part
            trades.append(
                remote(
                    dctx.at[j - 1], do_out.at[pl.ds(j * piece, piece)], do_s, do_r, j - 1, there(j)
                )
            )
            trades[-1].start()
        else:
            do_out[pl.ds(0, piece), :] = part

    tile = 2 * WQ
    per = tile // (2 * slab)
    tiles = wide // tile

    def down_copy(t):
        span = pl.ds(t * per, per)
        return remote(down_loc.at[1 - core, span], down_got.at[span], down_s, down_r, t, by_core)

    def up_copy(t):
        span = cols_of(t)
        return remote(
            up_loc.at[1 - core, :, :, span], up_got.at[:, :, span], up_s, up_r, t, by_core
        )

    def make_down(t, carry):
        cell = tn(hid[:, cols_of(t)], gm[...])
        for n in range(per):
            for k in range(2):
                at = (n * 2 + k) * slab
                down_loc[k, t * per + n] = cell[at : at + slab].astype(low)
        down_copy(t).start()
        return carry

    lax.fori_loop(0, tiles, make_down, 0)

    def make_up(t, carry):
        cell = tn(nl[...], gp[:, cols_of(t)])
        for q in range(pairs):
            for k in range(2):
                at = (q * 2 + k) * share
                up_loc[k, q, :, cols_of(t)] = cell[at : at + share].astype(low)
        up_copy(t).start()
        return carry

    lax.fori_loop(0, tiles, make_up, 0)
    moved = []

    def move(source, dest):
        moved.append(pltpu.make_async_copy(source, dest, mv_sem.at[len(moved)]))
        moved[-1].start()

    half = width // 2

    def sum_down(t, carry):
        down_copy(t).wait_recv()
        for n in range(per):
            q = t * per + n
            total = (
                down_loc[core, q].astype(jnp.float32) + down_got[q].astype(jnp.float32)
            ).astype(low)
            down_sum[0, q] = total[:, :half]
            down_sum[1, q] = total[:, half:]
        return carry

    lax.fori_loop(0, tiles, sum_down, 0)
    move(down_sum.at[x_at], down_keep)
    move(down_sum.at[1 - x_at], down_give)

    per_group = pairs // 4
    for j in range(4):
        cell = tn(ctx_ref[:, j * WIN : (j + 1) * WIN], ga[...])
        for n in range(per_group):
            for k in range(2):
                at = WIN - WQ + (n * 2 + k) * share
                out_loc[k, (group ^ j) * per_group + n, :share, :] = cell[at : at + share].astype(low)
    for q in range(pairs):
        for k in range(2):
            out_loc[k, q, share:, :] = side
    outs = remote(out_loc.at[1 - core], out_got, out_s, out_r, 0, by_core)
    outs.start()

    def sum_up(q, carry):
        up_got[q] = (up_loc[core, q].astype(jnp.float32) + up_got[q].astype(jnp.float32)).astype(low)
        return carry

    for t in range(tiles):
        up_copy(t).wait_recv()
    lax.fori_loop(0, pairs, sum_up, 0)
    outs.wait_recv()
    for p in range(planes):
        for y in range(2):
            q = p * 2 + y
            out_got[q] = (
                out_loc[core, q].astype(jnp.float32) + out_got[q].astype(jnp.float32)
            ).astype(low)
        for got, keep, give in ((up_got, up_keep, up_give), (out_got, out_keep, out_give)):
            move(got.at[p * 2 + y_at], keep.at[p])
            move(got.at[p * 2 + 1 - y_at], give.at[p])
    for copy in trades:
        copy.wait()
    for t in range(tiles):
        down_copy(t).wait_send()
        up_copy(t).wait_send()
    outs.wait_send()
    for copy in moved:
        copy.wait()


def dense_layers(tokens, ctx, cotangent, norms, wout, w_up, w_down, planes):
    low = jnp.bfloat16
    piece, width = tokens.shape
    pairs = 2 * planes
    wide = w_up.shape[1]
    share, slab, tall = width // (2 * pairs), wide // (2 * pairs), 16
    sds, vm, dma = jax.ShapeDtypeStruct, pltpu.VMEM, pltpu.SemaphoreType.DMA
    up, out = (planes, share, wide), (planes, share + tall, width)
    down = (pairs, slab, width // 2)
    tiles = wide // (2 * WQ)
    f32 = jnp.float32
    return pl.pallas_call(
        functools.partial(dense_kernel, planes),
        out_shape=[sds((piece, width), low), sds((piece, width), f32), sds((4 * piece, WIN), low)]
        + [sds(up, low)] * 2
        + [sds(out, low)] * 2
        + [sds(down, low)] * 2,
        in_specs=[VMEM] * 7 + [ANY] * 3,
        out_specs=[VMEM] * 3 + [ANY] * 6,
        scratch_shapes=[
            vm(w_up.shape, low),
            vm(w_down.shape, low),
            vm((piece, width), f32),
            vm((piece, width), f32),
            vm((piece, 128), f32),
            vm((piece, width), f32),
            vm((piece, width), low),
            vm((piece, wide), low),
            vm((piece, wide), f32),
            vm((piece, wide), low),
            vm((piece, width), low),
            vm((piece, width), low),
            vm((3, piece, WIN), low),
            vm((2, pairs, share, wide), low),
            vm((2, pairs, share + tall, width), low),
            vm((2, pairs, slab, width), low),
            vm((pairs, share, wide), low),
            vm((pairs, share + tall, width), low),
            vm((pairs, slab, width), low),
            vm((2, pairs, slab, width // 2), low),
            dma((6,)),
            dma((2 + 4 * planes,)),
        ]
        + [dma((3,))] * 2
        + [dma((tiles,))] * 2
        + [dma((1,))] * 2
        + [dma((tiles,))] * 2
        + [vm((4 * WIN, width), low)],
        compiler_params=pltpu.CompilerParams(
            collective_id=2, has_side_effects=True, vmem_limit_bytes=63 << 20
        ),
        cost_estimate=pl.CostEstimate(
            flops=2 * piece * width * (6 * wide + 3072), bytes_accessed=30 << 20, transcendentals=0
        ),
        name="dense_layers",
    )(tokens, ctx, cotangent, *norms, wout, w_up, w_down)


def finish_kernel(share, count, *refs):
    sources, rows_ref, dests = refs[:count], refs[count], refs[count + 1 : 2 * count + 1]
    parts = refs[2 * count + 1 : 2 * count + 5]
    held, sems = refs[2 * count + 5 : 3 * count + 5], refs[3 * count + 5]
    reads = [pltpu.make_async_copy(sources[n], held[n], sems.at[0, n]) for n in range(count)]
    writes = [pltpu.make_async_copy(held[n], dests[n], sems.at[1, n]) for n in range(count)]
    for copy in reads:
        copy.start()
    for n in range(count):
        reads[n].wait()
        writes[n].start()
    seq_at = lax.axis_index("seq")
    rows = rows_ref[...]
    width = rows.shape[1]
    spot = lax.broadcasted_iota(jnp.int32, (width, 128), 0) - seq_at * share
    chosen = (spot == lax.broadcasted_iota(jnp.int32, (width, 128), 1)).astype(jnp.float32)
    picked = jnp.dot(
        rows, chosen, preferred_element_type=jnp.float32, precision=lax.Precision.HIGHEST
    )
    for n in range(4):
        parts[n][...] = picked[n, :share]
    for copy in writes:
        copy.wait()


def finish(arrays, norm_rows, share):
    sds, count = jax.ShapeDtypeStruct, len(arrays)
    return pl.pallas_call(
        functools.partial(finish_kernel, share, count),
        out_shape=[sds(v.shape, v.dtype) for v in arrays] + [sds((share,), jnp.float32)] * 4,
        in_specs=[ANY] * count + [VMEM],
        out_specs=[ANY] * count + [VMEM] * 4,
        scratch_shapes=[pltpu.VMEM(v.shape, v.dtype) for v in arrays]
        + [pltpu.SemaphoreType.DMA((2, count))],
        compiler_params=pltpu.CompilerParams(vmem_limit_bytes=62 << 20),
        name="finish",
    )(*arrays, norm_rows)


def body(
    tokens,
    w_query,
    w_key,
    w_value,
    w_out,
    gain_attn,
    shift_attn,
    w_up,
    w_down,
    gain_mlp,
    shift_mlp,
    cotangent,
    lengths,
    seq_order,
    rand_blocks,
):
    piece, width = tokens.shape
    seqs, heads = lax.axis_size("seq"), lax.axis_size("head")
    planes = seqs // 4
    assert heads == 2 and 8 * piece == MAXB * BLK and width == 4 * WQ
    seq_at, x_at = lax.axis_index("seq"), lax.axis_index("head")
    plane, y_at, core = seq_at // 4, (seq_at // 2) % 2, seq_at % 2
    group = y_at * 2 + x_at

    keys_values, queries, stretch, context_tok, level, idx, live, wq_own, wkv_own, ctx_own = (
        forward_attention(
            tokens, w_query, w_key, w_value, lengths, seq_order, rand_blocks.T, planes
        )
    )
    share = width // seqs
    norms = [gain_attn, shift_attn, gain_mlp, shift_mlp]
    output, grad_one, grad_ctx, up_keep, up_give, out_keep, out_give, down_keep, down_give = (
        dense_layers(tokens, context_tok, cotangent, norms, w_out, w_up, w_down, planes)
    )
    up_pair = (up_keep, xor_swap(up_give, 4))
    out_pair = (out_keep, out_give)
    two_y = (planes, 2) + down_keep.shape[1:]
    down_pair = (down_keep.reshape(two_y), xor_swap(down_give, 1).reshape(two_y))

    grad_q, grad_kv = attend_back(
        idx,
        live,
        queries,
        grad_ctx,
        ctx_own.reshape(-1, WIN),
        level,
        keys_values.reshape(-1, 2 * WQ),
    )
    grad_tokens, grad_wq, grad_wk, grad_wv, up_total, out_total, norm_rows, down_total = reduce_all(
        grad_kv,
        grad_q,
        stretch,
        wq_own,
        wkv_own,
        grad_one,
        up_pair,
        out_pair,
        down_pair,
        planes,
    )

    finals = finish(
        (output, grad_tokens, grad_wq, grad_wk, grad_wv, out_total, up_total, down_total),
        norm_rows,
        share,
    )

    output, grad_tokens, grad_wq, grad_wk, grad_wv, grad_out, grad_up, grad_down = finals[:8]
    gain_one, shift_one, gain_two, shift_two = finals[8:]
    return (
        output,
        grad_tokens,
        grad_wq,
        grad_wk,
        grad_wv,
        grad_out,
        gain_one,
        shift_one,
        grad_up,
        grad_down,
        gain_two,
        shift_two,
    )


def solution(mesh):
    rows = P(("seq", "head"), None)
    seq_rows, seq_only = P("seq", None), P("seq")
    return jax.shard_map(
        body,
        mesh=mesh,
        in_specs=(rows,) + (P(),) * 10 + (rows, P(), P(), seq_rows),
        out_specs=(
            rows,
            rows,
            seq_rows,
            seq_rows,
            seq_rows,
            seq_rows,
            seq_only,
            seq_only,
            seq_rows,
            seq_rows,
            seq_only,
            seq_only,
        ),
        check_vma=False,
    )
```

```python
import functools

import jax
import jax.numpy as jnp
from jax import lax
from jax.experimental import pallas as pl
from jax.experimental.pallas import tpu as pltpu
from jax.sharding import PartitionSpec as P

DH = 64
BLK = 64
MAXB = 64
SLOTS = 8
HG = 3
WQ = HG * DH
WIN = 256
AXES = ("seq", "head")
NEG = -1e30

eps_norm = 1e-06


def xor_swap(value, bits):
    count = lax.axis_size("seq") * lax.axis_size("head")
    return lax.ppermute(value, AXES, [(d, d ^ bits) for d in range(count)])


def lane_groups(rows, offset):
    lane = lax.broadcasted_iota(jnp.int32, (rows, WIN), 1) - offset
    return [jnp.logical_and(lane >= h * DH, lane < (h + 1) * DH) for h in range(HG)]


def spread_heads(block, offset):
    zero = jnp.zeros_like(block)
    return jnp.concatenate([jnp.where(m, block, zero) for m in lane_groups(BLK, offset)], axis=0)


def fold_heads(stacked, offset):
    masks = lane_groups(BLK, offset)
    total = jnp.where(masks[0], stacked[:BLK], 0.0)
    for h in range(1, HG):
        total = total + jnp.where(masks[h], stacked[h * BLK : (h + 1) * BLK], 0.0)
    return total


def nt(a, b):
    return lax.dot_general(a, b, (((1,), (1,)), ((), ())), preferred_element_type=jnp.float32)


def tn(a, b):
    return lax.dot_general(a, b, (((0,), (0,)), ((), ())), preferred_element_type=jnp.float32)


def backward_kernel(idx_ref, live_ref, q_ref, do_ref, o_ref, lse_ref, *refs):
    kv_ref, dq_ref, dkv_ref, kv, acc, sems = refs

    def clear(n, carry):
        acc[pl.ds(pl.multiple_of(n * 256, 256), 256), :] = jnp.zeros((256, 2 * WQ), jnp.float32)
        return carry

    copy = pltpu.make_async_copy(kv_ref, kv, sems.at[0])
    copy.start()
    lax.fori_loop(0, acc.shape[0] // 256, clear, 0)
    copy.wait()

    def step(i, carry):
        q_rows = pl.multiple_of(i * BLK, BLK)
        qexp = spread_heads(q_ref[pl.ds(q_rows, BLK), :], 0)
        doexp = spread_heads(do_ref[pl.ds(q_rows, BLK), :], 64)
        rows = [
            pl.multiple_of(idx_ref[i * SLOTS + s] * BLK, BLK) for s in range(SLOTS)
        ]
        keys = jnp.concatenate([kv[pl.ds(r, BLK), 0:WIN] for r in rows], axis=0)
        values = jnp.concatenate([kv[pl.ds(r, BLK), 128 : 128 + WIN] for r in rows], axis=0)
        product = do_ref[pl.ds(q_rows, BLK), :].astype(jnp.float32) * o_ref[
            pl.ds(q_rows, BLK), :
        ].astype(jnp.float32)
        high = product.astype(jnp.bfloat16)
        ones = jnp.ones((8, WIN), jnp.bfloat16)
        inner = nt(ones, spread_heads(high, 64)) + nt(
            ones, spread_heads((product - high.astype(jnp.float32)).astype(jnp.bfloat16), 64)
        )
        inner = inner[0:1]
        level = lse_ref[pl.ds(i, 1), :]
        raw = nt(keys, qexp)
        grad_probs = nt(values, doexp)
        probs, grad_scores = [], []
        for s in range(SLOTS):
            at = slice(s * BLK, (s + 1) * BLK)
            off = level + jnp.where(live_ref[i * SLOTS + s] > 0, 0.0, -NEG)
            p = jnp.exp(raw[at] - off)
            probs.append(p.astype(jnp.bfloat16))
            grad_scores.append((p * (grad_probs[at] - inner)).astype(jnp.bfloat16))
        probs = jnp.concatenate(probs, axis=0)
        grad_scores = jnp.concatenate(grad_scores, axis=0)
        dk = jnp.dot(grad_scores, qexp, preferred_element_type=jnp.float32)
        dv = jnp.dot(probs, doexp, preferred_element_type=jnp.float32)
        dq = tn(grad_scores, keys)
        dq_ref[pl.ds(q_rows, BLK), :] = fold_heads(dq, 0).astype(jnp.bfloat16)
        for s in range(SLOTS):
            k_s, v_s = dk[s * BLK : (s + 1) * BLK], dv[s * BLK : (s + 1) * BLK]
            at = pl.ds(rows[s], BLK)
            acc[at, 0:128] += k_s[:, :128]
            acc[at, 128:256] += k_s[:, 128:] + v_s[:, :128]
            acc[at, 256:384] += v_s[:, 128:]
        return carry

    lax.fori_loop(0, q_ref.shape[0] // BLK, step, 0, unroll=8)

    def emit(n, carry):
        at = pl.ds(pl.multiple_of(n * 256, 256), 256)
        dkv_ref[at, :] = acc[at, :].astype(jnp.bfloat16)
        return carry

    lax.fori_loop(0, acc.shape[0] // 256, emit, 0)


VMEM = pl.BlockSpec(memory_space=pltpu.VMEM)
SMEM = pl.BlockSpec(memory_space=pltpu.SMEM)
ANY = pl.BlockSpec(memory_space=pl.ANY)


def device_at(plane, y_at, core, x_at):
    return (plane * 4 + y_at * 2 + core, x_at)


def place():
    seq_at, x_at = lax.axis_index("seq"), lax.axis_index("head")
    return seq_at // 4, (seq_at // 2) % 2, seq_at % 2, x_at


def remote(src, dst, sems, recvs, at, device):
    return pltpu.make_async_remote_copy(
        src_ref=src,
        dst_ref=dst,
        send_sem=sems.at[at],
        recv_sem=recvs.at[at],
        device_id=device,
        device_id_type=pl.DeviceIdType.MESH,
    )


def greet(partners):
    barrier = pltpu.get_barrier_semaphore()
    for device in partners:
        pl.semaphore_signal(
            barrier, inc=1, device_id=device, device_id_type=pl.DeviceIdType.MESH
        )
    pl.semaphore_wait(barrier, len(partners))


CHUNK_ORDER = (0, 1, 2, 4, 3, 5, 6, 7)


def slot_tables(plane, y_at, core, x_at, at, lengths, order, rand_own, rand_got, idx_ref, live_ref):
    per = at["piece_blocks"]

    def one(i, carry):
        far, near = i // per, i % per
        y_of, x_of = y_at ^ (far >> 1), x_at ^ (far & 1)
        block = plane * MAXB + y_of * (4 * per) + core * (2 * per) + x_of * per + near
        begin, first, span = jnp.int32(0), jnp.int32(0), jnp.int32(1)
        for m in range(at["seqs"]):
            size = lengths[order[m]]
            inside = begin <= block
            first = jnp.where(inside, begin, first)
            span = jnp.where(inside, size, span)
            begin = begin + size
        row = x_of * per + near
        draws = []
        for n in range(SLOTS - 5):
            draw = jnp.where(far >= 2, rand_got[n, row], rand_own[n, row])
            for power in range(16, -1, -1):
                multiple = span * (1 << power)
                draw = jnp.where(draw >= multiple, draw - multiple, draw)
            draws.append(first + draw)
        candidates = [block - 1, block, block + 1, first, first + span - 1] + draws
        kept = []
        for s in range(SLOTS):
            alive = jnp.int32(1)
            if s == 0:
                alive = (block > first).astype(jnp.int32)
            if s == 2:
                alive = (block < first + span - 1).astype(jnp.int32)
            for e in range(s):
                same = (candidates[e] == candidates[s]).astype(jnp.int32)
                alive = alive * (1 - kept[e] * same)
            kept.append(alive)
            key = jnp.where(alive > 0, candidates[s], block)
            rel = key // MAXB - plane + 1
            inner = key % MAXB
            y_key, rest = inner // (4 * per), inner % (4 * per)
            core_key, rest = rest // (2 * per), rest % (2 * per)
            x_key, near_key = rest // per, rest % per
            spot = (rel * 2 + (core_key ^ core)) * 4 + ((y_key ^ y_at) * 2 + (x_key ^ x_at))
            idx_ref[i * SLOTS + s] = jnp.clip(spot * per + near_key, 0, 24 * per - 1)
            live_ref[i * SLOTS + s] = alive
        return carry

    lax.fori_loop(at["begin"], at["end"], one, 0)


def attend_block(i, idx_ref, live_ref, q_ref, kv, lse_ref):
    qexp = spread_heads(q_ref[pl.ds(pl.multiple_of(i * BLK, BLK), BLK), :], 0)
    at = [idx_ref[i * SLOTS + s] for s in range(SLOTS)]
    off = [jnp.where(live_ref[i * SLOTS + s] > 0, 0.0, -NEG) for s in range(SLOTS)]
    keys = jnp.concatenate([kv[r, :, 0:WIN] for r in at], axis=0)
    values = jnp.concatenate([kv[r, :, 128 : 128 + WIN] for r in at], axis=0)
    raw = nt(keys, qexp)
    parts = [raw[s * BLK : (s + 1) * BLK] for s in range(SLOTS)]
    top = jnp.max(parts[1], axis=0, keepdims=True)
    for s in range(SLOTS):
        top = jnp.maximum(top, jnp.max(parts[s], axis=0, keepdims=True) - off[s])
    e = [jnp.exp(parts[s] - (top + off[s])) for s in range(SLOTS)]
    total = jnp.sum(e[0], axis=0, keepdims=True)
    for s in range(1, SLOTS):
        total = total + jnp.sum(e[s], axis=0, keepdims=True)
    lse_ref[pl.ds(i, 1), :] = top + jnp.log(total)
    scale = 1.0 / total
    probs = jnp.concatenate([(v * scale).astype(jnp.bfloat16) for v in e], axis=0)
    return fold_heads(tn(probs, values), 64).astype(jnp.bfloat16)


def forward_kernel(planes, tok_ref, wq_in, wk_in, wv_in, len_ref, ord_ref, rand_vm, rand_sm, *refs):
    kv_out, q_ref, x_out, ctx_out, lse_ref, idx_ref, live_ref, wq_out, wkv_out, ctx_keep = refs[:10]
    xs, kv, ctx, rand_got, rand_two, w_full, wq_ref, wkv_ref = refs[10:18]
    x_send, x_recv, k_send, k_recv, up_send, up_recv, dn_send, dn_recv = refs[18:26]
    f_send, f_recv, g_send, g_recv, s_sem, o_send, o_recv, r_send, r_recv, l_sem = refs[26:36]
    weights = [
        pltpu.make_async_copy(w, w_full.at[n], l_sem.at[2 + n])
        for n, w in enumerate((wk_in, wv_in, wq_in))
    ]
    for copy in weights:
        copy.start()
    plane, y_at, core, x_at = place()
    piece = tok_ref.shape[0]
    rows = piece // 2
    part = 4 * piece
    by_x = device_at(plane, y_at, core, 1 - x_at)
    by_y = device_at(plane, 1 - y_at, core, x_at)
    by_xy = device_at(plane, 1 - y_at, core, 1 - x_at)
    by_core = device_at(plane, y_at, 1 - core, x_at)
    above = device_at(plane + 1, y_at, core, x_at)
    below = device_at(plane - 1, y_at, core, x_at)
    has_above, has_below = plane < planes - 1, plane > 0
    ring = [device_at(lax.rem(plane + g, planes), y_at, core, x_at) for g in (1, planes - 1)]
    greet([by_x, by_y, by_xy, by_core] + ring)

    def x_rows(c):
        return xs.at[pl.ds((c - 2) * rows, rows)]

    def tok_rows(c):
        return tok_ref.at[pl.ds(c * rows, rows)]

    hops = {
        2: remote(tok_rows(0), x_rows(2), x_send, x_recv, 0, by_x),
        4: remote(tok_rows(0), x_rows(4), x_send, x_recv, 2, by_y),
        3: remote(tok_rows(1), x_rows(3), x_send, x_recv, 1, by_x),
        5: remote(tok_rows(1), x_rows(5), x_send, x_recv, 3, by_y),
        6: remote(x_rows(2), x_rows(6), x_send, x_recv, 4, by_y),
        7: remote(x_rows(5), x_rows(7), x_send, x_recv, 5, by_x),
    }
    rand_trade = remote(rand_vm, rand_got, r_send, r_recv, 0, by_y)
    rand_trade.start()
    for c in (2, 4, 3, 5):
        hops[c].start()

    wq_ref[:, WQ:] = jnp.zeros((wq_ref.shape[0], WIN - WQ), jnp.bfloat16)
    for copy in weights:
        copy.wait()
    for g in range(4):

        @pl.when(y_at * 2 + x_at == g)
        def _(g=g):
            cols = slice(g * WQ, (g + 1) * WQ)
            wkv_ref[:, :WQ] = w_full[0, :, cols]
            wkv_ref[:, WQ:] = w_full[1, :, cols]
            wq_ref[:, :WQ] = w_full[2, :, cols] * jnp.bfloat16(DH ** (-0.5))

    hand_on = [
        pltpu.make_async_copy(wq_ref, wq_out, l_sem.at[5]),
        pltpu.make_async_copy(wkv_ref, wkv_out, l_sem.at[6]),
    ]
    for copy in hand_on:
        copy.start()

    def kv_rows(part_at, c):
        return kv.at[pl.ds((part_at * part + c * rows) // BLK, rows // BLK)]

    to_core, to_above, to_below, pass_up, pass_down = {}, {}, {}, {}, {}
    for c in range(8):
        mine = kv_rows(2, c)
        to_core[c] = remote(mine, kv_rows(3, c), k_send, k_recv, c, by_core)
        to_above[c] = remote(mine, kv_rows(0, c), up_send, up_recv, c, above)
        to_below[c] = remote(mine, kv_rows(4, c), dn_send, dn_recv, c, below)
        pass_up[c] = remote(kv_rows(0, c), kv_rows(1, c), f_send, f_recv, c, by_core)
        pass_down[c] = remote(kv_rows(4, c), kv_rows(5, c), g_send, g_recv, c, by_core)
    keeps = {
        c: pltpu.make_async_copy(
            tok_rows(c) if c < 2 else x_rows(c), x_out.at[pl.ds(c * rows, rows)], s_sem.at[c]
        )
        for c in range(8)
    }

    def relay(c):
        @pl.when(has_below)
        def _():
            to_above[c].wait_recv()
            pass_up[c].start()

        @pl.when(has_above)
        def _():
            to_below[c].wait_recv()
            pass_down[c].start()

    def tables(begin, end):
        slot_tables(
            plane,
            y_at,
            core,
            x_at,
            dict(piece_blocks=piece // BLK, seqs=len_ref.shape[0], begin=begin, end=end),
            len_ref,
            ord_ref,
            rand_sm,
            rand_two,
            idx_ref,
            live_ref,
        )

    query_blocks = part // BLK
    for n, c in enumerate(CHUNK_ORDER):
        if n == 2:
            rand_trade.wait()
            to_scalar = pltpu.make_async_copy(rand_got, rand_two, l_sem.at[0])
            to_scalar.start()
            to_scalar.wait()
            tables(0, query_blocks // 3)
        if n == 4:
            tables(query_blocks // 3, 2 * query_blocks // 3)
        if n == 6:
            tables(2 * query_blocks // 3, query_blocks)
        if c >= 2:
            hops[c].wait_recv()
        if c == 2:
            hops[6].start()
        if c == 5:
            hops[7].start()
        keeps[c].start()
        block = tok_ref[pl.ds(c * rows, rows), :] if c < 2 else xs[pl.ds((c - 2) * rows, rows), :]
        made = jnp.dot(block, wkv_ref[...], preferred_element_type=jnp.float32).astype(jnp.bfloat16)
        kv[pl.ds((2 * part + c * rows) // BLK, rows // BLK)] = made.reshape(rows // BLK, BLK, -1)

        @pl.when(has_above)
        def _(c=c):
            to_above[c].start()

        @pl.when(has_below)
        def _(c=c):
            to_below[c].start()

        to_core[c].start()
        q_ref[pl.ds(c * rows, rows), :] = jnp.dot(
            block, wq_ref[...], preferred_element_type=jnp.float32
        ).astype(jnp.bfloat16)
        if n >= 3:
            relay(CHUNK_ORDER[n - 3])
    for c in CHUNK_ORDER[5:]:
        relay(c)
    for c in range(8):
        to_core[c].wait_recv()

        @pl.when(has_above)
        def _(c=c):
            pass_down[c].wait_recv()

        @pl.when(has_below)
        def _(c=c):
            pass_up[c].wait_recv()

    saved = pltpu.make_async_copy(kv, kv_out, l_sem.at[1])
    saved.start()
    per = piece // BLK

    def part_of(turn):
        middle = turn - 2
        j = jnp.where(turn < 2, 3, jnp.where(turn < 6, 1 + lax.rem(turn, 2), 0))
        half = jnp.where(turn < 2, turn, jnp.where(turn < 6, middle // 2, turn - 6))
        return j, half

    def trade(turn):
        j, half = part_of(turn)
        span = pl.ds(pl.multiple_of(half * rows, rows), rows)
        return remote(
            ctx.at[j, span],
            ctx_out.at[span, pl.ds(pl.multiple_of(j * WIN, WIN), WIN)],
            o_send,
            o_recv,
            turn,
            device_at(plane, y_at ^ (j >> 1), core, x_at ^ (j & 1)),
        )

    def attend_part(turn, carry):
        j, half = part_of(turn)

        def step(n, carry):
            at = pl.ds(pl.multiple_of(n * BLK, BLK), BLK)
            ctx[j, at, :] = attend_block(j * per + n, idx_ref, live_ref, q_ref, kv, lse_ref)
            return carry

        first = half * (per // 2)
        for n in range(per // 2):
            step(first + n, 0)

        @pl.when(turn < 6)
        def _():
            trade(turn).start()

        return carry

    lax.fori_loop(0, 8, attend_part, 0)
    ctx_out[:, 0:WIN] = ctx[0]
    hand_on.append(pltpu.make_async_copy(ctx, ctx_keep, l_sem.at[7]))
    hand_on[-1].start()
    for c in (2, 4, 3, 5, 6, 7):
        hops[c].wait_send()
    for c in range(8):
        to_core[c].wait_send()
        keeps[c].wait()

        @pl.when(has_above)
        def _(c=c):
            to_above[c].wait_send()
            pass_down[c].wait_send()

        @pl.when(has_below)
        def _(c=c):
            to_below[c].wait_send()
            pass_up[c].wait_send()

    saved.wait()
    for copy in hand_on:
        copy.wait()

    def settle(turn, carry):
        trade(turn).wait()
        return carry

    lax.fori_loop(0, 6, settle, 0)


def forward_attention(tokens, w_query, w_key, w_value, lengths, seq_order, rand_row, planes):
    piece, width = tokens.shape
    dma, low = pltpu.SemaphoreType.DMA, jnp.bfloat16
    sds = jax.ShapeDtypeStruct
    blocks = 4 * piece // BLK
    return pl.pallas_call(
        functools.partial(forward_kernel, planes),
        out_shape=[
            sds((24 * piece // BLK, BLK, 2 * WQ), low),
            sds((4 * piece, WIN), low),
            sds((4 * piece, width), low),
            sds((piece, 4 * WIN), low),
            sds((blocks, WQ), jnp.float32),
            sds((blocks * SLOTS,), jnp.int32),
            sds((blocks * SLOTS,), jnp.int32),
            sds((width, WIN), low),
            sds((width, 2 * WQ), low),
            sds((4, piece, WIN), low),
        ],
        in_specs=[VMEM] + [ANY] * 3 + [SMEM] * 2 + [VMEM, SMEM],
        out_specs=[ANY, VMEM, ANY, VMEM, VMEM, SMEM, SMEM, ANY, ANY, ANY],
        scratch_shapes=[
            pltpu.VMEM((3 * piece, width), low),
            pltpu.VMEM((24 * piece // BLK, BLK, 2 * WQ), low),
            pltpu.VMEM((4, piece, WIN), low),
            pltpu.VMEM(rand_row.shape, jnp.int32),
            pltpu.SMEM(rand_row.shape, jnp.int32),
            pltpu.VMEM((3, width, width), low),
            pltpu.VMEM((width, WIN), low),
            pltpu.VMEM((width, 2 * WQ), low),
            dma((6,)),
            dma((6,)),
        ]
        + [dma((8,))] * 11
        + [dma((6,))] * 2
        + [dma((1,))] * 2
        + [dma((8,))],
        compiler_params=pltpu.CompilerParams(
            collective_id=0, has_side_effects=True, vmem_limit_bytes=62 << 20
        ),
        cost_estimate=pl.CostEstimate(
            flops=2 * 4 * piece * width * 640, bytes_accessed=40 << 20, transcendentals=0
        ),
        name="forward_attention",
    )(tokens, w_query, w_key, w_value, lengths, seq_order, rand_row, rand_row)


def attend_back(idx, live, queries, grads, context, level, keys_values):
    rows, width = keys_values.shape[0] // 6, keys_values.shape[1]
    count = queries.shape[0]
    kv_shape = jax.ShapeDtypeStruct((6 * rows, width), jnp.bfloat16)
    return pl.pallas_call(
        backward_kernel,
        out_shape=[jax.ShapeDtypeStruct((count, WIN), jnp.bfloat16)] + [kv_shape],
        in_specs=[SMEM, SMEM, VMEM, VMEM, VMEM, VMEM, ANY],
        out_specs=[VMEM] * 2,
        scratch_shapes=[
            pltpu.VMEM((6 * rows, width), jnp.bfloat16),
            pltpu.VMEM((6 * rows, width), jnp.float32),
            pltpu.SemaphoreType.DMA((1,)),
        ],
        compiler_params=pltpu.CompilerParams(vmem_limit_bytes=62 << 20),
        cost_estimate=pl.CostEstimate(
            flops=2 * 10 * count * 3 * 256 * 512, bytes_accessed=24 * rows * width, transcendentals=count * 3 * 512
        ),
        name="attend_back",
    )(idx, live, queries, grads, context, level, keys_values)


def reduce_kernel(planes, *refs):
    dkv_in, dq_in, x_in, wq_in, wkv_in, one_in = refs[:6]
    pair_in = refs[6:12]
    tok_out, q_out, k_out, v_out, up_out, side_out, norm_out, down_out = refs[12:20]
    own, core_in, z_out, z_in, g_all, dx_out, dx_in, acc = refs[20:28]
    dq, xs, wq, wkv, one = refs[28:33]
    p_slab, p_core, p_z, p_zin, p_fin, p_all = refs[33:39]
    keep, give = refs[39:42], refs[42:45]
    got, two, fin = refs[45:48], refs[48:51], refs[51:54]
    line_out, line_in = refs[54:57], refs[57:60]
    l_sem, i_sem, c_s, c_r, u_s, u_r, d_s, d_r, x_s, x_r = refs[60:70]
    pk_s, pk_r, pz_s, pz_r, pf_s, pf_r = refs[70:76]
    w2_s, w2_r, w3_s, w3_r, w4_s, w4_r, w1_s, w1_r = refs[76:84]
    plane, y_at, core, x_at = place()
    piece = tok_out.shape[0]
    part = 4 * piece
    rest = planes - 1
    group = y_at * 2 + x_at
    low, f32 = jnp.bfloat16, jnp.float32

    def there(j):
        return device_at(plane, y_at ^ (j >> 1), core, x_at ^ (j & 1))

    by_x, by_y = there(1), there(2)
    by_core = device_at(plane, y_at, 1 - core, x_at)
    others = [device_at(lax.rem(plane + g, planes), y_at, core, x_at) for g in range(1, planes)]
    has_above, has_below = plane < planes - 1, plane > 0
    above = device_at(plane + 1, y_at, core, x_at)
    below = device_at(plane - 1, y_at, core, x_at)

    def chunk(base, j):
        return pl.ds(pl.multiple_of(base + j * piece, piece), piece)

    def load_own(turn, r, j):
        return pltpu.make_async_copy(
            dkv_in.at[chunk(2 * r * part, j)], own.at[chunk(r * part, j)], l_sem.at[turn]
        )

    def to_core(turn, r, j):
        return remote(
            dkv_in.at[chunk((2 * r + 1) * part, j)],
            core_in.at[chunk(r * part, j)],
            c_s,
            c_r,
            turn,
            by_core,
        )

    def to_below(j):
        return remote(z_out.at[chunk(0, j)], z_in.at[chunk(0, j)], d_s, d_r, j, below)

    def to_above(j):
        return remote(z_out.at[chunk(part, j)], z_in.at[chunk(part, j)], u_s, u_r, j, above)

    def to_owner(j):
        return remote(dx_out.at[j - 1], dx_in.at[j - 1], x_s, x_r, j - 1, there(j))

    half_piece = piece // 2

    def pass_on(j):
        span = pl.ds((j - 1) * half_piece, half_piece)
        return remote(dx_out.at[2, span], dx_in.at[2, span], x_s, x_r, 1 + j, there(j))

    def take_in(j):
        span = pl.ds((j - 1) * half_piece, half_piece)
        pass_on(j).wait_recv()
        spot = 2 - j
        dx_out[spot, span, :] = (
            dx_out[spot, span, :].astype(f32) + dx_in[2, span, :].astype(f32)
        ).astype(low)
        to_owner(3 - j).start()

    def every(n, action):
        j = 3 - n
        for turn, r in ((n * 2, 0), (n * 2 + 1, 2)):
            action(turn, r, j)

    greet([by_x, by_y, there(3), by_core] + others)

    def begin(n, carry):
        def go(turn, r, j):
            to_core(turn, r, j).start()
            load_own(turn, r, j).start()

        every(n, go)
        return carry

    lax.fori_loop(0, 4, begin, 0)

    def begin_mid(n, carry):
        to_core(8 + n, 1, 3 - n).start()
        load_own(8 + n, 1, 3 - n).start()
        return carry

    lax.fori_loop(0, 4, begin_mid, 0)
    inputs = [(pair_in[2 * n], keep[n]) for n in range(3)]
    inputs += [(pair_in[2 * n + 1], give[n]) for n in (0, 2)]
    inputs += [(wq_in, wq), (wkv_in, wkv), (dq_in, dq), (x_in, xs), (one_in, one)]
    inputs = [pltpu.make_async_copy(src, dst, i_sem.at[n]) for n, (src, dst) in enumerate(inputs)]
    for copy in inputs:
        copy.start()
    w1 = remote(pair_in[3], give[1], w1_s, w1_r, 0, by_y)
    w1.start()

    def both(turn, r, j):
        to_core(turn, r, j).wait_recv()
        load_own(turn, r, j).wait()
        at = chunk(r * part, j)
        return own[at, :].astype(f32) + core_in[at, :].astype(f32)

    def spread(n, carry):
        j = 3 - n
        z_out[chunk(0, j), :] = both(2 * n, 0, j).astype(low)

        @pl.when(jnp.logical_and(has_below, n < 3))
        def _():
            to_below(j).start()

        z_out[chunk(part, j), :] = both(2 * n + 1, 2, j).astype(low)

        @pl.when(jnp.logical_and(has_above, n < 3))
        def _():
            to_above(j).start()

        return carry

    lax.fori_loop(0, 4, spread, 0)

    for copy in inputs[:5]:
        copy.wait()
    halves = [keep[0].shape[2] // 2, keep[1].shape[2] // 2]
    w2 = {}
    for n in (0, 2, 1):
        if n == 1:
            w1.wait()

        def merge(p, carry, n=n):
            keep[n][p] = (keep[n][p].astype(f32) + give[n][p].astype(f32)).astype(low)
            return carry

        lax.fori_loop(0, planes, merge, 0)
        if n < 2:
            cols = pl.ds(pl.multiple_of((1 - x_at) * halves[n], 128), halves[n])
            w2[n] = remote(keep[n].at[:, :, cols], got[n], w2_s, w2_r, n, by_x)
        else:
            w2[n] = remote(keep[n].at[:, 1 - y_at], got[n], w2_s, w2_r, n, by_y)
        w2[n].start()
    for copy in inputs[5:]:
        copy.wait()
    acc[...] = jnp.zeros_like(acc)

    def arrive(n):
        j = 3 - n
        g_all[:, 2 * WQ :] = dq[chunk(0, j), :]
        g_all[:, : 2 * WQ] = both(8 + n, 1, j).astype(low)

        @pl.when(has_above)
        def _():
            to_below(j).wait_recv()
            g_all[:, : 2 * WQ] = (
                g_all[:, : 2 * WQ].astype(f32) + z_in[chunk(0, j), :].astype(f32)
            ).astype(low)

        @pl.when(has_below)
        def _():
            to_above(j).wait_recv()
            g_all[:, : 2 * WQ] = (
                g_all[:, : 2 * WQ].astype(f32) + z_in[chunk(part, j), :].astype(f32)
            ).astype(low)

    def back(j):
        grads = g_all[...]
        return nt(grads[:, 2 * WQ :], wq[...]) + nt(grads[:, : 2 * WQ], wkv[...])

    def outer(j):
        acc[...] += tn(xs[chunk(0, j), :], g_all[...])

    def turn_back(n, carry):
        arrive(n)
        dx_out[2 - n] = back(3 - n).astype(low)
        outer(3 - n)
        return carry

    turn_back(0, 0)
    pass_on(1).start()
    pass_on(2).start()
    turn_back(1, 0)

    for n in range(3):
        w2[n].wait_recv()

        def halve(p, carry, n=n):
            if n < 2:
                cols = pl.ds(pl.multiple_of(x_at * halves[n], 128), halves[n])
                mine = keep[n][p, :, cols]
            else:
                mine = keep[n][p, y_at]
            two[n][p] = (mine.astype(f32) + got[n][p].astype(f32)).astype(low)
            return carry

        lax.fori_loop(0, planes, halve, 0)

    def line_copy(n, way, t):
        return remote(
            line_out[n].at[way, t],
            line_in[n].at[way, t],
            w3_s,
            w3_r,
            (n * 2 + way) * rest + t,
            below if way else above,
        )

    def line_step(t):
        for n in range(3):
            for way in range(2):
                spot = (planes - 1 - plane) if way else plane
                gap = planes - 1 - t
                slab = (plane - gap) if way else (plane + gap)
                sends = jnp.logical_and(t >= spot, spot < planes - 1)

                @pl.when(jnp.logical_and(sends, spot == 0))
                def _():
                    line_out[n][way, t] = two[n][slab]
                    line_copy(n, way, t).start()

                @pl.when(jnp.logical_and(sends, spot > 0))
                def _():
                    line_copy(n, way, t - 1).wait_recv()
                    line_out[n][way, t] = (
                        two[n][slab].astype(f32) + line_in[n][way, t - 1].astype(f32)
                    ).astype(low)
                    line_copy(n, way, t).start()

    line_step(0)

    @pl.when(has_below)
    def _():
        to_below(0).start()

    @pl.when(has_above)
    def _():
        to_above(0).start()

    take_in(1)
    turn_back(2, 0)
    take_in(2)
    if planes > 2:
        line_step(1)
    arrive(3)
    outer(0)

    share = p_slab.shape[3]
    acc[:, 2 * WQ :] *= DH ** (-0.5)
    for p in range(planes):
        for y in range(2):
            for k in range(2):
                at = ((p * 2 + y) * 2 + k) * share
                p_slab[k, p, y] = acc[at : at + share, :].astype(low)
    pk = remote(p_slab.at[1 - core], p_core, pk_s, pk_r, 0, by_core)
    pk.start()
    tok_out[...] = one[...] + back(0)
    pk.wait_recv()

    def merge_core(p, carry):
        p_z[p] = (p_slab[core, p].astype(f32) + p_core[p].astype(f32)).astype(low)
        return carry

    lax.fori_loop(0, planes, merge_core, 0)
    pz = [
        remote(
            p_z.at[lax.rem(plane + g, planes)], p_zin.at[g - 1], pz_s, pz_r, g - 1, others[g - 1]
        )
        for g in range(1, planes)
    ]

    def next_step(t, carry):
        line_step(t)
        return carry

    lax.fori_loop(2, planes - 1, next_step, 0)
    for copy in pz:
        copy.start()
    w4 = []
    for n in range(3):
        fin[n][x_at] = two[n][plane]

        @pl.when(has_below)
        def _(n=n):
            line_copy(n, 0, rest - 1).wait_recv()
            fin[n][x_at] = (
                fin[n][x_at].astype(f32) + line_in[n][0, rest - 1].astype(f32)
            ).astype(low)

        @pl.when(has_above)
        def _(n=n):
            line_copy(n, 1, rest - 1).wait_recv()
            fin[n][x_at] = (
                fin[n][x_at].astype(f32) + line_in[n][1, rest - 1].astype(f32)
            ).astype(low)

        w4.append(remote(fin[n].at[x_at], fin[n].at[x_at], w4_s, w4_r, n, by_x))
        w4[n].start()

    for j in (2, 1):
        to_owner(j).wait_recv()
        tok_out[...] += dx_in[j - 1].astype(f32)

    for copy in list(w2.values()) + [pk]:
        copy.wait_send()

    def settle(n, carry):
        every(n, lambda turn, r, j: to_core(turn, r, j).wait_send())
        to_core(8 + n, 1, 3 - n).wait_send()

        @pl.when(has_below)
        def _():
            to_below(3 - n).wait_send()

        @pl.when(has_above)
        def _():
            to_above(3 - n).wait_send()

        return carry

    lax.fori_loop(0, 4, settle, 0)
    for j in (1, 2):
        to_owner(j).wait_send()
        pass_on(j).wait_send()

    def settle_line(t, carry):
        for n in range(3):
            for way in range(2):
                spot = (planes - 1 - plane) if way else plane

                @pl.when(jnp.logical_and(t >= spot, spot < planes - 1))
                def _():
                    line_copy(n, way, t).wait_send()

        return carry

    lax.fori_loop(0, planes - 1, settle_line, 0)

    total = p_z[plane].astype(f32)
    for g in range(1, planes):
        pz[g - 1].wait_recv()
        total = total + p_zin[g - 1].astype(f32)
    p_fin[...] = total.astype(low)
    pf = [
        remote(p_fin.at[y_at ^ (j >> 1)], p_all.at[j], pf_s, pf_r, j - 1, there(j))
        for j in (1, 2, 3)
    ]
    for copy in pf:
        copy.start()
    p_all[0] = p_fin[y_at]

    for n, dest in ((0, up_out), (2, down_out)):
        w4[n].wait()
        width = dest.shape[1] // 2
        for side in range(2):
            dest[:, side * width : (side + 1) * width] = fin[n][side].astype(f32)
    w4[1].wait()
    width = side_out.shape[1] // 2
    for side in range(2):
        done = fin[1][side].astype(f32)
        side_out[:, side * width : (side + 1) * width] = done[:share]
        norm_out[:, side * width : (side + 1) * width] = done[share : share + 8]

    for copy in pf:
        copy.wait()
    for a in range(4):
        grads = p_all[a ^ group].astype(f32)
        for n, dest in enumerate((k_out, v_out, q_out)):
            dest[:, a * WQ : (a + 1) * WQ] = grads[:, n * WQ : (n + 1) * WQ]
    for copy in pz:
        copy.wait_send()


def reduce_all(dkv, dq, stretch, wq, wkv, one, up, out, down, planes):
    low, f32 = jnp.bfloat16, jnp.float32
    piece = dq.shape[0] // 4
    width = stretch.shape[1]
    share = up[0].shape[1]
    rest = planes - 1
    dma, vm, sds = pltpu.SemaphoreType.DMA, pltpu.VMEM, jax.ShapeDtypeStruct
    cols = 2 * WQ + WIN
    tall = out[0].shape[1]
    wide = up[0].shape[2]
    kinds = [(share, wide // 2), (tall, width // 2), down[0].shape[2:]]
    pairs = [up[0].shape, out[0].shape, down[0].shape]
    return pl.pallas_call(
        functools.partial(reduce_kernel, planes),
        out_shape=[sds((piece, width), f32)]
        + [sds((share, width), f32)] * 3
        + [
            sds((share, wide), f32),
            sds((share, width), f32),
            sds((8, width), f32),
            sds((kinds[2][0], width), f32),
        ],
        in_specs=[ANY] * 12,
        out_specs=[VMEM] * 8,
        scratch_shapes=[
            vm((12 * piece, 2 * WQ), low),
            vm((12 * piece, 2 * WQ), low),
            vm((8 * piece, 2 * WQ), low),
            vm((8 * piece, 2 * WQ), low),
            vm((piece, cols), low),
            vm((3, piece, width), low),
            vm((3, piece, width), low),
            vm((width, cols), f32),
            vm(dq.shape, low),
            vm(stretch.shape, low),
            vm(wq.shape, low),
            vm(wkv.shape, low),
            vm(one.shape, f32),
            vm((2, planes, 2, share, cols), low),
            vm((planes, 2, share, cols), low),
            vm((planes, 2, share, cols), low),
            vm((rest, 2, share, cols), low),
            vm((2, share, cols), low),
            vm((4, share, cols), low),
        ]
        + [vm(p, low) for p in pairs] * 2
        + [vm((planes,) + k, low) for k in kinds] * 2
        + [vm((2,) + k, low) for k in kinds]
        + [vm((2, rest) + k, low) for k in kinds] * 2
        + [dma((12,)), dma((11,))]
        + [dma((12,))] * 2
        + [dma((4,))] * 6
        + [dma((1,))] * 2
        + [dma((rest,))] * 2
        + [dma((3,))] * 2
        + [dma((3,))] * 2
        + [dma((6 * rest,))] * 2
        + [dma((3,))] * 2
        + [dma((1,))] * 2,
        compiler_params=pltpu.CompilerParams(
            collective_id=1, has_side_effects=True, vmem_limit_bytes=60 << 20
        ),
        cost_estimate=pl.CostEstimate(
            flops=4 * 4 * piece * width * cols, bytes_accessed=40 << 20, transcendentals=0
        ),
        name="reduce_all",
    )(dkv, dq, stretch, wq, wkv, one, up[0], up[1], out[0], out[1], down[0], down[1])


def dense_kernel(
    planes,
    tok_ref,
    ctx_ref,
    cot_ref,
    g1_ref,
    b1_ref,
    g2_ref,
    b2_ref,
    wout_in,
    wup_in,
    wdown_in,
    *refs,
):
    out_ref, one_ref, do_out, up_keep, up_give, out_keep, out_give, down_keep, down_give = refs[:9]
    wup, wdown, acc, x1, s1, g_two, nl, hid, slope, gp, gm, ga = refs[9:21]
    dctx, up_loc, out_loc, down_loc, up_got, out_got, down_got, down_sum = refs[21:29]
    w_sem, mv_sem, do_s, do_r, up_s, up_r, out_s, out_r, down_s, down_r = refs[29:39]
    wout_ref = refs[39]
    plane, y_at, core, x_at = place()
    piece, width = tok_ref.shape
    share = up_loc.shape[2]
    slab = down_loc.shape[2]
    pairs = 2 * planes
    group = y_at * 2 + x_at
    f32 = jnp.float32
    fetch = [
        pltpu.make_async_copy(
            wout_in.at[pl.ds(pl.multiple_of((group ^ j) * WQ, WQ), WQ)],
            wout_ref.at[pl.ds(j * WIN + WIN - WQ, WQ)],
            w_sem.at[2 + j],
        )
        for j in range(4)
    ]
    for copy in fetch:
        copy.start()
    bring = [
        pltpu.make_async_copy(wup_in, wup, w_sem.at[0]),
        pltpu.make_async_copy(wdown_in, wdown, w_sem.at[1]),
    ]
    for copy in bring:
        copy.start()

    def there(j):
        return device_at(plane, y_at ^ (j >> 1), core, x_at ^ (j & 1))

    by_core = device_at(plane, y_at, 1 - core, x_at)
    height, tile = 32, 2 * WQ
    wide = wup.shape[1]

    def rows_of(n):
        return pl.ds(pl.multiple_of(n * height, height), height)

    def cols_of(n):
        return pl.ds(pl.multiple_of(n * tile, tile), tile)

    def mean(v):
        return jnp.mean(v, axis=1, keepdims=True)

    def fold(v):
        return v[:8] + v[8:16] + v[16:24] + v[24:]

    for j in range(4):
        wout_ref[j * WIN : j * WIN + WIN - WQ, :] = jnp.zeros((WIN - WQ, width), jnp.bfloat16)
    for copy in fetch:
        copy.wait()
    acc[...] = jnp.dot(ctx_ref[...], wout_ref[...], preferred_element_type=f32)
    g1, b1, g2, b2 = (r[...].reshape(1, width) for r in (g1_ref, b1_ref, g2_ref, b2_ref))

    def norm_one(n, carry):
        at = rows_of(n)
        value = tok_ref[at, :].astype(f32) + acc[at, :]
        center = value - mean(value)
        inverse = lax.rsqrt(mean(center * center) + eps_norm)
        hat = center * inverse
        x1[at, :] = hat
        s1[at, :] = jnp.broadcast_to(inverse, (height, 128))
        nl[at, :] = (hat * g1 + b1).astype(jnp.bfloat16)
        return carry

    lax.fori_loop(0, piece // height, norm_one, 0, unroll=4)
    bring[0].wait()

    def expand(n, carry):
        at = pl.ds(pl.multiple_of(n * 768, 768), 768)
        pre = jnp.dot(nl[...], wup[:, at], preferred_element_type=f32)
        square = pre * pre
        bend = jnp.tanh(pre * (0.7978845608028654 + 0.035677408136300125 * square))
        half_up = 0.5 + 0.5 * bend
        value = pre * half_up
        hid[:, at] = value.astype(jnp.bfloat16)
        slope[:, at] = half_up + value * (1.0 - bend) * (
            0.7978845608028654 + 0.10703222440890037 * square
        )
        return carry

    lax.fori_loop(0, wide // 768, expand, 0)
    bring[1].wait()
    acc[...] = jnp.dot(hid[...], wdown[...], preferred_element_type=f32)
    nothing = jnp.zeros((8, width), f32)

    def norm_two(n, carry):
        gain_sum, shift_sum = carry
        at = rows_of(n)
        value = x1[at, :] * g1 + b1 + acc[at, :]
        center = value - mean(value)
        inverse = lax.rsqrt(mean(center * center) + eps_norm)
        hat = center * inverse
        out_ref[at, :] = (hat * g2 + b2).astype(jnp.bfloat16)
        cot = cot_ref[at, :].astype(f32)
        gain_sum, shift_sum = gain_sum + fold(cot * hat), shift_sum + fold(cot)
        up = cot * g2
        grad = inverse * (up - mean(up) - hat * mean(up * hat))
        g_two[at, :] = grad
        gm[at, :] = grad.astype(jnp.bfloat16)
        return gain_sum, shift_sum

    gain_two, shift_two = lax.fori_loop(0, piece // height, norm_two, (nothing, nothing), unroll=4)

    def shrink(n, carry):
        at = cols_of(n)
        back = nt(gm[...], wdown[at, :])
        gp[:, at] = (back * slope[:, at]).astype(jnp.bfloat16)
        return carry

    lax.fori_loop(0, wide // tile, shrink, 0, unroll=2)
    acc[...] = nt(gp[...], wup[...])

    def norm_three(n, carry):
        gain_sum, shift_sum = carry
        at = rows_of(n)
        grad_in, hat = g_two[at, :] + acc[at, :], x1[at, :]
        gain_sum, shift_sum = gain_sum + fold(grad_in * hat), shift_sum + fold(grad_in)
        up = grad_in * g1
        grad = s1[at, 0:1] * (up - mean(up) - hat * mean(up * hat))
        one_ref[at, :] = grad
        ga[at, :] = grad.astype(jnp.bfloat16)
        return gain_sum, shift_sum

    gain_one, shift_one = lax.fori_loop(
        0, piece // height, norm_three, (nothing, nothing), unroll=4
    )
    side = jnp.concatenate(
        [jnp.sum(v, axis=0, keepdims=True) for v in (gain_one, shift_one, gain_two, shift_two)]
        + [jnp.zeros((12, width), f32)],
        axis=0,
    ).astype(jnp.bfloat16)

    low = jnp.bfloat16
    greet([there(1), there(2), there(3), by_core])
    trades = []
    for j in (3, 1, 2, 0):
        part = nt(ga[...], wout_ref[pl.ds(j * WIN, WIN), :]).astype(low)
        if j:
            dctx[j - 1] = part
            trades.append(
                remote(
                    dctx.at[j - 1], do_out.at[pl.ds(j * piece, piece)], do_s, do_r, j - 1, there(j)
                )
            )
            trades[-1].start()
        else:
            do_out[pl.ds(0, piece), :] = part

    tile = 2 * WQ
    per = tile // (2 * slab)
    tiles = wide // tile

    def down_copy(t):
        span = pl.ds(t * per, per)
        return remote(down_loc.at[1 - core, span], down_got.at[span], down_s, down_r, t, by_core)

    def up_copy(t):
        span = cols_of(t)
        return remote(
            up_loc.at[1 - core, :, :, span], up_got.at[:, :, span], up_s, up_r, t, by_core
        )

    def make_down(t, carry):
        cell = tn(hid[:, cols_of(t)], gm[...])
        for n in range(per):
            for k in range(2):
                at = (n * 2 + k) * slab
                down_loc[k, t * per + n] = cell[at : at + slab].astype(low)
        down_copy(t).start()
        return carry

    lax.fori_loop(0, tiles, make_down, 0)

    def make_up(t, carry):
        cell = tn(nl[...], gp[:, cols_of(t)])
        for q in range(pairs):
            for k in range(2):
                at = (q * 2 + k) * share
                up_loc[k, q, :, cols_of(t)] = cell[at : at + share].astype(low)
        up_copy(t).start()
        return carry

    lax.fori_loop(0, tiles, make_up, 0)
    moved = []

    def move(source, dest):
        moved.append(pltpu.make_async_copy(source, dest, mv_sem.at[len(moved)]))
        moved[-1].start()

    half = width // 2

    def sum_down(t, carry):
        down_copy(t).wait_recv()
        for n in range(per):
            q = t * per + n
            total = (
                down_loc[core, q].astype(jnp.float32) + down_got[q].astype(jnp.float32)
            ).astype(low)
            down_sum[0, q] = total[:, :half]
            down_sum[1, q] = total[:, half:]
        return carry

    lax.fori_loop(0, tiles, sum_down, 0)
    move(down_sum.at[x_at], down_keep)
    move(down_sum.at[1 - x_at], down_give)

    per_group = pairs // 4
    for j in range(4):
        cell = tn(ctx_ref[:, j * WIN : (j + 1) * WIN], ga[...])
        for n in range(per_group):
            for k in range(2):
                at = WIN - WQ + (n * 2 + k) * share
                out_loc[k, (group ^ j) * per_group + n, :share, :] = cell[at : at + share].astype(low)
    for q in range(pairs):
        for k in range(2):
            out_loc[k, q, share:, :] = side
    outs = remote(out_loc.at[1 - core], out_got, out_s, out_r, 0, by_core)
    outs.start()

    def sum_up(q, carry):
        up_got[q] = (up_loc[core, q].astype(jnp.float32) + up_got[q].astype(jnp.float32)).astype(low)
        return carry

    for t in range(tiles):
        up_copy(t).wait_recv()
    lax.fori_loop(0, pairs, sum_up, 0)
    outs.wait_recv()
    for p in range(planes):
        for y in range(2):
            q = p * 2 + y
            out_got[q] = (
                out_loc[core, q].astype(jnp.float32) + out_got[q].astype(jnp.float32)
            ).astype(low)
        for got, keep, give in ((up_got, up_keep, up_give), (out_got, out_keep, out_give)):
            move(got.at[p * 2 + y_at], keep.at[p])
            move(got.at[p * 2 + 1 - y_at], give.at[p])
    for copy in trades:
        copy.wait()
    for t in range(tiles):
        down_copy(t).wait_send()
        up_copy(t).wait_send()
    outs.wait_send()
    for copy in moved:
        copy.wait()


def dense_layers(tokens, ctx, cotangent, norms, wout, w_up, w_down, planes):
    low = jnp.bfloat16
    piece, width = tokens.shape
    pairs = 2 * planes
    wide = w_up.shape[1]
    share, slab, tall = width // (2 * pairs), wide // (2 * pairs), 16
    sds, vm, dma = jax.ShapeDtypeStruct, pltpu.VMEM, pltpu.SemaphoreType.DMA
    up, out = (planes, share, wide), (planes, share + tall, width)
    down = (pairs, slab, width // 2)
    tiles = wide // (2 * WQ)
    f32 = jnp.float32
    return pl.pallas_call(
        functools.partial(dense_kernel, planes),
        out_shape=[sds((piece, width), low), sds((piece, width), f32), sds((4 * piece, WIN), low)]
        + [sds(up, low)] * 2
        + [sds(out, low)] * 2
        + [sds(down, low)] * 2,
        in_specs=[VMEM] * 7 + [ANY] * 3,
        out_specs=[VMEM] * 3 + [ANY] * 6,
        scratch_shapes=[
            vm(w_up.shape, low),
            vm(w_down.shape, low),
            vm((piece, width), f32),
            vm((piece, width), f32),
            vm((piece, 128), f32),
            vm((piece, width), f32),
            vm((piece, width), low),
            vm((piece, wide), low),
            vm((piece, wide), f32),
            vm((piece, wide), low),
            vm((piece, width), low),
            vm((piece, width), low),
            vm((3, piece, WIN), low),
            vm((2, pairs, share, wide), low),
            vm((2, pairs, share + tall, width), low),
            vm((2, pairs, slab, width), low),
            vm((pairs, share, wide), low),
            vm((pairs, share + tall, width), low),
            vm((pairs, slab, width), low),
            vm((2, pairs, slab, width // 2), low),
            dma((6,)),
            dma((2 + 4 * planes,)),
        ]
        + [dma((3,))] * 2
        + [dma((tiles,))] * 2
        + [dma((1,))] * 2
        + [dma((tiles,))] * 2
        + [vm((4 * WIN, width), low)],
        compiler_params=pltpu.CompilerParams(
            collective_id=2, has_side_effects=True, vmem_limit_bytes=63 << 20
        ),
        cost_estimate=pl.CostEstimate(
            flops=2 * piece * width * (6 * wide + 3072), bytes_accessed=30 << 20, transcendentals=0
        ),
        name="dense_layers",
    )(tokens, ctx, cotangent, *norms, wout, w_up, w_down)


def finish_kernel(share, count, *refs):
    sources, rows_ref, dests = refs[:count], refs[count], refs[count + 1 : 2 * count + 1]
    parts = refs[2 * count + 1 : 2 * count + 5]
    held, sems = refs[2 * count + 5 : 3 * count + 5], refs[3 * count + 5]
    reads = [pltpu.make_async_copy(sources[n], held[n], sems.at[0, n]) for n in range(count)]
    writes = [pltpu.make_async_copy(held[n], dests[n], sems.at[1, n]) for n in range(count)]
    for copy in reads:
        copy.start()
    for n in range(count):
        reads[n].wait()
        writes[n].start()
    seq_at = lax.axis_index("seq")
    rows = rows_ref[...]
    width = rows.shape[1]
    spot = lax.broadcasted_iota(jnp.int32, (width, 128), 0) - seq_at * share
    chosen = (spot == lax.broadcasted_iota(jnp.int32, (width, 128), 1)).astype(jnp.float32)
    picked = jnp.dot(
        rows, chosen, preferred_element_type=jnp.float32, precision=lax.Precision.HIGHEST
    )
    for n in range(4):
        parts[n][...] = picked[n, :share]
    for copy in writes:
        copy.wait()


def finish(arrays, norm_rows, share):
    sds, count = jax.ShapeDtypeStruct, len(arrays)
    return pl.pallas_call(
        functools.partial(finish_kernel, share, count),
        out_shape=[sds(v.shape, v.dtype) for v in arrays] + [sds((share,), jnp.float32)] * 4,
        in_specs=[ANY] * count + [VMEM],
        out_specs=[ANY] * count + [VMEM] * 4,
        scratch_shapes=[pltpu.VMEM(v.shape, v.dtype) for v in arrays]
        + [pltpu.SemaphoreType.DMA((2, count))],
        compiler_params=pltpu.CompilerParams(vmem_limit_bytes=62 << 20),
        name="finish",
    )(*arrays, norm_rows)


def body(
    tokens,
    w_query,
    w_key,
    w_value,
    w_out,
    gain_attn,
    shift_attn,
    w_up,
    w_down,
    gain_mlp,
    shift_mlp,
    cotangent,
    lengths,
    seq_order,
    rand_blocks,
):
    piece, width = tokens.shape
    seqs, heads = lax.axis_size("seq"), lax.axis_size("head")
    planes = seqs // 4
    assert heads == 2 and 8 * piece == MAXB * BLK and width == 4 * WQ
    seq_at, x_at = lax.axis_index("seq"), lax.axis_index("head")
    plane, y_at, core = seq_at // 4, (seq_at // 2) % 2, seq_at % 2
    group = y_at * 2 + x_at

    keys_values, queries, stretch, context_tok, level, idx, live, wq_own, wkv_own, ctx_own = (
        forward_attention(
            tokens, w_query, w_key, w_value, lengths, seq_order, rand_blocks.T, planes
        )
    )
    share = width // seqs
    norms = [gain_attn, shift_attn, gain_mlp, shift_mlp]
    output, grad_one, grad_ctx, up_keep, up_give, out_keep, out_give, down_keep, down_give = (
        dense_layers(tokens, context_tok, cotangent, norms, w_out, w_up, w_down, planes)
    )
    up_pair = (up_keep, xor_swap(up_give, 4))
    out_pair = (out_keep, out_give)
    two_y = (planes, 2) + down_keep.shape[1:]
    down_pair = (down_keep.reshape(two_y), xor_swap(down_give, 1).reshape(two_y))

    grad_q, grad_kv = attend_back(
        idx,
        live,
        queries,
        grad_ctx,
        ctx_own.reshape(-1, WIN),
        level,
        keys_values.reshape(-1, 2 * WQ),
    )
    grad_tokens, grad_wq, grad_wk, grad_wv, up_total, out_total, norm_rows, down_total = reduce_all(
        grad_kv,
        grad_q,
        stretch,
        wq_own,
        wkv_own,
        grad_one,
        up_pair,
        out_pair,
        down_pair,
        planes,
    )

    finals = finish(
        (output, grad_tokens, grad_wq, grad_wk, grad_wv, out_total, up_total, down_total),
        norm_rows,
        share,
    )

    output, grad_tokens, grad_wq, grad_wk, grad_wv, grad_out, grad_up, grad_down = finals[:8]
    gain_one, shift_one, gain_two, shift_two = finals[8:]
    return (
        output,
        grad_tokens,
        grad_wq,
        grad_wk,
        grad_wv,
        grad_out,
        gain_one,
        shift_one,
        grad_up,
        grad_down,
        gain_two,
        shift_two,
    )


def solution(mesh):
    rows = P(("seq", "head"), None)
    seq_rows, seq_only = P("seq", None), P("seq")
    return jax.shard_map(
        body,
        mesh=mesh,
        in_specs=(rows,) + (P(),) * 10 + (rows, P(), P(), seq_rows),
        out_specs=(
            rows,
            rows,
            seq_rows,
            seq_rows,
            seq_rows,
            seq_rows,
            seq_only,
            seq_only,
            seq_rows,
            seq_rows,
            seq_only,
            seq_only,
        ),
        check_vma=False,
    )
```

```python
import functools

import jax
import jax.numpy as jnp
from jax import lax
from jax.experimental import pallas as pl
from jax.experimental.pallas import tpu as pltpu
from jax.sharding import PartitionSpec as P

DH = 64
BLK = 64
MAXB = 64
SLOTS = 8
HG = 3
WQ = HG * DH
WIN = 256
AXES = ("seq", "head")
NEG = -1e30

eps_norm = 1e-06


def xor_swap(value, bits):
    count = lax.axis_size("seq") * lax.axis_size("head")
    return lax.ppermute(value, AXES, [(d, d ^ bits) for d in range(count)])


def lane_groups(rows, offset):
    lane = lax.broadcasted_iota(jnp.int32, (rows, WIN), 1) - offset
    return [jnp.logical_and(lane >= h * DH, lane < (h + 1) * DH) for h in range(HG)]


def spread_heads(block, offset):
    zero = jnp.zeros_like(block)
    return jnp.concatenate([jnp.where(m, block, zero) for m in lane_groups(BLK, offset)], axis=0)


def fold_heads(stacked, offset):
    masks = lane_groups(BLK, offset)
    total = jnp.where(masks[0], stacked[:BLK], 0.0)
    for h in range(1, HG):
        total = total + jnp.where(masks[h], stacked[h * BLK : (h + 1) * BLK], 0.0)
    return total


def nt(a, b):
    return lax.dot_general(a, b, (((1,), (1,)), ((), ())), preferred_element_type=jnp.float32)


def tn(a, b):
    return lax.dot_general(a, b, (((0,), (0,)), ((), ())), preferred_element_type=jnp.float32)


def backward_kernel(idx_ref, live_ref, q_ref, do_ref, o_ref, lse_ref, *refs):
    kv_ref, dq_ref, dkv_ref, kv, acc, sems = refs

    def clear(n, carry):
        acc[pl.ds(pl.multiple_of(n * 256, 256), 256), :] = jnp.zeros((256, 2 * WQ), jnp.float32)
        return carry

    copy = pltpu.make_async_copy(kv_ref, kv, sems.at[0])
    copy.start()
    lax.fori_loop(0, acc.shape[0] // 256, clear, 0)
    copy.wait()

    def step(i, carry):
        q_rows = pl.multiple_of(i * BLK, BLK)
        qexp = spread_heads(q_ref[pl.ds(q_rows, BLK), :], 0)
        doexp = spread_heads(do_ref[pl.ds(q_rows, BLK), :], 64)
        rows = [
            pl.multiple_of(idx_ref[i * SLOTS + s] * BLK, BLK) for s in range(SLOTS)
        ]
        keys = jnp.concatenate([kv[pl.ds(r, BLK), 0:WIN] for r in rows], axis=0)
        values = jnp.concatenate([kv[pl.ds(r, BLK), 128 : 128 + WIN] for r in rows], axis=0)
        product = do_ref[pl.ds(q_rows, BLK), :].astype(jnp.float32) * o_ref[
            pl.ds(q_rows, BLK), :
        ].astype(jnp.float32)
        high = product.astype(jnp.bfloat16)
        ones = jnp.ones((8, WIN), jnp.bfloat16)
        inner = nt(ones, spread_heads(high, 64)) + nt(
            ones, spread_heads((product - high.astype(jnp.float32)).astype(jnp.bfloat16), 64)
        )
        inner = inner[0:1]
        level = lse_ref[pl.ds(i, 1), :]
        raw = nt(keys, qexp)
        grad_probs = nt(values, doexp)
        probs, grad_scores = [], []
        for s in range(SLOTS):
            at = slice(s * BLK, (s + 1) * BLK)
            off = level + jnp.where(live_ref[i * SLOTS + s] > 0, 0.0, -NEG)
            p = jnp.exp(raw[at] - off)
            probs.append(p.astype(jnp.bfloat16))
            grad_scores.append((p * (grad_probs[at] - inner)).astype(jnp.bfloat16))
        probs = jnp.concatenate(probs, axis=0)
        grad_scores = jnp.concatenate(grad_scores, axis=0)
        dk = jnp.dot(grad_scores, qexp, preferred_element_type=jnp.float32)
        dv = jnp.dot(probs, doexp, preferred_element_type=jnp.float32)
        dq = tn(grad_scores, keys)
        dq_ref[pl.ds(q_rows, BLK), :] = fold_heads(dq, 0).astype(jnp.bfloat16)
        for s in range(SLOTS):
            k_s, v_s = dk[s * BLK : (s + 1) * BLK], dv[s * BLK : (s + 1) * BLK]
            at = pl.ds(rows[s], BLK)
            acc[at, 0:128] += k_s[:, :128]
            acc[at, 128:256] += k_s[:, 128:] + v_s[:, :128]
            acc[at, 256:384] += v_s[:, 128:]
        return carry

    lax.fori_loop(0, q_ref.shape[0] // BLK, step, 0, unroll=8)

    def emit(n, carry):
        at = pl.ds(pl.multiple_of(n * 256, 256), 256)
        dkv_ref[at, :] = acc[at, :].astype(jnp.bfloat16)
        return carry

    lax.fori_loop(0, acc.shape[0] // 256, emit, 0)


VMEM = pl.BlockSpec(memory_space=pltpu.VMEM)
SMEM = pl.BlockSpec(memory_space=pltpu.SMEM)
ANY = pl.BlockSpec(memory_space=pl.ANY)


def device_at(plane, y_at, core, x_at):
    return (plane * 4 + y_at * 2 + core, x_at)


def place():
    seq_at, x_at = lax.axis_index("seq"), lax.axis_index("head")
    return seq_at // 4, (seq_at // 2) % 2, seq_at % 2, x_at


def remote(src, dst, sems, recvs, at, device):
    return pltpu.make_async_remote_copy(
        src_ref=src,
        dst_ref=dst,
        send_sem=sems.at[at],
        recv_sem=recvs.at[at],
        device_id=device,
        device_id_type=pl.DeviceIdType.MESH,
    )


def greet(partners):
    barrier = pltpu.get_barrier_semaphore()
    for device in partners:
        pl.semaphore_signal(
            barrier, inc=1, device_id=device, device_id_type=pl.DeviceIdType.MESH
        )
    pl.semaphore_wait(barrier, len(partners))


CHUNK_ORDER = (0, 1, 2, 4, 3, 5, 6, 7)


def slot_tables(plane, y_at, core, x_at, at, lengths, order, rand_own, rand_got, idx_ref, live_ref):
    per = at["piece_blocks"]

    def one(i, carry):
        far, near = i // per, i % per
        y_of, x_of = y_at ^ (far >> 1), x_at ^ (far & 1)
        block = plane * MAXB + y_of * (4 * per) + core * (2 * per) + x_of * per + near
        begin, first, span = jnp.int32(0), jnp.int32(0), jnp.int32(1)
        for m in range(at["seqs"]):
            size = lengths[order[m]]
            inside = begin <= block
            first = jnp.where(inside, begin, first)
            span = jnp.where(inside, size, span)
            begin = begin + size
        row = x_of * per + near
        draws = []
        for n in range(SLOTS - 5):
            draw = jnp.where(far >= 2, rand_got[n, row], rand_own[n, row])
            for power in range(16, -1, -1):
                multiple = span * (1 << power)
                draw = jnp.where(draw >= multiple, draw - multiple, draw)
            draws.append(first + draw)
        candidates = [block - 1, block, block + 1, first, first + span - 1] + draws
        kept = []
        for s in range(SLOTS):
            alive = jnp.int32(1)
            if s == 0:
                alive = (block > first).astype(jnp.int32)
            if s == 2:
                alive = (block < first + span - 1).astype(jnp.int32)
            for e in range(s):
                same = (candidates[e] == candidates[s]).astype(jnp.int32)
                alive = alive * (1 - kept[e] * same)
            kept.append(alive)
            key = jnp.where(alive > 0, candidates[s], block)
            rel = key // MAXB - plane + 1
            inner = key % MAXB
            y_key, rest = inner // (4 * per), inner % (4 * per)
            core_key, rest = rest // (2 * per), rest % (2 * per)
            x_key, near_key = rest // per, rest % per
            spot = (rel * 2 + (core_key ^ core)) * 4 + ((y_key ^ y_at) * 2 + (x_key ^ x_at))
            idx_ref[i * SLOTS + s] = jnp.clip(spot * per + near_key, 0, 24 * per - 1)
            live_ref[i * SLOTS + s] = alive
        return carry

    lax.fori_loop(at["begin"], at["end"], one, 0)


def attend_block(i, idx_ref, live_ref, q_ref, kv, lse_ref):
    qexp = spread_heads(q_ref[pl.ds(pl.multiple_of(i * BLK, BLK), BLK), :], 0)
    at = [idx_ref[i * SLOTS + s] for s in range(SLOTS)]
    off = [jnp.where(live_ref[i * SLOTS + s] > 0, 0.0, -NEG) for s in range(SLOTS)]
    keys = jnp.concatenate([kv[r, :, 0:WIN] for r in at], axis=0)
    values = jnp.concatenate([kv[r, :, 128 : 128 + WIN] for r in at], axis=0)
    raw = nt(keys, qexp)
    parts = [raw[s * BLK : (s + 1) * BLK] for s in range(SLOTS)]
    top = jnp.max(parts[1], axis=0, keepdims=True)
    for s in range(SLOTS):
        top = jnp.maximum(top, jnp.max(parts[s], axis=0, keepdims=True) - off[s])
    e = [jnp.exp(parts[s] - (top + off[s])) for s in range(SLOTS)]
    total = jnp.sum(e[0], axis=0, keepdims=True)
    for s in range(1, SLOTS):
        total = total + jnp.sum(e[s], axis=0, keepdims=True)
    lse_ref[pl.ds(i, 1), :] = top + jnp.log(total)
    scale = 1.0 / total
    probs = jnp.concatenate([(v * scale).astype(jnp.bfloat16) for v in e], axis=0)
    return fold_heads(tn(probs, values), 64).astype(jnp.bfloat16)


def forward_kernel(planes, tok_ref, wq_in, wk_in, wv_in, len_ref, ord_ref, rand_vm, rand_sm, *refs):
    kv_out, q_ref, x_out, ctx_out, lse_ref, idx_ref, live_ref, wq_out, wkv_out, ctx_keep = refs[:10]
    xs, kv, ctx, rand_got, rand_two, w_full, wq_ref, wkv_ref = refs[10:18]
    x_send, x_recv, k_send, k_recv, up_send, up_recv, dn_send, dn_recv = refs[18:26]
    f_send, f_recv, g_send, g_recv, s_sem, o_send, o_recv, r_send, r_recv, l_sem = refs[26:36]
    weights = [
        pltpu.make_async_copy(w, w_full.at[n], l_sem.at[2 + n])
        for n, w in enumerate((wk_in, wv_in, wq_in))
    ]
    for copy in weights:
        copy.start()
    plane, y_at, core, x_at = place()
    piece = tok_ref.shape[0]
    rows = piece // 2
    part = 4 * piece
    by_x = device_at(plane, y_at, core, 1 - x_at)
    by_y = device_at(plane, 1 - y_at, core, x_at)
    by_xy = device_at(plane, 1 - y_at, core, 1 - x_at)
    by_core = device_at(plane, y_at, 1 - core, x_at)
    above = device_at(plane + 1, y_at, core, x_at)
    below = device_at(plane - 1, y_at, core, x_at)
    has_above, has_below = plane < planes - 1, plane > 0
    ring = [device_at(lax.rem(plane + g, planes), y_at, core, x_at) for g in (1, planes - 1)]
    greet([by_x, by_y, by_xy, by_core] + ring)

    def x_rows(c):
        return xs.at[pl.ds((c - 2) * rows, rows)]

    def tok_rows(c):
        return tok_ref.at[pl.ds(c * rows, rows)]

    hops = {
        2: remote(tok_rows(0), x_rows(2), x_send, x_recv, 0, by_x),
        4: remote(tok_rows(0), x_rows(4), x_send, x_recv, 2, by_y),
        3: remote(tok_rows(1), x_rows(3), x_send, x_recv, 1, by_x),
        5: remote(tok_rows(1), x_rows(5), x_send, x_recv, 3, by_y),
        6: remote(x_rows(2), x_rows(6), x_send, x_recv, 4, by_y),
        7: remote(x_rows(5), x_rows(7), x_send, x_recv, 5, by_x),
    }
    rand_trade = remote(rand_vm, rand_got, r_send, r_recv, 0, by_y)
    rand_trade.start()
    for c in (2, 4, 3, 5):
        hops[c].start()

    wq_ref[:, WQ:] = jnp.zeros((wq_ref.shape[0], WIN - WQ), jnp.bfloat16)
    for copy in weights:
        copy.wait()
    for g in range(4):

        @pl.when(y_at * 2 + x_at == g)
        def _(g=g):
            cols = slice(g * WQ, (g + 1) * WQ)
            wkv_ref[:, :WQ] = w_full[0, :, cols]
            wkv_ref[:, WQ:] = w_full[1, :, cols]
            wq_ref[:, :WQ] = w_full[2, :, cols] * jnp.bfloat16(DH ** (-0.5))

    hand_on = [
        pltpu.make_async_copy(wq_ref, wq_out, l_sem.at[5]),
        pltpu.make_async_copy(wkv_ref, wkv_out, l_sem.at[6]),
    ]
    for copy in hand_on:
        copy.start()

    def kv_rows(part_at, c):
        return kv.at[pl.ds((part_at * part + c * rows) // BLK, rows // BLK)]

    to_core, to_above, to_below, pass_up, pass_down = {}, {}, {}, {}, {}
    for c in range(8):
        mine = kv_rows(2, c)
        to_core[c] = remote(mine, kv_rows(3, c), k_send, k_recv, c, by_core)
        to_above[c] = remote(mine, kv_rows(0, c), up_send, up_recv, c, above)
        to_below[c] = remote(mine, kv_rows(4, c), dn_send, dn_recv, c, below)
        pass_up[c] = remote(kv_rows(0, c), kv_rows(1, c), f_send, f_recv, c, by_core)
        pass_down[c] = remote(kv_rows(4, c), kv_rows(5, c), g_send, g_recv, c, by_core)
    keeps = {
        c: pltpu.make_async_copy(
            tok_rows(c) if c < 2 else x_rows(c), x_out.at[pl.ds(c * rows, rows)], s_sem.at[c]
        )
        for c in range(8)
    }

    def relay(c):
        @pl.when(has_below)
        def _():
            to_above[c].wait_recv()
            pass_up[c].start()

        @pl.when(has_above)
        def _():
            to_below[c].wait_recv()
            pass_down[c].start()

    def tables(begin, end):
        slot_tables(
            plane,
            y_at,
            core,
            x_at,
            dict(piece_blocks=piece // BLK, seqs=len_ref.shape[0], begin=begin, end=end),
            len_ref,
            ord_ref,
            rand_sm,
            rand_two,
            idx_ref,
            live_ref,
        )

    query_blocks = part // BLK
    for n, c in enumerate(CHUNK_ORDER):
        if n == 2:
            rand_trade.wait()
            to_scalar = pltpu.make_async_copy(rand_got, rand_two, l_sem.at[0])
            to_scalar.start()
            to_scalar.wait()
            tables(0, query_blocks // 3)
        if n == 4:
            tables(query_blocks // 3, 2 * query_blocks // 3)
        if n == 6:
            tables(2 * query_blocks // 3, query_blocks)
        if c >= 2:
            hops[c].wait_recv()
        if c == 2:
            hops[6].start()
        if c == 5:
            hops[7].start()
        keeps[c].start()
        block = tok_ref[pl.ds(c * rows, rows), :] if c < 2 else xs[pl.ds((c - 2) * rows, rows), :]
        made = jnp.dot(block, wkv_ref[...], preferred_element_type=jnp.float32).astype(jnp.bfloat16)
        kv[pl.ds((2 * part + c * rows) // BLK, rows // BLK)] = made.reshape(rows // BLK, BLK, -1)

        @pl.when(has_above)
        def _(c=c):
            to_above[c].start()

        @pl.when(has_below)
        def _(c=c):
            to_below[c].start()

        to_core[c].start()
        q_ref[pl.ds(c * rows, rows), :] = jnp.dot(
            block, wq_ref[...], preferred_element_type=jnp.float32
        ).astype(jnp.bfloat16)
        if n >= 3:
            relay(CHUNK_ORDER[n - 3])
    for c in CHUNK_ORDER[5:]:
        relay(c)
    for c in range(8):
        to_core[c].wait_recv()

        @pl.when(has_above)
        def _(c=c):
            pass_down[c].wait_recv()

        @pl.when(has_below)
        def _(c=c):
            pass_up[c].wait_recv()

    saved = pltpu.make_async_copy(kv, kv_out, l_sem.at[1])
    saved.start()
    per = piece // BLK

    def part_of(turn):
        middle = turn - 2
        j = jnp.where(turn < 2, 3, jnp.where(turn < 6, 1 + lax.rem(turn, 2), 0))
        half = jnp.where(turn < 2, turn, jnp.where(turn < 6, middle // 2, turn - 6))
        return j, half

    def trade(turn):
        j, half = part_of(turn)
        span = pl.ds(pl.multiple_of(half * rows, rows), rows)
        return remote(
            ctx.at[j, span],
            ctx_out.at[span, pl.ds(pl.multiple_of(j * WIN, WIN), WIN)],
            o_send,
            o_recv,
            turn,
            device_at(plane, y_at ^ (j >> 1), core, x_at ^ (j & 1)),
        )

    def attend_part(turn, carry):
        j, half = part_of(turn)

        def step(n, carry):
            at = pl.ds(pl.multiple_of(n * BLK, BLK), BLK)
            ctx[j, at, :] = attend_block(j * per + n, idx_ref, live_ref, q_ref, kv, lse_ref)
            return carry

        first = half * (per // 2)
        for n in range(per // 2):
            step(first + n, 0)

        @pl.when(turn < 6)
        def _():
            trade(turn).start()

        return carry

    lax.fori_loop(0, 8, attend_part, 0)
    ctx_out[:, 0:WIN] = ctx[0]
    hand_on.append(pltpu.make_async_copy(ctx, ctx_keep, l_sem.at[7]))
    hand_on[-1].start()
    for c in (2, 4, 3, 5, 6, 7):
        hops[c].wait_send()
    for c in range(8):
        to_core[c].wait_send()
        keeps[c].wait()

        @pl.when(has_above)
        def _(c=c):
            to_above[c].wait_send()
            pass_down[c].wait_send()

        @pl.when(has_below)
        def _(c=c):
            to_below[c].wait_send()
            pass_up[c].wait_send()

    saved.wait()
    for copy in hand_on:
        copy.wait()

    def settle(turn, carry):
        trade(turn).wait()
        return carry

    lax.fori_loop(0, 6, settle, 0)


def forward_attention(tokens, w_query, w_key, w_value, lengths, seq_order, rand_row, planes):
    piece, width = tokens.shape
    dma, low = pltpu.SemaphoreType.DMA, jnp.bfloat16
    sds = jax.ShapeDtypeStruct
    blocks = 4 * piece // BLK
    return pl.pallas_call(
        functools.partial(forward_kernel, planes),
        out_shape=[
            sds((24 * piece // BLK, BLK, 2 * WQ), low),
            sds((4 * piece, WIN), low),
            sds((4 * piece, width), low),
            sds((piece, 4 * WIN), low),
            sds((blocks, WQ), jnp.float32),
            sds((blocks * SLOTS,), jnp.int32),
            sds((blocks * SLOTS,), jnp.int32),
            sds((width, WIN), low),
            sds((width, 2 * WQ), low),
            sds((4, piece, WIN), low),
        ],
        in_specs=[VMEM] + [ANY] * 3 + [SMEM] * 2 + [VMEM, SMEM],
        out_specs=[ANY, VMEM, ANY, VMEM, VMEM, SMEM, SMEM, ANY, ANY, ANY],
        scratch_shapes=[
            pltpu.VMEM((3 * piece, width), low),
            pltpu.VMEM((24 * piece // BLK, BLK, 2 * WQ), low),
            pltpu.VMEM((4, piece, WIN), low),
            pltpu.VMEM(rand_row.shape, jnp.int32),
            pltpu.SMEM(rand_row.shape, jnp.int32),
            pltpu.VMEM((3, width, width), low),
            pltpu.VMEM((width, WIN), low),
            pltpu.VMEM((width, 2 * WQ), low),
            dma((6,)),
            dma((6,)),
        ]
        + [dma((8,))] * 11
        + [dma((6,))] * 2
        + [dma((1,))] * 2
        + [dma((8,))],
        compiler_params=pltpu.CompilerParams(
            collective_id=0, has_side_effects=True, vmem_limit_bytes=62 << 20
        ),
        cost_estimate=pl.CostEstimate(
            flops=2 * 4 * piece * width * 640, bytes_accessed=40 << 20, transcendentals=0
        ),
        name="forward_attention",
    )(tokens, w_query, w_key, w_value, lengths, seq_order, rand_row, rand_row)


def attend_back(idx, live, queries, grads, context, level, keys_values):
    rows, width = keys_values.shape[0] // 6, keys_values.shape[1]
    count = queries.shape[0]
    kv_shape = jax.ShapeDtypeStruct((6 * rows, width), jnp.bfloat16)
    return pl.pallas_call(
        backward_kernel,
        out_shape=[jax.ShapeDtypeStruct((count, WIN), jnp.bfloat16)] + [kv_shape],
        in_specs=[SMEM, SMEM, VMEM, VMEM, VMEM, VMEM, ANY],
        out_specs=[VMEM] * 2,
        scratch_shapes=[
            pltpu.VMEM((6 * rows, width), jnp.bfloat16),
            pltpu.VMEM((6 * rows, width), jnp.float32),
            pltpu.SemaphoreType.DMA((1,)),
        ],
        compiler_params=pltpu.CompilerParams(vmem_limit_bytes=62 << 20),
        cost_estimate=pl.CostEstimate(
            flops=2 * 10 * count * 3 * 256 * 512, bytes_accessed=24 * rows * width, transcendentals=count * 3 * 512
        ),
        name="attend_back",
    )(idx, live, queries, grads, context, level, keys_values)


def reduce_kernel(planes, *refs):
    dkv_in, dq_in, x_in, wq_in, wkv_in, one_in = refs[:6]
    pair_in = refs[6:12]
    tok_out, q_out, k_out, v_out, up_out, side_out, norm_out, down_out = refs[12:20]
    own, core_in, z_out, z_in, g_all, dx_out, dx_in, acc = refs[20:28]
    dq, xs, wq, wkv, one = refs[28:33]
    p_slab, p_core, p_z, p_zin, p_fin, p_all = refs[33:39]
    keep, give = refs[39:42], refs[42:45]
    got, two, fin = refs[45:48], refs[48:51], refs[51:54]
    line_out, line_in = refs[54:57], refs[57:60]
    l_sem, i_sem, c_s, c_r, u_s, u_r, d_s, d_r, x_s, x_r = refs[60:70]
    pk_s, pk_r, pz_s, pz_r, pf_s, pf_r = refs[70:76]
    w2_s, w2_r, w3_s, w3_r, w4_s, w4_r, w1_s, w1_r = refs[76:84]
    plane, y_at, core, x_at = place()
    piece = tok_out.shape[0]
    part = 4 * piece
    rest = planes - 1
    group = y_at * 2 + x_at
    low, f32 = jnp.bfloat16, jnp.float32

    def there(j):
        return device_at(plane, y_at ^ (j >> 1), core, x_at ^ (j & 1))

    by_x, by_y = there(1), there(2)
    by_core = device_at(plane, y_at, 1 - core, x_at)
    others = [device_at(lax.rem(plane + g, planes), y_at, core, x_at) for g in range(1, planes)]
    has_above, has_below = plane < planes - 1, plane > 0
    above = device_at(plane + 1, y_at, core, x_at)
    below = device_at(plane - 1, y_at, core, x_at)

    def chunk(base, j):
        return pl.ds(pl.multiple_of(base + j * piece, piece), piece)

    def load_own(turn, r, j):
        return pltpu.make_async_copy(
            dkv_in.at[chunk(2 * r * part, j)], own.at[chunk(r * part, j)], l_sem.at[turn]
        )

    def to_core(turn, r, j):
        return remote(
            dkv_in.at[chunk((2 * r + 1) * part, j)],
            core_in.at[chunk(r * part, j)],
            c_s,
            c_r,
            turn,
            by_core,
        )

    def to_below(j):
        return remote(z_out.at[chunk(0, j)], z_in.at[chunk(0, j)], d_s, d_r, j, below)

    def to_above(j):
        return remote(z_out.at[chunk(part, j)], z_in.at[chunk(part, j)], u_s, u_r, j, above)

    def to_owner(j):
        return remote(dx_out.at[j - 1], dx_in.at[j - 1], x_s, x_r, j - 1, there(j))

    half_piece = piece // 2

    def pass_on(j):
        span = pl.ds((j - 1) * half_piece, half_piece)
        return remote(dx_out.at[2, span], dx_in.at[2, span], x_s, x_r, 1 + j, there(j))

    def take_in(j):
        span = pl.ds((j - 1) * half_piece, half_piece)
        pass_on(j).wait_recv()
        spot = 2 - j
        dx_out[spot, span, :] = (
            dx_out[spot, span, :].astype(f32) + dx_in[2, span, :].astype(f32)
        ).astype(low)
        to_owner(3 - j).start()

    def every(n, action):
        j = 3 - n
        for turn, r in ((n * 2, 0), (n * 2 + 1, 2)):
            action(turn, r, j)

    greet([by_x, by_y, there(3), by_core] + others)

    def begin(n, carry):
        def go(turn, r, j):
            to_core(turn, r, j).start()
            load_own(turn, r, j).start()

        every(n, go)
        return carry

    lax.fori_loop(0, 4, begin, 0)

    def begin_mid(n, carry):
        to_core(8 + n, 1, 3 - n).start()
        load_own(8 + n, 1, 3 - n).start()
        return carry

    lax.fori_loop(0, 4, begin_mid, 0)
    inputs = [(pair_in[2 * n], keep[n]) for n in range(3)]
    inputs += [(pair_in[2 * n + 1], give[n]) for n in (0, 2)]
    inputs += [(wq_in, wq), (wkv_in, wkv), (dq_in, dq), (x_in, xs), (one_in, one)]
    inputs = [pltpu.make_async_copy(src, dst, i_sem.at[n]) for n, (src, dst) in enumerate(inputs)]
    for copy in inputs:
        copy.start()
    w1 = remote(pair_in[3], give[1], w1_s, w1_r, 0, by_y)
    w1.start()

    def both(turn, r, j):
        to_core(turn, r, j).wait_recv()
        load_own(turn, r, j).wait()
        at = chunk(r * part, j)
        return own[at, :].astype(f32) + core_in[at, :].astype(f32)

    def spread(n, carry):
        j = 3 - n
        z_out[chunk(0, j), :] = both(2 * n, 0, j).astype(low)

        @pl.when(jnp.logical_and(has_below, n < 3))
        def _():
            to_below(j).start()

        z_out[chunk(part, j), :] = both(2 * n + 1, 2, j).astype(low)

        @pl.when(jnp.logical_and(has_above, n < 3))
        def _():
            to_above(j).start()

        return carry

    lax.fori_loop(0, 4, spread, 0)

    for copy in inputs[:5]:
        copy.wait()
    halves = [keep[0].shape[2] // 2, keep[1].shape[2] // 2]
    w2 = {}
    for n in (0, 2, 1):
        if n == 1:
            w1.wait()

        def merge(p, carry, n=n):
            keep[n][p] = (keep[n][p].astype(f32) + give[n][p].astype(f32)).astype(low)
            return carry

        lax.fori_loop(0, planes, merge, 0)
        if n < 2:
            cols = pl.ds(pl.multiple_of((1 - x_at) * halves[n], 128), halves[n])
            w2[n] = remote(keep[n].at[:, :, cols], got[n], w2_s, w2_r, n, by_x)
        else:
            w2[n] = remote(keep[n].at[:, 1 - y_at], got[n], w2_s, w2_r, n, by_y)
        w2[n].start()
    for copy in inputs[5:]:
        copy.wait()
    acc[...] = jnp.zeros_like(acc)

    def arrive(n):
        j = 3 - n
        g_all[:, 2 * WQ :] = dq[chunk(0, j), :]
        g_all[:, : 2 * WQ] = both(8 + n, 1, j).astype(low)

        @pl.when(has_above)
        def _():
            to_below(j).wait_recv()
            g_all[:, : 2 * WQ] = (
                g_all[:, : 2 * WQ].astype(f32) + z_in[chunk(0, j), :].astype(f32)
            ).astype(low)

        @pl.when(has_below)
        def _():
            to_above(j).wait_recv()
            g_all[:, : 2 * WQ] = (
                g_all[:, : 2 * WQ].astype(f32) + z_in[chunk(part, j), :].astype(f32)
            ).astype(low)

    def back(j):
        grads = g_all[...]
        return nt(grads[:, 2 * WQ :], wq[...]) + nt(grads[:, : 2 * WQ], wkv[...])

    def outer(j):
        acc[...] += tn(xs[chunk(0, j), :], g_all[...])

    def turn_back(n, carry):
        arrive(n)
        dx_out[2 - n] = back(3 - n).astype(low)
        outer(3 - n)
        return carry

    turn_back(0, 0)
    pass_on(1).start()
    pass_on(2).start()
    turn_back(1, 0)

    for n in range(3):
        w2[n].wait_recv()

        def halve(p, carry, n=n):
            if n < 2:
                cols = pl.ds(pl.multiple_of(x_at * halves[n], 128), halves[n])
                mine = keep[n][p, :, cols]
            else:
                mine = keep[n][p, y_at]
            two[n][p] = (mine.astype(f32) + got[n][p].astype(f32)).astype(low)
            return carry

        lax.fori_loop(0, planes, halve, 0)

    def line_copy(n, way, t):
        return remote(
            line_out[n].at[way, t],
            line_in[n].at[way, t],
            w3_s,
            w3_r,
            (n * 2 + way) * rest + t,
            below if way else above,
        )

    def line_step(t):
        for n in range(3):
            for way in range(2):
                spot = (planes - 1 - plane) if way else plane
                gap = planes - 1 - t
                slab = (plane - gap) if way else (plane + gap)
                sends = jnp.logical_and(t >= spot, spot < planes - 1)

                @pl.when(jnp.logical_and(sends, spot == 0))
                def _():
                    line_out[n][way, t] = two[n][slab]
                    line_copy(n, way, t).start()

                @pl.when(jnp.logical_and(sends, spot > 0))
                def _():
                    line_copy(n, way, t - 1).wait_recv()
                    line_out[n][way, t] = (
                        two[n][slab].astype(f32) + line_in[n][way, t - 1].astype(f32)
                    ).astype(low)
                    line_copy(n, way, t).start()

    line_step(0)

    @pl.when(has_below)
    def _():
        to_below(0).start()

    @pl.when(has_above)
    def _():
        to_above(0).start()

    take_in(1)
    turn_back(2, 0)
    take_in(2)
    if planes > 2:
        line_step(1)
    arrive(3)
    outer(0)

    share = p_slab.shape[3]
    acc[:, 2 * WQ :] *= DH ** (-0.5)
    for p in range(planes):
        for y in range(2):
            for k in range(2):
                at = ((p * 2 + y) * 2 + k) * share
                p_slab[k, p, y] = acc[at : at + share, :].astype(low)
    pk = remote(p_slab.at[1 - core], p_core, pk_s, pk_r, 0, by_core)
    pk.start()
    tok_out[...] = one[...] + back(0)
    pk.wait_recv()

    def merge_core(p, carry):
        p_z[p] = (p_slab[core, p].astype(f32) + p_core[p].astype(f32)).astype(low)
        return carry

    lax.fori_loop(0, planes, merge_core, 0)
    pz = [
        remote(
            p_z.at[lax.rem(plane + g, planes)], p_zin.at[g - 1], pz_s, pz_r, g - 1, others[g - 1]
        )
        for g in range(1, planes)
    ]

    def next_step(t, carry):
        line_step(t)
        return carry

    lax.fori_loop(2, planes - 1, next_step, 0)
    for copy in pz:
        copy.start()
    w4 = []
    for n in range(3):
        fin[n][x_at] = two[n][plane]

        @pl.when(has_below)
        def _(n=n):
            line_copy(n, 0, rest - 1).wait_recv()
            fin[n][x_at] = (
                fin[n][x_at].astype(f32) + line_in[n][0, rest - 1].astype(f32)
            ).astype(low)

        @pl.when(has_above)
        def _(n=n):
            line_copy(n, 1, rest - 1).wait_recv()
            fin[n][x_at] = (
                fin[n][x_at].astype(f32) + line_in[n][1, rest - 1].astype(f32)
            ).astype(low)

        w4.append(remote(fin[n].at[x_at], fin[n].at[x_at], w4_s, w4_r, n, by_x))
        w4[n].start()

    for j in (2, 1):
        to_owner(j).wait_recv()
        tok_out[...] += dx_in[j - 1].astype(f32)

    for copy in list(w2.values()) + [pk]:
        copy.wait_send()

    def settle(n, carry):
        every(n, lambda turn, r, j: to_core(turn, r, j).wait_send())
        to_core(8 + n, 1, 3 - n).wait_send()

        @pl.when(has_below)
        def _():
            to_below(3 - n).wait_send()

        @pl.when(has_above)
        def _():
            to_above(3 - n).wait_send()

        return carry

    lax.fori_loop(0, 4, settle, 0)
    for j in (1, 2):
        to_owner(j).wait_send()
        pass_on(j).wait_send()

    def settle_line(t, carry):
        for n in range(3):
            for way in range(2):
                spot = (planes - 1 - plane) if way else plane

                @pl.when(jnp.logical_and(t >= spot, spot < planes - 1))
                def _():
                    line_copy(n, way, t).wait_send()

        return carry

    lax.fori_loop(0, planes - 1, settle_line, 0)

    total = p_z[plane].astype(f32)
    for g in range(1, planes):
        pz[g - 1].wait_recv()
        total = total + p_zin[g - 1].astype(f32)
    p_fin[...] = total.astype(low)
    pf = [
        remote(p_fin.at[y_at ^ (j >> 1)], p_all.at[j], pf_s, pf_r, j - 1, there(j))
        for j in (1, 2, 3)
    ]
    for copy in pf:
        copy.start()
    p_all[0] = p_fin[y_at]

    for n, dest in ((0, up_out), (2, down_out)):
        w4[n].wait()
        width = dest.shape[1] // 2
        for side in range(2):
            dest[:, side * width : (side + 1) * width] = fin[n][side].astype(f32)
    w4[1].wait()
    width = side_out.shape[1] // 2
    for side in range(2):
        done = fin[1][side].astype(f32)
        side_out[:, side * width : (side + 1) * width] = done[:share]
        norm_out[:, side * width : (side + 1) * width] = done[share : share + 8]

    for copy in pf:
        copy.wait()
    for a in range(4):
        grads = p_all[a ^ group].astype(f32)
        for n, dest in enumerate((k_out, v_out, q_out)):
            dest[:, a * WQ : (a + 1) * WQ] = grads[:, n * WQ : (n + 1) * WQ]
    for copy in pz:
        copy.wait_send()


def reduce_all(dkv, dq, stretch, wq, wkv, one, up, out, down, planes):
    low, f32 = jnp.bfloat16, jnp.float32
    piece = dq.shape[0] // 4
    width = stretch.shape[1]
    share = up[0].shape[1]
    rest = planes - 1
    dma, vm, sds = pltpu.SemaphoreType.DMA, pltpu.VMEM, jax.ShapeDtypeStruct
    cols = 2 * WQ + WIN
    tall = out[0].shape[1]
    wide = up[0].shape[2]
    kinds = [(share, wide // 2), (tall, width // 2), down[0].shape[2:]]
    pairs = [up[0].shape, out[0].shape, down[0].shape]
    return pl.pallas_call(
        functools.partial(reduce_kernel, planes),
        out_shape=[sds((piece, width), f32)]
        + [sds((share, width), f32)] * 3
        + [
            sds((share, wide), f32),
            sds((share, width), f32),
            sds((8, width), f32),
            sds((kinds[2][0], width), f32),
        ],
        in_specs=[ANY] * 12,
        out_specs=[VMEM] * 8,
        scratch_shapes=[
            vm((12 * piece, 2 * WQ), low),
            vm((12 * piece, 2 * WQ), low),
            vm((8 * piece, 2 * WQ), low),
            vm((8 * piece, 2 * WQ), low),
            vm((piece, cols), low),
            vm((3, piece, width), low),
            vm((3, piece, width), low),
            vm((width, cols), f32),
            vm(dq.shape, low),
            vm(stretch.shape, low),
            vm(wq.shape, low),
            vm(wkv.shape, low),
            vm(one.shape, f32),
            vm((2, planes, 2, share, cols), low),
            vm((planes, 2, share, cols), low),
            vm((planes, 2, share, cols), low),
            vm((rest, 2, share, cols), low),
            vm((2, share, cols), low),
            vm((4, share, cols), low),
        ]
        + [vm(p, low) for p in pairs] * 2
        + [vm((planes,) + k, low) for k in kinds] * 2
        + [vm((2,) + k, low) for k in kinds]
        + [vm((2, rest) + k, low) for k in kinds] * 2
        + [dma((12,)), dma((11,))]
        + [dma((12,))] * 2
        + [dma((4,))] * 6
        + [dma((1,))] * 2
        + [dma((rest,))] * 2
        + [dma((3,))] * 2
        + [dma((3,))] * 2
        + [dma((6 * rest,))] * 2
        + [dma((3,))] * 2
        + [dma((1,))] * 2,
        compiler_params=pltpu.CompilerParams(
            collective_id=1, has_side_effects=True, vmem_limit_bytes=60 << 20
        ),
        cost_estimate=pl.CostEstimate(
            flops=4 * 4 * piece * width * cols, bytes_accessed=40 << 20, transcendentals=0
        ),
        name="reduce_all",
    )(dkv, dq, stretch, wq, wkv, one, up[0], up[1], out[0], out[1], down[0], down[1])


def dense_kernel(
    planes,
    tok_ref,
    ctx_ref,
    cot_ref,
    g1_ref,
    b1_ref,
    g2_ref,
    b2_ref,
    wout_in,
    wup_in,
    wdown_in,
    *refs,
):
    out_ref, one_ref, do_out, up_keep, up_give, out_keep, out_give, down_keep, down_give = refs[:9]
    wup, wdown, acc, x1, s1, g_two, nl, hid, slope, gp, gm, ga = refs[9:21]
    dctx, up_loc, out_loc, down_loc, up_got, out_got, down_got, down_sum = refs[21:29]
    w_sem, mv_sem, do_s, do_r, up_s, up_r, out_s, out_r, down_s, down_r = refs[29:39]
    wout_ref = refs[39]
    plane, y_at, core, x_at = place()
    piece, width = tok_ref.shape
    share = up_loc.shape[2]
    slab = down_loc.shape[2]
    pairs = 2 * planes
    group = y_at * 2 + x_at
    f32 = jnp.float32
    fetch = [
        pltpu.make_async_copy(
            wout_in.at[pl.ds(pl.multiple_of((group ^ j) * WQ, WQ), WQ)],
            wout_ref.at[pl.ds(j * WIN + WIN - WQ, WQ)],
            w_sem.at[2 + j],
        )
        for j in range(4)
    ]
    for copy in fetch:
        copy.start()
    bring = [
        pltpu.make_async_copy(wup_in, wup, w_sem.at[0]),
        pltpu.make_async_copy(wdown_in, wdown, w_sem.at[1]),
    ]
    for copy in bring:
        copy.start()

    def there(j):
        return device_at(plane, y_at ^ (j >> 1), core, x_at ^ (j & 1))

    by_core = device_at(plane, y_at, 1 - core, x_at)
    height, tile = 32, 2 * WQ
    wide = wup.shape[1]

    def rows_of(n):
        return pl.ds(pl.multiple_of(n * height, height), height)

    def cols_of(n):
        return pl.ds(pl.multiple_of(n * tile, tile), tile)

    def mean(v):
        return jnp.mean(v, axis=1, keepdims=True)

    def fold(v):
        return v[:8] + v[8:16] + v[16:24] + v[24:]

    for j in range(4):
        wout_ref[j * WIN : j * WIN + WIN - WQ, :] = jnp.zeros((WIN - WQ, width), jnp.bfloat16)
    for copy in fetch:
        copy.wait()
    acc[...] = jnp.dot(ctx_ref[...], wout_ref[...], preferred_element_type=f32)
    g1, b1, g2, b2 = (r[...].reshape(1, width) for r in (g1_ref, b1_ref, g2_ref, b2_ref))

    def norm_one(n, carry):
        at = rows_of(n)
        value = tok_ref[at, :].astype(f32) + acc[at, :]
        center = value - mean(value)
        inverse = lax.rsqrt(mean(center * center) + eps_norm)
        hat = center * inverse
        x1[at, :] = hat
        s1[at, :] = jnp.broadcast_to(inverse, (height, 128))
        nl[at, :] = (hat * g1 + b1).astype(jnp.bfloat16)
        return carry

    lax.fori_loop(0, piece // height, norm_one, 0, unroll=4)
    bring[0].wait()

    def expand(n, carry):
        at = pl.ds(pl.multiple_of(n * 768, 768), 768)
        pre = jnp.dot(nl[...], wup[:, at], preferred_element_type=f32)
        square = pre * pre
        bend = jnp.tanh(pre * (0.7978845608028654 + 0.035677408136300125 * square))
        half_up = 0.5 + 0.5 * bend
        value = pre * half_up
        hid[:, at] = value.astype(jnp.bfloat16)
        slope[:, at] = half_up + value * (1.0 - bend) * (
            0.7978845608028654 + 0.10703222440890037 * square
        )
        return carry

    lax.fori_loop(0, wide // 768, expand, 0)
    bring[1].wait()
    acc[...] = jnp.dot(hid[...], wdown[...], preferred_element_type=f32)
    nothing = jnp.zeros((8, width), f32)

    def norm_two(n, carry):
        gain_sum, shift_sum = carry
        at = rows_of(n)
        value = x1[at, :] * g1 + b1 + acc[at, :]
        center = value - mean(value)
        inverse = lax.rsqrt(mean(center * center) + eps_norm)
        hat = center * inverse
        out_ref[at, :] = (hat * g2 + b2).astype(jnp.bfloat16)
        cot = cot_ref[at, :].astype(f32)
        gain_sum, shift_sum = gain_sum + fold(cot * hat), shift_sum + fold(cot)
        up = cot * g2
        grad = inverse * (up - mean(up) - hat * mean(up * hat))
        g_two[at, :] = grad
        gm[at, :] = grad.astype(jnp.bfloat16)
        return gain_sum, shift_sum

    gain_two, shift_two = lax.fori_loop(0, piece // height, norm_two, (nothing, nothing), unroll=4)

    def shrink(n, carry):
        at = pl.ds(pl.multiple_of(n * 768, 768), 768)
        back = nt(gm[...], wdown[at, :])
        gp[:, at] = (back * slope[:, at]).astype(jnp.bfloat16)
        return carry

    lax.fori_loop(0, wide // 768, shrink, 0)
    acc[...] = nt(gp[...], wup[...])

    def norm_three(n, carry):
        gain_sum, shift_sum = carry
        at = rows_of(n)
        grad_in, hat = g_two[at, :] + acc[at, :], x1[at, :]
        gain_sum, shift_sum = gain_sum + fold(grad_in * hat), shift_sum + fold(grad_in)
        up = grad_in * g1
        grad = s1[at, 0:1] * (up - mean(up) - hat * mean(up * hat))
        one_ref[at, :] = grad
        ga[at, :] = grad.astype(jnp.bfloat16)
        return gain_sum, shift_sum

    gain_one, shift_one = lax.fori_loop(
        0, piece // height, norm_three, (nothing, nothing), unroll=4
    )
    side = jnp.concatenate(
        [jnp.sum(v, axis=0, keepdims=True) for v in (gain_one, shift_one, gain_two, shift_two)]
        + [jnp.zeros((12, width), f32)],
        axis=0,
    ).astype(jnp.bfloat16)

    low = jnp.bfloat16
    greet([there(1), there(2), there(3), by_core])
    trades = []
    for j in (3, 1, 2, 0):
        part = nt(ga[...], wout_ref[pl.ds(j * WIN, WIN), :]).astype(low)
        if j:
            dctx[j - 1] = part
            trades.append(
                remote(
                    dctx.at[j - 1], do_out.at[pl.ds(j * piece, piece)], do_s, do_r, j - 1, there(j)
                )
            )
            trades[-1].start()
        else:
            do_out[pl.ds(0, piece), :] = part

    tile = 2 * WQ
    per = tile // (2 * slab)
    tiles = wide // tile

    def down_copy(t):
        span = pl.ds(t * per, per)
        return remote(down_loc.at[1 - core, span], down_got.at[span], down_s, down_r, t, by_core)

    def up_copy(t):
        span = cols_of(t)
        return remote(
            up_loc.at[1 - core, :, :, span], up_got.at[:, :, span], up_s, up_r, t, by_core
        )

    def make_down(t, carry):
        cell = tn(hid[:, cols_of(t)], gm[...])
        for n in range(per):
            for k in range(2):
                at = (n * 2 + k) * slab
                down_loc[k, t * per + n] = cell[at : at + slab].astype(low)
        down_copy(t).start()
        return carry

    lax.fori_loop(0, tiles, make_down, 0)

    def make_up(t, carry):
        cell = tn(nl[...], gp[:, cols_of(t)])
        for q in range(pairs):
            for k in range(2):
                at = (q * 2 + k) * share
                up_loc[k, q, :, cols_of(t)] = cell[at : at + share].astype(low)
        up_copy(t).start()
        return carry

    lax.fori_loop(0, tiles, make_up, 0)
    moved = []

    def move(source, dest):
        moved.append(pltpu.make_async_copy(source, dest, mv_sem.at[len(moved)]))
        moved[-1].start()

    half = width // 2

    def sum_down(t, carry):
        down_copy(t).wait_recv()
        for n in range(per):
            q = t * per + n
            total = (
                down_loc[core, q].astype(jnp.float32) + down_got[q].astype(jnp.float32)
            ).astype(low)
            down_sum[0, q] = total[:, :half]
            down_sum[1, q] = total[:, half:]
        return carry

    lax.fori_loop(0, tiles, sum_down, 0)
    move(down_sum.at[x_at], down_keep)
    move(down_sum.at[1 - x_at], down_give)

    per_group = pairs // 4
    for j in range(4):
        cell = tn(ctx_ref[:, j * WIN : (j + 1) * WIN], ga[...])
        for n in range(per_group):
            for k in range(2):
                at = WIN - WQ + (n * 2 + k) * share
                out_loc[k, (group ^ j) * per_group + n, :share, :] = cell[at : at + share].astype(low)
    for q in range(pairs):
        for k in range(2):
            out_loc[k, q, share:, :] = side
    outs = remote(out_loc.at[1 - core], out_got, out_s, out_r, 0, by_core)
    outs.start()

    def sum_up(q, carry):
        up_got[q] = (up_loc[core, q].astype(jnp.float32) + up_got[q].astype(jnp.float32)).astype(low)
        return carry

    for t in range(tiles):
        up_copy(t).wait_recv()
    lax.fori_loop(0, pairs, sum_up, 0)
    outs.wait_recv()
    for p in range(planes):
        for y in range(2):
            q = p * 2 + y
            out_got[q] = (
                out_loc[core, q].astype(jnp.float32) + out_got[q].astype(jnp.float32)
            ).astype(low)
        for got, keep, give in ((up_got, up_keep, up_give), (out_got, out_keep, out_give)):
            move(got.at[p * 2 + y_at], keep.at[p])
            move(got.at[p * 2 + 1 - y_at], give.at[p])
    for copy in trades:
        copy.wait()
    for t in range(tiles):
        down_copy(t).wait_send()
        up_copy(t).wait_send()
    outs.wait_send()
    for copy in moved:
        copy.wait()


def dense_layers(tokens, ctx, cotangent, norms, wout, w_up, w_down, planes):
    low = jnp.bfloat16
    piece, width = tokens.shape
    pairs = 2 * planes
    wide = w_up.shape[1]
    share, slab, tall = width // (2 * pairs), wide // (2 * pairs), 16
    sds, vm, dma = jax.ShapeDtypeStruct, pltpu.VMEM, pltpu.SemaphoreType.DMA
    up, out = (planes, share, wide), (planes, share + tall, width)
    down = (pairs, slab, width // 2)
    tiles = wide // (2 * WQ)
    f32 = jnp.float32
    return pl.pallas_call(
        functools.partial(dense_kernel, planes),
        out_shape=[sds((piece, width), low), sds((piece, width), f32), sds((4 * piece, WIN), low)]
        + [sds(up, low)] * 2
        + [sds(out, low)] * 2
        + [sds(down, low)] * 2,
        in_specs=[VMEM] * 7 + [ANY] * 3,
        out_specs=[VMEM] * 3 + [ANY] * 6,
        scratch_shapes=[
            vm(w_up.shape, low),
            vm(w_down.shape, low),
            vm((piece, width), f32),
            vm((piece, width), f32),
            vm((piece, 128), f32),
            vm((piece, width), f32),
            vm((piece, width), low),
            vm((piece, wide), low),
            vm((piece, wide), f32),
            vm((piece, wide), low),
            vm((piece, width), low),
            vm((piece, width), low),
            vm((3, piece, WIN), low),
            vm((2, pairs, share, wide), low),
            vm((2, pairs, share + tall, width), low),
            vm((2, pairs, slab, width), low),
            vm((pairs, share, wide), low),
            vm((pairs, share + tall, width), low),
            vm((pairs, slab, width), low),
            vm((2, pairs, slab, width // 2), low),
            dma((6,)),
            dma((2 + 4 * planes,)),
        ]
        + [dma((3,))] * 2
        + [dma((tiles,))] * 2
        + [dma((1,))] * 2
        + [dma((tiles,))] * 2
        + [vm((4 * WIN, width), low)],
        compiler_params=pltpu.CompilerParams(
            collective_id=2, has_side_effects=True, vmem_limit_bytes=63 << 20
        ),
        cost_estimate=pl.CostEstimate(
            flops=2 * piece * width * (6 * wide + 3072), bytes_accessed=30 << 20, transcendentals=0
        ),
        name="dense_layers",
    )(tokens, ctx, cotangent, *norms, wout, w_up, w_down)


def finish_kernel(share, count, *refs):
    sources, rows_ref, dests = refs[:count], refs[count], refs[count + 1 : 2 * count + 1]
    parts = refs[2 * count + 1 : 2 * count + 5]
    held, sems = refs[2 * count + 5 : 3 * count + 5], refs[3 * count + 5]
    reads = [pltpu.make_async_copy(sources[n], held[n], sems.at[0, n]) for n in range(count)]
    writes = [pltpu.make_async_copy(held[n], dests[n], sems.at[1, n]) for n in range(count)]
    for copy in reads:
        copy.start()
    for n in range(count):
        reads[n].wait()
        writes[n].start()
    seq_at = lax.axis_index("seq")
    rows = rows_ref[...]
    width = rows.shape[1]
    spot = lax.broadcasted_iota(jnp.int32, (width, 128), 0) - seq_at * share
    chosen = (spot == lax.broadcasted_iota(jnp.int32, (width, 128), 1)).astype(jnp.float32)
    picked = jnp.dot(
        rows, chosen, preferred_element_type=jnp.float32, precision=lax.Precision.HIGHEST
    )
    for n in range(4):
        parts[n][...] = picked[n, :share]
    for copy in writes:
        copy.wait()


def finish(arrays, norm_rows, share):
    sds, count = jax.ShapeDtypeStruct, len(arrays)
    return pl.pallas_call(
        functools.partial(finish_kernel, share, count),
        out_shape=[sds(v.shape, v.dtype) for v in arrays] + [sds((share,), jnp.float32)] * 4,
        in_specs=[ANY] * count + [VMEM],
        out_specs=[ANY] * count + [VMEM] * 4,
        scratch_shapes=[pltpu.VMEM(v.shape, v.dtype) for v in arrays]
        + [pltpu.SemaphoreType.DMA((2, count))],
        compiler_params=pltpu.CompilerParams(vmem_limit_bytes=62 << 20),
        name="finish",
    )(*arrays, norm_rows)


def body(
    tokens,
    w_query,
    w_key,
    w_value,
    w_out,
    gain_attn,
    shift_attn,
    w_up,
    w_down,
    gain_mlp,
    shift_mlp,
    cotangent,
    lengths,
    seq_order,
    rand_blocks,
):
    piece, width = tokens.shape
    seqs, heads = lax.axis_size("seq"), lax.axis_size("head")
    planes = seqs // 4
    assert heads == 2 and 8 * piece == MAXB * BLK and width == 4 * WQ
    seq_at, x_at = lax.axis_index("seq"), lax.axis_index("head")
    plane, y_at, core = seq_at // 4, (seq_at // 2) % 2, seq_at % 2
    group = y_at * 2 + x_at

    keys_values, queries, stretch, context_tok, level, idx, live, wq_own, wkv_own, ctx_own = (
        forward_attention(
            tokens, w_query, w_key, w_value, lengths, seq_order, rand_blocks.T, planes
        )
    )
    share = width // seqs
    norms = [gain_attn, shift_attn, gain_mlp, shift_mlp]
    output, grad_one, grad_ctx, up_keep, up_give, out_keep, out_give, down_keep, down_give = (
        dense_layers(tokens, context_tok, cotangent, norms, w_out, w_up, w_down, planes)
    )
    up_pair = (up_keep, xor_swap(up_give, 4))
    out_pair = (out_keep, out_give)
    two_y = (planes, 2) + down_keep.shape[1:]
    down_pair = (down_keep.reshape(two_y), xor_swap(down_give, 1).reshape(two_y))

    grad_q, grad_kv = attend_back(
        idx,
        live,
        queries,
        grad_ctx,
        ctx_own.reshape(-1, WIN),
        level,
        keys_values.reshape(-1, 2 * WQ),
    )
    grad_tokens, grad_wq, grad_wk, grad_wv, up_total, out_total, norm_rows, down_total = reduce_all(
        grad_kv,
        grad_q,
        stretch,
        wq_own,
        wkv_own,
        grad_one,
        up_pair,
        out_pair,
        down_pair,
        planes,
    )

    finals = finish(
        (output, grad_tokens, grad_wq, grad_wk, grad_wv, out_total, up_total, down_total),
        norm_rows,
        share,
    )

    output, grad_tokens, grad_wq, grad_wk, grad_wv, grad_out, grad_up, grad_down = finals[:8]
    gain_one, shift_one, gain_two, shift_two = finals[8:]
    return (
        output,
        grad_tokens,
        grad_wq,
        grad_wk,
        grad_wv,
        grad_out,
        gain_one,
        shift_one,
        grad_up,
        grad_down,
        gain_two,
        shift_two,
    )


def solution(mesh):
    rows = P(("seq", "head"), None)
    seq_rows, seq_only = P("seq", None), P("seq")
    return jax.shard_map(
        body,
        mesh=mesh,
        in_specs=(rows,) + (P(),) * 10 + (rows, P(), P(), seq_rows),
        out_specs=(
            rows,
            rows,
            seq_rows,
            seq_rows,
            seq_rows,
            seq_rows,
            seq_only,
            seq_only,
            seq_rows,
            seq_rows,
            seq_only,
            seq_only,
        ),
        check_vma=False,
    )
```
